32 devices in a mesh: gx: 16 (over z, x, core), gz: 2 (over y).
Axes of the slice: x: 2, y: 2, z: 4, core: 2. Of those that a mesh axis runs over, the one named last changes fastest.
Arguments:
- saved_flow_speed_vector: bfloat16 [2, 3, 64, 32, 256], P(None, None, 'gx', None, 'gz'), may hold values from -11 to 11
- saved_mass_concentration: bfloat16 [2, 64, 32, 256], P(None, 'gx', None, 'gz'), may hold values from 0.5 to 2
- saved_thermal_excess: bfloat16 [2, 64, 32, 256], P(None, 'gx', None, 'gz'), may hold values from -5 to 5
- costate_vector_subsequent: float32 [5, 64, 32, 256], P(None, 'gx', None, 'gz'), may hold values from -6 to 6
Outputs:
- adjoint_out: float32 [5, 64, 32, 256], P(None, 'gx', None, 'gz')
- coef_grad: float32 [2, 64, 32], P(None, 'gx')
The draws below stay inside these ranges and needn't reach their ends.
All inputs are finite; a program needn't handle non-finite values.
Results may differ from the reference program's by a relative error of at most 0.00065.
Values may be sent and summed in bfloat16 or wider, within the bound.
No kernel may reach another device: no remote copies, remote signals or barrier semaphores. Data moves between devices by JAX's collectives and lax.ppermute only.
A program may use at most 64 MiB of HBM per device.

```python
import math
import jax
import jax.numpy as jnp
from jax import lax

CX = 4
WALLWARD_GRID = 32
REVERSE_MARCHES = 2
DOWNWIND_GRID = 64
LATERAL_GRID = 256


def draw_saved_flow_speed_vector(key, part):
    key_noise, key_scale = jax.random.split(key)
    full_shape = (REVERSE_MARCHES, 3, DOWNWIND_GRID, WALLWARD_GRID, LATERAL_GRID)
    span_pos = jnp.arange(LATERAL_GRID, dtype=jnp.float32) / (LATERAL_GRID - 1)
    envelope = jnp.exp(math.log(3.0) * (0.5 * span_pos - 0.25))
    noise_part = jax.random.truncated_normal(key_noise, -4.0, 4.0, full_shape, jnp.float32)
    scales = jnp.exp(jax.random.uniform(key_scale, (REVERSE_MARCHES, 3, DOWNWIND_GRID, WALLWARD_GRID, 1), jnp.float32, -0.7, 0.7))
    values = noise_part * scales * envelope
    return values.astype(jnp.bfloat16)


def block_scale(rng, shape, cuts, low, high):
    level, own = 1.0, jax.random.fold_in(rng, 6)
    for axis_at, shards_of in cuts:
        draws = jnp.exp(jax.random.uniform(jax.random.fold_in(own, axis_at), (shards_of,), jnp.float32, low / len(cuts), high / len(cuts)))
        level = level * jnp.repeat(draws, shape[axis_at] // shards_of).reshape([-1 if axis == axis_at else 1 for axis in range(len(shape))])
    return level


def bell_draw(rng, shape, spread, bound, pieces=(), kind=jnp.bfloat16):
    result = spread * jax.random.normal(rng, shape, jnp.float32)
    if pieces:
        result = result * block_scale(rng, shape, pieces, -0.22, 0.18)
    return jnp.clip(result, -bound, bound).astype(kind)


def setup_inputs(seed: int = 0) -> dict:
    keys = jax.random.split(jax.random.key(seed), 5)
    saved_flow_speed_vector = draw_saved_flow_speed_vector(jax.random.fold_in(keys[4], 71), 0)
    saved_mass_concentration = jnp.clip(jnp.exp(math.log(2.0) - 1.3862944 * jax.random.uniform(keys[1], (REVERSE_MARCHES, DOWNWIND_GRID, WALLWARD_GRID, LATERAL_GRID), jnp.float32) ** block_scale(keys[1], (REVERSE_MARCHES, DOWNWIND_GRID, WALLWARD_GRID, LATERAL_GRID), ((1, 16), (3, 2)), -0.2, 0.2)), 0.5, 2.0).astype(jnp.bfloat16)
    saved_thermal_excess = bell_draw(keys[2], (REVERSE_MARCHES, DOWNWIND_GRID, WALLWARD_GRID, LATERAL_GRID), 1.0, 5.0, ((1, 16), (3, 2)))
    costate_vector_subsequent = bell_draw(keys[3], (5, DOWNWIND_GRID, WALLWARD_GRID, LATERAL_GRID), 1.0, 6.0, ((1, 16), (3, 2)), jnp.float32)
    return {"saved_flow_speed_vector": saved_flow_speed_vector, "saved_mass_concentration": saved_mass_concentration, "saved_thermal_excess": saved_thermal_excess, "costate_vector_subsequent": costate_vector_subsequent}


PAIRS = ((0, 0), (1, 1), (2, 2), (0, 1), (0, 2), (1, 2))
WEIGHTS = (1.0, 1.0, 1.0, 2.0, 2.0, 2.0)
EPSILON = 1e-06
NU_MOL = 0.05
PRANDTL = 0.72
PRANDTL_TURB = 0.9
TIME_STEP = 0.04

def trimmed(values, offset_x, offset_z, margin):
    size_x = values.shape[-3]
    size_z = values.shape[-1]
    return values[..., margin + offset_x:size_x - margin + offset_x, :, margin + offset_z:size_z - margin + offset_z]

def deriv_x(values, margin):
    return (8.0 * (trimmed(values, 1, 0, margin) - trimmed(values, -1, 0, margin)) - (trimmed(values, 2, 0, margin) - trimmed(values, -2, 0, margin))) / 12.0

def deriv_z(values, margin):
    return (8.0 * (trimmed(values, 0, 1, margin) - trimmed(values, 0, -1, margin)) - (trimmed(values, 0, 2, margin) - trimmed(values, 0, -2, margin))) / 12.0

def wall_shifts(center):
    zeros_row = jnp.zeros(center.shape[:-2] + (1,) + center.shape[-1:], jnp.float32)
    shifted_up = jnp.concatenate([center[..., 1:, :], zeros_row], axis=-2)
    shifted_down = jnp.concatenate([zeros_row, center[..., :-1, :]], axis=-2)
    return (shifted_up, shifted_down)

def deriv_y(center):
    shifted_up, shifted_down = wall_shifts(center)
    return 0.5 * (shifted_up - shifted_down)

def laplace(values, margin):
    center = trimmed(values, 0, 0, margin)
    shifted_up, shifted_down = wall_shifts(center)
    neighbours = trimmed(values, 1, 0, margin) + trimmed(values, -1, 0, margin) + trimmed(values, 0, 1, margin) + trimmed(values, 0, -1, margin)
    return neighbours + shifted_up + shifted_down - 6.0 * center

def gradients(saved_primal_fields, margin):
    return jnp.stack([deriv_x(saved_primal_fields, margin), deriv_y(trimmed(saved_primal_fields, 0, 0, margin)), deriv_z(saved_primal_fields, margin)])

def strain_parts(gradient):
    return [0.5 * (gradient[index_a, index_b] + gradient[index_b, index_a]) for index_a, index_b in PAIRS]

def norm_of(components):
    running = 0.0
    for weight, component in zip(WEIGHTS, components):
        running = running + weight * component * component
    return jnp.sqrt(2.0 * running + EPSILON)

def filter_inputs(center, gradient):
    components = strain_parts(gradient)
    strain_size = norm_of(components)
    velocity = [center[0], center[1], center[2]]
    products = [velocity[index_a] * velocity[index_b] for index_a, index_b in PAIRS]
    scaled = [strain_size * component for component in components]
    return (jnp.stack(velocity + products + components + scaled), strain_size)

def smooth(values):
    size_x = values.shape[-3]
    along_x = 0.25 * values[..., :size_x - 2, :, :] + 0.5 * values[..., 1:size_x - 1, :, :] + 0.25 * values[..., 2:, :, :]
    size_z = along_x.shape[-1]
    return 0.25 * along_x[..., :size_z - 2] + 0.5 * along_x[..., 1:size_z - 1] + 0.25 * along_x[..., 2:]

def germano_partials(filtered):
    hat_strain = [filtered[9 + number] for number in range(6)]
    hat_size = norm_of(hat_strain)
    cross_sum = 0.0
    square_sum = 0.0
    for number in range(6):
        index_a, index_b = PAIRS[number]
        leonard = filtered[3 + number] - filtered[index_a] * filtered[index_b]
        model_term = filtered[15 + number] - 4.0 * hat_size * hat_strain[number]
        cross_sum = cross_sum + WEIGHTS[number] * leonard * model_term
        square_sum = square_sum + WEIGHTS[number] * model_term * model_term
    return jnp.stack([lax.optimization_barrier(jnp.sum(cross_sum, axis=-1)), lax.optimization_barrier(jnp.sum(square_sum, axis=-1))])

def forward_terms(saved_primal_fields, margin):
    center = trimmed(saved_primal_fields, 0, 0, margin)
    lap_vel = laplace(saved_primal_fields[0:3], margin)
    lap_temp = laplace(saved_primal_fields[4], margin)
    inv_rho = 1.0 / center[3]
    return (center, lap_vel, lap_temp, inv_rho)

def coef_partial(terms, strain_size, adjoint):
    center, lap_vel, lap_temp, inv_rho = terms
    work_term = adjoint[0] * lap_vel[0] + adjoint[1] * lap_vel[1] + adjoint[2] * lap_vel[2] + adjoint[4] * lap_temp / PRANDTL_TURB
    return lax.optimization_barrier(jnp.sum(strain_size * work_term * inv_rho, axis=-1))

def adjoint_update(terms, gradient, strain_size, model_coef, adjoint_pad):
    center, lap_vel, lap_temp, inv_rho = terms
    adjoint = trimmed(adjoint_pad, 0, 0, 2)
    eddy_visc = model_coef[:, :, None] * strain_size
    mu_mom = NU_MOL + eddy_visc
    mu_heat = NU_MOL / PRANDTL + eddy_visc / PRANDTL_TURB
    advect = center[0] * deriv_x(adjoint_pad, 2) + center[1] * deriv_y(adjoint) + center[2] * deriv_z(adjoint_pad, 2)
    lap_adj = laplace(adjoint_pad, 2)
    source_mom = lax.optimization_barrier(jnp.sum(gradient * adjoint[None], axis=1))
    new_mom = adjoint[0:3] + TIME_STEP * (advect[0:3] + mu_mom * inv_rho * lap_adj[0:3] + source_mom)
    work_term = mu_mom * (adjoint[0] * lap_vel[0] + adjoint[1] * lap_vel[1] + adjoint[2] * lap_vel[2]) + mu_heat * adjoint[4] * lap_temp
    new_rho = adjoint[3] + TIME_STEP * (advect[3] - work_term * inv_rho * inv_rho)
    new_temp = adjoint[4] + TIME_STEP * (advect[4] + mu_heat * inv_rho * lap_adj[4])
    return jnp.concatenate([new_mom, new_rho[None], new_temp[None]], axis=0)

def reference(saved_flow_speed_vector, saved_mass_concentration, saved_thermal_excess, costate_vector_subsequent):
    adjoint = costate_vector_subsequent
    blocks = DOWNWIND_GRID // CX
    block_ids = jnp.arange(blocks, dtype=jnp.int32)
    coef_grads = []
    for march_index in range(REVERSE_MARCHES):
        saved_primal_fields = jnp.concatenate([saved_flow_speed_vector[march_index], saved_mass_concentration[march_index][None], saved_thermal_excess[march_index][None]], axis=0).astype(jnp.float32)
        forward_pad = jnp.pad(saved_primal_fields, ((0, 0), (3, 3), (0, 0), (3, 3)), mode='wrap')

        def partial_block(index):
            block = lax.dynamic_slice_in_dim(forward_pad, index * CX, CX + 6, 1)
            gradient_rim = gradients(block, 2)
            inputs_rim, size_rim = filter_inputs(trimmed(block, 0, 0, 2), gradient_rim)
            return germano_partials(smooth(inputs_rim))
        partials = lax.map(partial_block, block_ids)
        germano = jnp.transpose(partials, (1, 0, 2, 3)).reshape(2, DOWNWIND_GRID, WALLWARD_GRID)
        model_coef = germano[0] / (germano[1] + EPSILON)
        adjoint_pad = jnp.pad(adjoint, ((0, 0), (2, 2), (0, 0), (2, 2)), mode='wrap')

        def update_block(index):
            block = lax.dynamic_slice_in_dim(forward_pad, index * CX, CX + 6, 1)
            gradient = trimmed(gradients(block, 2), 0, 0, 1)
            strain_size = norm_of(strain_parts(gradient))
            terms = forward_terms(block, 3)
            coef_block = lax.dynamic_slice_in_dim(model_coef, index * CX, CX, 0)
            adjoint_block = lax.dynamic_slice_in_dim(adjoint_pad, index * CX, CX + 4, 1)
            sensitivity = coef_partial(terms, strain_size, trimmed(adjoint_block, 0, 0, 2))
            return (adjoint_update(terms, gradient, strain_size, coef_block, adjoint_block), sensitivity)
        new_blocks, sens_blocks = lax.map(update_block, block_ids)
        adjoint = jnp.transpose(new_blocks, (1, 0, 2, 3, 4)).reshape(5, DOWNWIND_GRID, WALLWARD_GRID, LATERAL_GRID)
        coef_grads.append(sens_blocks.reshape(DOWNWIND_GRID, WALLWARD_GRID) / LATERAL_GRID)
    return (adjoint, jnp.stack(coef_grads))
```

```python
import functools

import jax
import jax.numpy as jnp
from jax import lax
from jax.experimental import pallas as pl
from jax.experimental.pallas import tpu as pltpu
from jax.sharding import PartitionSpec as P

EPSILON = 1e-06
NU_MOL = 0.05
PRANDTL = 0.72
PRANDTL_TURB = 0.9
TIME_STEP = 0.04
PAIRS = ((0, 0), (1, 1), (2, 2), (0, 1), (0, 2), (1, 2))
WEIGHTS = (1.0, 1.0, 1.0, 2.0, 2.0, 2.0)

CX = 4
ROWS = 32
LANES = 128
STRIP = 8
F32 = jnp.float32
BF16 = jnp.bfloat16
SLOT_T = 8
SLOT_PSI_HI = 10
SLOT_PSI_LO = 15


def lane_ids():
    return lax.broadcasted_iota(jnp.int32, (ROWS, LANES), 1)


def row_ids():
    return lax.broadcasted_iota(jnp.int32, (ROWS, LANES), 0)


def turn(values, shift):
    shift = shift % LANES
    return values if shift == 0 else pltpu.roll(values, shift, 1)


class Ops:
    def __init__(self):
        self.lane = lane_ids()
        row = row_ids()
        self.top = row == ROWS - 1
        self.bottom = row == 0

    def z_at(self, values, halo, step):
        if step > 0:
            return turn(jnp.where(self.lane < step, halo, values), -step)
        return turn(jnp.where(self.lane >= LANES + step, halo, values), -step)

    def y_up(self, values):
        return jnp.where(self.top, 0.0, pltpu.roll(values, ROWS - 1, 0))

    def y_down(self, values):
        return jnp.where(self.bottom, 0.0, pltpu.roll(values, 1, 0))

    def unpack(self, block, strip):
        return turn(block, LANES - 4 - STRIP * strip)


def fourth(plus, minus, plus_2, minus_2):
    return (2.0 / 3.0) * (plus - minus) - (1.0 / 12.0) * (plus_2 - minus_2)


def strain_of(grad):
    return [
        grad[0][0],
        grad[1][1],
        grad[2][2],
        0.5 * (grad[0][1] + grad[1][0]),
        0.5 * (grad[0][2] + grad[2][0]),
        0.5 * (grad[1][2] + grad[2][1]),
    ]


def size_of(strain):
    diagonal = strain[0] * strain[0] + strain[1] * strain[1] + strain[2] * strain[2]
    other = strain[3] * strain[3] + strain[4] * strain[4] + strain[5] * strain[5]
    return jnp.sqrt(2.0 * diagonal + (4.0 * other + EPSILON))


def filter_fields(velocity, strain, size):
    products = [velocity[a] * velocity[b] for a, b in PAIRS]
    return list(velocity) + products + strain + [size * part for part in strain]


def pack_strips(ops, planes):
    block = jnp.zeros((ROWS, LANES), F32)
    strip_id = ops.lane // STRIP
    for strip, values in planes.items():
        block = jnp.where(strip_id == strip, turn(values, STRIP * strip + 4), block)
    return block


def split_halves(values):
    upper = values.astype(BF16)
    lower = (values - upper.astype(F32)).astype(BF16)
    return upper, lower


def pack_kernel(flow, rho, temp, psi, packed):
    ops = Ops()
    items = []
    for t in range(2):
        items += [[flow[t, k, x].astype(F32) for x in range(CX)] for k in range(3)]
        items += [[rho[t, x].astype(F32) for x in range(CX)]]
    items += [[temp[t, x].astype(F32) for x in range(CX)] for t in range(2)]
    halves = [[split_halves(psi[k, x]) for x in range(CX)] for k in range(5)]
    for half in range(2):
        items += [[halves[k][x][half].astype(F32) for x in range(CX)] for k in range(5)]
    for number in range(5):
        planes = {}
        for slot in range(4):
            for x in range(CX):
                planes[4 * slot + x] = items[4 * number + slot][x]
        packed[number] = pack_strips(ops, planes).astype(BF16)


def message_kernel(flow, rho, temp, psi, packed, first_up, first_down, second_up, second_down):
    for t in range(2):
        for k in range(3):
            for i in range(3):
                first_up[t * 9 + k * 3 + i] = flow[t, k, 1 + i]
                first_down[t * 9 + k * 3 + i] = flow[t, k, i]
        for i in range(2):
            second_up[t * 4 + i] = rho[t, 2 + i]
            second_down[t * 4 + i] = rho[t, i]
            second_up[t * 4 + 2 + i] = temp[t, 2 + i]
            second_down[t * 4 + 2 + i] = temp[t, i]
        first_up[18 + t] = packed[t]
        first_down[18 + t] = packed[t]
    for k in range(5):
        for i in range(2):
            upper, lower = split_halves(psi[k, 2 + i])
            second_up[8 + k * 2 + i] = upper
            second_up[18 + k * 2 + i] = lower
            upper, lower = split_halves(psi[k, i])
            second_down[8 + k * 2 + i] = upper
            second_down[18 + k * 2 + i] = lower
    zero = jnp.zeros((ROWS, LANES), BF16)
    for t in range(2):
        first_up[20 + t] = zero
        first_down[20 + t] = zero


def germano_kernel(flow, left, right, own_pack, own_halo, sums, fields, edges):
    t = pl.program_id(0)
    ops = Ops()

    def plane(k, x):
        if x < 0:
            return left[t * 9 + k * 3 + x + 3].astype(F32)
        if x >= CX:
            return right[t * 9 + k * 3 + x - CX].astype(F32)
        return flow[0, k, x].astype(F32)

    own_o = own_pack[t].astype(F32)
    own_h = own_halo[t].astype(F32)
    left_o = left[18 + t].astype(F32)
    left_h = left[20 + t].astype(F32)
    right_o = right[18 + t].astype(F32)
    right_h = right[20 + t].astype(F32)

    def halo(k, x):
        if x < 0:
            return ops.unpack(left_h, 4 * k + CX + x)
        if x >= CX:
            return ops.unpack(right_h, 4 * k + x - CX)
        return ops.unpack(own_h, 4 * k + x)

    for x in range(-1, CX + 1):
        grad = [[None] * 3 for _ in range(3)]
        for k in range(3):
            center = plane(k, x)
            edge = halo(k, x)
            grad[0][k] = fourth(plane(k, x + 1), plane(k, x - 1), plane(k, x + 2), plane(k, x - 2))
            grad[1][k] = 0.5 * (ops.y_up(center) - ops.y_down(center))
            grad[2][k] = fourth(*(ops.z_at(center, edge, step) for step in (1, -1, 2, -2)))
        strain = strain_of(grad)
        size = size_of(strain)
        for number, values in enumerate(
            filter_fields([plane(k, x) for k in range(3)], strain, size)
        ):
            fields[number, x + 1] = values

    strip_id = ops.lane // STRIP
    low_half = ops.lane % STRIP < 4

    def gathered(k, from_left, own, from_right):
        own_turned = turn(own, STRIP * (3 - 4 * k))
        left_turned = turn(from_left, STRIP * (-1 - 4 * k))
        right_turned = turn(from_right, STRIP * (7 - 4 * k))
        return jnp.where(
            strip_id < 3, left_turned, jnp.where(strip_id < 7, own_turned, right_turned)
        )

    inner = [gathered(k, left_o, own_o, right_o) for k in range(3)]
    outer = [gathered(k, left_h, own_h, right_h) for k in range(3)]
    sides = []
    for side in range(2):
        velocity = [
            jnp.where(low_half, outer[k], inner[k])
            if side == 0
            else jnp.where(low_half, inner[k], outer[k])
            for k in range(3)
        ]
        grad = [[None] * 3 for _ in range(3)]
        for k in range(3):
            center = velocity[k]
            grad[0][k] = fourth(*(turn(center, -STRIP * step) for step in (1, -1, 2, -2)))
            grad[1][k] = 0.5 * (ops.y_up(center) - ops.y_down(center))
            grad[2][k] = fourth(*(turn(center, -step) for step in (1, -1, 2, -2)))
        strain = strain_of(grad)
        sides.append(filter_fields(velocity, strain, size_of(strain)))
    for number in range(21):
        both = jnp.where(low_half, sides[0][number], sides[1][number])
        edges[number] = turn(both, STRIP) + turn(both, -STRIP) + 2.0 * both

    last = ops.lane == LANES - 1
    first = ops.lane == 0
    columns = jnp.zeros((ROWS, LANES), F32)
    for x in range(CX):

        def hat(number):
            along_x = fields[number, x] + fields[number, x + 2] + 2.0 * fields[number, x + 1]
            edge = ops.unpack(edges[number], x + 3)
            before = turn(jnp.where(last, edge, along_x), 1)
            after = turn(jnp.where(first, edge, along_x), -1)
            return before + after + 2.0 * along_x

        velocity = [hat(k) for k in range(3)]
        strain = [hat(9 + number) for number in range(6)]
        diagonal = strain[0] * strain[0] + strain[1] * strain[1] + strain[2] * strain[2]
        other = strain[3] * strain[3] + strain[4] * strain[4] + strain[5] * strain[5]
        size = jnp.sqrt((2.0 / 256.0) * diagonal + ((4.0 / 256.0) * other + EPSILON))
        size = 4.0 * size
        cross = 0.0
        square = 0.0
        for number, (a, b) in enumerate(PAIRS):
            leonard = hat(3 + number) - (1.0 / 16.0) * velocity[a] * velocity[b]
            model = hat(15 + number) - size * strain[number]
            if WEIGHTS[number] != 1.0:
                weighted = WEIGHTS[number] * model
            else:
                weighted = model
            cross = cross + leonard * weighted
            square = square + model * weighted
        cross = (1.0 / 256.0) * jnp.sum(cross, axis=1, keepdims=True)
        square = (1.0 / 256.0) * jnp.sum(square, axis=1, keepdims=True)
        columns = jnp.where(ops.lane == 8 * t + x, cross, columns)
        columns = jnp.where(ops.lane == 8 * t + 4 + x, square, columns)

    @pl.when(t == 0)
    def _():
        sums[...] = columns

    @pl.when(t == 1)
    def _():
        sums[...] = sums[...] + columns


class State:
    def __init__(self, ops, t, where, flow, rho, temp, left_1, right_1, left_2, right_2, own_halo):
        self.ops, self.t, self.where = ops, t, where
        self.flow, self.rho, self.temp = flow, rho, temp
        self.left_1, self.right_1, self.left_2, self.right_2 = left_1, right_1, left_2, right_2
        self.own_halo = own_halo

    def plane(self, k, x):
        t = self.t
        if k < 3:
            if x < 0:
                return self.left_1[t * 9 + k * 3 + x + 3].astype(F32)
            if x >= CX:
                return self.right_1[t * 9 + k * 3 + x - CX].astype(F32)
            return self.flow[self.where, k, x].astype(F32)
        if x < 0:
            return self.left_2[t * 4 + (k - 3) * 2 + x + 2].astype(F32)
        if x >= CX:
            return self.right_2[t * 4 + (k - 3) * 2 + x - CX].astype(F32)
        return (self.rho if k == 3 else self.temp)[self.where, x].astype(F32)

    def halo(self, k, x):
        slot = 4 * self.t + k if k < 4 else SLOT_T + self.t
        return self.ops.unpack(self.own_halo[slot // 4].astype(F32), 4 * (slot % 4) + x)

    def terms(self, x, need_all=True):
        ops = self.ops
        grad = [[None] * 5 for _ in range(3)]
        lap = [None] * 5
        center = [self.plane(k, x) for k in range(5)]
        for k in range(5):
            if k == 3 and not need_all:
                continue
            edge = self.halo(k, x)
            up, down = ops.y_up(center[k]), ops.y_down(center[k])
            xs = [self.plane(k, x + step) for step in (1, -1, 2, -2)]
            zs = [ops.z_at(center[k], edge, step) for step in (1, -1, 2, -2)]
            if k < 3 or need_all:
                grad[0][k] = fourth(*xs)
                grad[1][k] = 0.5 * (up - down)
                grad[2][k] = fourth(*zs)
            if k != 3:
                lap[k] = xs[0] + xs[1] + zs[0] + zs[1] + up + down - 6.0 * center[k]
        size = size_of(strain_of(grad))
        return center, grad, lap, size, 1.0 / center[3]


def affine_update(ops, x, terms, psi_plane, psi_halo):
    center, grad, lap, size, inv_rho = terms
    psi = [psi_plane(k, x) for k in range(5)]
    work_mom = psi[0] * lap[0] + psi[1] * lap[1] + psi[2] * lap[2]
    work_heat = psi[4] * lap[4]
    turbulent = work_mom + work_heat * (1.0 / PRANDTL_TURB)
    inv_rho_2 = inv_rho * inv_rho
    size_rho = size * inv_rho
    first, second = [], []
    for k in range(5):
        edge = psi_halo(k, x)
        up, down = ops.y_up(psi[k]), ops.y_down(psi[k])
        xs = [psi_plane(k, x + step) for step in (1, -1, 2, -2)]
        zs = [ops.z_at(psi[k], edge, step) for step in (1, -1, 2, -2)]
        rate = (
            center[0] * fourth(*xs) + center[1] * (0.5 * (up - down)) + center[2] * fourth(*zs)
        )
        if k == 3:
            rate = rate - (NU_MOL * work_mom + (NU_MOL / PRANDTL) * work_heat) * inv_rho_2
            eddy = -(size * turbulent) * inv_rho_2
        else:
            lap_psi = xs[0] + xs[1] + zs[0] + zs[1] + up + down - 6.0 * psi[k]
            if k < 3:
                for other in range(5):
                    rate = rate + psi[other] * grad[k][other]
                rate = rate + NU_MOL * (inv_rho * lap_psi)
                eddy = size_rho * lap_psi
            else:
                rate = rate + (NU_MOL / PRANDTL) * (inv_rho * lap_psi)
                eddy = (1.0 / PRANDTL_TURB) * (size_rho * lap_psi)
        first.append(psi[k] + TIME_STEP * rate)
        second.append(TIME_STEP * eddy)
    return first, second, size_rho * turbulent


def first_kernel(
    flow, rho, temp, psi, left_1, right_1, left_2, right_2, own_halo,
    first, second, weight, sums,
):
    ops = Ops()
    state = State(ops, 0, 0, flow, rho, temp, left_1, right_1, left_2, right_2, own_halo)

    def psi_plane(k, x):
        if x < 0:
            return left_2[8 + k * 2 + x + 2].astype(F32) + left_2[18 + k * 2 + x + 2].astype(F32)
        if x >= CX:
            return right_2[8 + k * 2 + x - CX].astype(F32) + right_2[18 + k * 2 + x - CX].astype(F32)
        return psi[k, x]

    def psi_halo(k, x):
        slot = SLOT_PSI_HI + k
        upper = ops.unpack(own_halo[slot // 4].astype(F32), 4 * (slot % 4) + x)
        slot = SLOT_PSI_LO + k
        return upper + ops.unpack(own_halo[slot // 4].astype(F32), 4 * (slot % 4) + x)

    columns = jnp.zeros((ROWS, LANES), F32)
    for x in range(CX):
        new, slope, sensitivity = affine_update(ops, x, state.terms(x), psi_plane, psi_halo)
        for k in range(5):
            first[k, x] = new[k]
            second[k, x] = slope[k]
        total = jnp.sum(sensitivity, axis=1, keepdims=True)
        columns = jnp.where(ops.lane == x, total, columns)
    sums[...] = columns
    state = State(ops, 1, 1, flow, rho, temp, left_1, right_1, left_2, right_2, own_halo)
    for x in range(CX):
        _, _, lap, size, inv_rho = state.terms(x, need_all=False)
        size_rho = size * inv_rho
        for number, k in enumerate((0, 1, 2, 4)):
            scale = 1.0 if k < 3 else 1.0 / PRANDTL_TURB
            weight[number, x] = (scale * size_rho) * lap[k]


def coefficients(ops, own, other):
    total = own + other
    return total / (turn(total, -4) + EPSILON)


def middle_kernel(first, second, weight, partial, own, other, psi, up, down, packed):
    ops = Ops()
    coef = coefficients(ops, own[...], other[...])
    columns = partial[...]
    planes = [{}, {}]
    for x in range(CX):
        coef_x = jnp.broadcast_to(coef[:, x : x + 1], (ROWS, LANES))
        values = [first[k, x] + coef_x * second[k, x] for k in range(5)]
        for k in range(5):
            psi[k, x] = values[k]
            if x >= 2:
                up[k, x - 2] = values[k]
            else:
                down[k, x] = values[k]
            planes[k // 4][4 * (k % 4) + x] = values[k]
        work = weight[0, x] * values[0] + weight[1, x] * values[1]
        work = work + weight[2, x] * values[2] + weight[3, x] * values[4]
        columns = jnp.where(
            ops.lane == 4 + x, jnp.sum(work, axis=1, keepdims=True), columns
        )
    for number in range(2):
        packed[number] = pack_strips(ops, planes[number])
    packed[2] = columns


def last_kernel(
    flow, rho, temp, psi, left_1, right_1, left_2, right_2, own_halo,
    left_psi, right_psi, psi_edges, own, other, out,
):
    ops = Ops()
    coef = coefficients(ops, own[...], other[...])
    state = State(ops, 1, 0, flow, rho, temp, left_1, right_1, left_2, right_2, own_halo)

    def psi_plane(k, x):
        if x < 0:
            return left_psi[k, x + 2]
        if x >= CX:
            return right_psi[k, x - CX]
        return psi[k, x]

    def psi_halo(k, x):
        return ops.unpack(psi_edges[k // 4], 4 * (k % 4) + x)

    for x in range(CX):
        new, slope, _ = affine_update(ops, x, state.terms(x), psi_plane, psi_halo)
        coef_x = jnp.broadcast_to(coef[:, 8 + x : 9 + x], (ROWS, LANES))
        for k in range(5):
            out[k, x] = new[k] + coef_x * slope[k]


def ring(axis):
    count = lax.axis_size(axis)
    forward = [(i, (i + 1) % count) for i in range(count)]
    return forward, [(target, source) for source, target in forward]


def span_edges(block):
    forward, backward = ring("gz")
    before = lax.ppermute(block, "gz", forward)
    if lax.axis_size("gz") == 2:
        return before
    after = lax.ppermute(block, "gz", backward)
    lane = lax.broadcasted_iota(jnp.int32, block.shape, block.ndim - 1)
    return jnp.where(lane % STRIP < 4, before, after)


def span_sum(block):
    if lax.axis_size("gz") == 2:
        return block, lax.ppermute(block, "gz", ring("gz")[0])
    return lax.psum(block, "gz"), jnp.zeros_like(block)


def shape_of(dims, kind):
    return jax.ShapeDtypeStruct(dims, kind)


def whole(count):
    return [pl.BlockSpec(memory_space=pltpu.VMEM)] * count


def cost(operations, size):
    return pl.CostEstimate(flops=operations, bytes_accessed=size, transcendentals=0)


def local(flow, rho, temp, psi):
    block = (ROWS, LANES)
    forward, backward = ring("gx")
    own_pack = pl.pallas_call(
        pack_kernel,
        in_specs=whole(4),
        out_specs=whole(1)[0],
        out_shape=shape_of((5,) + block, BF16),
        cost_estimate=cost(2_000_000, 700_000),
        name="pack",
    )(flow, rho, temp, psi)
    own_halo = span_edges(own_pack)
    first_up, first_down, second_up, second_down = pl.pallas_call(
        message_kernel,
        in_specs=whole(5),
        out_specs=whole(4),
        out_shape=[shape_of((22,) + block, BF16)] * 2 + [shape_of((28,) + block, BF16)] * 2,
        cost_estimate=cost(1_000_000, 1_500_000),
        name="message",
    )(flow, rho, temp, psi, own_pack)
    first_up = lax.dynamic_update_slice(first_up, own_halo[:2], (20, 0, 0))
    first_down = lax.dynamic_update_slice(first_down, own_halo[:2], (20, 0, 0))
    left_1 = lax.ppermute(first_up, "gx", forward)
    right_1 = lax.ppermute(first_down, "gx", backward)
    left_2 = lax.ppermute(second_up, "gx", forward)
    right_2 = lax.ppermute(second_down, "gx", backward)

    def fixed(dims):
        return pl.BlockSpec(dims, lambda t: (0,) * len(dims))

    own = pl.pallas_call(
        germano_kernel,
        grid=(2,),
        in_specs=[
            pl.BlockSpec((1, 3, CX) + block, lambda t: (t, 0, 0, 0, 0)),
            fixed((22,) + block),
            fixed((22,) + block),
            fixed((5,) + block),
            fixed((5,) + block),
        ],
        out_specs=fixed(block),
        out_shape=shape_of(block, F32),
        scratch_shapes=[pltpu.VMEM((21, CX + 2) + block, F32), pltpu.VMEM((21,) + block, F32)],
        cost_estimate=cost(40_000_000, 1_000_000),
        name="germano",
    )(flow, left_1, right_1, own_pack, own_halo)
    own, other = span_sum(own)
    first, second, weight, partial = pl.pallas_call(
        first_kernel,
        in_specs=whole(9),
        out_specs=whole(4),
        out_shape=[
            shape_of((5, CX) + block, F32),
            shape_of((5, CX) + block, F32),
            shape_of((4, CX) + block, F32),
            shape_of(block, F32),
        ],
        cost_estimate=cost(20_000_000, 2_500_000),
        name="first",
    )(flow, rho, temp, psi, left_1, right_1, left_2, right_2, own_halo)
    psi, up, down, packed = pl.pallas_call(
        middle_kernel,
        in_specs=whole(6),
        out_specs=whole(4),
        out_shape=[
            shape_of((5, CX) + block, F32),
            shape_of((5, 2) + block, F32),
            shape_of((5, 2) + block, F32),
            shape_of((3,) + block, F32),
        ],
        cost_estimate=cost(1_000_000, 2_000_000),
        name="middle",
    )(first, second, weight, partial, own, other)
    left_psi = lax.ppermute(up, "gx", forward)
    right_psi = lax.ppermute(down, "gx", backward)
    psi_edges = span_edges(packed)
    if lax.axis_size("gz") == 2:
        totals = packed[2] + psi_edges[2]
    else:
        totals = lax.psum(packed[2], "gz")
    out = pl.pallas_call(
        last_kernel,
        grid=(1,),
        in_specs=[
            pl.BlockSpec((1, 3, CX) + block, lambda t: (1, 0, 0, 0, 0)),
            pl.BlockSpec((1, CX) + block, lambda t: (1, 0, 0, 0)),
            pl.BlockSpec((1, CX) + block, lambda t: (1, 0, 0, 0)),
            fixed((5, CX) + block),
            fixed((22,) + block),
            fixed((22,) + block),
            fixed((28,) + block),
            fixed((28,) + block),
            fixed((5,) + block),
            fixed((5, 2) + block),
            fixed((5, 2) + block),
            fixed((3,) + block),
            fixed(block),
            fixed(block),
        ],
        out_specs=fixed((5, CX) + block),
        out_shape=shape_of((5, CX) + block, F32),
        cost_estimate=cost(15_000_000, 2_500_000),
        name="last",
    )(
        flow, rho, temp, psi, left_1, right_1, left_2, right_2, own_halo,
        left_psi, right_psi, psi_edges, own, other,
    )
    span_cells = LANES * lax.axis_size("gz")
    coef_grad = totals[:, :8].T.reshape(2, CX, ROWS) * (1.0 / span_cells)
    return out, coef_grad


def solution(mesh):
    return jax.shard_map(
        local,
        mesh=mesh,
        in_specs=(
            P(None, None, "gx", None, "gz"),
            P(None, "gx", None, "gz"),
            P(None, "gx", None, "gz"),
            P(None, "gx", None, "gz"),
        ),
        out_specs=(P(None, "gx", None, "gz"), P(None, "gx", None)),
        check_vma=False,
    )
```

```python
import functools

import jax
import jax.numpy as jnp
from jax import lax
from jax.experimental import pallas as pl
from jax.experimental.pallas import tpu as pltpu
from jax.sharding import PartitionSpec as P

EPSILON = 1e-06
NU_MOL = 0.05
PRANDTL = 0.72
PRANDTL_TURB = 0.9
TIME_STEP = 0.04
PAIRS = ((0, 0), (1, 1), (2, 2), (0, 1), (0, 2), (1, 2))
WEIGHTS = (1.0, 1.0, 1.0, 2.0, 2.0, 2.0)

CX = 4
ROWS = 32
LANES = 128
STRIP = 8
F32 = jnp.float32
BF16 = jnp.bfloat16
SLOT_T = 8
SLOT_PSI_HI = 10
SLOT_PSI_LO = 15


def lane_ids():
    return lax.broadcasted_iota(jnp.int32, (ROWS, LANES), 1)


def row_ids():
    return lax.broadcasted_iota(jnp.int32, (ROWS, LANES), 0)


def turn(values, shift):
    shift = shift % LANES
    return values if shift == 0 else pltpu.roll(values, shift, 1)


class Ops:
    def __init__(self):
        self.lane = lane_ids()
        row = row_ids()
        self.top = row == ROWS - 1
        self.bottom = row == 0

    def z_at(self, values, halo, step):
        if step > 0:
            return turn(jnp.where(self.lane < step, halo, values), -step)
        return turn(jnp.where(self.lane >= LANES + step, halo, values), -step)

    def y_up(self, values):
        return jnp.where(self.top, 0.0, pltpu.roll(values, ROWS - 1, 0))

    def y_down(self, values):
        return jnp.where(self.bottom, 0.0, pltpu.roll(values, 1, 0))

    def unpack(self, block, strip):
        return turn(block, LANES - 4 - STRIP * strip)


def fourth(plus, minus, plus_2, minus_2):
    return (2.0 / 3.0) * (plus - minus) - (1.0 / 12.0) * (plus_2 - minus_2)


def strain_of(grad):
    return [
        grad[0][0],
        grad[1][1],
        grad[2][2],
        0.5 * (grad[0][1] + grad[1][0]),
        0.5 * (grad[0][2] + grad[2][0]),
        0.5 * (grad[1][2] + grad[2][1]),
    ]


def size_of(strain):
    diagonal = strain[0] * strain[0] + strain[1] * strain[1] + strain[2] * strain[2]
    other = strain[3] * strain[3] + strain[4] * strain[4] + strain[5] * strain[5]
    return jnp.sqrt(2.0 * diagonal + (4.0 * other + EPSILON))


def filter_fields(velocity, strain, size):
    products = [velocity[a] * velocity[b] for a, b in PAIRS]
    return list(velocity) + products + strain + [size * part for part in strain]


def pack_strips(ops, planes):
    block = jnp.zeros((ROWS, LANES), F32)
    strip_id = (ops.lane >> 3)
    for strip, values in planes.items():
        block = jnp.where(strip_id == strip, turn(values, STRIP * strip + 4), block)
    return block


def split_halves(values):
    upper = values.astype(BF16)
    lower = (values - upper.astype(F32)).astype(BF16)
    return upper, lower


def pack_kernel(flow, rho, temp, psi, packed):
    ops = Ops()
    items = []
    for t in range(2):
        items += [[flow[t, k, x].astype(F32) for x in range(CX)] for k in range(3)]
        items += [[rho[t, x].astype(F32) for x in range(CX)]]
    items += [[temp[t, x].astype(F32) for x in range(CX)] for t in range(2)]
    halves = [[split_halves(psi[k, x]) for x in range(CX)] for k in range(5)]
    for half in range(2):
        items += [[halves[k][x][half].astype(F32) for x in range(CX)] for k in range(5)]
    for number in range(5):
        planes = {}
        for slot in range(4):
            for x in range(CX):
                planes[4 * slot + x] = items[4 * number + slot][x]
        packed[number] = pack_strips(ops, planes).astype(BF16)


def message_kernel(flow, rho, temp, psi, packed, first_up, first_down, second_up, second_down):
    for t in range(2):
        for k in range(3):
            for i in range(3):
                first_up[t * 9 + k * 3 + i] = flow[t, k, 1 + i]
                first_down[t * 9 + k * 3 + i] = flow[t, k, i]
        for i in range(2):
            second_up[t * 4 + i] = rho[t, 2 + i]
            second_down[t * 4 + i] = rho[t, i]
            second_up[t * 4 + 2 + i] = temp[t, 2 + i]
            second_down[t * 4 + 2 + i] = temp[t, i]
        first_up[18 + t] = packed[t]
        first_down[18 + t] = packed[t]
    for k in range(5):
        for i in range(2):
            upper, lower = split_halves(psi[k, 2 + i])
            second_up[8 + k * 2 + i] = upper
            second_up[18 + k * 2 + i] = lower
            upper, lower = split_halves(psi[k, i])
            second_down[8 + k * 2 + i] = upper
            second_down[18 + k * 2 + i] = lower
    zero = jnp.zeros((ROWS, LANES), BF16)
    for t in range(2):
        first_up[20 + t] = zero
        first_down[20 + t] = zero


def germano_kernel(flow, left, right, own_pack, own_halo, sums, wide, halos, fields, edges, spread, hats):
    t = pl.program_id(0)
    ops = Ops()
    for k in range(3):
        for i in range(3):
            wide[k, i] = left[t * 9 + k * 3 + i].astype(F32)
            wide[k, 7 + i] = right[t * 9 + k * 3 + i].astype(F32)
        for x in range(CX):
            wide[k, 3 + x] = flow[0, k, x].astype(F32)
    own_o = own_pack[t].astype(F32)
    own_h = own_halo[t].astype(F32)
    left_o = left[18 + t].astype(F32)
    left_h = left[20 + t].astype(F32)
    right_o = right[18 + t].astype(F32)
    right_h = right[20 + t].astype(F32)
    for k in range(3):
        halos[k, 0] = ops.unpack(left_h, 4 * k + 3)
        for x in range(CX):
            halos[k, 1 + x] = ops.unpack(own_h, 4 * k + x)
        halos[k, 5] = ops.unpack(right_h, 4 * k)
    strip_id = ops.lane >> 3
    low_half = (ops.lane & 7) < 4

    def gathered(k, from_left, own, from_right):
        own_turned = turn(own, STRIP * (3 - 4 * k))
        left_turned = turn(from_left, STRIP * (-1 - 4 * k))
        right_turned = turn(from_right, STRIP * (7 - 4 * k))
        return jnp.where(strip_id < 3, left_turned, jnp.where(strip_id < 7, own_turned, right_turned))

    for k in range(3):
        inner = gathered(k, left_o, own_o, right_o)
        outer = gathered(k, left_h, own_h, right_h)
        edges[k] = jnp.where(low_half, outer, inner)
        edges[3 + k] = jnp.where(low_half, inner, outer)

    for x in range(-1, CX + 1):
        grad = [[None] * 3 for _ in range(3)]
        for k in range(3):
            center = wide[k, x + 3]
            edge = halos[k, x + 1]
            grad[0][k] = fourth(wide[k, x + 4], wide[k, x + 2], wide[k, x + 5], wide[k, x + 1])
            grad[1][k] = 0.5 * (ops.y_up(center) - ops.y_down(center))
            grad[2][k] = fourth(*(ops.z_at(center, edge, step) for step in (1, -1, 2, -2)))
        strain = strain_of(grad)
        size = size_of(strain)
        for number, values in enumerate(filter_fields([wide[k, x + 3] for k in range(3)], strain, size)):
            fields[number, x + 1] = values

    sides = []
    for side in range(2):
        velocity = [edges[3 * side + k] for k in range(3)]
        grad = [[None] * 3 for _ in range(3)]
        for k in range(3):
            center = velocity[k]
            grad[0][k] = fourth(*(turn(center, -STRIP * step) for step in (1, -1, 2, -2)))
            grad[1][k] = 0.5 * (ops.y_up(center) - ops.y_down(center))
            grad[2][k] = fourth(*(turn(center, -step) for step in (1, -1, 2, -2)))
        strain = strain_of(grad)
        for number, values in enumerate(filter_fields(velocity, strain, size_of(strain))):
            if side == 0:
                spread[number] = values
            else:
                spread[number] = jnp.where(low_half, spread[number], values)
    for number in range(21):
        both = spread[number]
        edges[number] = turn(both, STRIP) + turn(both, -STRIP) + 2.0 * both
    for number in range(21):
        for x in range(CX):
            hats[number, x] = ops.unpack(edges[number], x + 3)
    last = ops.lane == LANES - 1
    first = ops.lane == 0
    for x in range(CX):
        for number in range(21):
            along_x = fields[number, x] + fields[number, x + 2] + 2.0 * fields[number, x + 1]
            edge = hats[number, x]
            before = turn(jnp.where(last, edge, along_x), 1)
            after = turn(jnp.where(first, edge, along_x), -1)
            hats[number, x] = before + after + 2.0 * along_x
    columns = jnp.zeros((ROWS, LANES), F32)
    for x in range(CX):
        velocity = [hats[k, x] for k in range(3)]
        strain = [hats[9 + number, x] for number in range(6)]
        diagonal = strain[0] * strain[0] + strain[1] * strain[1] + strain[2] * strain[2]
        other = strain[3] * strain[3] + strain[4] * strain[4] + strain[5] * strain[5]
        size = jnp.sqrt((2.0 / 256.0) * diagonal + ((4.0 / 256.0) * other + EPSILON))
        size = 4.0 * size
        cross = 0.0
        square = 0.0
        for number, (a, b) in enumerate(PAIRS):
            leonard = hats[3 + number, x] - (1.0 / 16.0) * velocity[a] * velocity[b]
            model = hats[15 + number, x] - size * strain[number]
            weighted = WEIGHTS[number] * model if WEIGHTS[number] != 1.0 else model
            cross = cross + leonard * weighted
            square = square + model * weighted
        cross = (1.0 / 256.0) * jnp.sum(cross, axis=1, keepdims=True)
        square = (1.0 / 256.0) * jnp.sum(square, axis=1, keepdims=True)
        columns = jnp.where(ops.lane == 8 * t + x, cross, columns)
        columns = jnp.where(ops.lane == 8 * t + 4 + x, square, columns)

    @pl.when(t == 0)
    def _():
        sums[...] = columns

    @pl.when(t == 1)
    def _():
        sums[...] = sums[...] + columns


def spread_state(ops, t, where, flow, rho, temp, left_1, right_1, left_2, right_2, own_halo, wide, halos):
    for k in range(3):
        for i in range(2):
            wide[k, i] = left_1[t * 9 + k * 3 + 1 + i].astype(F32)
            wide[k, 2 + CX + i] = right_1[t * 9 + k * 3 + i].astype(F32)
        for x in range(CX):
            wide[k, 2 + x] = flow[where, k, x].astype(F32)
    for k in range(3, 5):
        for i in range(2):
            wide[k, i] = left_2[t * 4 + (k - 3) * 2 + i].astype(F32)
            wide[k, 2 + CX + i] = right_2[t * 4 + (k - 3) * 2 + i].astype(F32)
        for x in range(CX):
            wide[k, 2 + x] = (rho if k == 3 else temp)[where, x].astype(F32)
    for k in range(5):
        slot = 4 * t + k if k < 4 else SLOT_T + t
        strips = own_halo[slot // 4].astype(F32)
        for x in range(CX):
            halos[k, x] = ops.unpack(strips, 4 * (slot % 4) + x)


def state_terms(ops, wide, halos, x, need_all=True):
    grad = [[None] * 5 for _ in range(3)]
    lap = [None] * 5
    center = [wide[k, x + 2] for k in range(5)]
    for k in range(5):
        if k == 3 and not need_all:
            continue
        edge = halos[k, x]
        up, down = ops.y_up(center[k]), ops.y_down(center[k])
        xs = [wide[k, x + 2 + step] for step in (1, -1, 2, -2)]
        zs = [ops.z_at(center[k], edge, step) for step in (1, -1, 2, -2)]
        if k < 3 or need_all:
            grad[0][k] = fourth(*xs)
            grad[1][k] = 0.5 * (up - down)
            grad[2][k] = fourth(*zs)
        if k != 3:
            lap[k] = xs[0] + xs[1] + zs[0] + zs[1] + up + down - 6.0 * center[k]
    size = size_of(strain_of(grad))
    return center, grad, lap, size, 1.0 / center[3]


def affine_update(ops, x, terms, psi_wide, psi_halos):
    center, grad, lap, size, inv_rho = terms
    psi = [psi_wide[k, x + 2] for k in range(5)]
    work_mom = psi[0] * lap[0] + psi[1] * lap[1] + psi[2] * lap[2]
    work_heat = psi[4] * lap[4]
    turbulent = work_mom + work_heat * (1.0 / PRANDTL_TURB)
    inv_rho_2 = inv_rho * inv_rho
    size_rho = size * inv_rho
    first, second = [], []
    for k in range(5):
        edge = psi_halos[k, x]
        up, down = ops.y_up(psi[k]), ops.y_down(psi[k])
        xs = [psi_wide[k, x + 2 + step] for step in (1, -1, 2, -2)]
        zs = [ops.z_at(psi[k], edge, step) for step in (1, -1, 2, -2)]
        rate = (
            center[0] * fourth(*xs) + center[1] * (0.5 * (up - down)) + center[2] * fourth(*zs)
        )
        if k == 3:
            rate = rate - (NU_MOL * work_mom + (NU_MOL / PRANDTL) * work_heat) * inv_rho_2
            eddy = -(size * turbulent) * inv_rho_2
        else:
            lap_psi = xs[0] + xs[1] + zs[0] + zs[1] + up + down - 6.0 * psi[k]
            if k < 3:
                for other in range(5):
                    rate = rate + psi[other] * grad[k][other]
                rate = rate + NU_MOL * (inv_rho * lap_psi)
                eddy = size_rho * lap_psi
            else:
                rate = rate + (NU_MOL / PRANDTL) * (inv_rho * lap_psi)
                eddy = (1.0 / PRANDTL_TURB) * (size_rho * lap_psi)
        first.append(psi[k] + TIME_STEP * rate)
        second.append(TIME_STEP * eddy)
    return first, second, size_rho * turbulent


def first_kernel(
    flow, rho, temp, psi, left_1, right_1, left_2, right_2, own_halo,
    first, second, weight, sums,
    wide, halos, psi_wide, psi_halos, work,
):
    ops = Ops()
    for k in range(5):
        for i in range(2):
            psi_wide[k, i] = left_2[8 + k * 2 + i].astype(F32) + left_2[18 + k * 2 + i].astype(F32)
            psi_wide[k, 2 + CX + i] = (
                right_2[8 + k * 2 + i].astype(F32) + right_2[18 + k * 2 + i].astype(F32)
            )
        upper, lower = SLOT_PSI_HI + k, SLOT_PSI_LO + k
        upper_strips = own_halo[upper // 4].astype(F32)
        lower_strips = own_halo[lower // 4].astype(F32)
        for x in range(CX):
            psi_wide[k, 2 + x] = psi[k, x]
            psi_halos[k, x] = ops.unpack(upper_strips, 4 * (upper % 4) + x) + ops.unpack(
                lower_strips, 4 * (lower % 4) + x
            )
    spread_state(
        ops, 0, 0, flow, rho, temp, left_1, right_1, left_2, right_2, own_halo,
        wide.at[0], halos.at[0],
    )
    spread_state(
        ops, 1, 1, flow, rho, temp, left_1, right_1, left_2, right_2, own_halo,
        wide.at[1], halos.at[1],
    )
    for x in range(CX):
        terms = state_terms(ops, wide.at[0], halos.at[0], x)
        new, slope, sensitivity = affine_update(ops, x, terms, psi_wide, psi_halos)
        for k in range(5):
            first[k, x] = new[k]
            second[k, x] = slope[k]
        work[x] = sensitivity
    for x in range(CX):
        _, _, lap, size, inv_rho = state_terms(ops, wide.at[1], halos.at[1], x, need_all=False)
        size_rho = size * inv_rho
        for number, k in enumerate((0, 1, 2, 4)):
            scale = 1.0 if k < 3 else 1.0 / PRANDTL_TURB
            weight[number, x] = (scale * size_rho) * lap[k]
    columns = jnp.zeros((ROWS, LANES), F32)
    for x in range(CX):
        columns = jnp.where(ops.lane == x, jnp.sum(work[x], axis=1, keepdims=True), columns)
    sums[...] = columns


def coefficients(ops, own, other):
    total = own + other
    return total / (turn(total, -4) + EPSILON)


def middle_kernel(
    first, second, weight, partial, own, other, psi, up, down, packed, coef_planes, work
):
    ops = Ops()
    coef = coefficients(ops, own[...], other[...])
    for x in range(CX):
        coef_planes[x] = jnp.broadcast_to(coef[:, x : x + 1], (ROWS, LANES))
    for x in range(CX):
        values = [first[k, x] + coef_planes[x] * second[k, x] for k in range(5)]
        for k in range(5):
            psi[k, x] = values[k]
            if x >= 2:
                up[k, x - 2] = values[k]
            else:
                down[k, x] = values[k]
        total = weight[0, x] * values[0] + weight[1, x] * values[1]
        work[x] = total + weight[2, x] * values[2] + weight[3, x] * values[4]
    for number in range(2):
        planes = {}
        for k in range(4 * number, min(4 * number + 4, 5)):
            for x in range(CX):
                planes[4 * (k % 4) + x] = psi[k, x]
        packed[number] = pack_strips(ops, planes)
    columns = partial[...]
    for x in range(CX):
        columns = jnp.where(
            ops.lane == 4 + x, jnp.sum(work[x], axis=1, keepdims=True), columns
        )
    packed[2] = columns


def last_kernel(
    flow, rho, temp, psi, left_1, right_1, left_2, right_2, own_halo,
    left_psi, right_psi, psi_edges, own, other, out,
    wide, halos, psi_wide, psi_halos, coef_planes,
):
    ops = Ops()
    coef = coefficients(ops, own[...], other[...])
    for x in range(CX):
        coef_planes[x] = jnp.broadcast_to(coef[:, 8 + x : 9 + x], (ROWS, LANES))
    for k in range(5):
        for i in range(2):
            psi_wide[k, i] = left_psi[k, i]
            psi_wide[k, 2 + CX + i] = right_psi[k, i]
        for x in range(CX):
            psi_wide[k, 2 + x] = psi[k, x]
            psi_halos[k, x] = ops.unpack(psi_edges[k // 4], 4 * (k % 4) + x)
    spread_state(
        ops, 1, 0, flow, rho, temp, left_1, right_1, left_2, right_2, own_halo, wide, halos
    )
    for x in range(CX):
        terms = state_terms(ops, wide, halos, x)
        new, slope, _ = affine_update(ops, x, terms, psi_wide, psi_halos)
        for k in range(5):
            out[k, x] = new[k] + coef_planes[x] * slope[k]


def ring(axis):
    count = lax.axis_size(axis)
    forward = [(i, (i + 1) % count) for i in range(count)]
    return forward, [(target, source) for source, target in forward]


def span_edges(block):
    forward, backward = ring("gz")
    before = lax.ppermute(block, "gz", forward)
    if lax.axis_size("gz") == 2:
        return before
    after = lax.ppermute(block, "gz", backward)
    lane = lax.broadcasted_iota(jnp.int32, block.shape, block.ndim - 1)
    return jnp.where(lane % STRIP < 4, before, after)


def span_sum(block):
    if lax.axis_size("gz") == 2:
        return block, lax.ppermute(block, "gz", ring("gz")[0])
    return lax.psum(block, "gz"), jnp.zeros_like(block)


def shape_of(dims, kind):
    return jax.ShapeDtypeStruct(dims, kind)


def whole(count):
    return [pl.BlockSpec(memory_space=pltpu.VMEM)] * count


def scratch(*dims):
    return [pltpu.VMEM(d + (ROWS, LANES), F32) for d in dims]


PARAMS = pltpu.CompilerParams(vmem_limit_bytes=24 * 2**20)


def cost(operations, size):
    return pl.CostEstimate(flops=operations, bytes_accessed=size, transcendentals=0)


def local(flow, rho, temp, psi):
    block = (ROWS, LANES)
    forward, backward = ring("gx")
    own_pack = pl.pallas_call(
        pack_kernel,
        in_specs=whole(4),
        out_specs=whole(1)[0],
        out_shape=shape_of((5,) + block, BF16),
        cost_estimate=cost(2_000_000, 700_000),
        compiler_params=PARAMS,
        name="pack",
    )(flow, rho, temp, psi)
    own_halo = span_edges(own_pack)
    first_up, first_down, second_up, second_down = pl.pallas_call(
        message_kernel,
        in_specs=whole(5),
        out_specs=whole(4),
        out_shape=[shape_of((22,) + block, BF16)] * 2 + [shape_of((28,) + block, BF16)] * 2,
        cost_estimate=cost(1_000_000, 1_500_000),
        compiler_params=PARAMS,
        name="message",
    )(flow, rho, temp, psi, own_pack)
    first_up = lax.dynamic_update_slice(first_up, own_halo[:2], (20, 0, 0))
    first_down = lax.dynamic_update_slice(first_down, own_halo[:2], (20, 0, 0))
    left_1 = lax.ppermute(first_up, "gx", forward)
    right_1 = lax.ppermute(first_down, "gx", backward)
    second_up, second_down, left_1, right_1 = lax.optimization_barrier(
        (second_up, second_down, left_1, right_1)
    )
    left_2 = lax.ppermute(second_up, "gx", forward)
    right_2 = lax.ppermute(second_down, "gx", backward)

    def fixed(dims):
        return pl.BlockSpec(dims, lambda t: (0,) * len(dims))

    own = pl.pallas_call(
        germano_kernel,
        grid=(2,),
        in_specs=[
            pl.BlockSpec((1, 3, CX) + block, lambda t: (t, 0, 0, 0, 0)),
            fixed((22,) + block),
            fixed((22,) + block),
            fixed((5,) + block),
            fixed((5,) + block),
        ],
        out_specs=fixed(block),
        out_shape=shape_of(block, F32),
        scratch_shapes=scratch(
            (3, CX + 6), (3, CX + 2), (21, CX + 2), (21,), (21,), (21, CX)
        ),
        cost_estimate=cost(40_000_000, 1_000_000),
        compiler_params=PARAMS,
        name="germano",
    )(flow, left_1, right_1, own_pack, own_halo)
    own, other = span_sum(own)
    first, second, weight, partial = pl.pallas_call(
        first_kernel,
        in_specs=whole(9),
        out_specs=whole(4),
        out_shape=[
            shape_of((5, CX) + block, F32),
            shape_of((5, CX) + block, F32),
            shape_of((4, CX) + block, F32),
            shape_of(block, F32),
        ],
        scratch_shapes=scratch((2, 5, CX + 4), (2, 5, CX), (5, CX + 4), (5, CX), (CX,)),
        cost_estimate=cost(20_000_000, 2_500_000),
        compiler_params=PARAMS,
        name="first",
    )(flow, rho, temp, psi, left_1, right_1, left_2, right_2, own_halo)
    psi, up, down, packed = pl.pallas_call(
        middle_kernel,
        in_specs=whole(6),
        out_specs=whole(4),
        out_shape=[
            shape_of((5, CX) + block, F32),
            shape_of((5, 2) + block, F32),
            shape_of((5, 2) + block, F32),
            shape_of((3,) + block, F32),
        ],
        scratch_shapes=scratch((CX,), (CX,)),
        cost_estimate=cost(1_000_000, 2_000_000),
        compiler_params=PARAMS,
        name="middle",
    )(first, second, weight, partial, own, other)
    left_psi = lax.ppermute(up, "gx", forward)
    right_psi = lax.ppermute(down, "gx", backward)
    psi_edges = span_edges(packed)
    if lax.axis_size("gz") == 2:
        totals = packed[2] + psi_edges[2]
    else:
        totals = lax.psum(packed[2], "gz")
    out = pl.pallas_call(
        last_kernel,
        grid=(1,),
        in_specs=[
            pl.BlockSpec((1, 3, CX) + block, lambda t: (1, 0, 0, 0, 0)),
            pl.BlockSpec((1, CX) + block, lambda t: (1, 0, 0, 0)),
            pl.BlockSpec((1, CX) + block, lambda t: (1, 0, 0, 0)),
            fixed((5, CX) + block),
            fixed((22,) + block),
            fixed((22,) + block),
            fixed((28,) + block),
            fixed((28,) + block),
            fixed((5,) + block),
            fixed((5, 2) + block),
            fixed((5, 2) + block),
            fixed((3,) + block),
            fixed(block),
            fixed(block),
        ],
        out_specs=fixed((5, CX) + block),
        out_shape=shape_of((5, CX) + block, F32),
        scratch_shapes=scratch((5, CX + 4), (5, CX), (5, CX + 4), (5, CX), (CX,)),
        cost_estimate=cost(15_000_000, 2_500_000),
        compiler_params=PARAMS,
        name="last",
    )(
        flow, rho, temp, psi, left_1, right_1, left_2, right_2, own_halo,
        left_psi, right_psi, psi_edges, own, other,
    )
    span_cells = LANES * lax.axis_size("gz")
    coef_grad = totals[:, :8].T.reshape(2, CX, ROWS) * (1.0 / span_cells)
    return out, coef_grad


def solution(mesh):
    return jax.shard_map(
        local,
        mesh=mesh,
        in_specs=(
            P(None, None, "gx", None, "gz"),
            P(None, "gx", None, "gz"),
            P(None, "gx", None, "gz"),
            P(None, "gx", None, "gz"),
        ),
        out_specs=(P(None, "gx", None, "gz"), P(None, "gx", None)),
        check_vma=False,
    )
```

```python
import functools
import math

import jax
import jax.numpy as jnp
from jax import lax
from jax.experimental import pallas as pl
from jax.experimental.pallas import tpu as pltpu
from jax.sharding import PartitionSpec as P

EPSILON = 1e-06
NU_MOL = 0.05
PRANDTL = 0.72
PRANDTL_TURB = 0.9
TIME_STEP = 0.04
PAIRS = ((0, 0), (1, 1), (2, 2), (0, 1), (0, 2), (1, 2))
WEIGHTS = (1.0, 1.0, 1.0, 2.0, 2.0, 2.0)

CX = 4
ROWS = 32
LANES = 128
STRIP = 8
F32 = jnp.float32
BF16 = jnp.bfloat16
SLOT_T = 8
SLOT_PSI_HI = 10
SLOT_PSI_LO = 15
BAND = 12
STRIP_BLOCKS = 5
VELOCITY = 0
SCALARS = 18
PSI_HI = 26
PSI_LO = 36
MESSAGE = 46


def lane_ids():
    return lax.broadcasted_iota(jnp.int32, (ROWS, LANES), 1)


def row_ids():
    return lax.broadcasted_iota(jnp.int32, (ROWS, LANES), 0)


def turn(values, shift):
    shift = shift % LANES
    return values if shift == 0 else pltpu.roll(values, shift, 1)


class Ops:
    def __init__(self):
        self.lane = lane_ids()
        row = row_ids()
        self.top = row == ROWS - 1
        self.bottom = row == 0

    def z_at(self, values, halo, step):
        if step > 0:
            return turn(jnp.where(self.lane < step, halo, values), -step)
        return turn(jnp.where(self.lane >= LANES + step, halo, values), -step)

    def y_up(self, values):
        return jnp.where(self.top, 0.0, pltpu.roll(values, ROWS - 1, 0))

    def y_down(self, values):
        return jnp.where(self.bottom, 0.0, pltpu.roll(values, 1, 0))

    def unpack(self, block, strip):
        return turn(block, LANES - 4 - STRIP * strip)


def fourth(plus, minus, plus_2, minus_2):
    return (2.0 / 3.0) * (plus - minus) - (1.0 / 12.0) * (plus_2 - minus_2)


def strain_of(grad):
    return [
        grad[0][0],
        grad[1][1],
        grad[2][2],
        0.5 * (grad[0][1] + grad[1][0]),
        0.5 * (grad[0][2] + grad[2][0]),
        0.5 * (grad[1][2] + grad[2][1]),
    ]


def size_of(strain):
    diagonal = strain[0] * strain[0] + strain[1] * strain[1] + strain[2] * strain[2]
    other = strain[3] * strain[3] + strain[4] * strain[4] + strain[5] * strain[5]
    return jnp.sqrt(2.0 * diagonal + (4.0 * other + EPSILON))


def filter_fields(velocity, strain, size):
    products = [velocity[a] * velocity[b] for a, b in PAIRS]
    return list(velocity) + products + strain + [size * part for part in strain]


def pack_strips(ops, planes):
    block = jnp.zeros((ROWS, LANES), F32)
    strip_id = (ops.lane >> 3)
    for strip, values in planes.items():
        block = jnp.where(strip_id == strip, turn(values, STRIP * strip + 4), block)
    return block


def split_halves(values):
    upper = values.astype(BF16)
    lower = (values - upper.astype(F32)).astype(BF16)
    return upper, lower


def spread_state(ops, t, where, flow, rho, temp, left, right, own_halo, wide, halos):
    for k in range(3):
        for i in range(2):
            wide[k, i] = left[t * 9 + k * 3 + 1 + i].astype(F32)
            wide[k, 2 + CX + i] = right[t * 9 + k * 3 + i].astype(F32)
        for x in range(CX):
            wide[k, 2 + x] = flow[where, k, x].astype(F32)
    for k in range(3, 5):
        for i in range(2):
            wide[k, i] = left[SCALARS + t * 4 + (k - 3) * 2 + i].astype(F32)
            wide[k, 2 + CX + i] = right[SCALARS + t * 4 + (k - 3) * 2 + i].astype(F32)
        for x in range(CX):
            wide[k, 2 + x] = (rho if k == 3 else temp)[where, x].astype(F32)
    for k in range(5):
        slot = 4 * t + k if k < 4 else SLOT_T + t
        strips = own_halo[slot // 4].astype(F32)
        for x in range(CX):
            halos[k, x] = ops.unpack(strips, 4 * (slot % 4) + x)


def state_terms(ops, wide, halos, x, need_all=True):
    grad = [[None] * 5 for _ in range(3)]
    lap = [None] * 5
    center = [wide[k, x + 2] for k in range(5)]
    for k in range(5):
        if k == 3 and not need_all:
            continue
        edge = halos[k, x]
        up, down = ops.y_up(center[k]), ops.y_down(center[k])
        xs = [wide[k, x + 2 + step] for step in (1, -1, 2, -2)]
        zs = [ops.z_at(center[k], edge, step) for step in (1, -1, 2, -2)]
        if k < 3 or need_all:
            grad[0][k] = fourth(*xs)
            grad[1][k] = 0.5 * (up - down)
            grad[2][k] = fourth(*zs)
        if k != 3:
            lap[k] = xs[0] + xs[1] + zs[0] + zs[1] + up + down - 6.0 * center[k]
    size = size_of(strain_of(grad))
    return center, grad, lap, size, 1.0 / center[3]


def affine_update(ops, x, terms, psi_wide, psi_halos):
    center, grad, lap, size, inv_rho = terms
    psi = [psi_wide[k, x + 2] for k in range(5)]
    work_mom = psi[0] * lap[0] + psi[1] * lap[1] + psi[2] * lap[2]
    work_heat = psi[4] * lap[4]
    turbulent = work_mom + work_heat * (1.0 / PRANDTL_TURB)
    inv_rho_2 = inv_rho * inv_rho
    size_rho = size * inv_rho
    first, second = [], []
    for k in range(5):
        edge = psi_halos[k, x]
        up, down = ops.y_up(psi[k]), ops.y_down(psi[k])
        xs = [psi_wide[k, x + 2 + step] for step in (1, -1, 2, -2)]
        zs = [ops.z_at(psi[k], edge, step) for step in (1, -1, 2, -2)]
        rate = (
            center[0] * fourth(*xs) + center[1] * (0.5 * (up - down)) + center[2] * fourth(*zs)
        )
        if k == 3:
            rate = rate - (NU_MOL * work_mom + (NU_MOL / PRANDTL) * work_heat) * inv_rho_2
            eddy = -(size * turbulent) * inv_rho_2
        else:
            lap_psi = xs[0] + xs[1] + zs[0] + zs[1] + up + down - 6.0 * psi[k]
            if k < 3:
                for other in range(5):
                    rate = rate + psi[other] * grad[k][other]
                rate = rate + NU_MOL * (inv_rho * lap_psi)
                eddy = size_rho * lap_psi
            else:
                rate = rate + (NU_MOL / PRANDTL) * (inv_rho * lap_psi)
                eddy = (1.0 / PRANDTL_TURB) * (size_rho * lap_psi)
        first.append(psi[k] + TIME_STEP * rate)
        second.append(TIME_STEP * eddy)
    return first, second, size_rho * turbulent


def band_of(lane):
    return (lane * 43) >> 9


def message_kernel(
    flow_far, rho_far, temp_far, psi_far, up, down, flow, rho, temp, psi, sems
):
    copies = [
        pltpu.make_async_copy(source, target, sems.at[i])
        for i, (source, target) in enumerate(
            ((flow_far, flow), (psi_far, psi), (rho_far, rho), (temp_far, temp))
        )
    ]
    for copy in copies:
        copy.start()
    copies[0].wait()
    for t in range(2):
        for k in range(3):
            for i in range(3):
                up[t * 9 + k * 3 + i] = flow[t, k, 1 + i]
                down[t * 9 + k * 3 + i] = flow[t, k, i]
    copies[1].wait()
    for k in range(5):
        for i in range(2):
            upper, lower = split_halves(psi[k, 2 + i])
            up[PSI_HI + k * 2 + i] = upper
            up[PSI_LO + k * 2 + i] = lower
            upper, lower = split_halves(psi[k, i])
            down[PSI_HI + k * 2 + i] = upper
            down[PSI_LO + k * 2 + i] = lower
    copies[2].wait()
    copies[3].wait()
    for t in range(2):
        for i in range(2):
            up[SCALARS + t * 4 + i] = rho[t, 2 + i]
            down[SCALARS + t * 4 + i] = rho[t, i]
            up[SCALARS + t * 4 + 2 + i] = temp[t, 2 + i]
            down[SCALARS + t * 4 + 2 + i] = temp[t, i]


def pack_kernel(flow, rho, temp, psi, packed):
    ops = Ops()
    items = []
    for t in range(2):
        items += [[flow[t, k, x].astype(F32) for x in range(CX)] for k in range(3)]
        items += [[rho[t, x].astype(F32) for x in range(CX)]]
    items += [[temp[t, x].astype(F32) for x in range(CX)] for t in range(2)]
    halves = [[split_halves(psi[k, x]) for x in range(CX)] for k in range(5)]
    for half in range(2):
        items += [[halves[k][x][half].astype(F32) for x in range(CX)] for k in range(5)]
    for number in range(STRIP_BLOCKS):
        planes = {}
        for slot in range(4):
            for x in range(CX):
                planes[4 * slot + x] = items[4 * number + slot][x]
        packed[number] = pack_strips(ops, planes).astype(BF16)
    band = band_of(ops.lane)
    for t in range(2):
        for k in range(3):
            block = jnp.zeros((ROWS, LANES), F32)
            for x in range(CX):
                moved = turn(flow[t, k, x].astype(F32), BAND * (x + 3) + 3)
                block = jnp.where(band == x + 3, moved, block)
            packed[STRIP_BLOCKS + 3 * t + k] = block.astype(BF16)


def bands_kernel(packed, left, right, out):
    ops = Ops()
    for number in range(STRIP_BLOCKS):
        out[number] = packed[number]
    band = band_of(ops.lane)
    for t in range(2):
        for k in range(3):
            block = packed[STRIP_BLOCKS + 3 * t + k].astype(F32)
            for i in range(3):
                number = VELOCITY + t * 9 + k * 3 + i
                moved = turn(left[number].astype(F32), BAND * i + 3)
                block = jnp.where(band == i, moved, block)
                moved = turn(right[number].astype(F32), BAND * (7 + i) + 3)
                block = jnp.where(band == 7 + i, moved, block)
            out[STRIP_BLOCKS + 3 * t + k] = block.astype(BF16)


def products_of(hat):
    velocity = [hat(k) for k in range(3)]
    strain = [hat(9 + number) for number in range(6)]
    diagonal = strain[0] * strain[0] + strain[1] * strain[1] + strain[2] * strain[2]
    other = strain[3] * strain[3] + strain[4] * strain[4] + strain[5] * strain[5]
    size = 4.0 * jnp.sqrt((2.0 / 256.0) * diagonal + ((4.0 / 256.0) * other + EPSILON))
    cross = 0.0
    square = 0.0
    for number, (a, b) in enumerate(PAIRS):
        leonard = hat(3 + number) - (1.0 / 16.0) * velocity[a] * velocity[b]
        model = hat(15 + number) - size * strain[number]
        weighted = WEIGHTS[number] * model if WEIGHTS[number] != 1.0 else model
        cross = cross + leonard * weighted
        square = square + model * weighted
    return cross, square


def inner_kernel(flow, left, right, inner, high, wide, fields, hats):
    ops = Ops()
    valid = (ops.lane >= 3) & (ops.lane < LANES - 3)
    band = band_of(jnp.maximum(ops.lane - 2, 0))

    def step(t, carry):
        for k in range(3):
            for i in range(3):
                wide[k, i] = left[VELOCITY + t * 9 + k * 3 + i].astype(F32)
                wide[k, 7 + i] = right[VELOCITY + t * 9 + k * 3 + i].astype(F32)
            for x in range(CX):
                wide[k, 3 + x] = flow[t, k, x].astype(F32)
        for x in range(-1, CX + 1):
            grad = [[None] * 3 for _ in range(3)]
            for k in range(3):
                center = wide[k, x + 3]
                grad[0][k] = fourth(
                    wide[k, x + 4], wide[k, x + 2], wide[k, x + 5], wide[k, x + 1]
                )
                grad[1][k] = 0.5 * (ops.y_up(center) - ops.y_down(center))
                grad[2][k] = fourth(*(turn(center, -step) for step in (1, -1, 2, -2)))
            strain = strain_of(grad)
            size = size_of(strain)
            velocity = [wide[k, x + 3] for k in range(3)]
            for number, values in enumerate(filter_fields(velocity, strain, size)):
                fields[number, x + 1] = values
        for x in range(CX):
            for number in range(21):
                along_x = (
                    fields[number, x] + fields[number, x + 2] + 2.0 * fields[number, x + 1]
                )
                hats[number, x] = turn(along_x, 1) + turn(along_x, -1) + 2.0 * along_x
        for k in range(3):
            block = jnp.zeros((ROWS, LANES), F32)
            for q in range(CX + 6):
                block = jnp.where(band == q, turn(wide[k, q], BAND * q + 11), block)
            high[t, k] = block
        for x in range(CX):
            cross, square = products_of(lambda number: hats[number, x])
            inner[t, 0, x] = jnp.where(valid, cross, 0.0)
            inner[t, 1, x] = jnp.where(valid, square, 0.0)
        return carry

    lax.fori_loop(0, 2, step, 0)


def edge_kernel(
    flow, rho, temp, psi, left, right, own_pack, own_halo, inner, high,
    first, second, message,
    wide, halos, psi_wide, psi_halos, weight, work, bands, spread, sums,
):
    ops = Ops()
    band = band_of(ops.lane)
    place = ops.lane - BAND * band
    from_low = place < 3
    from_high = (place == 11) | (place < 2)
    low_side = place < 7
    at_edge = ((place >= 3) & (place <= 5)) | ((place >= 8) & (place <= 10))
    for t in range(2):
        for k in range(3):
            number = STRIP_BLOCKS + 3 * t + k
            far = own_halo[number].astype(F32)
            bands[t, 0, k] = jnp.where(from_low, far, own_pack[number].astype(F32))
            bands[t, 1, k] = jnp.where(from_high, turn(far, 8), high[t, k])
    for k in range(5):
        for i in range(2):
            psi_wide[k, i] = left[PSI_HI + k * 2 + i].astype(F32) + left[
                PSI_LO + k * 2 + i
            ].astype(F32)
            psi_wide[k, 2 + CX + i] = right[PSI_HI + k * 2 + i].astype(F32) + right[
                PSI_LO + k * 2 + i
            ].astype(F32)
        upper, lower = SLOT_PSI_HI + k, SLOT_PSI_LO + k
        upper_strips = own_halo[upper // 4].astype(F32)
        lower_strips = own_halo[lower // 4].astype(F32)
        for x in range(CX):
            psi_wide[k, 2 + x] = psi[k, x]
            psi_halos[k, x] = ops.unpack(upper_strips, 4 * (upper % 4) + x) + ops.unpack(
                lower_strips, 4 * (lower % 4) + x
            )
    for t in range(2):
        spread_state(
            ops, t, t, flow, rho, temp, left, right, own_halo, wide.at[t], halos.at[t]
        )
    for t in range(2):
        for side in range(2):
            velocity = [bands[t, side, k] for k in range(3)]
            grad = [[None] * 3 for _ in range(3)]
            for k in range(3):
                center = velocity[k]
                grad[0][k] = fourth(*(turn(center, -BAND * step) for step in (1, -1, 2, -2)))
                grad[1][k] = 0.5 * (ops.y_up(center) - ops.y_down(center))
                grad[2][k] = fourth(*(turn(center, -step) for step in (1, -1, 2, -2)))
            strain = strain_of(grad)
            for number, values in enumerate(filter_fields(velocity, strain, size_of(strain))):
                if side == 0:
                    spread[t, number] = values
                else:
                    spread[t, number] = jnp.where(low_side, spread[t, number], values)
    for t in range(2):
        for number in range(21):
            both = spread[t, number]
            spread[t, number] = turn(both, BAND) + turn(both, -BAND) + 2.0 * both
    for t in range(2):
        for number in range(21):
            both = spread[t, number]
            spread[t, number] = turn(both, 1) + turn(both, -1) + 2.0 * both
    for x in range(CX):
        terms = state_terms(ops, wide.at[0], halos.at[0], x)
        new, slope, sensitivity = affine_update(ops, x, terms, psi_wide, psi_halos)
        for k in range(5):
            first[k, x] = new[k]
            second[k, x] = slope[k]
        work[0, x] = sensitivity
    for x in range(CX):
        _, _, lap, size, inv_rho = state_terms(ops, wide.at[1], halos.at[1], x, need_all=False)
        size_rho = size * inv_rho
        for part, source in enumerate((first, second)):
            total = lap[0] * source[0, x] + lap[1] * source[1, x] + lap[2] * source[2, x]
            work[1 + part, x] = size_rho * (
                total + (1.0 / PRANDTL_TURB) * (lap[4] * source[4, x])
            )
    for t in range(2):
        for part, values in enumerate(products_of(lambda number: spread[t, number])):
            values = jnp.where(at_edge, values, 0.0)
            for x in range(CX):
                sums[t, part, x] = inner[t, part, x] + jnp.where(band == x + 3, values, 0.0)
    columns = jnp.zeros((ROWS, LANES), F32)
    for t in range(2):
        for part in range(2):
            for x in range(CX):
                total = (1.0 / 256.0) * jnp.sum(sums[t, part, x], axis=1, keepdims=True)
                columns = jnp.where(ops.lane == 8 * t + 4 * part + x, total, columns)
    for part in range(3):
        for x in range(CX):
            total = jnp.sum(work[part, x], axis=1, keepdims=True)
            columns = jnp.where(ops.lane == 16 + 4 * part + x, total, columns)
    for number in range(3):
        planes = {}
        for slot in range(4 * number, min(4 * number + 4, 10)):
            source = first if slot < 5 else second
            for x in range(CX):
                planes[4 * (slot % 4) + x] = source[slot % 5, x]
        message[number] = pack_strips(ops, planes)
    message[3] = columns


def middle_kernel(
    add_own, first, second, own, other, psi, up, down, psi_halos, coef_planes, grads, coef_first
):
    ops = Ops()
    total = own[3] + other[3] if add_own else other[3]
    coef = total / (turn(total, -4) + EPSILON)
    after = total + turn(coef, 20) * turn(total, -4)
    grads[...] = jnp.where(ops.lane < 20, total, after)
    for x in range(CX):
        coef_first[x] = jnp.broadcast_to(coef[:, x : x + 1], (ROWS, LANES))
        coef_planes[x] = jnp.broadcast_to(coef[:, 8 + x : 9 + x], (ROWS, LANES))
    for x in range(CX):
        for k in range(5):
            values = first[k, x] + coef_first[x] * second[k, x]
            psi[k, x] = values
            if x >= 2:
                up[k, x - 2] = values
            else:
                down[k, x] = values
    for k in range(5):
        for x in range(CX):
            base = ops.unpack(other[k // 4], 4 * (k % 4) + x)
            slope = ops.unpack(other[(5 + k) // 4], 4 * ((5 + k) % 4) + x)
            psi_halos[k, x] = base + coef_first[x] * slope


def base_kernel(
    flow, rho, temp, left, right, own_halo, psi, psi_halos, coef_planes,
    base, drift, spread,
    wide, halos, psi_wide,
):
    ops = Ops()
    zero = jnp.zeros((ROWS, LANES), F32)
    for k in range(5):
        for i in range(2):
            psi_wide[k, i] = zero
            psi_wide[k, 2 + CX + i] = zero
        for x in range(CX):
            psi_wide[k, 2 + x] = psi[k, x]
    spread_state(ops, 1, 1, flow, rho, temp, left, right, own_halo, wide, halos)
    for x in range(CX):
        terms = state_terms(ops, wide, halos, x)
        new, slope, _ = affine_update(ops, x, terms, psi_wide, psi_halos)
        for k in range(5):
            base[k, x] = new[k] + coef_planes[x] * slope[k]
        center, _, _, size, inv_rho = terms
        drift[x] = TIME_STEP * center[0]
        if x in (0, CX - 1):
            eddy = coef_planes[x] * size
            scaled = TIME_STEP * inv_rho
            spread[x // (CX - 1), 0] = scaled * (NU_MOL + eddy)
            spread[x // (CX - 1), 1] = scaled * (
                NU_MOL / PRANDTL + (1.0 / PRANDTL_TURB) * eddy
            )


def last_kernel(base, drift, spread, left_psi, right_psi, out):
    for k in range(5):
        far, near = left_psi[k, 0], left_psi[k, 1]
        after, beyond = right_psi[k, 0], right_psi[k, 1]
        low = drift[0] * ((1.0 / 12.0) * far - (2.0 / 3.0) * near)
        high = drift[CX - 1] * ((2.0 / 3.0) * after - (1.0 / 12.0) * beyond)
        if k != 3:
            kind = 1 if k == 4 else 0
            low = low + spread[0, kind] * near
            high = high + spread[1, kind] * after
        out[k, 0] = base[k, 0] + low
        out[k, 1] = base[k, 1] + drift[1] * ((1.0 / 12.0) * near)
        out[k, CX - 2] = base[k, CX - 2] - drift[CX - 2] * ((1.0 / 12.0) * after)
        out[k, CX - 1] = base[k, CX - 1] + high


def ring(axis):
    count = lax.axis_size(axis)
    forward = [(i, (i + 1) % count) for i in range(count)]
    return forward, [(target, source) for source, target in forward]


def span_edges(message, strips):
    forward, backward = ring("gz")
    before = lax.ppermute(message, "gz", forward)
    if lax.axis_size("gz") == 2:
        return before
    after = lax.ppermute(message, "gz", backward)
    lane = lax.broadcasted_iota(jnp.int32, message.shape, 2)
    number = lax.broadcasted_iota(jnp.int32, message.shape, 0)
    low = jnp.where(number < strips, lane % STRIP < 4, lane % BAND < 3)
    return jnp.where(low, before, after)


def shape_of(dims, kind=F32):
    return jax.ShapeDtypeStruct(dims + (ROWS, LANES), kind)


def whole(count):
    return [pl.BlockSpec(memory_space=pltpu.VMEM)] * count


def scratch(*dims):
    return [pltpu.VMEM(d + (ROWS, LANES), F32) for d in dims]


def call(kernel, name, inputs, outputs, operations, buffers=(), in_specs=None):
    size = sum(math.prod(a.shape) * a.dtype.itemsize for a in list(inputs) + list(outputs))
    return pl.pallas_call(
        kernel,
        in_specs=in_specs or whole(len(inputs)),
        out_specs=whole(len(outputs)),
        out_shape=list(outputs),
        scratch_shapes=list(buffers),
        compiler_params=pltpu.CompilerParams(vmem_limit_bytes=24 * 2**20),
        cost_estimate=pl.CostEstimate(
            flops=operations, bytes_accessed=size, transcendentals=0
        ),
        name=name,
    )(*inputs)


def local(flow, rho, temp, psi):
    forward, backward = ring("gx")
    up, down, flow, rho, temp, psi = call(
        message_kernel,
        "message",
        (flow, rho, temp, psi),
        [shape_of((MESSAGE,), BF16)] * 2
        + [
            shape_of((2, 3, CX), BF16),
            shape_of((2, CX), BF16),
            shape_of((2, CX), BF16),
            shape_of((5, CX)),
        ],
        1_000_000,
        [pltpu.SemaphoreType.DMA((4,))],
        [pl.BlockSpec(memory_space=pltpu.MemorySpace.HBM)] * 4,
    )
    left = lax.ppermute(up, "gx", forward)
    right = lax.ppermute(down, "gx", backward)
    (packed,) = call(
        pack_kernel,
        "pack",
        (flow, rho, temp, psi),
        [shape_of((STRIP_BLOCKS + 6,), BF16)],
        2_000_000,
    )
    (packed,) = call(
        bands_kernel,
        "bands",
        (packed, left, right),
        [shape_of((STRIP_BLOCKS + 6,), BF16)],
        1_000_000,
    )
    own_halo = span_edges(packed, STRIP_BLOCKS)
    inner, high = call(
        inner_kernel,
        "inner",
        (flow, left, right),
        [shape_of((2, 2, CX)), shape_of((2, 3))],
        30_000_000,
        scratch((3, CX + 6), (21, CX + 2), (21, CX)),
    )
    first, second, message = call(
        edge_kernel,
        "edge",
        (flow, rho, temp, psi, left, right, packed, own_halo, inner, high),
        [shape_of((5, CX)), shape_of((5, CX)), shape_of((4,))],
        20_000_000,
        scratch(
            (2, 5, CX + 4), (2, 5, CX), (5, CX + 4), (5, CX), (4, CX), (3, CX),
            (2, 2, 3), (2, 21), (2, 2, CX),
        ),
    )
    other = span_edges(message, 4)
    add_own = lax.axis_size("gz") == 2
    if not add_own:
        total = lax.psum(message[3], "gz")
        other = jnp.concatenate([other[:3], total[None]], axis=0)
    psi, up, down, psi_halos, coef_planes, grads = call(
        functools.partial(middle_kernel, add_own),
        "middle",
        (first, second, message, other),
        [
            shape_of((5, CX)), shape_of((5, 2)), shape_of((5, 2)),
            shape_of((5, CX)), shape_of((CX,)), shape_of(()),
        ],
        1_000_000,
        scratch((CX,)),
    )
    left_psi = lax.ppermute(up, "gx", forward)
    right_psi = lax.ppermute(down, "gx", backward)
    base, drift, spread = call(
        base_kernel,
        "base",
        (flow, rho, temp, left, right, own_halo, psi, psi_halos, coef_planes),
        [shape_of((5, CX)), shape_of((CX,)), shape_of((2, 2))],
        15_000_000,
        scratch((5, CX + 4), (5, CX), (5, CX + 4)),
    )
    (out,) = call(
        last_kernel,
        "last",
        (base, drift, spread, left_psi, right_psi),
        [shape_of((5, CX))],
        1_000_000,
    )
    span_cells = LANES * lax.axis_size("gz")
    coef_grad = grads[:, 16:24].T.reshape(2, CX, ROWS) * (1.0 / span_cells)
    return out, coef_grad


def solution(mesh):
    return jax.shard_map(
        local,
        mesh=mesh,
        in_specs=(
            P(None, None, "gx", None, "gz"),
            P(None, "gx", None, "gz"),
            P(None, "gx", None, "gz"),
            P(None, "gx", None, "gz"),
        ),
        out_specs=(P(None, "gx", None, "gz"), P(None, "gx", None)),
        check_vma=False,
    )
```

```python
import functools
import math

import jax
import jax.numpy as jnp
from jax import lax
from jax.experimental import pallas as pl
from jax.experimental.pallas import tpu as pltpu
from jax.sharding import PartitionSpec as P

EPSILON = 1e-06
NU_MOL = 0.05
PRANDTL = 0.72
PRANDTL_TURB = 0.9
TIME_STEP = 0.04
PAIRS = ((0, 0), (1, 1), (2, 2), (0, 1), (0, 2), (1, 2))
WEIGHTS = (1.0, 1.0, 1.0, 2.0, 2.0, 2.0)

CX = 4
ROWS = 32
LANES = 128
STRIP = 8
F32 = jnp.float32
BF16 = jnp.bfloat16
SLOT_T = 8
SLOT_PSI = 10
BAND = 12
STRIP_BLOCKS = 4
VELOCITY = 0
SCALARS = 18
PSI = 26
MESSAGE = 36


def lane_ids():
    return lax.broadcasted_iota(jnp.int32, (ROWS, LANES), 1)


def row_ids():
    return lax.broadcasted_iota(jnp.int32, (ROWS, LANES), 0)


def turn(values, shift):
    shift = shift % LANES
    return values if shift == 0 else pltpu.roll(values, shift, 1)


class Ops:
    def __init__(self):
        self.lane = lane_ids()
        row = row_ids()
        self.top = row == ROWS - 1
        self.bottom = row == 0

    def z_at(self, values, halo, step):
        if step > 0:
            return turn(jnp.where(self.lane < step, halo, values), -step)
        return turn(jnp.where(self.lane >= LANES + step, halo, values), -step)

    def y_up(self, values):
        return jnp.where(self.top, 0.0, pltpu.roll(values, ROWS - 1, 0))

    def y_down(self, values):
        return jnp.where(self.bottom, 0.0, pltpu.roll(values, 1, 0))

    def unpack(self, block, strip):
        return turn(block, LANES - 4 - STRIP * strip)


def fourth(plus, minus, plus_2, minus_2):
    return (2.0 / 3.0) * (plus - minus) - (1.0 / 12.0) * (plus_2 - minus_2)


def strain_of(grad):
    return [
        grad[0][0],
        grad[1][1],
        grad[2][2],
        0.5 * (grad[0][1] + grad[1][0]),
        0.5 * (grad[0][2] + grad[2][0]),
        0.5 * (grad[1][2] + grad[2][1]),
    ]


def size_of(strain):
    diagonal = strain[0] * strain[0] + strain[1] * strain[1] + strain[2] * strain[2]
    other = strain[3] * strain[3] + strain[4] * strain[4] + strain[5] * strain[5]
    return jnp.sqrt(2.0 * diagonal + (4.0 * other + EPSILON))


def filter_fields(velocity, strain, size):
    products = [velocity[a] * velocity[b] for a, b in PAIRS]
    return list(velocity) + products + strain + [size * part for part in strain]


def pack_strips(ops, planes):
    block = jnp.zeros((ROWS, LANES), F32)
    strip_id = (ops.lane >> 3)
    for strip, values in planes.items():
        block = jnp.where(strip_id == strip, turn(values, STRIP * strip + 4), block)
    return block


def place_halos(ops, t, own_halo, halos):
    for k in range(5):
        slot = 4 * t + k if k < 4 else SLOT_T + t
        strips = own_halo[slot // 4].astype(F32)
        for x in range(CX):
            halos[k, x] = ops.unpack(strips, 4 * (slot % 4) + x)


def state_terms(ops, wide, halos, x, need_all=True):
    grad = [[None] * 5 for _ in range(3)]
    lap = [None] * 5
    center = [wide[k, x + 3] for k in range(5)]
    for k in range(5):
        if k == 3 and not need_all:
            continue
        edge = halos[k, x]
        up, down = ops.y_up(center[k]), ops.y_down(center[k])
        xs = [wide[k, x + 3 + step] for step in (1, -1, 2, -2)]
        zs = [ops.z_at(center[k], edge, step) for step in (1, -1, 2, -2)]
        if k < 3 or need_all:
            grad[0][k] = fourth(*xs)
            grad[1][k] = 0.5 * (up - down)
            grad[2][k] = fourth(*zs)
        if k != 3:
            lap[k] = xs[0] + xs[1] + zs[0] + zs[1] + up + down - 6.0 * center[k]
    size = size_of(strain_of(grad))
    return center, grad, lap, size, 1.0 / center[3]


def affine_update(ops, x, terms, psi_wide, psi_halos):
    center, grad, lap, size, inv_rho = terms
    psi = [psi_wide[k, x + 2] for k in range(5)]
    work_mom = psi[0] * lap[0] + psi[1] * lap[1] + psi[2] * lap[2]
    work_heat = psi[4] * lap[4]
    turbulent = work_mom + work_heat * (1.0 / PRANDTL_TURB)
    inv_rho_2 = inv_rho * inv_rho
    size_rho = size * inv_rho
    first, second = [], []
    for k in range(5):
        edge = psi_halos[k, x]
        up, down = ops.y_up(psi[k]), ops.y_down(psi[k])
        xs = [psi_wide[k, x + 2 + step] for step in (1, -1, 2, -2)]
        zs = [ops.z_at(psi[k], edge, step) for step in (1, -1, 2, -2)]
        rate = (
            center[0] * fourth(*xs) + center[1] * (0.5 * (up - down)) + center[2] * fourth(*zs)
        )
        if k == 3:
            rate = rate - (NU_MOL * work_mom + (NU_MOL / PRANDTL) * work_heat) * inv_rho_2
            eddy = -(size * turbulent) * inv_rho_2
        else:
            lap_psi = xs[0] + xs[1] + zs[0] + zs[1] + up + down - 6.0 * psi[k]
            if k < 3:
                for other in range(5):
                    rate = rate + psi[other] * grad[k][other]
                rate = rate + NU_MOL * (inv_rho * lap_psi)
                eddy = size_rho * lap_psi
            else:
                rate = rate + (NU_MOL / PRANDTL) * (inv_rho * lap_psi)
                eddy = (1.0 / PRANDTL_TURB) * (size_rho * lap_psi)
        first.append(psi[k] + TIME_STEP * rate)
        second.append(TIME_STEP * eddy)
    return first, second, size_rho * turbulent


def band_of(lane):
    return (lane * 43) >> 9


def is_even():
    return lax.rem(lax.axis_index("gx"), 2) == 0


def message_kernel(
    flow_far, rho_far, temp_far, psi_far, near, far, flow, rho, temp, psi, sems
):
    copies = [
        pltpu.make_async_copy(source, target, sems.at[i])
        for i, (source, target) in enumerate(
            ((flow_far, flow), (psi_far, psi), (rho_far, rho), (temp_far, temp))
        )
    ]
    for copy in copies:
        copy.start()
    even = is_even().astype(jnp.int32)
    sides = ((near, even), (far, 1 - even))
    copies[0].wait()
    for out, side in sides:
        for t in range(2):
            for k in range(3):
                for i in range(3):
                    out[t * 9 + k * 3 + i] = flow[t, k, side + i]
    copies[1].wait()
    for out, side in sides:
        for k in range(5):
            for i in range(2):
                out[PSI + k * 2 + i] = psi[k, 2 * side + i].astype(BF16)
    copies[2].wait()
    copies[3].wait()
    for out, side in sides:
        for t in range(2):
            for i in range(2):
                out[SCALARS + t * 4 + i] = rho[t, 2 * side + i]
                out[SCALARS + t * 4 + 2 + i] = temp[t, 2 * side + i]


def pack_kernel(flow, rho, temp, psi, packed):
    ops = Ops()
    items = []
    for t in range(2):
        items += [[flow[t, k, x].astype(F32) for x in range(CX)] for k in range(3)]
        items += [[rho[t, x].astype(F32) for x in range(CX)]]
    items += [[temp[t, x].astype(F32) for x in range(CX)] for t in range(2)]
    items += [[psi[k, x] for x in range(CX)] for k in range(5)]
    for number in range(STRIP_BLOCKS):
        planes = {}
        for slot, item in enumerate(items[4 * number : 4 * number + 4]):
            for x in range(CX):
                planes[4 * slot + x] = item[x]
        packed[number] = pack_strips(ops, planes).astype(BF16)
    band = band_of(ops.lane)
    for t in range(2):
        for k in range(3):
            block = jnp.zeros((ROWS, LANES), F32)
            for x in range(CX):
                moved = turn(flow[t, k, x].astype(F32), BAND * (x + 3) + 3)
                block = jnp.where(band == x + 3, moved, block)
            packed[STRIP_BLOCKS + 3 * t + k] = block.astype(BF16)


def bands_kernel(packed, near, far, out):
    ops = Ops()
    even = is_even()
    for number in range(STRIP_BLOCKS):
        out[number] = packed[number]
    band = band_of(ops.lane)
    for t in range(2):
        for k in range(3):
            block = packed[STRIP_BLOCKS + 3 * t + k].astype(F32)
            for i in range(3):
                number = VELOCITY + t * 9 + k * 3 + i
                one, two = near[number].astype(F32), far[number].astype(F32)
                moved = turn(jnp.where(even, two, one), BAND * i + 3)
                block = jnp.where(band == i, moved, block)
                moved = turn(jnp.where(even, one, two), BAND * (7 + i) + 3)
                block = jnp.where(band == 7 + i, moved, block)
            out[STRIP_BLOCKS + 3 * t + k] = block.astype(BF16)


def products_of(hat):
    velocity = [hat(k) for k in range(3)]
    strain = [hat(9 + number) for number in range(6)]
    diagonal = strain[0] * strain[0] + strain[1] * strain[1] + strain[2] * strain[2]
    other = strain[3] * strain[3] + strain[4] * strain[4] + strain[5] * strain[5]
    size = 4.0 * jnp.sqrt((2.0 / 256.0) * diagonal + ((4.0 / 256.0) * other + EPSILON))
    cross = 0.0
    square = 0.0
    for number, (a, b) in enumerate(PAIRS):
        leonard = hat(3 + number) - (1.0 / 16.0) * velocity[a] * velocity[b]
        model = hat(15 + number) - size * strain[number]
        weighted = WEIGHTS[number] * model if WEIGHTS[number] != 1.0 else model
        cross = cross + leonard * weighted
        square = square + model * weighted
    return cross, square


def inner_kernel(
    flow, rho, temp, psi, near, far, inner, high, wide, psi_wide, fields, hats
):
    ops = Ops()
    even = is_even()
    valid = (ops.lane >= 3) & (ops.lane < LANES - 3)
    band = band_of(jnp.maximum(ops.lane - 2, 0))

    def sides(number):
        one, two = near[number].astype(F32), far[number].astype(F32)
        return jnp.where(even, two, one), jnp.where(even, one, two)

    for k in range(5):
        for i in range(2):
            psi_wide[k, i], psi_wide[k, 2 + CX + i] = sides(PSI + k * 2 + i)
        for x in range(CX):
            psi_wide[k, 2 + x] = psi[k, x]

    def step(t, carry):
        for k in range(3):
            for i in range(3):
                wide[t, k, i], wide[t, k, 7 + i] = sides(VELOCITY + t * 9 + k * 3 + i)
            for x in range(CX):
                wide[t, k, 3 + x] = flow[t, k, x].astype(F32)
        for k, source in ((3, rho), (4, temp)):
            for i in range(2):
                wide[t, k, 1 + i], wide[t, k, 7 + i] = sides(
                    SCALARS + t * 4 + (k - 3) * 2 + i
                )
            for x in range(CX):
                wide[t, k, 3 + x] = source[t, x].astype(F32)
        for x in range(-1, CX + 1):
            grad = [[None] * 3 for _ in range(3)]
            for k in range(3):
                center = wide[t, k, x + 3]
                grad[0][k] = fourth(
                    wide[t, k, x + 4], wide[t, k, x + 2], wide[t, k, x + 5], wide[t, k, x + 1]
                )
                grad[1][k] = 0.5 * (ops.y_up(center) - ops.y_down(center))
                grad[2][k] = fourth(*(turn(center, -step) for step in (1, -1, 2, -2)))
            strain = strain_of(grad)
            size = size_of(strain)
            velocity = [wide[t, k, x + 3] for k in range(3)]
            for number, values in enumerate(filter_fields(velocity, strain, size)):
                fields[number, x + 1] = values
        for x in range(CX):
            for number in range(21):
                along_x = (
                    fields[number, x] + fields[number, x + 2] + 2.0 * fields[number, x + 1]
                )
                hats[number, x] = turn(along_x, 1) + turn(along_x, -1) + 2.0 * along_x
        for k in range(3):
            block = jnp.zeros((ROWS, LANES), F32)
            for q in range(CX + 6):
                block = jnp.where(band == q, turn(wide[t, k, q], BAND * q + 11), block)
            high[t, k] = block
        for x in range(CX):
            cross, square = products_of(lambda number: hats[number, x])
            inner[t, 0, x] = jnp.where(valid, cross, 0.0)
            inner[t, 1, x] = jnp.where(valid, square, 0.0)
        return carry

    lax.fori_loop(0, 2, step, 0)


def edge_kernel(
    wide, psi_wide, own_pack, own_halo, inner, high,
    first, second, message,
    halos, psi_halos, work, bands, spread, sums,
):
    ops = Ops()
    band = band_of(ops.lane)
    place = ops.lane - BAND * band
    from_low = place < 3
    from_high = (place == 11) | (place < 2)
    low_side = place < 7
    at_edge = ((place >= 3) & (place <= 5)) | ((place >= 8) & (place <= 10))
    for t in range(2):
        for k in range(3):
            number = STRIP_BLOCKS + 3 * t + k
            far = own_halo[number].astype(F32)
            bands[t, 0, k] = jnp.where(from_low, far, own_pack[number].astype(F32))
            bands[t, 1, k] = jnp.where(from_high, turn(far, 8), high[t, k])
    for k in range(5):
        strips = own_halo[(SLOT_PSI + k) // 4].astype(F32)
        for x in range(CX):
            psi_halos[k, x] = ops.unpack(strips, 4 * ((SLOT_PSI + k) % 4) + x)
    for t in range(2):
        place_halos(ops, t, own_halo, halos.at[t])
    for t in range(2):
        for side in range(2):
            velocity = [bands[t, side, k] for k in range(3)]
            grad = [[None] * 3 for _ in range(3)]
            for k in range(3):
                center = velocity[k]
                grad[0][k] = fourth(*(turn(center, -BAND * step) for step in (1, -1, 2, -2)))
                grad[1][k] = 0.5 * (ops.y_up(center) - ops.y_down(center))
                grad[2][k] = fourth(*(turn(center, -step) for step in (1, -1, 2, -2)))
            strain = strain_of(grad)
            for number, values in enumerate(filter_fields(velocity, strain, size_of(strain))):
                if side == 0:
                    spread[t, number] = values
                else:
                    spread[t, number] = jnp.where(low_side, spread[t, number], values)
    for t in range(2):
        for number in range(21):
            both = spread[t, number]
            spread[t, number] = turn(both, BAND) + turn(both, -BAND) + 2.0 * both
    for t in range(2):
        for number in range(21):
            both = spread[t, number]
            spread[t, number] = turn(both, 1) + turn(both, -1) + 2.0 * both
    for x in range(CX):
        terms = state_terms(ops, wide.at[0], halos.at[0], x)
        new, slope, sensitivity = affine_update(ops, x, terms, psi_wide, psi_halos)
        for k in range(5):
            first[k, x] = new[k]
            second[k, x] = slope[k]
        work[0, x] = sensitivity
    for x in range(CX):
        _, _, lap, size, inv_rho = state_terms(ops, wide.at[1], halos.at[1], x, need_all=False)
        size_rho = size * inv_rho
        for part, source in enumerate((first, second)):
            total = lap[0] * source[0, x] + lap[1] * source[1, x] + lap[2] * source[2, x]
            work[1 + part, x] = size_rho * (
                total + (1.0 / PRANDTL_TURB) * (lap[4] * source[4, x])
            )
    for t in range(2):
        for part, values in enumerate(products_of(lambda number: spread[t, number])):
            values = jnp.where(at_edge, values, 0.0)
            for x in range(CX):
                sums[t, part, x] = inner[t, part, x] + jnp.where(band == x + 3, values, 0.0)
    columns = jnp.zeros((ROWS, LANES), F32)
    for t in range(2):
        for part in range(2):
            for x in range(CX):
                total = (1.0 / 256.0) * jnp.sum(sums[t, part, x], axis=1, keepdims=True)
                columns = jnp.where(ops.lane == 8 * t + 4 * part + x, total, columns)
    for part in range(3):
        for x in range(CX):
            total = jnp.sum(work[part, x], axis=1, keepdims=True)
            columns = jnp.where(ops.lane == 16 + 4 * part + x, total, columns)
    for number in range(3):
        planes = {}
        for slot in range(4 * number, min(4 * number + 4, 10)):
            source = first if slot < 5 else second
            for x in range(CX):
                planes[4 * (slot % 4) + x] = source[slot % 5, x]
        message[number] = pack_strips(ops, planes)
    message[3] = columns


def middle_kernel(
    add_own, first, second, own, other, psi, near, far, psi_halos, coef_planes, grads, coef_first
):
    ops = Ops()
    total = own[3] + other[3] if add_own else other[3]
    coef = total / (turn(total, -4) + EPSILON)
    after = total + turn(coef, 20) * turn(total, -4)
    grads[...] = jnp.where(ops.lane < 20, total, after)
    for x in range(CX):
        coef_first[x] = jnp.broadcast_to(coef[:, x : x + 1], (ROWS, LANES))
        coef_planes[x] = jnp.broadcast_to(coef[:, 8 + x : 9 + x], (ROWS, LANES))
    for x in range(CX):
        for k in range(5):
            values = first[k, x] + coef_first[x] * second[k, x]
            psi[k, x] = values
    for k in range(5):
        for x in range(CX):
            base = ops.unpack(other[k // 4], 4 * (k % 4) + x)
            slope = ops.unpack(other[(5 + k) // 4], 4 * ((5 + k) % 4) + x)
            psi_halos[k, x] = base + coef_first[x] * slope
    even = is_even().astype(jnp.int32)
    for out, side in ((near, even), (far, 1 - even)):
        for k in range(5):
            for i in range(2):
                out[k, i] = psi[k, 2 * side + i].astype(BF16)


def base_kernel(
    wide, own_halo, psi, psi_halos, coef_planes,
    base, drift, spread,
    halos, psi_wide,
):
    ops = Ops()
    zero = jnp.zeros((ROWS, LANES), F32)
    for k in range(5):
        for i in range(2):
            psi_wide[k, i] = zero
            psi_wide[k, 2 + CX + i] = zero
        for x in range(CX):
            psi_wide[k, 2 + x] = psi[k, x]
    place_halos(ops, 1, own_halo, halos)
    for x in range(CX):
        terms = state_terms(ops, wide.at[1], halos, x)
        new, slope, _ = affine_update(ops, x, terms, psi_wide, psi_halos)
        for k in range(5):
            base[k, x] = new[k] + coef_planes[x] * slope[k]
        center, _, _, size, inv_rho = terms
        drift[x] = TIME_STEP * center[0]
        if x in (0, CX - 1):
            eddy = coef_planes[x] * size
            scaled = TIME_STEP * inv_rho
            spread[x // (CX - 1), 0] = scaled * (NU_MOL + eddy)
            spread[x // (CX - 1), 1] = scaled * (
                NU_MOL / PRANDTL + (1.0 / PRANDTL_TURB) * eddy
            )


def last_kernel(base, drift, spread, near_psi, far_psi, out):
    even = is_even()
    for k in range(5):
        ones = [near_psi[k, i].astype(F32) for i in range(2)]
        twos = [far_psi[k, i].astype(F32) for i in range(2)]
        far, near = (jnp.where(even, two, one) for one, two in zip(ones, twos))
        after, beyond = (jnp.where(even, one, two) for one, two in zip(ones, twos))
        low = drift[0] * ((1.0 / 12.0) * far - (2.0 / 3.0) * near)
        high = drift[CX - 1] * ((2.0 / 3.0) * after - (1.0 / 12.0) * beyond)
        if k != 3:
            kind = 1 if k == 4 else 0
            low = low + spread[0, kind] * near
            high = high + spread[1, kind] * after
        out[k, 0] = base[k, 0] + low
        out[k, 1] = base[k, 1] + drift[1] * ((1.0 / 12.0) * near)
        out[k, CX - 2] = base[k, CX - 2] - drift[CX - 2] * ((1.0 / 12.0) * after)
        out[k, CX - 1] = base[k, CX - 1] + high


def ring(axis):
    count = lax.axis_size(axis)
    forward = [(i, (i + 1) % count) for i in range(count)]
    return forward, [(target, source) for source, target in forward]


def pairs():
    count = lax.axis_size("gx")
    if count % 2:
        raise ValueError("odd gx")
    inside = [(i, i ^ 1) for i in range(count)]
    across = [(i, (i + 1 if i % 2 else i - 1) % count) for i in range(count)]
    return inside, across


def span_edges(message, strips):
    forward, backward = ring("gz")
    before = lax.ppermute(message, "gz", forward)
    if lax.axis_size("gz") == 2:
        return before
    after = lax.ppermute(message, "gz", backward)
    lane = lax.broadcasted_iota(jnp.int32, message.shape, 2)
    number = lax.broadcasted_iota(jnp.int32, message.shape, 0)
    low = jnp.where(number < strips, lane % STRIP < 4, lane % BAND < 3)
    return jnp.where(low, before, after)


def shape_of(dims, kind=F32):
    return jax.ShapeDtypeStruct(dims + (ROWS, LANES), kind)


def whole(count):
    return [pl.BlockSpec(memory_space=pltpu.VMEM)] * count


def scratch(*dims):
    return [pltpu.VMEM(d + (ROWS, LANES), F32) for d in dims]


def call(kernel, name, inputs, outputs, operations, buffers=(), in_specs=None):
    size = sum(math.prod(a.shape) * a.dtype.itemsize for a in list(inputs) + list(outputs))
    return pl.pallas_call(
        kernel,
        in_specs=in_specs or whole(len(inputs)),
        out_specs=whole(len(outputs)),
        out_shape=list(outputs),
        scratch_shapes=list(buffers),
        compiler_params=pltpu.CompilerParams(vmem_limit_bytes=24 * 2**20),
        cost_estimate=pl.CostEstimate(
            flops=operations, bytes_accessed=size, transcendentals=0
        ),
        name=name,
    )(*inputs)


def local(flow, rho, temp, psi):
    inside, across = pairs()
    near, far, flow, rho, temp, psi = call(
        message_kernel,
        "message",
        tuple(
            pltpu.with_memory_space_constraint(a, pltpu.MemorySpace.HBM)
            for a in (flow, rho, temp, psi)
        ),
        [shape_of((MESSAGE,), BF16)] * 2
        + [
            shape_of((2, 3, CX), BF16),
            shape_of((2, CX), BF16),
            shape_of((2, CX), BF16),
            shape_of((5, CX)),
        ],
        1_000_000,
        [pltpu.SemaphoreType.DMA((4,))],
        [pl.BlockSpec(memory_space=pltpu.MemorySpace.HBM)] * 4,
    )
    far = lax.ppermute(far, "gx", across)
    near = lax.ppermute(near, "gx", inside)
    (packed,) = call(
        pack_kernel,
        "pack",
        (flow, rho, temp, psi),
        [shape_of((STRIP_BLOCKS + 6,), BF16)],
        2_000_000,
    )
    (packed,) = call(
        bands_kernel,
        "bands",
        (packed, near, far),
        [shape_of((STRIP_BLOCKS + 6,), BF16)],
        1_000_000,
    )
    own_halo = span_edges(packed, STRIP_BLOCKS)
    inner, high, wide, psi_wide = call(
        inner_kernel,
        "inner",
        (flow, rho, temp, psi, near, far),
        [
            shape_of((2, 2, CX)), shape_of((2, 3)),
            shape_of((2, 5, CX + 6)), shape_of((5, CX + 4)),
        ],
        30_000_000,
        scratch((21, CX + 2), (21, CX)),
    )
    first, second, message = call(
        edge_kernel,
        "edge",
        (wide, psi_wide, packed, own_halo, inner, high),
        [shape_of((5, CX)), shape_of((5, CX)), shape_of((4,))],
        20_000_000,
        scratch(
            (2, 5, CX), (5, CX), (3, CX), (2, 2, 3), (2, 21), (2, 2, CX)
        ),
    )
    other = span_edges(message, 4)
    add_own = lax.axis_size("gz") == 2
    if not add_own:
        total = lax.psum(message[3], "gz")
        other = jnp.concatenate([other[:3], total[None]], axis=0)
    psi, near, far, psi_halos, coef_planes, grads = call(
        functools.partial(middle_kernel, add_own),
        "middle",
        (first, second, message, other),
        [
            shape_of((5, CX)), shape_of((5, 2), BF16), shape_of((5, 2), BF16),
            shape_of((5, CX)), shape_of((CX,)), shape_of(()),
        ],
        1_000_000,
        scratch((CX,)),
    )
    far = lax.ppermute(far, "gx", across)
    near = lax.ppermute(near, "gx", inside)
    base, drift, spread = call(
        base_kernel,
        "base",
        (wide, own_halo, psi, psi_halos, coef_planes),
        [shape_of((5, CX)), shape_of((CX,)), shape_of((2, 2))],
        15_000_000,
        scratch((5, CX), (5, CX + 4)),
    )
    (out,) = call(
        last_kernel,
        "last",
        (base, drift, spread, near, far),
        [shape_of((5, CX))],
        1_000_000,
    )
    span_cells = LANES * lax.axis_size("gz")
    coef_grad = grads[:, 16:24].T.reshape(2, CX, ROWS) * (1.0 / span_cells)
    return out, coef_grad


def solution(mesh):
    return jax.shard_map(
        local,
        mesh=mesh,
        in_specs=(
            P(None, None, "gx", None, "gz"),
            P(None, "gx", None, "gz"),
            P(None, "gx", None, "gz"),
            P(None, "gx", None, "gz"),
        ),
        out_specs=(P(None, "gx", None, "gz"), P(None, "gx", None)),
        check_vma=False,
    )
```

```python
import functools
import math

import jax
import jax.numpy as jnp
from jax import lax
from jax.experimental import pallas as pl
from jax.experimental.pallas import tpu as pltpu
from jax.sharding import PartitionSpec as P

EPSILON = 1e-06
NU_MOL = 0.05
PRANDTL = 0.72
PRANDTL_TURB = 0.9
TIME_STEP = 0.04
PAIRS = ((0, 0), (1, 1), (2, 2), (0, 1), (0, 2), (1, 2))
WEIGHTS = (1.0, 1.0, 1.0, 2.0, 2.0, 2.0)

CX = 4
ROWS = 32
LANES = 128
STRIP = 4
F32 = jnp.float32
BF16 = jnp.bfloat16
SLOT_PSI = 4
BAND = 12
STRIP_BLOCKS = 2
BAND_BLOCKS = 3
VELOCITY = 0
SCALARS = 18
PSI = 26
MESSAGE = 36


def lane_ids():
    return lax.broadcasted_iota(jnp.int32, (ROWS, LANES), 1)


def row_ids():
    return lax.broadcasted_iota(jnp.int32, (ROWS, LANES), 0)


def turn(values, shift):
    shift = shift % LANES
    return values if shift == 0 else pltpu.roll(values, shift, 1)


class Ops:
    def __init__(self):
        self.lane = lane_ids()
        row = row_ids()
        self.top = row == ROWS - 1
        self.bottom = row == 0

    def z_at(self, values, halo, step):
        if step > 0:
            return turn(jnp.where(self.lane < step, halo, values), -step)
        return turn(jnp.where(self.lane >= LANES + step, halo, values), -step)

    def y_up(self, values):
        return jnp.where(self.top, 0.0, pltpu.roll(values, ROWS - 1, 0))

    def y_down(self, values):
        return jnp.where(self.bottom, 0.0, pltpu.roll(values, 1, 0))

    def strip(self, blocks, slot, x):
        return turn(blocks[slot // 8], -(STRIP * (4 * (slot % 8) + x) + 2))


def fourth(plus, minus, plus_2, minus_2):
    return (2.0 / 3.0) * (plus - minus) - (1.0 / 12.0) * (plus_2 - minus_2)


def strain_of(grad):
    return [
        grad[0][0],
        grad[1][1],
        grad[2][2],
        0.5 * (grad[0][1] + grad[1][0]),
        0.5 * (grad[0][2] + grad[2][0]),
        0.5 * (grad[1][2] + grad[2][1]),
    ]


def size_of(strain):
    diagonal = strain[0] * strain[0] + strain[1] * strain[1] + strain[2] * strain[2]
    other = strain[3] * strain[3] + strain[4] * strain[4] + strain[5] * strain[5]
    return jnp.sqrt(2.0 * diagonal + (4.0 * other + EPSILON))


def filter_fields(velocity, strain, size):
    products = [velocity[a] * velocity[b] for a, b in PAIRS]
    return list(velocity) + products + strain + [size * part for part in strain]


def pack_strips(ops, items):
    block = jnp.zeros((ROWS, LANES), F32)
    strip_id = ops.lane >> 2
    for slot, planes in enumerate(items):
        for x in range(CX):
            number = 4 * slot + x
            block = jnp.where(strip_id == number, turn(planes[x], STRIP * number + 2), block)
    return block


def place_halos(ops, t, own_halo, halos):
    strips = [own_halo[number].astype(F32) for number in range(STRIP_BLOCKS)]
    for k in range(3):
        number = 3 * t + k
        bands = own_halo[STRIP_BLOCKS + number // 2].astype(F32)
        for x in range(CX):
            halos[k, x] = turn(bands, -(BAND * (x + 3) + 3 + 6 * (number % 2)))
    for k in range(3, 5):
        for x in range(CX):
            halos[k, x] = ops.strip(strips, 2 * t + k - 3, x)


def plane_terms(ops, values, xs):
    up, down = ops.y_up(values), ops.y_down(values)
    lap = xs[0] + xs[1] + up + down - 6.0 * values
    return fourth(*xs), 0.5 * (up - down), lap


def state_terms(ops, wide, grad_xy, lap_xy, halos, x, need_all=True):
    grad = [[None] * 5 for _ in range(3)]
    lap = [None] * 5
    center = [wide[k, x + 3] for k in range(5)]
    for k in range(5):
        if k == 3 and not need_all:
            continue
        zs = [ops.z_at(center[k], halos[k, x], step) for step in (1, -1, 2, -2)]
        if k < 3 or need_all:
            grad[0][k] = grad_xy[k, 0, x]
            grad[1][k] = grad_xy[k, 1, x]
            grad[2][k] = fourth(*zs)
        if k != 3:
            lap[k] = lap_xy[k, x] + (zs[0] + zs[1])
    size = size_of(strain_of(grad))
    return center, grad, lap, size, 1.0 / center[3]


def affine_update(ops, x, terms, psi, rate_xy, lap_psi_xy, psi_halos):
    center, grad, lap, size, inv_rho = terms
    work_mom = psi[0] * lap[0] + psi[1] * lap[1] + psi[2] * lap[2]
    work_heat = psi[4] * lap[4]
    turbulent = work_mom + work_heat * (1.0 / PRANDTL_TURB)
    inv_rho_2 = inv_rho * inv_rho
    size_rho = size * inv_rho
    first, second = [], []
    for k in range(5):
        zs = [ops.z_at(psi[k], psi_halos[k, x], step) for step in (1, -1, 2, -2)]
        rate = rate_xy[k] + center[2] * fourth(*zs)
        if k == 3:
            rate = rate - (NU_MOL * work_mom + (NU_MOL / PRANDTL) * work_heat) * inv_rho_2
            eddy = -(size * turbulent) * inv_rho_2
        else:
            lap_psi = lap_psi_xy[k] + (zs[0] + zs[1])
            if k < 3:
                for other in range(5):
                    rate = rate + psi[other] * grad[k][other]
                rate = rate + NU_MOL * (inv_rho * lap_psi)
                eddy = size_rho * lap_psi
            else:
                rate = rate + (NU_MOL / PRANDTL) * (inv_rho * lap_psi)
                eddy = (1.0 / PRANDTL_TURB) * (size_rho * lap_psi)
        first.append(psi[k] + TIME_STEP * rate)
        second.append(TIME_STEP * eddy)
    return first, second, size_rho * turbulent


def band_of(lane):
    return (lane * 43) >> 9


def is_even():
    return lax.rem(lax.axis_index("gx"), 2) == 0


def message_kernel(
    flow_far, rho_far, temp_far, psi_far, near, far, flow, rho, temp, psi, sems
):
    copies = [
        pltpu.make_async_copy(source, target, sems.at[i])
        for i, (source, target) in enumerate(
            ((flow_far, flow), (psi_far, psi), (rho_far, rho), (temp_far, temp))
        )
    ]
    for copy in copies:
        copy.start()
    even = is_even().astype(jnp.int32)
    sides = ((near, even), (far, 1 - even))
    copies[0].wait()
    for out, side in sides:
        for t in range(2):
            for k in range(3):
                for i in range(3):
                    out[t * 9 + k * 3 + i] = flow[t, k, side + i]
    copies[1].wait()
    for out, side in sides:
        for k in range(5):
            for i in range(2):
                out[PSI + k * 2 + i] = psi[k, 2 * side + i].astype(BF16)
    copies[2].wait()
    copies[3].wait()
    for out, side in sides:
        for t in range(2):
            for i in range(2):
                out[SCALARS + t * 4 + i] = rho[t, 2 * side + i]
                out[SCALARS + t * 4 + 2 + i] = temp[t, 2 * side + i]


def pack_kernel(flow, rho, temp, psi, strips, low):
    ops = Ops()
    items = []
    for t in range(2):
        for source in (rho, temp):
            items.append([source[t, x].astype(F32) for x in range(CX)])
    items += [[psi[k, x] for x in range(CX)] for k in range(5)]
    for number in range(STRIP_BLOCKS):
        strips[number] = pack_strips(ops, items[8 * number : 8 * number + 8]).astype(BF16)
    band = band_of(ops.lane)
    for t in range(2):
        for k in range(3):
            block = jnp.zeros((ROWS, LANES), F32)
            for x in range(CX):
                moved = turn(flow[t, k, x].astype(F32), BAND * (x + 3) + 3)
                block = jnp.where(band == x + 3, moved, block)
            low[3 * t + k] = block


def bands_kernel(strips, own_low, near, far, message, low):
    ops = Ops()
    even = is_even()
    for number in range(STRIP_BLOCKS):
        message[number] = strips[number]
    band = band_of(ops.lane)
    for t in range(2):
        for k in range(3):
            block = own_low[3 * t + k]
            for i in range(3):
                number = VELOCITY + t * 9 + k * 3 + i
                one, two = near[number].astype(F32), far[number].astype(F32)
                moved = turn(jnp.where(even, two, one), BAND * i + 3)
                block = jnp.where(band == i, moved, block)
                moved = turn(jnp.where(even, one, two), BAND * (7 + i) + 3)
                block = jnp.where(band == 7 + i, moved, block)
            low[3 * t + k] = block
    lower = ops.lane - BAND * band < 6
    for number in range(BAND_BLOCKS):
        both = jnp.where(lower, low[2 * number], turn(low[2 * number + 1], 6))
        message[STRIP_BLOCKS + number] = both.astype(BF16)


def products_of(hat):
    velocity = [hat(k) for k in range(3)]
    strain = [hat(9 + number) for number in range(6)]
    diagonal = strain[0] * strain[0] + strain[1] * strain[1] + strain[2] * strain[2]
    other = strain[3] * strain[3] + strain[4] * strain[4] + strain[5] * strain[5]
    size = 4.0 * jnp.sqrt((2.0 / 256.0) * diagonal + ((4.0 / 256.0) * other + EPSILON))
    cross = 0.0
    square = 0.0
    for number, (a, b) in enumerate(PAIRS):
        leonard = hat(3 + number) - (1.0 / 16.0) * velocity[a] * velocity[b]
        model = hat(15 + number) - size * strain[number]
        weighted = WEIGHTS[number] * model if WEIGHTS[number] != 1.0 else model
        cross = cross + leonard * weighted
        square = square + model * weighted
    return cross, square


def inner_kernel(
    flow, rho, temp, psi, near, far,
    inner, high, wide_0, wide_1, grad_0, grad_1, lap_0, lap_1, psi_rate, psi_lap,
    psi_wide, fields, hats,
):
    ops = Ops()
    even = is_even()
    valid = (ops.lane >= 3) & (ops.lane < LANES - 3)
    band = band_of(jnp.maximum(ops.lane - 2, 0))

    def sides(number):
        one, two = near[number].astype(F32), far[number].astype(F32)
        return jnp.where(even, two, one), jnp.where(even, one, two)

    for k in range(5):
        for i in range(2):
            psi_wide[k, i], psi_wide[k, 2 + CX + i] = sides(PSI + k * 2 + i)
        for x in range(CX):
            psi_wide[k, 2 + x] = psi[k, x]

    for t, wide, grad_xy, lap_xy in ((0, wide_0, grad_0, lap_0), (1, wide_1, grad_1, lap_1)):
        for k in range(3):
            for i in range(3):
                wide[k, i], wide[k, 7 + i] = sides(VELOCITY + t * 9 + k * 3 + i)
            for x in range(CX):
                wide[k, 3 + x] = flow[t, k, x].astype(F32)
        for k, source in ((3, rho), (4, temp)):
            for i in range(2):
                wide[k, 1 + i], wide[k, 7 + i] = sides(
                    SCALARS + t * 4 + (k - 3) * 2 + i
                )
            for x in range(CX):
                wide[k, 3 + x] = source[t, x].astype(F32)
        for x in range(-1, CX + 1):
            grad = [[None] * 3 for _ in range(3)]
            for k in range(3):
                center = wide[k, x + 3]
                grad[0][k] = fourth(
                    wide[k, x + 4], wide[k, x + 2], wide[k, x + 5], wide[k, x + 1]
                )
                grad[1][k] = 0.5 * (ops.y_up(center) - ops.y_down(center))
                grad[2][k] = fourth(*(turn(center, -step) for step in (1, -1, 2, -2)))
            strain = strain_of(grad)
            size = size_of(strain)
            velocity = [wide[k, x + 3] for k in range(3)]
            for number, values in enumerate(filter_fields(velocity, strain, size)):
                fields[number, x + 1] = values
        for x in range(CX):
            for number in range(21):
                along_x = (
                    fields[number, x] + fields[number, x + 2] + 2.0 * fields[number, x + 1]
                )
                hats[number, x] = turn(along_x, 1) + turn(along_x, -1) + 2.0 * along_x
        for k in range(3):
            block = jnp.zeros((ROWS, LANES), F32)
            for q in range(CX + 6):
                block = jnp.where(band == q, turn(wide[k, q], BAND * q + 11), block)
            high[t, k] = block
        for x in range(CX):
            for k in range(5):
                grad_xy[k, 0, x], grad_xy[k, 1, x], lap_xy[k, x] = plane_terms(
                    ops, wide[k, x + 3], [wide[k, x + 3 + i] for i in (1, -1, 2, -2)]
                )
        for x in range(CX):
            cross, square = products_of(lambda number: hats[number, x])
            inner[t, 0, x] = jnp.where(valid, cross, 0.0)
            inner[t, 1, x] = jnp.where(valid, square, 0.0)
    for x in range(CX):
        for k in range(5):
            along_x, along_y, lap = plane_terms(
                ops, psi_wide[k, x + 2], [psi_wide[k, x + 2 + i] for i in (1, -1, 2, -2)]
            )
            psi_rate[k, x] = wide_0[0, x + 3] * along_x + wide_0[1, x + 3] * along_y
            psi_lap[k, x] = lap


def edge_kernel(
    psi, low, high, own_halo, inner, wide_0, wide_1, grad_0, grad_1, lap_0, lap_1, psi_rate, psi_lap,
    first, second, message, columns,
    halos, psi_halos, work, bands, spread, sums,
):
    ops = Ops()
    band = band_of(ops.lane)
    place = ops.lane - BAND * band
    from_low = place < 3
    from_high = (place == 11) | (place < 2)
    low_side = place < 7
    at_edge = ((place >= 3) & (place <= 5)) | ((place >= 8) & (place <= 10))
    for t in range(2):
        for k in range(3):
            number = 3 * t + k
            far = own_halo[STRIP_BLOCKS + number // 2].astype(F32)
            shift = 6 * (number % 2)
            bands[t, 0, k] = jnp.where(from_low, turn(far, -shift), low[number])
            bands[t, 1, k] = jnp.where(from_high, turn(far, 8 - shift), high[t, k])
    strips = [own_halo[number].astype(F32) for number in range(STRIP_BLOCKS)]
    for k in range(5):
        for x in range(CX):
            psi_halos[k, x] = ops.strip(strips, SLOT_PSI + k, x)
    for t in range(2):
        place_halos(ops, t, own_halo, halos.at[t])
    for t in range(2):
        for side in range(2):
            velocity = [bands[t, side, k] for k in range(3)]
            grad = [[None] * 3 for _ in range(3)]
            for k in range(3):
                center = velocity[k]
                grad[0][k] = fourth(*(turn(center, -BAND * step) for step in (1, -1, 2, -2)))
                grad[1][k] = 0.5 * (ops.y_up(center) - ops.y_down(center))
                grad[2][k] = fourth(*(turn(center, -step) for step in (1, -1, 2, -2)))
            strain = strain_of(grad)
            for number, values in enumerate(filter_fields(velocity, strain, size_of(strain))):
                if side == 0:
                    spread[t, number] = values
                else:
                    spread[t, number] = jnp.where(low_side, spread[t, number], values)
    for t in range(2):
        for number in range(21):
            both = spread[t, number]
            spread[t, number] = turn(both, BAND) + turn(both, -BAND) + 2.0 * both
    for t in range(2):
        for number in range(21):
            both = spread[t, number]
            spread[t, number] = turn(both, 1) + turn(both, -1) + 2.0 * both
    for x in range(CX):
        terms = state_terms(ops, wide_0, grad_0, lap_0, halos.at[0], x)
        new, slope, sensitivity = affine_update(
            ops, x, terms,
            [psi[k, x] for k in range(5)],
            [psi_rate[k, x] for k in range(5)],
            [psi_lap[k, x] for k in range(5)],
            psi_halos,
        )
        for k in range(5):
            first[k, x] = new[k]
            second[k, x] = slope[k]
        work[0, x] = sensitivity
    for x in range(CX):
        _, _, lap, size, inv_rho = state_terms(
            ops, wide_1, grad_1, lap_1, halos.at[1], x, need_all=False
        )
        size_rho = size * inv_rho
        for part, source in enumerate((first, second)):
            total = lap[0] * source[0, x] + lap[1] * source[1, x] + lap[2] * source[2, x]
            work[1 + part, x] = size_rho * (
                total + (1.0 / PRANDTL_TURB) * (lap[4] * source[4, x])
            )
    for t in range(2):
        for part, values in enumerate(products_of(lambda number: spread[t, number])):
            values = jnp.where(at_edge, values, 0.0)
            for x in range(CX):
                sums[t, part, x] = inner[t, part, x] + jnp.where(band == x + 3, values, 0.0)
    total = jnp.zeros((ROWS, LANES), F32)
    for t in range(2):
        for part in range(2):
            for x in range(CX):
                value = (1.0 / 256.0) * jnp.sum(sums[t, part, x], axis=1, keepdims=True)
                total = jnp.where(ops.lane == 8 * t + 4 * part + x, value, total)
    for part in range(3):
        for x in range(CX):
            value = jnp.sum(work[part, x], axis=1, keepdims=True)
            total = jnp.where(ops.lane == 16 + 4 * part + x, value, total)
    columns[...] = total
    items = [[part[k, x] for x in range(CX)] for part in (first, second) for k in range(5)]
    message[0] = pack_strips(ops, items[:8]).astype(BF16)
    upper = total.astype(BF16).astype(F32)
    rest = total - upper
    middle = rest.astype(BF16).astype(F32)
    block = pack_strips(ops, items[8:])
    for number, part in enumerate((upper, middle, rest - middle)):
        block = jnp.where(ops.lane >> 5 == 1 + number, turn(part, 32 * (1 + number)), block)
    message[1] = block.astype(BF16)


def middle_kernel(
    add_other, first, second, columns, other, psi, near, far, psi_halos, coef_planes, grads, coef_first
):
    ops = Ops()
    total = columns[...]
    if add_other:
        parts = other[1].astype(F32)
        total = total + ((turn(parts, -32) + turn(parts, -64)) + turn(parts, -96))
    coef = total / (turn(total, -4) + EPSILON)
    after = total + turn(coef, 20) * turn(total, -4)
    grads[...] = jnp.where(ops.lane < 20, total, after)
    for x in range(CX):
        coef_first[x] = jnp.broadcast_to(coef[:, x : x + 1], (ROWS, LANES))
        coef_planes[x] = jnp.broadcast_to(coef[:, 8 + x : 9 + x], (ROWS, LANES))
    for x in range(CX):
        for k in range(5):
            values = first[k, x] + coef_first[x] * second[k, x]
            psi[k, x] = values
    strips = [other[number].astype(F32) for number in range(2)]
    for k in range(5):
        for x in range(CX):
            psi_halos[k, x] = ops.strip(strips, k, x)
    for k in range(5):
        for x in range(CX):
            psi_halos[k, x] = psi_halos[k, x] + coef_first[x] * ops.strip(strips, 5 + k, x)
    even = is_even().astype(jnp.int32)
    for out, side in ((near, even), (far, 1 - even)):
        for k in range(5):
            for i in range(2):
                out[k, i] = psi[k, 2 * side + i].astype(BF16)


def base_kernel(
    span_cells, wide, grad_xy, lap_xy, own_halo, psi, psi_halos, coef_planes, grads,
    base, drift, spread, coef_grad,
    halos, psi_wide,
):
    ops = Ops()
    turned = jnp.concatenate([grads[...]] * (LANES // ROWS), axis=0).T * (1.0 / span_cells)
    for t in range(2):
        coef_grad[t] = turned[16 + 4 * t : 20 + 4 * t, :ROWS]
    zero = jnp.zeros((ROWS, LANES), F32)
    for k in range(5):
        for i in range(2):
            psi_wide[k, i] = zero
            psi_wide[k, 2 + CX + i] = zero
        for x in range(CX):
            psi_wide[k, 2 + x] = psi[k, x]
    place_halos(ops, 1, own_halo, halos)
    for x in range(CX):
        terms = state_terms(ops, wide, grad_xy, lap_xy, halos, x)
        center = terms[0]
        rates, laps = [], []
        for k in range(5):
            along_x, along_y, lap = plane_terms(
                ops, psi_wide[k, x + 2], [psi_wide[k, x + 2 + i] for i in (1, -1, 2, -2)]
            )
            rates.append(center[0] * along_x + center[1] * along_y)
            laps.append(lap)
        new, slope, _ = affine_update(
            ops, x, terms, [psi[k, x] for k in range(5)], rates, laps, psi_halos
        )
        for k in range(5):
            base[k, x] = new[k] + coef_planes[x] * slope[k]
        size, inv_rho = terms[3:]
        drift[x] = TIME_STEP * center[0]
        if x in (0, CX - 1):
            eddy = coef_planes[x] * size
            scaled = TIME_STEP * inv_rho
            spread[x // (CX - 1), 0] = scaled * (NU_MOL + eddy)
            spread[x // (CX - 1), 1] = scaled * (
                NU_MOL / PRANDTL + (1.0 / PRANDTL_TURB) * eddy
            )


def last_kernel(base, drift, spread, near_psi, far_psi, out):
    even = is_even()
    for k in range(5):
        ones = [near_psi[k, i].astype(F32) for i in range(2)]
        twos = [far_psi[k, i].astype(F32) for i in range(2)]
        far, near = (jnp.where(even, two, one) for one, two in zip(ones, twos))
        after, beyond = (jnp.where(even, one, two) for one, two in zip(ones, twos))
        low = drift[0] * ((1.0 / 12.0) * far - (2.0 / 3.0) * near)
        high = drift[CX - 1] * ((2.0 / 3.0) * after - (1.0 / 12.0) * beyond)
        if k != 3:
            kind = 1 if k == 4 else 0
            low = low + spread[0, kind] * near
            high = high + spread[1, kind] * after
        out[k, 0] = base[k, 0] + low
        out[k, 1] = base[k, 1] + drift[1] * ((1.0 / 12.0) * near)
        out[k, CX - 2] = base[k, CX - 2] - drift[CX - 2] * ((1.0 / 12.0) * after)
        out[k, CX - 1] = base[k, CX - 1] + high


def ring(axis):
    count = lax.axis_size(axis)
    forward = [(i, (i + 1) % count) for i in range(count)]
    return forward, [(target, source) for source, target in forward]


def pairs():
    count = lax.axis_size("gx")
    if count % 2:
        raise ValueError("odd gx")
    inside = [(i, i ^ 1) for i in range(count)]
    across = [(i, (i + 1 if i % 2 else i - 1) % count) for i in range(count)]
    return inside, across


def span_edges(message, strips):
    forward, backward = ring("gz")
    before = lax.ppermute(message, "gz", forward)
    if lax.axis_size("gz") == 2:
        return before
    after = lax.ppermute(message, "gz", backward)
    lane = lax.broadcasted_iota(jnp.int32, message.shape, 2)
    number = lax.broadcasted_iota(jnp.int32, message.shape, 0)
    low = jnp.where(number < strips, lane % STRIP < 2, lane % 6 < 3)
    return jnp.where(low, before, after)


def shape_of(dims, kind=F32):
    return jax.ShapeDtypeStruct(dims + (ROWS, LANES), kind)


def whole(count):
    return [pl.BlockSpec(memory_space=pltpu.VMEM)] * count


def scratch(*dims):
    return [pltpu.VMEM(d + (ROWS, LANES), F32) for d in dims]


def call(kernel, name, inputs, outputs, operations, buffers=(), in_specs=None):
    space = pltpu.MemorySpace.HBM if in_specs else pltpu.MemorySpace.VMEM
    inputs = [pltpu.with_memory_space_constraint(a, space) for a in inputs]
    size = sum(math.prod(a.shape) * a.dtype.itemsize for a in list(inputs) + list(outputs))
    return pl.pallas_call(
        kernel,
        in_specs=in_specs or whole(len(inputs)),
        out_specs=whole(len(outputs)),
        out_shape=list(outputs),
        scratch_shapes=list(buffers),
        compiler_params=pltpu.CompilerParams(vmem_limit_bytes=8 * 2**20),
        cost_estimate=pl.CostEstimate(
            flops=operations, bytes_accessed=size, transcendentals=0
        ),
        name=name,
    )(*inputs)


def local(flow, rho, temp, psi):
    inside, across = pairs()
    near, far, flow, rho, temp, psi = call(
        message_kernel,
        "message",
        (flow, rho, temp, psi),
        [shape_of((MESSAGE,), BF16)] * 2
        + [
            shape_of((2, 3, CX), BF16),
            shape_of((2, CX), BF16),
            shape_of((2, CX), BF16),
            shape_of((5, CX)),
        ],
        1_000_000,
        [pltpu.SemaphoreType.DMA((4,))],
        [pl.BlockSpec(memory_space=pltpu.MemorySpace.HBM)] * 4,
    )
    near = lax.ppermute(near, "gx", inside)
    far = lax.ppermute(far, "gx", across)
    strips, own_low = call(
        pack_kernel,
        "pack",
        (flow, rho, temp, psi),
        [shape_of((STRIP_BLOCKS,), BF16), shape_of((6,))],
        2_000_000,
    )
    message, low = call(
        bands_kernel,
        "bands",
        (strips, own_low, near, far),
        [shape_of((STRIP_BLOCKS + BAND_BLOCKS,), BF16), shape_of((6,))],
        1_000_000,
    )
    own_halo = span_edges(message, STRIP_BLOCKS)
    inner, high, wide_0, wide_1, grad_0, grad_1, lap_0, lap_1, psi_rate, psi_lap = call(
        inner_kernel,
        "inner",
        (flow, rho, temp, psi, near, far),
        [
            shape_of((2, 2, CX)), shape_of((2, 3)),
            shape_of((5, CX + 6)), shape_of((5, CX + 6)),
            shape_of((5, 2, CX)), shape_of((5, 2, CX)),
            shape_of((5, CX)), shape_of((5, CX)),
            shape_of((5, CX)), shape_of((5, CX)),
        ],
        30_000_000,
        scratch((5, CX + 4), (21, CX + 2), (21, CX)),
    )
    first, second, message, columns = call(
        edge_kernel,
        "edge",
        (
            psi, low, high, own_halo, inner,
            wide_0, wide_1, grad_0, grad_1, lap_0, lap_1, psi_rate, psi_lap,
        ),
        [shape_of((5, CX)), shape_of((5, CX)), shape_of((2,), BF16), shape_of(())],
        20_000_000,
        scratch((2, 5, CX), (5, CX), (3, CX), (2, 2, 3), (2, 21), (2, 2, CX)),
    )
    other = span_edges(message, 2)
    add_other = lax.axis_size("gz") == 2
    if not add_other:
        columns = lax.psum(columns, "gz")
    psi, near, far, psi_halos, coef_planes, grads = call(
        functools.partial(middle_kernel, add_other),
        "middle",
        (first, second, columns, other),
        [
            shape_of((5, CX)), shape_of((5, 2), BF16), shape_of((5, 2), BF16),
            shape_of((5, CX)), shape_of((CX,)), shape_of(()),
        ],
        1_000_000,
        scratch((CX,)),
    )
    near = lax.ppermute(near, "gx", inside)
    far = lax.ppermute(far, "gx", across)
    base, drift, spread, coef_grad = call(
        functools.partial(base_kernel, LANES * lax.axis_size("gz")),
        "base",
        (wide_1, grad_1, lap_1, own_halo, psi, psi_halos, coef_planes, grads),
        [
            shape_of((5, CX)), shape_of((CX,)), shape_of((2, 2)),
            jax.ShapeDtypeStruct((2, CX, ROWS), F32),
        ],
        15_000_000,
        scratch((5, CX), (5, CX + 4)),
    )
    (out,) = call(
        last_kernel,
        "last",
        (base, drift, spread, near, far),
        [shape_of((5, CX))],
        1_000_000,
    )
    return out, coef_grad


def solution(mesh):
    return jax.shard_map(
        local,
        mesh=mesh,
        in_specs=(
            P(None, None, "gx", None, "gz"),
            P(None, "gx", None, "gz"),
            P(None, "gx", None, "gz"),
            P(None, "gx", None, "gz"),
        ),
        out_specs=(P(None, "gx", None, "gz"), P(None, "gx", None)),
        check_vma=False,
    )
```

```python
import functools
import math

import jax
import jax.numpy as jnp
from jax import lax
from jax.experimental import pallas as pl
from jax.experimental.pallas import tpu as pltpu
from jax.sharding import PartitionSpec as P

EPSILON = 1e-06
NU_MOL = 0.05
PRANDTL = 0.72
PRANDTL_TURB = 0.9
TIME_STEP = 0.04
PAIRS = ((0, 0), (1, 1), (2, 2), (0, 1), (0, 2), (1, 2))
WEIGHTS = (1.0, 1.0, 1.0, 2.0, 2.0, 2.0)

CX = 4
ROWS = 32
LANES = 128
STRIP = 4
F32 = jnp.float32
BF16 = jnp.bfloat16
SLOT_PSI = 4
BAND = 12
STRIP_BLOCKS = 2
BAND_BLOCKS = 3
VELOCITY = 0
SCALARS = 18
PSI = 26
MESSAGE = 36


def lane_ids():
    return lax.broadcasted_iota(jnp.int32, (ROWS, LANES), 1)


def row_ids():
    return lax.broadcasted_iota(jnp.int32, (ROWS, LANES), 0)


def turn(values, shift):
    shift = shift % LANES
    return values if shift == 0 else pltpu.roll(values, shift, 1)


class Ops:
    def __init__(self):
        self.lane = lane_ids()
        row = row_ids()
        self.top = row == ROWS - 1
        self.bottom = row == 0

    def z_at(self, values, halo, step):
        if step > 0:
            return turn(jnp.where(self.lane < step, halo, values), -step)
        return turn(jnp.where(self.lane >= LANES + step, halo, values), -step)

    def y_up(self, values):
        return jnp.where(self.top, 0.0, pltpu.roll(values, ROWS - 1, 0))

    def y_down(self, values):
        return jnp.where(self.bottom, 0.0, pltpu.roll(values, 1, 0))

    def strip(self, blocks, slot, x):
        return turn(blocks[slot // 8], -(STRIP * (4 * (slot % 8) + x) + 2))


def fourth(plus, minus, plus_2, minus_2):
    return (2.0 / 3.0) * (plus - minus) - (1.0 / 12.0) * (plus_2 - minus_2)


def strain_of(grad):
    return [
        grad[0][0],
        grad[1][1],
        grad[2][2],
        0.5 * (grad[0][1] + grad[1][0]),
        0.5 * (grad[0][2] + grad[2][0]),
        0.5 * (grad[1][2] + grad[2][1]),
    ]


def size_of(strain):
    diagonal = strain[0] * strain[0] + strain[1] * strain[1] + strain[2] * strain[2]
    other = strain[3] * strain[3] + strain[4] * strain[4] + strain[5] * strain[5]
    return jnp.sqrt(2.0 * diagonal + (4.0 * other + EPSILON))


def filter_fields(velocity, strain, size):
    products = [velocity[a] * velocity[b] for a, b in PAIRS]
    return list(velocity) + products + strain + [size * part for part in strain]


def pack_strips(ops, items):
    block = jnp.zeros((ROWS, LANES), F32)
    strip_id = ops.lane >> 2
    for slot, planes in enumerate(items):
        for x in range(CX):
            number = 4 * slot + x
            block = jnp.where(strip_id == number, turn(planes[x], STRIP * number + 2), block)
    return block


def place_halos(ops, t, own_halo, halos):
    strips = [own_halo[number].astype(F32) for number in range(STRIP_BLOCKS)]
    for k in range(3):
        number = 3 * t + k
        bands = own_halo[STRIP_BLOCKS + number // 2].astype(F32)
        for x in range(CX):
            halos[k, x] = turn(bands, -(BAND * (x + 3) + 3 + 6 * (number % 2)))
    for k in range(3, 5):
        for x in range(CX):
            halos[k, x] = ops.strip(strips, 2 * t + k - 3, x)


def plane_terms(ops, values, xs):
    up, down = ops.y_up(values), ops.y_down(values)
    lap = xs[0] + xs[1] + up + down - 6.0 * values
    return fourth(*xs), 0.5 * (up - down), lap


def state_terms(ops, wide, grad_xy, lap_xy, halos, x, need_all=True):
    grad = [[None] * 5 for _ in range(3)]
    lap = [None] * 5
    center = [wide[k, x + 3] for k in range(5)]
    for k in range(5):
        if k == 3 and not need_all:
            continue
        zs = [ops.z_at(center[k], halos[k, x], step) for step in (1, -1, 2, -2)]
        if k < 3 or need_all:
            grad[0][k] = grad_xy[k, 0, x]
            grad[1][k] = grad_xy[k, 1, x]
            grad[2][k] = fourth(*zs)
        if k != 3:
            lap[k] = lap_xy[k, x] + (zs[0] + zs[1])
    size = size_of(strain_of(grad))
    return center, grad, lap, size, 1.0 / center[3]


def affine_update(ops, x, terms, psi, rate_xy, lap_psi_xy, psi_halos):
    center, grad, lap, size, inv_rho = terms
    work_mom = psi[0] * lap[0] + psi[1] * lap[1] + psi[2] * lap[2]
    work_heat = psi[4] * lap[4]
    turbulent = work_mom + work_heat * (1.0 / PRANDTL_TURB)
    inv_rho_2 = inv_rho * inv_rho
    size_rho = size * inv_rho
    first, second = [], []
    for k in range(5):
        zs = [ops.z_at(psi[k], psi_halos[k, x], step) for step in (1, -1, 2, -2)]
        rate = rate_xy[k] + center[2] * fourth(*zs)
        if k == 3:
            rate = rate - (NU_MOL * work_mom + (NU_MOL / PRANDTL) * work_heat) * inv_rho_2
            eddy = -(size * turbulent) * inv_rho_2
        else:
            lap_psi = lap_psi_xy[k] + (zs[0] + zs[1])
            if k < 3:
                for other in range(5):
                    rate = rate + psi[other] * grad[k][other]
                rate = rate + NU_MOL * (inv_rho * lap_psi)
                eddy = size_rho * lap_psi
            else:
                rate = rate + (NU_MOL / PRANDTL) * (inv_rho * lap_psi)
                eddy = (1.0 / PRANDTL_TURB) * (size_rho * lap_psi)
        first.append(psi[k] + TIME_STEP * rate)
        second.append(TIME_STEP * eddy)
    return first, second, size_rho * turbulent


def band_of(lane):
    return (lane * 43) >> 9


def is_even():
    return lax.rem(lax.axis_index("gx"), 2) == 0


def fill_message(out, side, flow, rho, temp, psi):
    for t in range(2):
        for k in range(3):
            for i in range(3):
                out[VELOCITY + t * 9 + k * 3 + i] = flow[t, k, side + i]
        for i in range(2):
            out[SCALARS + t * 4 + i] = rho[t, 2 * side + i]
            out[SCALARS + t * 4 + 2 + i] = temp[t, 2 * side + i]
    for k in range(5):
        for i in range(2):
            out[PSI + k * 2 + i] = psi[k, 2 * side + i].astype(BF16)


def message_kernel(flow_far, rho_far, temp_far, psi_far, far, flow, rho, temp, psi, sems):
    copies = [
        pltpu.make_async_copy(source, target, sems.at[i])
        for i, (source, target) in enumerate(
            ((flow_far, flow), (psi_far, psi), (rho_far, rho), (temp_far, temp))
        )
    ]
    for copy in copies:
        copy.start()
    side = 1 - is_even().astype(jnp.int32)
    for copy in copies:
        copy.wait()
    fill_message(far, side, flow, rho, temp, psi)


def pack_kernel(flow, rho, temp, psi, near, strips, low):
    ops = Ops()
    fill_message(near, is_even().astype(jnp.int32), flow, rho, temp, psi)
    items = []
    for t in range(2):
        for source in (rho, temp):
            items.append([source[t, x].astype(F32) for x in range(CX)])
    items += [[psi[k, x] for x in range(CX)] for k in range(5)]
    for number in range(STRIP_BLOCKS):
        strips[number] = pack_strips(ops, items[8 * number : 8 * number + 8]).astype(BF16)
    band = band_of(ops.lane)
    for t in range(2):
        for k in range(3):
            block = jnp.zeros((ROWS, LANES), F32)
            for x in range(CX):
                moved = turn(flow[t, k, x].astype(F32), BAND * (x + 3) + 3)
                block = jnp.where(band == x + 3, moved, block)
            low[3 * t + k] = block


def bands_kernel(strips, own_low, near, far, message, low):
    ops = Ops()
    even = is_even()
    for number in range(STRIP_BLOCKS):
        message[number] = strips[number]
    band = band_of(ops.lane)
    for t in range(2):
        for k in range(3):
            block = own_low[3 * t + k]
            for i in range(3):
                number = VELOCITY + t * 9 + k * 3 + i
                one, two = near[number].astype(F32), far[number].astype(F32)
                moved = turn(jnp.where(even, two, one), BAND * i + 3)
                block = jnp.where(band == i, moved, block)
                moved = turn(jnp.where(even, one, two), BAND * (7 + i) + 3)
                block = jnp.where(band == 7 + i, moved, block)
            low[3 * t + k] = block
    lower = ops.lane - BAND * band < 6
    for number in range(BAND_BLOCKS):
        both = jnp.where(lower, low[2 * number], turn(low[2 * number + 1], 6))
        message[STRIP_BLOCKS + number] = both.astype(BF16)


def products_of(hat):
    velocity = [hat(k) for k in range(3)]
    strain = [hat(9 + number) for number in range(6)]
    diagonal = strain[0] * strain[0] + strain[1] * strain[1] + strain[2] * strain[2]
    other = strain[3] * strain[3] + strain[4] * strain[4] + strain[5] * strain[5]
    size = 4.0 * jnp.sqrt((2.0 / 256.0) * diagonal + ((4.0 / 256.0) * other + EPSILON))
    cross = 0.0
    square = 0.0
    for number, (a, b) in enumerate(PAIRS):
        leonard = hat(3 + number) - (1.0 / 16.0) * velocity[a] * velocity[b]
        model = hat(15 + number) - size * strain[number]
        weighted = WEIGHTS[number] * model if WEIGHTS[number] != 1.0 else model
        cross = cross + leonard * weighted
        square = square + model * weighted
    return cross, square


def widen(k, source, number, count, even, near, far, wide):
    for i in range(count):
        one, two = near[number + i].astype(F32), far[number + i].astype(F32)
        wide[k, 3 - count + i] = jnp.where(even, two, one)
        wide[k, 3 + CX + i] = jnp.where(even, one, two)
    for x in range(CX):
        wide[k, 3 + x] = source(x).astype(F32)


def inner_products(ops, t, flow, rho, temp, near, far, sums, high, wide, grad_xy, lap_xy, fields, hats):
    even = is_even()
    valid = (ops.lane >= 3) & (ops.lane < LANES - 3)
    band = band_of(jnp.maximum(ops.lane - 2, 0))
    for k in range(3):
        widen(k, lambda x: flow[t, k, x], VELOCITY + t * 9 + k * 3, 3, even, near, far, wide)
    for k, source in ((3, rho), (4, temp)):
        number = SCALARS + t * 4 + (k - 3) * 2
        widen(k, lambda x: source[t, x], number, 2, even, near, far, wide)
    for x in range(-1, CX + 1):
        grad = [[None] * 3 for _ in range(3)]
        for k in range(3):
            center = wide[k, x + 3]
            along_x, along_y, lap = plane_terms(
                ops, center, [wide[k, x + 3 + i] for i in (1, -1, 2, -2)]
            )
            grad[0][k], grad[1][k] = along_x, along_y
            grad[2][k] = fourth(*(turn(center, -step) for step in (1, -1, 2, -2)))
            if 0 <= x < CX:
                grad_xy[k, 0, x], grad_xy[k, 1, x], lap_xy[k, x] = along_x, along_y, lap
        strain = strain_of(grad)
        size = size_of(strain)
        velocity = [wide[k, x + 3] for k in range(3)]
        for number, values in enumerate(filter_fields(velocity, strain, size)):
            fields[number, x + 1] = values
    for x in range(CX):
        for number in range(21):
            along_x = fields[number, x] + fields[number, x + 2] + 2.0 * fields[number, x + 1]
            hats[number, x] = turn(along_x, 1) + turn(along_x, -1) + 2.0 * along_x
    for k in range(3):
        block = jnp.zeros((ROWS, LANES), F32)
        for q in range(CX + 6):
            block = jnp.where(band == q, turn(wide[k, q], BAND * q + 11), block)
        high[k] = block
    for x in range(CX):
        for k in range(3, 5):
            grad_xy[k, 0, x], grad_xy[k, 1, x], lap_xy[k, x] = plane_terms(
                ops, wide[k, x + 3], [wide[k, x + 3 + i] for i in (1, -1, 2, -2)]
            )
    for x in range(CX):
        cross, square = products_of(lambda number: hats[number, x])
        sums[0, x] = jnp.where(valid, cross, 0.0)
        sums[1, x] = jnp.where(valid, square, 0.0)


def edge_products(ops, t, low, high, own_halo, sums, bands, spread):
    band = band_of(ops.lane)
    place = ops.lane - BAND * band
    from_low = place < 3
    from_high = (place == 11) | (place < 2)
    low_side = place < 7
    at_edge = ((place >= 3) & (place <= 5)) | ((place >= 8) & (place <= 10))
    for k in range(3):
        number = 3 * t + k
        far = own_halo[STRIP_BLOCKS + number // 2].astype(F32)
        shift = 6 * (number % 2)
        bands[0, k] = jnp.where(from_low, turn(far, -shift), low[number])
        bands[1, k] = jnp.where(from_high, turn(far, 8 - shift), high[k])
    for side in range(2):
        velocity = [bands[side, k] for k in range(3)]
        grad = [[None] * 3 for _ in range(3)]
        for k in range(3):
            center = velocity[k]
            grad[0][k] = fourth(*(turn(center, -BAND * step) for step in (1, -1, 2, -2)))
            grad[1][k] = 0.5 * (ops.y_up(center) - ops.y_down(center))
            grad[2][k] = fourth(*(turn(center, -step) for step in (1, -1, 2, -2)))
        strain = strain_of(grad)
        for number, values in enumerate(filter_fields(velocity, strain, size_of(strain))):
            if side == 0:
                spread[number] = values
            else:
                spread[number] = jnp.where(low_side, spread[number], values)
    for number in range(21):
        both = spread[number]
        spread[number] = turn(both, BAND) + turn(both, -BAND) + 2.0 * both
    for number in range(21):
        both = spread[number]
        spread[number] = turn(both, 1) + turn(both, -1) + 2.0 * both
    for part, values in enumerate(products_of(lambda number: spread[number])):
        values = jnp.where(at_edge, values, 0.0)
        for x in range(CX):
            sums[part, x] = sums[part, x] + jnp.where(band == x + 3, values, 0.0)


def add_columns(ops, total, first_lane, planes, scale=1.0):
    for x in range(CX):
        value = scale * jnp.sum(planes(x), axis=1, keepdims=True)
        total = jnp.where(ops.lane == first_lane + x, value, total)
    return total


def add_parts(ops, block, total):
    upper = total.astype(BF16).astype(F32)
    rest = total - upper
    middle = rest.astype(BF16).astype(F32)
    for number, part in enumerate((upper, middle, rest - middle)):
        block = jnp.where(ops.lane >> 5 == 1 + number, turn(part, 32 * (1 + number)), block)
    return block


def span_total(add_other, columns, other):
    total = columns[...]
    if add_other:
        parts = other.astype(F32)
        total = total + ((turn(parts, -32) + turn(parts, -64)) + turn(parts, -96))
    return total


def inner_kernel(
    flow, rho, temp, psi, near, far,
    sums, high, wide, grad_xy, lap_xy, psi_rate, psi_lap,
    psi_wide, fields, hats,
):
    ops = Ops()
    even = is_even()
    for k in range(5):
        widen(k, lambda x: psi[k, x], PSI + k * 2, 2, even, near, far, psi_wide)
    inner_products(
        ops, 0, flow, rho, temp, near, far, sums, high, wide, grad_xy, lap_xy, fields, hats
    )
    for x in range(CX):
        for k in range(5):
            along_x, along_y, lap = plane_terms(
                ops, psi_wide[k, x + 3], [psi_wide[k, x + 3 + i] for i in (1, -1, 2, -2)]
            )
            psi_rate[k, x] = wide[0, x + 3] * along_x + wide[1, x + 3] * along_y
            psi_lap[k, x] = lap


def edge_kernel(
    psi, low, high, own_halo, inner, wide, grad_xy, lap_xy, psi_rate, psi_lap,
    first, second, message, columns,
    halos, psi_halos, work, bands, spread, sums,
):
    ops = Ops()
    strips = [own_halo[number].astype(F32) for number in range(STRIP_BLOCKS)]
    for k in range(5):
        for x in range(CX):
            psi_halos[k, x] = ops.strip(strips, SLOT_PSI + k, x)
    place_halos(ops, 0, own_halo, halos)
    for part in range(2):
        for x in range(CX):
            sums[part, x] = inner[part, x]
    edge_products(ops, 0, low, high, own_halo, sums, bands, spread)
    for x in range(CX):
        terms = state_terms(ops, wide, grad_xy, lap_xy, halos, x)
        new, slope, sensitivity = affine_update(
            ops, x, terms,
            [psi[k, x] for k in range(5)],
            [psi_rate[k, x] for k in range(5)],
            [psi_lap[k, x] for k in range(5)],
            psi_halos,
        )
        for k in range(5):
            first[k, x] = new[k]
            second[k, x] = slope[k]
        work[x] = sensitivity
    total = jnp.zeros((ROWS, LANES), F32)
    for part in range(2):
        total = add_columns(ops, total, 4 * part, lambda x: sums[part, x], 1.0 / 256.0)
    total = add_columns(ops, total, 16, lambda x: work[x])
    columns[...] = total
    items = [[part[k, x] for x in range(CX)] for part in (first, second) for k in range(5)]
    message[0] = pack_strips(ops, items[:8]).astype(BF16)
    message[1] = add_parts(ops, pack_strips(ops, items[8:]), total).astype(BF16)


def later_kernel(
    flow, rho, temp, near, far, low, own_halo, first, second,
    wide, grad_xy, lap_xy, message, columns,
    high, halos, fields, hats, work, bands, spread, sums,
):
    ops = Ops()
    place_halos(ops, 1, own_halo, halos)
    inner_products(
        ops, 1, flow, rho, temp, near, far, sums, high, wide, grad_xy, lap_xy, fields, hats
    )
    edge_products(ops, 1, low, high, own_halo, sums, bands, spread)
    for x in range(CX):
        _, _, lap, size, inv_rho = state_terms(
            ops, wide, grad_xy, lap_xy, halos, x, need_all=False
        )
        size_rho = size * inv_rho
        for part, source in enumerate((first, second)):
            total = lap[0] * source[0, x] + lap[1] * source[1, x] + lap[2] * source[2, x]
            work[part, x] = size_rho * (
                total + (1.0 / PRANDTL_TURB) * (lap[4] * source[4, x])
            )
    total = jnp.zeros((ROWS, LANES), F32)
    for part in range(2):
        total = add_columns(ops, total, 8 + 4 * part, lambda x: sums[part, x], 1.0 / 256.0)
        total = add_columns(ops, total, 20 + 4 * part, lambda x: work[part, x])
    columns[...] = total
    message[0] = add_parts(ops, jnp.zeros((ROWS, LANES), F32), total).astype(BF16)


def coefficients(ops, total):
    return total / (turn(total, -4) + EPSILON)


def middle_kernel(add_other, first, second, columns, other, psi, far, coef_first):
    ops = Ops()
    coef = coefficients(ops, span_total(add_other, columns, other[1]))
    for x in range(CX):
        coef_first[x] = jnp.broadcast_to(coef[:, x : x + 1], (ROWS, LANES))
    for x in range(CX):
        for k in range(5):
            psi[k, x] = first[k, x] + coef_first[x] * second[k, x]
    side = 1 - is_even().astype(jnp.int32)
    for k in range(5):
        for i in range(2):
            far[k, i] = psi[k, 2 * side + i].astype(BF16)


def near_kernel(psi, _, near):
    side = is_even().astype(jnp.int32)
    for k in range(5):
        for i in range(2):
            near[k, i] = psi[k, 2 * side + i].astype(BF16)


def base_kernel(
    add_other, span_cells,
    wide, grad_xy, lap_xy, own_halo, psi, coef_first, columns, other, later, later_other,
    base, drift, spread, coef_grad,
    halos, psi_halos, psi_wide, coef_planes,
):
    ops = Ops()
    place_halos(ops, 1, own_halo, halos)
    strips = [other[number].astype(F32) for number in range(2)]
    for k in range(5):
        for x in range(CX):
            psi_halos[k, x] = ops.strip(strips, k, x)
    total = span_total(add_other, columns, other[1]) + span_total(
        add_other, later, later_other[0]
    )
    coef = coefficients(ops, total)
    after = total + turn(coef, 20) * turn(total, -4)
    grads = jnp.where(ops.lane < 20, total, after) * (1.0 / span_cells)
    turned = jnp.concatenate([grads] * (LANES // ROWS), axis=0).T
    for t in range(2):
        coef_grad[t] = turned[16 + 4 * t : 20 + 4 * t, :ROWS]
    for x in range(CX):
        coef_planes[x] = jnp.broadcast_to(coef[:, 8 + x : 9 + x], (ROWS, LANES))
    for k in range(5):
        for x in range(CX):
            psi_halos[k, x] = psi_halos[k, x] + coef_first[x] * ops.strip(strips, 5 + k, x)
    zero = jnp.zeros((ROWS, LANES), F32)
    for k in range(5):
        for i in range(2):
            psi_wide[k, i] = zero
            psi_wide[k, 2 + CX + i] = zero
        for x in range(CX):
            psi_wide[k, 2 + x] = psi[k, x]
    for x in range(CX):
        terms = state_terms(ops, wide, grad_xy, lap_xy, halos, x)
        center = terms[0]
        rates, laps = [], []
        for k in range(5):
            along_x, along_y, lap = plane_terms(
                ops, psi_wide[k, x + 2], [psi_wide[k, x + 2 + i] for i in (1, -1, 2, -2)]
            )
            rates.append(center[0] * along_x + center[1] * along_y)
            laps.append(lap)
        new, slope, _ = affine_update(
            ops, x, terms, [psi[k, x] for k in range(5)], rates, laps, psi_halos
        )
        for k in range(5):
            base[k, x] = new[k] + coef_planes[x] * slope[k]
        size, inv_rho = terms[3:]
        drift[x] = TIME_STEP * center[0]
        if x in (0, CX - 1):
            eddy = coef_planes[x] * size
            scaled = TIME_STEP * inv_rho
            spread[x // (CX - 1), 0] = scaled * (NU_MOL + eddy)
            spread[x // (CX - 1), 1] = scaled * (
                NU_MOL / PRANDTL + (1.0 / PRANDTL_TURB) * eddy
            )


def widen_kernel(far, out):
    for k in range(5):
        for i in range(2):
            out[k, i] = far[k, i].astype(F32)


def last_kernel(base, drift, spread, near_psi, far_psi, out):
    even = is_even()
    for k in range(5):
        ones = [near_psi[k, i].astype(F32) for i in range(2)]
        twos = [far_psi[k, i].astype(F32) for i in range(2)]
        far, near = (jnp.where(even, two, one) for one, two in zip(ones, twos))
        after, beyond = (jnp.where(even, one, two) for one, two in zip(ones, twos))
        low = drift[0] * ((1.0 / 12.0) * far - (2.0 / 3.0) * near)
        high = drift[CX - 1] * ((2.0 / 3.0) * after - (1.0 / 12.0) * beyond)
        if k != 3:
            kind = 1 if k == 4 else 0
            low = low + spread[0, kind] * near
            high = high + spread[1, kind] * after
        out[k, 0] = base[k, 0] + low
        out[k, 1] = base[k, 1] + drift[1] * ((1.0 / 12.0) * near)
        out[k, CX - 2] = base[k, CX - 2] - drift[CX - 2] * ((1.0 / 12.0) * after)
        out[k, CX - 1] = base[k, CX - 1] + high


def ring(axis):
    count = lax.axis_size(axis)
    forward = [(i, (i + 1) % count) for i in range(count)]
    return forward, [(target, source) for source, target in forward]


def pairs():
    count = lax.axis_size("gx")
    if count % 2:
        raise ValueError("odd gx")
    inside = [(i, i ^ 1) for i in range(count)]
    across = [(i, (i + 1 if i % 2 else i - 1) % count) for i in range(count)]
    return inside, across


def span_edges(message, strips):
    forward, backward = ring("gz")
    before = lax.ppermute(message, "gz", forward)
    if lax.axis_size("gz") == 2:
        return before
    after = lax.ppermute(message, "gz", backward)
    lane = lax.broadcasted_iota(jnp.int32, message.shape, 2)
    number = lax.broadcasted_iota(jnp.int32, message.shape, 0)
    low = jnp.where(number < strips, lane % STRIP < 2, lane % 6 < 3)
    return jnp.where(low, before, after)


def shape_of(dims, kind=F32):
    return jax.ShapeDtypeStruct(dims + (ROWS, LANES), kind)


def whole(count):
    return [pl.BlockSpec(memory_space=pltpu.VMEM)] * count


def scratch(*dims):
    return [pltpu.VMEM(d + (ROWS, LANES), F32) for d in dims]


def call(kernel, name, inputs, outputs, operations, buffers=(), in_specs=None):
    space = pltpu.MemorySpace.HBM if in_specs else pltpu.MemorySpace.VMEM
    inputs = [pltpu.with_memory_space_constraint(a, space) for a in inputs]
    size = sum(math.prod(a.shape) * a.dtype.itemsize for a in list(inputs) + list(outputs))
    return pl.pallas_call(
        kernel,
        in_specs=in_specs or whole(len(inputs)),
        out_specs=whole(len(outputs)),
        out_shape=list(outputs),
        scratch_shapes=list(buffers),
        compiler_params=pltpu.CompilerParams(vmem_limit_bytes=8 * 2**20),
        cost_estimate=pl.CostEstimate(
            flops=operations, bytes_accessed=size, transcendentals=0
        ),
        name=name,
    )(*inputs)


def span_sums(columns):
    if lax.axis_size("gz") == 2:
        return columns
    return lax.psum(columns, "gz")


def local(flow, rho, temp, psi):
    inside, across = pairs()
    add_other = lax.axis_size("gz") == 2
    field, planes, edges = shape_of((5, CX)), shape_of((5, CX + 6)), shape_of((5, 2), BF16)
    far, flow, rho, temp, psi = call(
        message_kernel,
        "message",
        (flow, rho, temp, psi),
        [
            shape_of((MESSAGE,), BF16),
            shape_of((2, 3, CX), BF16),
            shape_of((2, CX), BF16),
            shape_of((2, CX), BF16),
            field,
        ],
        1_000_000,
        [pltpu.SemaphoreType.DMA((4,))],
        [pl.BlockSpec(memory_space=pltpu.MemorySpace.HBM)] * 4,
    )
    far = lax.ppermute(far, "gx", across)
    near, strips, own_low = call(
        pack_kernel,
        "pack",
        (flow, rho, temp, psi),
        [shape_of((MESSAGE,), BF16), shape_of((STRIP_BLOCKS,), BF16), shape_of((6,))],
        2_000_000,
    )
    near = lax.ppermute(near, "gx", inside)
    message, low = call(
        bands_kernel,
        "bands",
        (strips, own_low, near, far),
        [shape_of((STRIP_BLOCKS + BAND_BLOCKS,), BF16), shape_of((6,))],
        1_000_000,
    )
    own_halo = span_edges(message, STRIP_BLOCKS)
    inner, high, wide, grad_xy, lap_xy, psi_rate, psi_lap = call(
        inner_kernel,
        "inner",
        (flow, rho, temp, psi, near, far),
        [shape_of((2, CX)), shape_of((3,)), planes, shape_of((5, 2, CX)), field, field, field],
        20_000_000,
        scratch((5, CX + 6), (21, CX + 2), (21, CX)),
    )
    first, second, message, columns = call(
        edge_kernel,
        "edge",
        (psi, low, high, own_halo, inner, wide, grad_xy, lap_xy, psi_rate, psi_lap),
        [field, field, shape_of((2,), BF16), shape_of(())],
        20_000_000,
        scratch((5, CX), (5, CX), (CX,), (2, 3), (21,), (2, CX)),
    )
    other = span_edges(message, 2)
    columns = span_sums(columns)
    wide, grad_xy, lap_xy, message, later = call(
        later_kernel,
        "later",
        (flow, rho, temp, near, far, low, own_halo, first, second),
        [planes, shape_of((5, 2, CX)), field, shape_of((1,), BF16), shape_of(())],
        20_000_000,
        scratch((3,), (5, CX), (21, CX + 2), (21, CX), (2, CX), (2, 3), (21,), (2, CX)),
    )
    later_other = span_edges(message, 1)
    later = span_sums(later)
    first, later = lax.optimization_barrier((first, later))
    psi, far, coef_first = call(
        functools.partial(middle_kernel, add_other),
        "middle",
        (first, second, columns, other),
        [field, edges, shape_of((CX,))],
        1_000_000,
    )
    far = lax.ppermute(far, "gx", across)
    (near,) = call(near_kernel, "near", (psi, later_other), [edges], 100_000)
    near = lax.ppermute(near, "gx", inside)
    base, drift, spread, coef_grad = call(
        functools.partial(base_kernel, add_other, LANES * lax.axis_size("gz")),
        "base",
        (
            wide, grad_xy, lap_xy, own_halo, psi, coef_first,
            columns, other, later, later_other,
        ),
        [
            field, shape_of((CX,)), shape_of((2, 2)),
            jax.ShapeDtypeStruct((2, CX, ROWS), F32),
        ],
        15_000_000,
        scratch((5, CX), (5, CX), (5, CX + 4), (CX,)),
    )
    (far,) = call(widen_kernel, "widen", (far,), [shape_of((5, 2))], 100_000)
    (out,) = call(last_kernel, "last", (base, drift, spread, near, far), [field], 1_000_000)
    return out, coef_grad


def solution(mesh):
    return jax.shard_map(
        local,
        mesh=mesh,
        in_specs=(
            P(None, None, "gx", None, "gz"),
            P(None, "gx", None, "gz"),
            P(None, "gx", None, "gz"),
            P(None, "gx", None, "gz"),
        ),
        out_specs=(P(None, "gx", None, "gz"), P(None, "gx", None)),
        check_vma=False,
    )
```

```python
import functools
import math

import jax
import jax.numpy as jnp
from jax import lax
from jax.experimental import pallas as pl
from jax.experimental.pallas import tpu as pltpu
from jax.sharding import PartitionSpec as P

EPSILON = 1e-06
NU_MOL = 0.05
PRANDTL = 0.72
PRANDTL_TURB = 0.9
TIME_STEP = 0.04
PAIRS = ((0, 0), (1, 1), (2, 2), (0, 1), (0, 2), (1, 2))
WEIGHTS = (1.0, 1.0, 1.0, 2.0, 2.0, 2.0)

CX = 4
ROWS = 32
LANES = 128
STRIP = 4
F32 = jnp.float32
BF16 = jnp.bfloat16
SLOT_PSI = 4
BAND = 12
STRIP_BLOCKS = 2
BAND_BLOCKS = 3
VELOCITY = 0
SCALARS = 18
PSI = 26
MESSAGE = 36


def lane_ids():
    return lax.broadcasted_iota(jnp.int32, (ROWS, LANES), 1)


def row_ids():
    return lax.broadcasted_iota(jnp.int32, (ROWS, LANES), 0)


def turn(values, shift):
    shift = shift % LANES
    return values if shift == 0 else pltpu.roll(values, shift, 1)


class Ops:
    def __init__(self):
        self.lane = lane_ids()
        row = row_ids()
        self.top = row == ROWS - 1
        self.bottom = row == 0

    def z_at(self, values, halo, step):
        if step > 0:
            return turn(jnp.where(self.lane < step, halo, values), -step)
        return turn(jnp.where(self.lane >= LANES + step, halo, values), -step)

    def y_up(self, values):
        return jnp.where(self.top, 0.0, pltpu.roll(values, ROWS - 1, 0))

    def y_down(self, values):
        return jnp.where(self.bottom, 0.0, pltpu.roll(values, 1, 0))

    def strip(self, blocks, slot, x):
        return turn(blocks[slot // 8], -(STRIP * (4 * (slot % 8) + x) + 2))


def fourth(plus, minus, plus_2, minus_2):
    return (2.0 / 3.0) * (plus - minus) - (1.0 / 12.0) * (plus_2 - minus_2)


def strain_of(grad):
    return [
        grad[0][0],
        grad[1][1],
        grad[2][2],
        0.5 * (grad[0][1] + grad[1][0]),
        0.5 * (grad[0][2] + grad[2][0]),
        0.5 * (grad[1][2] + grad[2][1]),
    ]


def size_of(strain):
    diagonal = strain[0] * strain[0] + strain[1] * strain[1] + strain[2] * strain[2]
    other = strain[3] * strain[3] + strain[4] * strain[4] + strain[5] * strain[5]
    return jnp.sqrt(2.0 * diagonal + (4.0 * other + EPSILON))


def filter_fields(velocity, strain, size):
    products = [velocity[a] * velocity[b] for a, b in PAIRS]
    return list(velocity) + products + strain + [size * part for part in strain]


def pack_strips(ops, items):
    block = jnp.zeros((ROWS, LANES), F32)
    strip_id = ops.lane >> 2
    for slot, planes in enumerate(items):
        for x in range(CX):
            number = 4 * slot + x
            block = jnp.where(strip_id == number, turn(planes[x], STRIP * number + 2), block)
    return block


def place_halos(ops, t, own_halo, halos):
    strips = [own_halo[number].astype(F32) for number in range(STRIP_BLOCKS)]
    for k in range(3):
        number = 3 * t + k
        bands = own_halo[STRIP_BLOCKS + number // 2].astype(F32)
        for x in range(CX):
            halos[k, x] = turn(bands, -(BAND * (x + 3) + 3 + 6 * (number % 2)))
    for k in range(3, 5):
        for x in range(CX):
            halos[k, x] = ops.strip(strips, 2 * t + k - 3, x)


def across_terms(ops, values, halo):
    up, down = ops.y_up(values), ops.y_down(values)
    zs = [ops.z_at(values, halo, step) for step in (1, -1, 2, -2)]
    lap = (up + down) + (zs[0] + zs[1]) - 6.0 * values
    return 0.5 * (up - down), fourth(*zs), lap


def state_terms(wide, grad_yz, lap_yz, x):
    grad = [[None] * 5 for _ in range(3)]
    lap = [None] * 5
    center = [wide[k, x + 3] for k in range(5)]
    for k in range(5):
        xs = [wide[k, x + 3 + step] for step in (1, -1, 2, -2)]
        grad[0][k] = fourth(*xs)
        grad[1][k], grad[2][k] = grad_yz[k, 0, x], grad_yz[k, 1, x]
        if k != 3:
            lap[k] = lap_yz[k, x] + (xs[0] + xs[1])
    size = size_of(strain_of(grad))
    return center, grad, lap, size, 1.0 / center[3]


def affine_update(terms, psi, rates, laps):
    center, grad, lap, size, inv_rho = terms
    work_mom = psi[0] * lap[0] + psi[1] * lap[1] + psi[2] * lap[2]
    work_heat = psi[4] * lap[4]
    turbulent = work_mom + work_heat * (1.0 / PRANDTL_TURB)
    inv_rho_2 = inv_rho * inv_rho
    size_rho = size * inv_rho
    first, second = [], []
    for k in range(5):
        rate = rates[k]
        if k == 3:
            rate = rate - (NU_MOL * work_mom + (NU_MOL / PRANDTL) * work_heat) * inv_rho_2
            eddy = -(size * turbulent) * inv_rho_2
        else:
            lap_psi = laps[k]
            if k < 3:
                for other in range(5):
                    rate = rate + psi[other] * grad[k][other]
                rate = rate + NU_MOL * (inv_rho * lap_psi)
                eddy = size_rho * lap_psi
            else:
                rate = rate + (NU_MOL / PRANDTL) * (inv_rho * lap_psi)
                eddy = (1.0 / PRANDTL_TURB) * (size_rho * lap_psi)
        first.append(psi[k] + TIME_STEP * rate)
        second.append(TIME_STEP * eddy)
    return first, second, size_rho * turbulent


def band_of(lane):
    return (lane * 43) >> 9


def is_even():
    return lax.rem(lax.axis_index("gx"), 2) == 0


def fill_message(out, side, flow, rho, temp, psi):
    for t in range(2):
        for k in range(3):
            for i in range(3):
                out[VELOCITY + t * 9 + k * 3 + i] = flow[t, k, side + i]
        for i in range(2):
            out[SCALARS + t * 4 + i] = rho[t, 2 * side + i]
            out[SCALARS + t * 4 + 2 + i] = temp[t, 2 * side + i]
    for k in range(5):
        for i in range(2):
            out[PSI + k * 2 + i] = psi[k, 2 * side + i].astype(BF16)


def message_kernel(flow_far, rho_far, temp_far, psi_far, far, outer, sems):
    side = 1 - is_even().astype(jnp.int32)
    pieces = [(psi_far.at[:, pl.ds(2 * side, 2)], outer)]
    for t in range(2):
        for k in range(3):
            target = far.at[pl.ds(VELOCITY + t * 9 + k * 3, 3)]
            pieces.append((flow_far.at[t, k, pl.ds(side, 3)], target))
        for number, source in enumerate((rho_far, temp_far)):
            target = far.at[pl.ds(SCALARS + t * 4 + 2 * number, 2)]
            pieces.append((source.at[t, pl.ds(2 * side, 2)], target))
    copies = [
        pltpu.make_async_copy(source, target, sems.at[number])
        for number, (source, target) in enumerate(pieces)
    ]
    for copy in copies:
        copy.start()
    copies[0].wait()
    for k in range(5):
        for i in range(2):
            far[PSI + k * 2 + i] = outer[k, i].astype(BF16)
    for copy in copies[1:]:
        copy.wait()


def merge_bands(ops, low, message, first):
    lower = ops.lane - BAND * band_of(ops.lane) < 6
    for number in range(BAND_BLOCKS):
        both = jnp.where(lower, low[2 * number], turn(low[2 * number + 1], 6))
        message[first + number] = both.astype(BF16)


def pack_kernel(
    flow_far, rho_far, temp_far, psi_far, _, near, message, low, flow, rho, temp, psi, sems
):
    copies = [
        pltpu.make_async_copy(source, target, sems.at[i])
        for i, (source, target) in enumerate(
            ((flow_far, flow), (psi_far, psi), (rho_far, rho), (temp_far, temp))
        )
    ]
    for copy in copies:
        copy.start()
    ops = Ops()
    for copy in copies:
        copy.wait()
    fill_message(near, is_even().astype(jnp.int32), flow, rho, temp, psi)
    items = []
    for t in range(2):
        for source in (rho, temp):
            items.append([source[t, x].astype(F32) for x in range(CX)])
    items += [[psi[k, x] for x in range(CX)] for k in range(5)]
    for number in range(STRIP_BLOCKS):
        message[number] = pack_strips(ops, items[8 * number : 8 * number + 8]).astype(BF16)
    band = band_of(ops.lane)
    for t in range(2):
        for k in range(3):
            block = jnp.zeros((ROWS, LANES), F32)
            for x in range(CX):
                moved = turn(flow[t, k, x].astype(F32), BAND * (x + 3) + 3)
                block = jnp.where(band == x + 3, moved, block)
            low[3 * t + k] = block
    merge_bands(ops, low, message, STRIP_BLOCKS)


def own_kernel(
    flow, rho, temp, psi, own_halo, grad_0, grad_1, lap_0, lap_1, psi_rate, psi_lap, halos, psi_halos
):
    ops = Ops()
    for t in range(2):
        place_halos(ops, t, own_halo, halos.at[t])
    strips = [own_halo[number].astype(F32) for number in range(STRIP_BLOCKS)]
    for k in range(5):
        for x in range(CX):
            psi_halos[k, x] = ops.strip(strips, SLOT_PSI + k, x)
    for t, grad_yz, lap_yz in ((0, grad_0, lap_0), (1, grad_1, lap_1)):
        for k in range(5):
            for x in range(CX):
                values = flow[t, k, x] if k < 3 else (rho if k == 3 else temp)[t, x]
                grad_yz[k, 0, x], grad_yz[k, 1, x], lap_yz[k, x] = across_terms(
                    ops, values.astype(F32), halos[t, k, x]
                )
    for x in range(CX):
        along_y, along_z = flow[0, 1, x].astype(F32), flow[0, 2, x].astype(F32)
        for k in range(5):
            by_y, by_z, lap = across_terms(ops, psi[k, x], psi_halos[k, x])
            psi_rate[k, x] = along_y * by_y + along_z * by_z
            psi_lap[k, x] = lap


def bands_kernel(own_low, near, far, _, message, low):
    ops = Ops()
    even = is_even()
    band = band_of(ops.lane)
    for t in range(2):
        for k in range(3):
            block = own_low[3 * t + k]
            for i in range(3):
                number = VELOCITY + t * 9 + k * 3 + i
                one, two = near[number].astype(F32), far[number].astype(F32)
                moved = turn(jnp.where(even, two, one), BAND * i + 3)
                block = jnp.where(band == i, moved, block)
                moved = turn(jnp.where(even, one, two), BAND * (7 + i) + 3)
                block = jnp.where(band == 7 + i, moved, block)
            low[3 * t + k] = block
    merge_bands(ops, low, message, 0)


def products_of(hat):
    velocity = [hat(k) for k in range(3)]
    strain = [hat(9 + number) for number in range(6)]
    diagonal = strain[0] * strain[0] + strain[1] * strain[1] + strain[2] * strain[2]
    other = strain[3] * strain[3] + strain[4] * strain[4] + strain[5] * strain[5]
    size = 4.0 * jnp.sqrt((2.0 / 256.0) * diagonal + ((4.0 / 256.0) * other + EPSILON))
    cross = 0.0
    square = 0.0
    for number, (a, b) in enumerate(PAIRS):
        leonard = hat(3 + number) - (1.0 / 16.0) * velocity[a] * velocity[b]
        model = hat(15 + number) - size * strain[number]
        weighted = WEIGHTS[number] * model if WEIGHTS[number] != 1.0 else model
        cross = cross + leonard * weighted
        square = square + model * weighted
    return cross, square


def widen(k, source, number, count, even, near, far, wide):
    for i in range(count):
        one, two = near[number + i].astype(F32), far[number + i].astype(F32)
        wide[k, 3 - count + i] = jnp.where(even, two, one)
        wide[k, 3 + CX + i] = jnp.where(even, one, two)
    for x in range(CX):
        wide[k, 3 + x] = source(x).astype(F32)


def inner_products(ops, t, flow, rho, temp, near, far, grad_yz, sums, high, wide, fields, hats):
    even = is_even()
    valid = (ops.lane >= 3) & (ops.lane < LANES - 3)
    band = band_of(jnp.maximum(ops.lane - 2, 0))
    for k in range(3):
        widen(k, lambda x: flow[t, k, x], VELOCITY + t * 9 + k * 3, 3, even, near, far, wide)
    for k, source in ((3, rho), (4, temp)):
        number = SCALARS + t * 4 + (k - 3) * 2
        widen(k, lambda x: source[t, x], number, 2, even, near, far, wide)
    for x in range(-1, CX + 1):
        grad = [[None] * 3 for _ in range(3)]
        for k in range(3):
            center = wide[k, x + 3]
            grad[0][k] = fourth(*(wide[k, x + 3 + step] for step in (1, -1, 2, -2)))
            if 0 <= x < CX:
                grad[1][k], grad[2][k] = grad_yz[k, 0, x], grad_yz[k, 1, x]
            else:
                grad[1][k] = 0.5 * (ops.y_up(center) - ops.y_down(center))
                grad[2][k] = fourth(*(turn(center, -step) for step in (1, -1, 2, -2)))
        strain = strain_of(grad)
        size = size_of(strain)
        velocity = [wide[k, x + 3] for k in range(3)]
        for number, values in enumerate(filter_fields(velocity, strain, size)):
            fields[number, x + 1] = values
    for x in range(CX):
        for number in range(21):
            along_x = fields[number, x] + fields[number, x + 2] + 2.0 * fields[number, x + 1]
            hats[number, x] = turn(along_x, 1) + turn(along_x, -1) + 2.0 * along_x
    for k in range(3):
        block = jnp.zeros((ROWS, LANES), F32)
        for q in range(CX + 6):
            block = jnp.where(band == q, turn(wide[k, q], BAND * q + 11), block)
        high[k] = block
    for x in range(CX):
        cross, square = products_of(lambda number: hats[number, x])
        sums[0, x] = jnp.where(valid, cross, 0.0)
        sums[1, x] = jnp.where(valid, square, 0.0)


def edge_products(ops, t, low, high, halo, sums, bands, spread):
    band = band_of(ops.lane)
    place = ops.lane - BAND * band
    from_low = place < 3
    from_high = (place == 11) | (place < 2)
    low_side = place < 7
    at_edge = ((place >= 3) & (place <= 5)) | ((place >= 8) & (place <= 10))
    for k in range(3):
        number = 3 * t + k
        far = halo[number // 2].astype(F32)
        shift = 6 * (number % 2)
        bands[0, k] = jnp.where(from_low, turn(far, -shift), low[number])
        bands[1, k] = jnp.where(from_high, turn(far, 8 - shift), high[k])
    for side in range(2):
        velocity = [bands[side, k] for k in range(3)]
        grad = [[None] * 3 for _ in range(3)]
        for k in range(3):
            center = velocity[k]
            grad[0][k] = fourth(*(turn(center, -BAND * step) for step in (1, -1, 2, -2)))
            grad[1][k] = 0.5 * (ops.y_up(center) - ops.y_down(center))
            grad[2][k] = fourth(*(turn(center, -step) for step in (1, -1, 2, -2)))
        strain = strain_of(grad)
        for number, values in enumerate(filter_fields(velocity, strain, size_of(strain))):
            if side == 0:
                spread[number] = values
            else:
                spread[number] = jnp.where(low_side, spread[number], values)
    for number in range(21):
        both = spread[number]
        spread[number] = turn(both, BAND) + turn(both, -BAND) + 2.0 * both
    for number in range(21):
        both = spread[number]
        spread[number] = turn(both, 1) + turn(both, -1) + 2.0 * both
    for part, values in enumerate(products_of(lambda number: spread[number])):
        values = jnp.where(at_edge, values, 0.0)
        for x in range(CX):
            sums[part, x] = sums[part, x] + jnp.where(band == x + 3, values, 0.0)


def add_columns(ops, total, first_lane, planes, scale=1.0):
    for x in range(CX):
        value = scale * jnp.sum(planes(x), axis=1, keepdims=True)
        total = jnp.where(ops.lane == first_lane + x, value, total)
    return total


def add_parts(ops, block, total):
    upper = total.astype(BF16).astype(F32)
    rest = total - upper
    middle = rest.astype(BF16).astype(F32)
    for number, part in enumerate((upper, middle, rest - middle)):
        block = jnp.where(ops.lane >> 5 == 1 + number, turn(part, 32 * (1 + number)), block)
    return block


def span_total(add_other, columns, other):
    total = columns[...]
    if add_other:
        parts = other.astype(F32)
        total = total + ((turn(parts, -32) + turn(parts, -64)) + turn(parts, -96))
    return total


def psi_terms(psi_wide, rate_yz, lap_yz, velocity, x):
    rates, laps = [], []
    for k in range(5):
        xs = [psi_wide[k, x + 3 + step] for step in (1, -1, 2, -2)]
        rates.append(rate_yz[k, x] + velocity * fourth(*xs))
        laps.append(lap_yz[k, x] + (xs[0] + xs[1]))
    return rates, laps


def inner_kernel(
    flow, rho, temp, psi, near, far, grad_yz, lap_yz, psi_rate, psi_lap,
    sums, high, first, second, message, columns,
    wide, psi_wide, fields, hats, work,
):
    ops = Ops()
    even = is_even()
    for k in range(5):
        widen(k, lambda x: psi[k, x], PSI + k * 2, 2, even, near, far, psi_wide)
    inner_products(
        ops, 0, flow, rho, temp, near, far, grad_yz, sums, high, wide, fields, hats
    )
    for x in range(CX):
        terms = state_terms(wide, grad_yz, lap_yz, x)
        rates, laps = psi_terms(psi_wide, psi_rate, psi_lap, terms[0][0], x)
        new, slope, sensitivity = affine_update(
            terms, [psi[k, x] for k in range(5)], rates, laps
        )
        for k in range(5):
            first[k, x] = new[k]
            second[k, x] = slope[k]
        work[x] = sensitivity
    columns[...] = add_columns(ops, jnp.zeros((ROWS, LANES), F32), 16, lambda x: work[x])
    items = [[part[k, x] for x in range(CX)] for part in (first, second) for k in range(5)]
    for number in range(2):
        message[number] = pack_strips(ops, items[8 * number : 8 * number + 8])


def edge_kernel(
    low, high, halo, inner, strips, sensitivity, message, columns, bands, spread, sums
):
    ops = Ops()
    for part in range(2):
        for x in range(CX):
            sums[part, x] = inner[part, x]
    edge_products(ops, 0, low, high, halo, sums, bands, spread)
    total = sensitivity[...]
    for part in range(2):
        total = add_columns(ops, total, 4 * part, lambda x: sums[part, x], 1.0 / 256.0)
    columns[...] = total
    message[0] = strips[0].astype(BF16)
    message[1] = add_parts(ops, strips[1], total).astype(BF16)


def later_kernel(
    flow, rho, temp, near, far, grad_yz, lap_yz, low, halo, first, second,
    wide, message, columns,
    high, fields, hats, work, bands, spread, sums,
):
    ops = Ops()
    inner_products(
        ops, 1, flow, rho, temp, near, far, grad_yz, sums, high, wide, fields, hats
    )
    edge_products(ops, 1, low, high, halo, sums, bands, spread)
    for x in range(CX):
        _, _, lap, size, inv_rho = state_terms(wide, grad_yz, lap_yz, x)
        size_rho = size * inv_rho
        for part, source in enumerate((first, second)):
            total = lap[0] * source[0, x] + lap[1] * source[1, x] + lap[2] * source[2, x]
            work[part, x] = size_rho * (
                total + (1.0 / PRANDTL_TURB) * (lap[4] * source[4, x])
            )
    total = jnp.zeros((ROWS, LANES), F32)
    for part in range(2):
        total = add_columns(ops, total, 8 + 4 * part, lambda x: sums[part, x], 1.0 / 256.0)
        total = add_columns(ops, total, 20 + 4 * part, lambda x: work[part, x])
    columns[...] = total
    message[0] = add_parts(ops, jnp.zeros((ROWS, LANES), F32), total).astype(BF16)


def coefficients(ops, total):
    return total / (turn(total, -4) + EPSILON)


def middle_kernel(add_other, first, second, columns, other, psi, far, coef_first):
    ops = Ops()
    coef = coefficients(ops, span_total(add_other, columns, other[1]))
    for x in range(CX):
        coef_first[x] = jnp.broadcast_to(coef[:, x : x + 1], (ROWS, LANES))
    for x in range(CX):
        for k in range(5):
            psi[k, x] = first[k, x] + coef_first[x] * second[k, x]
    side = 1 - is_even().astype(jnp.int32)
    for k in range(5):
        for i in range(2):
            far[k, i] = psi[k, 2 * side + i].astype(BF16)


def base_kernel(
    add_other, span_cells,
    wide, grad_yz, lap_yz, psi, coef_first, columns, other, later, later_other,
    base, drift, spread, coef_grad, near,
    psi_halos, psi_wide, coef_planes, psi_rate, psi_lap,
):
    ops = Ops()
    side = is_even().astype(jnp.int32)
    for k in range(5):
        for i in range(2):
            near[k, i] = psi[k, 2 * side + i].astype(BF16)
    strips = [other[number].astype(F32) for number in range(2)]
    for k in range(5):
        for x in range(CX):
            psi_halos[k, x] = ops.strip(strips, k, x)
    total = span_total(add_other, columns, other[1]) + span_total(
        add_other, later, later_other[0]
    )
    coef = coefficients(ops, total)
    after = total + turn(coef, 20) * turn(total, -4)
    grads = jnp.where(ops.lane < 20, total, after) * (1.0 / span_cells)
    turned = jnp.concatenate([grads] * (LANES // ROWS), axis=0).T
    for t in range(2):
        coef_grad[t] = turned[16 + 4 * t : 20 + 4 * t, :ROWS]
    for x in range(CX):
        coef_planes[x] = jnp.broadcast_to(coef[:, 8 + x : 9 + x], (ROWS, LANES))
    for k in range(5):
        for x in range(CX):
            psi_halos[k, x] = psi_halos[k, x] + coef_first[x] * ops.strip(strips, 5 + k, x)
    zero = jnp.zeros((ROWS, LANES), F32)
    for k in range(5):
        for i in range(2):
            psi_wide[k, 1 + i] = zero
            psi_wide[k, 3 + CX + i] = zero
        for x in range(CX):
            psi_wide[k, 3 + x] = psi[k, x]
    for x in range(CX):
        for k in range(5):
            by_y, by_z, lap = across_terms(ops, psi[k, x], psi_halos[k, x])
            psi_rate[k, x] = wide[1, x + 3] * by_y + wide[2, x + 3] * by_z
            psi_lap[k, x] = lap
    for x in range(CX):
        terms = state_terms(wide, grad_yz, lap_yz, x)
        center = terms[0]
        rates, laps = psi_terms(psi_wide, psi_rate, psi_lap, center[0], x)
        new, slope, _ = affine_update(terms, [psi[k, x] for k in range(5)], rates, laps)
        for k in range(5):
            base[k, x] = new[k] + coef_planes[x] * slope[k]
        size, inv_rho = terms[3:]
        drift[x] = TIME_STEP * center[0]
        if x in (0, CX - 1):
            eddy = coef_planes[x] * size
            scaled = TIME_STEP * inv_rho
            spread[x // (CX - 1), 0] = scaled * (NU_MOL + eddy)
            spread[x // (CX - 1), 1] = scaled * (
                NU_MOL / PRANDTL + (1.0 / PRANDTL_TURB) * eddy
            )


def widen_kernel(far, out):
    for k in range(5):
        for i in range(2):
            out[k, i] = far[k, i].astype(F32)


def last_kernel(base, drift, spread, near_psi, far_psi, out):
    even = is_even()
    for k in range(5):
        ones = [near_psi[k, i].astype(F32) for i in range(2)]
        twos = [far_psi[k, i].astype(F32) for i in range(2)]
        far, near = (jnp.where(even, two, one) for one, two in zip(ones, twos))
        after, beyond = (jnp.where(even, one, two) for one, two in zip(ones, twos))
        low = drift[0] * ((1.0 / 12.0) * far - (2.0 / 3.0) * near)
        high = drift[CX - 1] * ((2.0 / 3.0) * after - (1.0 / 12.0) * beyond)
        if k != 3:
            kind = 1 if k == 4 else 0
            low = low + spread[0, kind] * near
            high = high + spread[1, kind] * after
        out[k, 0] = base[k, 0] + low
        out[k, 1] = base[k, 1] + drift[1] * ((1.0 / 12.0) * near)
        out[k, CX - 2] = base[k, CX - 2] - drift[CX - 2] * ((1.0 / 12.0) * after)
        out[k, CX - 1] = base[k, CX - 1] + high


def ring(axis):
    count = lax.axis_size(axis)
    forward = [(i, (i + 1) % count) for i in range(count)]
    return forward, [(target, source) for source, target in forward]


def pairs():
    count = lax.axis_size("gx")
    if count % 2:
        raise ValueError("odd gx")
    inside = [(i, i ^ 1) for i in range(count)]
    across = [(i, (i + 1 if i % 2 else i - 1) % count) for i in range(count)]
    return inside, across


def span_edges(message, strips):
    forward, backward = ring("gz")
    before = lax.ppermute(message, "gz", forward)
    if lax.axis_size("gz") == 2:
        return before
    after = lax.ppermute(message, "gz", backward)
    lane = lax.broadcasted_iota(jnp.int32, message.shape, 2)
    number = lax.broadcasted_iota(jnp.int32, message.shape, 0)
    low = jnp.where(number < strips, lane % STRIP < 2, lane % 6 < 3)
    return jnp.where(low, before, after)


def shape_of(dims, kind=F32):
    return jax.ShapeDtypeStruct(dims + (ROWS, LANES), kind)


def whole(count):
    return [pl.BlockSpec(memory_space=pltpu.VMEM)] * count


def scratch(*dims):
    return [pltpu.VMEM(d + (ROWS, LANES), F32) for d in dims]


def call(kernel, name, inputs, outputs, operations, buffers=(), in_specs=None):
    inputs = list(inputs)
    if in_specs:
        inputs[:4] = [
            pltpu.with_memory_space_constraint(a, pltpu.MemorySpace.HBM) for a in inputs[:4]
        ]
    size = sum(math.prod(a.shape) * a.dtype.itemsize for a in list(inputs) + list(outputs))
    return pl.pallas_call(
        kernel,
        in_specs=in_specs or whole(len(inputs)),
        out_specs=whole(len(outputs)),
        out_shape=list(outputs),
        scratch_shapes=list(buffers),
        compiler_params=pltpu.CompilerParams(vmem_limit_bytes=8 * 2**20),
        cost_estimate=pl.CostEstimate(
            flops=operations, bytes_accessed=size, transcendentals=0
        ),
        name=name,
    )(*inputs)


def span_sums(columns):
    if lax.axis_size("gz") == 2:
        return columns
    return lax.psum(columns, "gz")


def local(flow_far, rho_far, temp_far, psi_far):
    inside, across = pairs()
    add_other = lax.axis_size("gz") == 2
    field, planes, edges = shape_of((5, CX)), shape_of((5, CX + 6)), shape_of((5, 2), BF16)
    slopes = shape_of((5, 2, CX))
    inputs = (flow_far, rho_far, temp_far, psi_far)
    stay = [pl.BlockSpec(memory_space=pltpu.MemorySpace.HBM)] * 4
    far, outer = call(
        message_kernel,
        "message",
        inputs,
        [shape_of((MESSAGE,), BF16), shape_of((5, 2))],
        1_000_000,
        [pltpu.SemaphoreType.DMA((11,))],
        stay,
    )
    far = lax.ppermute(far, "gx", across)
    near, message, own_low, flow, rho, temp, psi = call(
        pack_kernel,
        "pack",
        inputs + (outer,),
        [
            shape_of((MESSAGE,), BF16),
            shape_of((STRIP_BLOCKS + BAND_BLOCKS,), BF16),
            shape_of((6,)),
            shape_of((2, 3, CX), BF16),
            shape_of((2, CX), BF16),
            shape_of((2, CX), BF16),
            field,
        ],
        2_000_000,
        [pltpu.SemaphoreType.DMA((4,))],
        stay + whole(1),
    )
    near = lax.ppermute(near, "gx", inside)
    own_halo = span_edges(message, STRIP_BLOCKS)
    grad_0, grad_1, lap_0, lap_1, psi_rate, psi_lap = call(
        own_kernel,
        "own",
        (flow, rho, temp, psi, own_halo),
        [slopes, slopes, field, field, field, field],
        5_000_000,
        scratch((2, 5, CX), (5, CX)),
    )
    message, low = call(
        bands_kernel,
        "bands",
        (own_low, near, far, psi_lap),
        [shape_of((BAND_BLOCKS,), BF16), shape_of((6,))],
        1_000_000,
    )
    halo = span_edges(message, 0)
    inner, high, first, second, strips, sensitivity = call(
        inner_kernel,
        "inner",
        (flow, rho, temp, psi, near, far, grad_0, lap_0, psi_rate, psi_lap),
        [shape_of((2, CX)), shape_of((3,)), field, field, shape_of((2,)), shape_of(())],
        20_000_000,
        scratch((5, CX + 6), (5, CX + 6), (21, CX + 2), (21, CX), (CX,)),
    )
    message, columns = call(
        edge_kernel,
        "edge",
        (low, high, halo, inner, strips, sensitivity),
        [shape_of((2,), BF16), shape_of(())],
        20_000_000,
        scratch((2, 3), (21,), (2, CX)),
    )
    other = span_edges(message, 2)
    columns = span_sums(columns)
    wide, message, later = call(
        later_kernel,
        "later",
        (flow, rho, temp, near, far, grad_1, lap_1, low, halo, first, second),
        [planes, shape_of((1,), BF16), shape_of(())],
        20_000_000,
        scratch((3,), (21, CX + 2), (21, CX), (2, CX), (2, 3), (21,), (2, CX)),
    )
    later_other = span_edges(message, 1)
    later = span_sums(later)
    first, later = lax.optimization_barrier((first, later))
    psi, far, coef_first = call(
        functools.partial(middle_kernel, add_other),
        "middle",
        (first, second, columns, other),
        [field, edges, shape_of((CX,))],
        1_000_000,
    )
    far = lax.ppermute(far, "gx", across)
    base, drift, spread, coef_grad, near = call(
        functools.partial(base_kernel, add_other, LANES * lax.axis_size("gz")),
        "base",
        (wide, grad_1, lap_1, psi, coef_first, columns, other, later, later_other),
        [
            field, shape_of((CX,)), shape_of((2, 2)),
            jax.ShapeDtypeStruct((2, CX, ROWS), F32), edges,
        ],
        15_000_000,
        scratch((5, CX), (5, CX + 6), (CX,), (5, CX), (5, CX)),
    )
    near = lax.ppermute(near, "gx", inside)
    (far,) = call(widen_kernel, "widen", (far,), [shape_of((5, 2))], 100_000)
    (out,) = call(last_kernel, "last", (base, drift, spread, near, far), [field], 1_000_000)
    return out, coef_grad


def solution(mesh):
    return jax.shard_map(
        local,
        mesh=mesh,
        in_specs=(
            P(None, None, "gx", None, "gz"),
            P(None, "gx", None, "gz"),
            P(None, "gx", None, "gz"),
            P(None, "gx", None, "gz"),
        ),
        out_specs=(P(None, "gx", None, "gz"), P(None, "gx", None)),
        check_vma=False,
    )
```

```python
import functools
import math

import jax
import jax.numpy as jnp
from jax import lax
from jax.experimental import pallas as pl
from jax.experimental.pallas import tpu as pltpu
from jax.sharding import PartitionSpec as P

EPSILON = 1e-06
NU_MOL = 0.05
PRANDTL = 0.72
PRANDTL_TURB = 0.9
TIME_STEP = 0.04
PAIRS = ((0, 0), (1, 1), (2, 2), (0, 1), (0, 2), (1, 2))
WEIGHTS = (1.0, 1.0, 1.0, 2.0, 2.0, 2.0)

CX = 4
ROWS = 32
LANES = 128
STRIP = 4
F32 = jnp.float32
BF16 = jnp.bfloat16
SLOT_PSI = 4
BAND = 12
STRIP_BLOCKS = 2
BAND_BLOCKS = 3
VELOCITY = 0
SCALARS = 18
PSI = 26
MESSAGE = 36


def lane_ids():
    return lax.broadcasted_iota(jnp.int32, (ROWS, LANES), 1)


def row_ids():
    return lax.broadcasted_iota(jnp.int32, (ROWS, LANES), 0)


def turn(values, shift):
    shift = shift % LANES
    return values if shift == 0 else pltpu.roll(values, shift, 1)


class Ops:
    def __init__(self):
        self.lane = lane_ids()
        row = row_ids()
        self.top = row == ROWS - 1
        self.bottom = row == 0

    def z_at(self, values, halo, step):
        if step > 0:
            return turn(jnp.where(self.lane < step, halo, values), -step)
        return turn(jnp.where(self.lane >= LANES + step, halo, values), -step)

    def y_up(self, values):
        return jnp.where(self.top, 0.0, pltpu.roll(values, ROWS - 1, 0))

    def y_down(self, values):
        return jnp.where(self.bottom, 0.0, pltpu.roll(values, 1, 0))

    def strip(self, blocks, slot, x):
        return turn(blocks[slot // 8], -(STRIP * (4 * (slot % 8) + x) + 2))


def fourth(plus, minus, plus_2, minus_2):
    return (2.0 / 3.0) * (plus - minus) - (1.0 / 12.0) * (plus_2 - minus_2)


def strain_of(grad):
    return [
        grad[0][0],
        grad[1][1],
        grad[2][2],
        0.5 * (grad[0][1] + grad[1][0]),
        0.5 * (grad[0][2] + grad[2][0]),
        0.5 * (grad[1][2] + grad[2][1]),
    ]


def size_of(strain):
    diagonal = strain[0] * strain[0] + strain[1] * strain[1] + strain[2] * strain[2]
    other = strain[3] * strain[3] + strain[4] * strain[4] + strain[5] * strain[5]
    return jnp.sqrt(2.0 * diagonal + (4.0 * other + EPSILON))


def filter_fields(velocity, strain, size):
    products = [velocity[a] * velocity[b] for a, b in PAIRS]
    return list(velocity) + products + strain + [size * part for part in strain]


def pack_strips(ops, items):
    block = jnp.zeros((ROWS, LANES), F32)
    strip_id = ops.lane >> 2
    for slot, planes in enumerate(items):
        for x in range(CX):
            number = 4 * slot + x
            block = jnp.where(strip_id == number, turn(planes[x], STRIP * number + 2), block)
    return block


def place_halos(ops, t, own_halo, halos):
    strips = [own_halo[number].astype(F32) for number in range(STRIP_BLOCKS)]
    for k in range(3):
        number = 3 * t + k
        bands = own_halo[STRIP_BLOCKS + number // 2].astype(F32)
        for x in range(CX):
            halos[k, x] = turn(bands, -(BAND * (x + 3) + 3 + 6 * (number % 2)))
    for k in range(3, 5):
        for x in range(CX):
            halos[k, x] = ops.strip(strips, 2 * t + k - 3, x)


def across_terms(ops, values, halo):
    up, down = ops.y_up(values), ops.y_down(values)
    zs = [ops.z_at(values, halo, step) for step in (1, -1, 2, -2)]
    lap = (up + down) + (zs[0] + zs[1]) - 6.0 * values
    return 0.5 * (up - down), fourth(*zs), lap


def state_terms(wide, grad_yz, lap_yz, x):
    grad = [[None] * 5 for _ in range(3)]
    lap = [None] * 5
    center = [wide[k, x + 3] for k in range(5)]
    for k in range(5):
        xs = [wide[k, x + 3 + step] for step in (1, -1, 2, -2)]
        grad[0][k] = fourth(*xs)
        grad[1][k], grad[2][k] = grad_yz[k, 0, x], grad_yz[k, 1, x]
        if k != 3:
            lap[k] = lap_yz[k, x] + (xs[0] + xs[1])
    size = size_of(strain_of(grad))
    return center, grad, lap, size, 1.0 / center[3]


def affine_update(terms, psi, rates, laps):
    center, grad, lap, size, inv_rho = terms
    work_mom = psi[0] * lap[0] + psi[1] * lap[1] + psi[2] * lap[2]
    work_heat = psi[4] * lap[4]
    turbulent = work_mom + work_heat * (1.0 / PRANDTL_TURB)
    inv_rho_2 = inv_rho * inv_rho
    size_rho = size * inv_rho
    first, second = [], []
    for k in range(5):
        rate = rates[k]
        if k == 3:
            rate = rate - (NU_MOL * work_mom + (NU_MOL / PRANDTL) * work_heat) * inv_rho_2
            eddy = -(size * turbulent) * inv_rho_2
        else:
            lap_psi = laps[k]
            if k < 3:
                for other in range(5):
                    rate = rate + psi[other] * grad[k][other]
                rate = rate + NU_MOL * (inv_rho * lap_psi)
                eddy = size_rho * lap_psi
            else:
                rate = rate + (NU_MOL / PRANDTL) * (inv_rho * lap_psi)
                eddy = (1.0 / PRANDTL_TURB) * (size_rho * lap_psi)
        first.append(psi[k] + TIME_STEP * rate)
        second.append(TIME_STEP * eddy)
    return first, second, size_rho * turbulent


def band_of(lane):
    return (lane * 43) >> 9


def is_even():
    return lax.rem(lax.axis_index("gx"), 2) == 0


def fill_message(out, side, flow, rho, temp, psi):
    for t in range(2):
        for k in range(3):
            for i in range(3):
                out[VELOCITY + t * 9 + k * 3 + i] = flow[t, k, side + i]
        for i in range(2):
            out[SCALARS + 2 * t + i] = rho[t, 2 * side + i]
            out[SCALARS + 4 + 2 * t + i] = temp[t, 2 * side + i]
    for k in range(5):
        for i in range(2):
            out[PSI + k * 2 + i] = psi[k, 2 * side + i].astype(BF16)


def message_kernel(flow_far, rho_far, temp_far, psi_far, far, outer, sems):
    side = 1 - is_even().astype(jnp.int32)
    block = (ROWS, LANES)
    pieces = [
        (psi_far.at[:, pl.ds(2 * side, 2)], outer),
        (
            flow_far.at[:, :, pl.ds(side, 3)],
            far.at[pl.ds(VELOCITY, 18)].reshape((2, 3, 3) + block),
        ),
        (rho_far.at[:, pl.ds(2 * side, 2)], far.at[pl.ds(SCALARS, 4)].reshape((2, 2) + block)),
        (
            temp_far.at[:, pl.ds(2 * side, 2)],
            far.at[pl.ds(SCALARS + 4, 4)].reshape((2, 2) + block),
        ),
    ]
    copies = [
        pltpu.make_async_copy(source, target, sems.at[number])
        for number, (source, target) in enumerate(pieces)
    ]
    for copy in copies:
        copy.start()
    copies[0].wait()
    for k in range(5):
        for i in range(2):
            far[PSI + k * 2 + i] = outer[k, i].astype(BF16)
    for copy in copies[1:]:
        copy.wait()


def merge_bands(ops, low, message, first):
    lower = ops.lane - BAND * band_of(ops.lane) < 6
    for number in range(BAND_BLOCKS):
        both = jnp.where(lower, low[2 * number], turn(low[2 * number + 1], 6))
        message[first + number] = both.astype(BF16)


def pack_kernel(
    flow_far, rho_far, temp_far, psi_far, _, near, message, low, flow, rho, temp, psi, sems
):
    copies = [
        pltpu.make_async_copy(source, target, sems.at[i])
        for i, (source, target) in enumerate(
            ((flow_far, flow), (psi_far, psi), (rho_far, rho), (temp_far, temp))
        )
    ]
    for copy in copies:
        copy.start()
    ops = Ops()
    for copy in copies:
        copy.wait()
    fill_message(near, is_even().astype(jnp.int32), flow, rho, temp, psi)
    items = []
    for t in range(2):
        for source in (rho, temp):
            items.append([source[t, x].astype(F32) for x in range(CX)])
    items += [[psi[k, x] for x in range(CX)] for k in range(5)]
    for number in range(STRIP_BLOCKS):
        message[number] = pack_strips(ops, items[8 * number : 8 * number + 8]).astype(BF16)
    band = band_of(ops.lane)
    for t in range(2):
        for k in range(3):
            block = jnp.zeros((ROWS, LANES), F32)
            for x in range(CX):
                moved = turn(flow[t, k, x].astype(F32), BAND * (x + 3) + 3)
                block = jnp.where(band == x + 3, moved, block)
            low[3 * t + k] = block
    merge_bands(ops, low, message, STRIP_BLOCKS)


def own_kernel(
    flow, rho, temp, psi, own_halo, grad_0, grad_1, lap_0, lap_1, psi_rate, psi_lap, halos, psi_halos
):
    ops = Ops()
    for t in range(2):
        place_halos(ops, t, own_halo, halos.at[t])
    strips = [own_halo[number].astype(F32) for number in range(STRIP_BLOCKS)]
    for k in range(5):
        for x in range(CX):
            psi_halos[k, x] = ops.strip(strips, SLOT_PSI + k, x)
    for t, grad_yz, lap_yz in ((0, grad_0, lap_0), (1, grad_1, lap_1)):
        for k in range(5):
            for x in range(CX):
                values = flow[t, k, x] if k < 3 else (rho if k == 3 else temp)[t, x]
                grad_yz[k, 0, x], grad_yz[k, 1, x], lap_yz[k, x] = across_terms(
                    ops, values.astype(F32), halos[t, k, x]
                )
    for x in range(CX):
        along_y, along_z = flow[0, 1, x].astype(F32), flow[0, 2, x].astype(F32)
        for k in range(5):
            by_y, by_z, lap = across_terms(ops, psi[k, x], psi_halos[k, x])
            psi_rate[k, x] = along_y * by_y + along_z * by_z
            psi_lap[k, x] = lap


def token_kernel(far, out):
    out[...] = far[0].astype(F32)


def bands_kernel(own_low, near, far, _, message, low):
    ops = Ops()
    even = is_even()
    band = band_of(ops.lane)
    for t in range(2):
        for k in range(3):
            block = own_low[3 * t + k]
            for i in range(3):
                number = VELOCITY + t * 9 + k * 3 + i
                one, two = near[number].astype(F32), far[number].astype(F32)
                moved = turn(jnp.where(even, two, one), BAND * i + 3)
                block = jnp.where(band == i, moved, block)
                moved = turn(jnp.where(even, one, two), BAND * (7 + i) + 3)
                block = jnp.where(band == 7 + i, moved, block)
            low[3 * t + k] = block
    merge_bands(ops, low, message, 0)


def products_of(hat):
    velocity = [hat(k) for k in range(3)]
    strain = [hat(9 + number) for number in range(6)]
    diagonal = strain[0] * strain[0] + strain[1] * strain[1] + strain[2] * strain[2]
    other = strain[3] * strain[3] + strain[4] * strain[4] + strain[5] * strain[5]
    size = 4.0 * jnp.sqrt((2.0 / 256.0) * diagonal + ((4.0 / 256.0) * other + EPSILON))
    cross = 0.0
    square = 0.0
    for number, (a, b) in enumerate(PAIRS):
        leonard = hat(3 + number) - (1.0 / 16.0) * velocity[a] * velocity[b]
        model = hat(15 + number) - size * strain[number]
        weighted = WEIGHTS[number] * model if WEIGHTS[number] != 1.0 else model
        cross = cross + leonard * weighted
        square = square + model * weighted
    return cross, square


def widen(k, source, number, count, even, near, far, wide):
    for i in range(count):
        one, two = near[number + i].astype(F32), far[number + i].astype(F32)
        wide[k, 3 - count + i] = jnp.where(even, two, one)
        wide[k, 3 + CX + i] = jnp.where(even, one, two)
    for x in range(CX):
        wide[k, 3 + x] = source(x).astype(F32)


def inner_products(ops, t, flow, rho, temp, near, far, grad_yz, sums, high, wide, fields, hats):
    even = is_even()
    valid = (ops.lane >= 3) & (ops.lane < LANES - 3)
    band = band_of(jnp.maximum(ops.lane - 2, 0))
    for k in range(3):
        widen(k, lambda x: flow[t, k, x], VELOCITY + t * 9 + k * 3, 3, even, near, far, wide)
    for k, source in ((3, rho), (4, temp)):
        number = SCALARS + (k - 3) * 4 + 2 * t
        widen(k, lambda x: source[t, x], number, 2, even, near, far, wide)
    for x in range(-1, CX + 1):
        grad = [[None] * 3 for _ in range(3)]
        for k in range(3):
            center = wide[k, x + 3]
            grad[0][k] = fourth(*(wide[k, x + 3 + step] for step in (1, -1, 2, -2)))
            if 0 <= x < CX:
                grad[1][k], grad[2][k] = grad_yz[k, 0, x], grad_yz[k, 1, x]
            else:
                grad[1][k] = 0.5 * (ops.y_up(center) - ops.y_down(center))
                grad[2][k] = fourth(*(turn(center, -step) for step in (1, -1, 2, -2)))
        strain = strain_of(grad)
        size = size_of(strain)
        velocity = [wide[k, x + 3] for k in range(3)]
        for number, values in enumerate(filter_fields(velocity, strain, size)):
            fields[number, x + 1] = values
    for x in range(CX):
        for number in range(21):
            along_x = fields[number, x] + fields[number, x + 2] + 2.0 * fields[number, x + 1]
            hats[number, x] = turn(along_x, 1) + turn(along_x, -1) + 2.0 * along_x
    for k in range(3):
        block = jnp.zeros((ROWS, LANES), F32)
        for q in range(CX + 6):
            block = jnp.where(band == q, turn(wide[k, q], BAND * q + 11), block)
        high[k] = block
    for x in range(CX):
        cross, square = products_of(lambda number: hats[number, x])
        sums[0, x] = jnp.where(valid, cross, 0.0)
        sums[1, x] = jnp.where(valid, square, 0.0)


def edge_products(ops, t, low, high, halo, sums, bands, spread):
    band = band_of(ops.lane)
    place = ops.lane - BAND * band
    from_low = place < 3
    from_high = (place == 11) | (place < 2)
    low_side = place < 7
    at_edge = ((place >= 3) & (place <= 5)) | ((place >= 8) & (place <= 10))
    for k in range(3):
        number = 3 * t + k
        far = halo[number // 2].astype(F32)
        shift = 6 * (number % 2)
        bands[0, k] = jnp.where(from_low, turn(far, -shift), low[number])
        bands[1, k] = jnp.where(from_high, turn(far, 8 - shift), high[k])
    for side in range(2):
        velocity = [bands[side, k] for k in range(3)]
        grad = [[None] * 3 for _ in range(3)]
        for k in range(3):
            center = velocity[k]
            grad[0][k] = fourth(*(turn(center, -BAND * step) for step in (1, -1, 2, -2)))
            grad[1][k] = 0.5 * (ops.y_up(center) - ops.y_down(center))
            grad[2][k] = fourth(*(turn(center, -step) for step in (1, -1, 2, -2)))
        strain = strain_of(grad)
        for number, values in enumerate(filter_fields(velocity, strain, size_of(strain))):
            if side == 0:
                spread[number] = values
            else:
                spread[number] = jnp.where(low_side, spread[number], values)
    for number in range(21):
        both = spread[number]
        spread[number] = turn(both, BAND) + turn(both, -BAND) + 2.0 * both
    for number in range(21):
        both = spread[number]
        spread[number] = turn(both, 1) + turn(both, -1) + 2.0 * both
    for part, values in enumerate(products_of(lambda number: spread[number])):
        values = jnp.where(at_edge, values, 0.0)
        for x in range(CX):
            sums[part, x] = sums[part, x] + jnp.where(band == x + 3, values, 0.0)


def add_columns(ops, total, first_lane, planes, scale=1.0):
    for x in range(CX):
        value = scale * jnp.sum(planes(x), axis=1, keepdims=True)
        total = jnp.where(ops.lane == first_lane + x, value, total)
    return total


def add_parts(ops, block, total):
    upper = total.astype(BF16).astype(F32)
    rest = total - upper
    middle = rest.astype(BF16).astype(F32)
    for number, part in enumerate((upper, middle, rest - middle)):
        block = jnp.where(ops.lane >> 5 == 1 + number, turn(part, 32 * (1 + number)), block)
    return block


def span_total(add_other, columns, other):
    total = columns[...]
    if add_other:
        parts = other.astype(F32)
        total = total + ((turn(parts, -32) + turn(parts, -64)) + turn(parts, -96))
    return total


def psi_terms(psi_wide, rate_yz, lap_yz, velocity, x):
    rates, laps = [], []
    for k in range(5):
        xs = [psi_wide[k, x + 3 + step] for step in (1, -1, 2, -2)]
        rates.append(rate_yz[k, x] + velocity * fourth(*xs))
        laps.append(lap_yz[k, x] + (xs[0] + xs[1]))
    return rates, laps


def inner_kernel(
    flow, rho, temp, psi, near, far, grad_yz, lap_yz, psi_rate, psi_lap,
    sums, high, first, second, message, columns,
    wide, psi_wide, fields, hats, work,
):
    ops = Ops()
    even = is_even()
    for k in range(5):
        widen(k, lambda x: psi[k, x], PSI + k * 2, 2, even, near, far, psi_wide)
    inner_products(
        ops, 0, flow, rho, temp, near, far, grad_yz, sums, high, wide, fields, hats
    )
    for x in range(CX):
        terms = state_terms(wide, grad_yz, lap_yz, x)
        rates, laps = psi_terms(psi_wide, psi_rate, psi_lap, terms[0][0], x)
        new, slope, sensitivity = affine_update(
            terms, [psi[k, x] for k in range(5)], rates, laps
        )
        for k in range(5):
            first[k, x] = new[k]
            second[k, x] = slope[k]
        work[x] = sensitivity
    columns[...] = add_columns(ops, jnp.zeros((ROWS, LANES), F32), 16, lambda x: work[x])
    items = [[part[k, x] for x in range(CX)] for part in (first, second) for k in range(5)]
    for number in range(2):
        message[number] = pack_strips(ops, items[8 * number : 8 * number + 8])


def edge_kernel(
    low, high, halo, inner, strips, sensitivity, message, columns, bands, spread, sums
):
    ops = Ops()
    for part in range(2):
        for x in range(CX):
            sums[part, x] = inner[part, x]
    edge_products(ops, 0, low, high, halo, sums, bands, spread)
    total = sensitivity[...]
    for part in range(2):
        total = add_columns(ops, total, 4 * part, lambda x: sums[part, x], 1.0 / 256.0)
    columns[...] = total
    message[0] = strips[0].astype(BF16)
    message[1] = add_parts(ops, strips[1], total).astype(BF16)


def later_kernel(
    flow, rho, temp, near, far, grad_yz, lap_yz, low, halo, first, second,
    wide, message, columns,
    high, fields, hats, work, bands, spread, sums,
):
    ops = Ops()
    inner_products(
        ops, 1, flow, rho, temp, near, far, grad_yz, sums, high, wide, fields, hats
    )
    edge_products(ops, 1, low, high, halo, sums, bands, spread)
    for x in range(CX):
        _, _, lap, size, inv_rho = state_terms(wide, grad_yz, lap_yz, x)
        size_rho = size * inv_rho
        for part, source in enumerate((first, second)):
            total = lap[0] * source[0, x] + lap[1] * source[1, x] + lap[2] * source[2, x]
            work[part, x] = size_rho * (
                total + (1.0 / PRANDTL_TURB) * (lap[4] * source[4, x])
            )
    total = jnp.zeros((ROWS, LANES), F32)
    for part in range(2):
        total = add_columns(ops, total, 8 + 4 * part, lambda x: sums[part, x], 1.0 / 256.0)
        total = add_columns(ops, total, 20 + 4 * part, lambda x: work[part, x])
    columns[...] = total
    message[0] = add_parts(ops, jnp.zeros((ROWS, LANES), F32), total).astype(BF16)


def coefficients(ops, total):
    return total / (turn(total, -4) + EPSILON)


def middle_kernel(add_other, first, second, columns, other, psi, far, coef_first):
    ops = Ops()
    coef = coefficients(ops, span_total(add_other, columns, other[1]))
    for x in range(CX):
        coef_first[x] = jnp.broadcast_to(coef[:, x : x + 1], (ROWS, LANES))
    for x in range(CX):
        for k in range(5):
            psi[k, x] = first[k, x] + coef_first[x] * second[k, x]
    side = 1 - is_even().astype(jnp.int32)
    for k in range(5):
        for i in range(2):
            far[k, i] = psi[k, 2 * side + i].astype(BF16)


def base_kernel(
    add_other, span_cells,
    wide, grad_yz, lap_yz, psi, coef_first, columns, other, later, later_other,
    base, drift, spread, coef_grad, near,
    psi_halos, psi_wide, coef_planes, psi_rate, psi_lap,
):
    ops = Ops()
    side = is_even().astype(jnp.int32)
    for k in range(5):
        for i in range(2):
            near[k, i] = psi[k, 2 * side + i].astype(BF16)
    strips = [other[number].astype(F32) for number in range(2)]
    for k in range(5):
        for x in range(CX):
            psi_halos[k, x] = ops.strip(strips, k, x)
    total = span_total(add_other, columns, other[1]) + span_total(
        add_other, later, later_other[0]
    )
    coef = coefficients(ops, total)
    after = total + turn(coef, 20) * turn(total, -4)
    grads = jnp.where(ops.lane < 20, total, after) * (1.0 / span_cells)
    turned = jnp.concatenate([grads] * (LANES // ROWS), axis=0).T
    for t in range(2):
        coef_grad[t] = turned[16 + 4 * t : 20 + 4 * t, :ROWS]
    for x in range(CX):
        coef_planes[x] = jnp.broadcast_to(coef[:, 8 + x : 9 + x], (ROWS, LANES))
    for k in range(5):
        for x in range(CX):
            psi_halos[k, x] = psi_halos[k, x] + coef_first[x] * ops.strip(strips, 5 + k, x)
    zero = jnp.zeros((ROWS, LANES), F32)
    for k in range(5):
        for i in range(2):
            psi_wide[k, 1 + i] = zero
            psi_wide[k, 3 + CX + i] = zero
        for x in range(CX):
            psi_wide[k, 3 + x] = psi[k, x]
    for x in range(CX):
        for k in range(5):
            by_y, by_z, lap = across_terms(ops, psi[k, x], psi_halos[k, x])
            psi_rate[k, x] = wide[1, x + 3] * by_y + wide[2, x + 3] * by_z
            psi_lap[k, x] = lap
    for x in range(CX):
        terms = state_terms(wide, grad_yz, lap_yz, x)
        center = terms[0]
        rates, laps = psi_terms(psi_wide, psi_rate, psi_lap, center[0], x)
        new, slope, _ = affine_update(terms, [psi[k, x] for k in range(5)], rates, laps)
        for k in range(5):
            base[k, x] = new[k] + coef_planes[x] * slope[k]
        size, inv_rho = terms[3:]
        drift[x] = TIME_STEP * center[0]
        if x in (0, CX - 1):
            eddy = coef_planes[x] * size
            scaled = TIME_STEP * inv_rho
            spread[x // (CX - 1), 0] = scaled * (NU_MOL + eddy)
            spread[x // (CX - 1), 1] = scaled * (
                NU_MOL / PRANDTL + (1.0 / PRANDTL_TURB) * eddy
            )


def widen_kernel(far, out):
    for k in range(5):
        for i in range(2):
            out[k, i] = far[k, i].astype(F32)


def last_kernel(base, drift, spread, near_psi, far_psi, out):
    even = is_even()
    for k in range(5):
        ones = [near_psi[k, i].astype(F32) for i in range(2)]
        twos = [far_psi[k, i].astype(F32) for i in range(2)]
        far, near = (jnp.where(even, two, one) for one, two in zip(ones, twos))
        after, beyond = (jnp.where(even, one, two) for one, two in zip(ones, twos))
        low = drift[0] * ((1.0 / 12.0) * far - (2.0 / 3.0) * near)
        high = drift[CX - 1] * ((2.0 / 3.0) * after - (1.0 / 12.0) * beyond)
        if k != 3:
            kind = 1 if k == 4 else 0
            low = low + spread[0, kind] * near
            high = high + spread[1, kind] * after
        out[k, 0] = base[k, 0] + low
        out[k, 1] = base[k, 1] + drift[1] * ((1.0 / 12.0) * near)
        out[k, CX - 2] = base[k, CX - 2] - drift[CX - 2] * ((1.0 / 12.0) * after)
        out[k, CX - 1] = base[k, CX - 1] + high


def ring(axis):
    count = lax.axis_size(axis)
    forward = [(i, (i + 1) % count) for i in range(count)]
    return forward, [(target, source) for source, target in forward]


def pairs():
    count = lax.axis_size("gx")
    if count % 2:
        raise ValueError("odd gx")
    inside = [(i, i ^ 1) for i in range(count)]
    across = [(i, (i + 1 if i % 2 else i - 1) % count) for i in range(count)]
    return inside, across


def span_edges(message, strips):
    forward, backward = ring("gz")
    before = lax.ppermute(message, "gz", forward)
    if lax.axis_size("gz") == 2:
        return before
    after = lax.ppermute(message, "gz", backward)
    lane = lax.broadcasted_iota(jnp.int32, message.shape, 2)
    number = lax.broadcasted_iota(jnp.int32, message.shape, 0)
    low = jnp.where(number < strips, lane % STRIP < 2, lane % 6 < 3)
    return jnp.where(low, before, after)


def shape_of(dims, kind=F32):
    return jax.ShapeDtypeStruct(dims + (ROWS, LANES), kind)


def whole(count):
    return [pl.BlockSpec(memory_space=pltpu.VMEM)] * count


def scratch(*dims):
    return [pltpu.VMEM(d + (ROWS, LANES), F32) for d in dims]


def call(kernel, name, inputs, outputs, operations, buffers=(), in_specs=None):
    inputs = list(inputs)
    if in_specs:
        inputs[:4] = [
            pltpu.with_memory_space_constraint(a, pltpu.MemorySpace.HBM) for a in inputs[:4]
        ]
    size = sum(math.prod(a.shape) * a.dtype.itemsize for a in list(inputs) + list(outputs))
    return pl.pallas_call(
        kernel,
        in_specs=in_specs or whole(len(inputs)),
        out_specs=whole(len(outputs)),
        out_shape=list(outputs),
        scratch_shapes=list(buffers),
        compiler_params=pltpu.CompilerParams(vmem_limit_bytes=8 * 2**20),
        cost_estimate=pl.CostEstimate(
            flops=operations, bytes_accessed=size, transcendentals=0
        ),
        name=name,
    )(*inputs)


def span_sums(columns):
    if lax.axis_size("gz") == 2:
        return columns
    return lax.psum(columns, "gz")


def local(flow_far, rho_far, temp_far, psi_far):
    inside, across = pairs()
    add_other = lax.axis_size("gz") == 2
    field, planes, edges = shape_of((5, CX)), shape_of((5, CX + 6)), shape_of((5, 2), BF16)
    slopes = shape_of((5, 2, CX))
    inputs = (flow_far, rho_far, temp_far, psi_far)
    stay = [pl.BlockSpec(memory_space=pltpu.MemorySpace.HBM)] * 4
    far, outer = call(
        message_kernel,
        "message",
        inputs,
        [shape_of((MESSAGE,), BF16), shape_of((5, 2))],
        1_000_000,
        [pltpu.SemaphoreType.DMA((4,))],
        stay,
    )
    far = lax.ppermute(far, "gx", across)
    near, message, own_low, flow, rho, temp, psi = call(
        pack_kernel,
        "pack",
        inputs + (outer,),
        [
            shape_of((MESSAGE,), BF16),
            shape_of((STRIP_BLOCKS + BAND_BLOCKS,), BF16),
            shape_of((6,)),
            shape_of((2, 3, CX), BF16),
            shape_of((2, CX), BF16),
            shape_of((2, CX), BF16),
            field,
        ],
        2_000_000,
        [pltpu.SemaphoreType.DMA((4,))],
        stay + whole(1),
    )
    near = lax.ppermute(near, "gx", inside)
    own_halo = span_edges(message, STRIP_BLOCKS)
    grad_0, grad_1, lap_0, lap_1, psi_rate, psi_lap = call(
        own_kernel,
        "own",
        (flow, rho, temp, psi, own_halo),
        [slopes, slopes, field, field, field, field],
        5_000_000,
        scratch((2, 5, CX), (5, CX)),
    )
    (token,) = call(token_kernel, "token", (far,), [shape_of(())], 100_000)
    message, low = call(
        bands_kernel,
        "bands",
        (own_low, near, far, token),
        [shape_of((BAND_BLOCKS,), BF16), shape_of((6,))],
        1_000_000,
    )
    halo = span_edges(message, 0)
    inner, high, first, second, strips, sensitivity = call(
        inner_kernel,
        "inner",
        (flow, rho, temp, psi, near, far, grad_0, lap_0, psi_rate, psi_lap),
        [shape_of((2, CX)), shape_of((3,)), field, field, shape_of((2,)), shape_of(())],
        20_000_000,
        scratch((5, CX + 6), (5, CX + 6), (21, CX + 2), (21, CX), (CX,)),
    )
    message, columns = call(
        edge_kernel,
        "edge",
        (low, high, halo, inner, strips, sensitivity),
        [shape_of((2,), BF16), shape_of(())],
        20_000_000,
        scratch((2, 3), (21,), (2, CX)),
    )
    other = span_edges(message, 2)
    columns = span_sums(columns)
    wide, message, later = call(
        later_kernel,
        "later",
        (flow, rho, temp, near, far, grad_1, lap_1, low, halo, first, second),
        [planes, shape_of((1,), BF16), shape_of(())],
        20_000_000,
        scratch((3,), (21, CX + 2), (21, CX), (2, CX), (2, 3), (21,), (2, CX)),
    )
    later_other = span_edges(message, 1)
    later = span_sums(later)
    first, later = lax.optimization_barrier((first, later))
    psi, far, coef_first = call(
        functools.partial(middle_kernel, add_other),
        "middle",
        (first, second, columns, other),
        [field, edges, shape_of((CX,))],
        1_000_000,
    )
    far = lax.ppermute(far, "gx", across)
    base, drift, spread, coef_grad, near = call(
        functools.partial(base_kernel, add_other, LANES * lax.axis_size("gz")),
        "base",
        (wide, grad_1, lap_1, psi, coef_first, columns, other, later, later_other),
        [
            field, shape_of((CX,)), shape_of((2, 2)),
            jax.ShapeDtypeStruct((2, CX, ROWS), F32), edges,
        ],
        15_000_000,
        scratch((5, CX), (5, CX + 6), (CX,), (5, CX), (5, CX)),
    )
    near = lax.ppermute(near, "gx", inside)
    (far,) = call(widen_kernel, "widen", (far,), [shape_of((5, 2))], 100_000)
    (out,) = call(last_kernel, "last", (base, drift, spread, near, far), [field], 1_000_000)
    return out, coef_grad


def solution(mesh):
    return jax.shard_map(
        local,
        mesh=mesh,
        in_specs=(
            P(None, None, "gx", None, "gz"),
            P(None, "gx", None, "gz"),
            P(None, "gx", None, "gz"),
            P(None, "gx", None, "gz"),
        ),
        out_specs=(P(None, "gx", None, "gz"), P(None, "gx", None)),
        check_vma=False,
    )
```

```python
import functools
import math

import jax
import jax.numpy as jnp
from jax import lax
from jax.experimental import pallas as pl
from jax.experimental.pallas import tpu as pltpu
from jax.sharding import PartitionSpec as P

EPSILON = 1e-06
NU_MOL = 0.05
PRANDTL = 0.72
PRANDTL_TURB = 0.9
TIME_STEP = 0.04
PAIRS = ((0, 0), (1, 1), (2, 2), (0, 1), (0, 2), (1, 2))
WEIGHTS = (1.0, 1.0, 1.0, 2.0, 2.0, 2.0)

CX = 4
ROWS = 32
LANES = 128
STRIP = 4
F32 = jnp.float32
BF16 = jnp.bfloat16
SLOT_PSI = 4
BAND = 12
STRIP_BLOCKS = 2
BAND_BLOCKS = 3
VELOCITY = 0
SCALARS = 18
PSI = 8
SCALAR_PLANES = 18


def lane_ids():
    return lax.broadcasted_iota(jnp.int32, (ROWS, LANES), 1)


def row_ids():
    return lax.broadcasted_iota(jnp.int32, (ROWS, LANES), 0)


def turn(values, shift):
    shift = shift % LANES
    return values if shift == 0 else pltpu.roll(values, shift, 1)


class Ops:
    def __init__(self):
        self.lane = lane_ids()
        row = row_ids()
        self.top = row == ROWS - 1
        self.bottom = row == 0

    def z_at(self, values, halo, step):
        if step > 0:
            return turn(jnp.where(self.lane < step, halo, values), -step)
        return turn(jnp.where(self.lane >= LANES + step, halo, values), -step)

    def y_up(self, values):
        return jnp.where(self.top, 0.0, pltpu.roll(values, ROWS - 1, 0))

    def y_down(self, values):
        return jnp.where(self.bottom, 0.0, pltpu.roll(values, 1, 0))

    def strip(self, blocks, slot, x):
        return turn(blocks[slot // 8], -(STRIP * (4 * (slot % 8) + x) + 2))


def fourth(plus, minus, plus_2, minus_2):
    return (2.0 / 3.0) * (plus - minus) - (1.0 / 12.0) * (plus_2 - minus_2)


def strain_of(grad):
    return [
        grad[0][0],
        grad[1][1],
        grad[2][2],
        0.5 * (grad[0][1] + grad[1][0]),
        0.5 * (grad[0][2] + grad[2][0]),
        0.5 * (grad[1][2] + grad[2][1]),
    ]


def size_of(strain):
    diagonal = strain[0] * strain[0] + strain[1] * strain[1] + strain[2] * strain[2]
    other = strain[3] * strain[3] + strain[4] * strain[4] + strain[5] * strain[5]
    return jnp.sqrt(2.0 * diagonal + (4.0 * other + EPSILON))


def filter_fields(velocity, strain, size):
    products = [velocity[a] * velocity[b] for a, b in PAIRS]
    return list(velocity) + products + strain + [size * part for part in strain]


def pack_strips(ops, items):
    block = jnp.zeros((ROWS, LANES), F32)
    strip_id = ops.lane >> 2
    for slot, planes in enumerate(items):
        for x in range(CX):
            number = 4 * slot + x
            block = jnp.where(strip_id == number, turn(planes[x], STRIP * number + 2), block)
    return block


def place_halos(ops, t, own_halo, halos):
    strips = [own_halo[number].astype(F32) for number in range(STRIP_BLOCKS)]
    for k in range(3):
        number = 3 * t + k
        bands = own_halo[STRIP_BLOCKS + number // 2].astype(F32)
        for x in range(CX):
            halos[k, x] = turn(bands, -(BAND * (x + 3) + 3 + 6 * (number % 2)))
    for k in range(3, 5):
        for x in range(CX):
            halos[k, x] = ops.strip(strips, 2 * t + k - 3, x)


def across_terms(ops, values, halo):
    up, down = ops.y_up(values), ops.y_down(values)
    zs = [ops.z_at(values, halo, step) for step in (1, -1, 2, -2)]
    lap = (up + down) + (zs[0] + zs[1]) - 6.0 * values
    return 0.5 * (up - down), fourth(*zs), lap


def state_terms(wide, grad_yz, lap_yz, x):
    grad = [[None] * 5 for _ in range(3)]
    lap = [None] * 5
    center = [wide[k, x + 3] for k in range(5)]
    for k in range(5):
        xs = [wide[k, x + 3 + step] for step in (1, -1, 2, -2)]
        grad[0][k] = fourth(*xs)
        grad[1][k], grad[2][k] = grad_yz[k, 0, x], grad_yz[k, 1, x]
        if k != 3:
            lap[k] = lap_yz[k, x] + (xs[0] + xs[1])
    size = size_of(strain_of(grad))
    return center, grad, lap, size, 1.0 / center[3]


def affine_update(terms, psi, rates, laps):
    center, grad, lap, size, inv_rho = terms
    work_mom = psi[0] * lap[0] + psi[1] * lap[1] + psi[2] * lap[2]
    work_heat = psi[4] * lap[4]
    turbulent = work_mom + work_heat * (1.0 / PRANDTL_TURB)
    inv_rho_2 = inv_rho * inv_rho
    size_rho = size * inv_rho
    first, second = [], []
    for k in range(5):
        rate = rates[k]
        if k == 3:
            rate = rate - (NU_MOL * work_mom + (NU_MOL / PRANDTL) * work_heat) * inv_rho_2
            eddy = -(size * turbulent) * inv_rho_2
        else:
            lap_psi = laps[k]
            if k < 3:
                for other in range(5):
                    rate = rate + psi[other] * grad[k][other]
                rate = rate + NU_MOL * (inv_rho * lap_psi)
                eddy = size_rho * lap_psi
            else:
                rate = rate + (NU_MOL / PRANDTL) * (inv_rho * lap_psi)
                eddy = (1.0 / PRANDTL_TURB) * (size_rho * lap_psi)
        first.append(psi[k] + TIME_STEP * rate)
        second.append(TIME_STEP * eddy)
    return first, second, size_rho * turbulent


def band_of(lane):
    return (lane * 43) >> 9


def is_even():
    return lax.rem(lax.axis_index("gx"), 2) == 0


def fill_scalars(out, side, rho, temp, psi):
    for t in range(2):
        for i in range(2):
            out[2 * t + i] = rho[t, 2 * side + i]
            out[4 + 2 * t + i] = temp[t, 2 * side + i]
    for k in range(5):
        for i in range(2):
            out[PSI + k * 2 + i] = psi[k, 2 * side + i].astype(BF16)


def merge_bands(ops, low, message, first):
    lower = ops.lane - BAND * band_of(ops.lane) < 6
    for number in range(BAND_BLOCKS):
        both = jnp.where(lower, low[2 * number], turn(low[2 * number + 1], 6))
        message[first + number] = both.astype(BF16)


def message_kernel(flow_far, rho_far, temp_far, psi_far, far, ahead, sem):
    side = 1 - is_even().astype(jnp.int32)
    copy = pltpu.make_async_copy(
        flow_far.at[:, :, pl.ds(side, 3)], far.reshape((2, 3, 3, ROWS, LANES)), sem
    )
    copy.start()
    ahead[...] = jnp.zeros((ROWS, LANES), F32)
    copy.wait()


def pack_kernel(
    flow_far, rho_far, temp_far, psi_far, _,
    near, near_scalars, far_scalars, message, low, flow, rho, temp, psi, sems,
):
    copies = [
        pltpu.make_async_copy(source, target, sems.at[i])
        for i, (source, target) in enumerate(
            ((flow_far, flow), (psi_far, psi), (rho_far, rho), (temp_far, temp))
        )
    ]
    for copy in copies:
        copy.start()
    ops = Ops()
    for copy in copies:
        copy.wait()
    side = is_even().astype(jnp.int32)
    for t in range(2):
        for k in range(3):
            for i in range(3):
                near[VELOCITY + t * 9 + k * 3 + i] = flow[t, k, side + i]
    fill_scalars(near_scalars, side, rho, temp, psi)
    fill_scalars(far_scalars, 1 - side, rho, temp, psi)
    items = []
    for t in range(2):
        for source in (rho, temp):
            items.append([source[t, x].astype(F32) for x in range(CX)])
    items += [[psi[k, x] for x in range(CX)] for k in range(5)]
    for number in range(STRIP_BLOCKS):
        message[number] = pack_strips(ops, items[8 * number : 8 * number + 8]).astype(BF16)
    band = band_of(ops.lane)
    for t in range(2):
        for k in range(3):
            block = jnp.zeros((ROWS, LANES), F32)
            for x in range(CX):
                moved = turn(flow[t, k, x].astype(F32), BAND * (x + 3) + 3)
                block = jnp.where(band == x + 3, moved, block)
            low[3 * t + k] = block
    merge_bands(ops, low, message, STRIP_BLOCKS)


def own_kernel(
    flow, rho, temp, psi, own_halo, grad_0, grad_1, lap_0, lap_1, psi_rate, psi_lap, halos, psi_halos
):
    ops = Ops()
    for t in range(2):
        place_halos(ops, t, own_halo, halos.at[t])
    strips = [own_halo[number].astype(F32) for number in range(STRIP_BLOCKS)]
    for k in range(5):
        for x in range(CX):
            psi_halos[k, x] = ops.strip(strips, SLOT_PSI + k, x)
    for t, grad_yz, lap_yz in ((0, grad_0, lap_0), (1, grad_1, lap_1)):
        for k in range(5):
            for x in range(CX):
                values = flow[t, k, x] if k < 3 else (rho if k == 3 else temp)[t, x]
                grad_yz[k, 0, x], grad_yz[k, 1, x], lap_yz[k, x] = across_terms(
                    ops, values.astype(F32), halos[t, k, x]
                )
    for x in range(CX):
        along_y, along_z = flow[0, 1, x].astype(F32), flow[0, 2, x].astype(F32)
        for k in range(5):
            by_y, by_z, lap = across_terms(ops, psi[k, x], psi_halos[k, x])
            psi_rate[k, x] = along_y * by_y + along_z * by_z
            psi_lap[k, x] = lap


def token_kernel(far, out):
    out[...] = far[0].astype(F32)


def bands_kernel(own_low, near, far, _, message, low):
    ops = Ops()
    even = is_even()
    band = band_of(ops.lane)
    for t in range(2):
        for k in range(3):
            block = own_low[3 * t + k]
            for i in range(3):
                number = VELOCITY + t * 9 + k * 3 + i
                one, two = near[number].astype(F32), far[number].astype(F32)
                moved = turn(jnp.where(even, two, one), BAND * i + 3)
                block = jnp.where(band == i, moved, block)
                moved = turn(jnp.where(even, one, two), BAND * (7 + i) + 3)
                block = jnp.where(band == 7 + i, moved, block)
            low[3 * t + k] = block
    merge_bands(ops, low, message, 0)


def products_of(hat):
    velocity = [hat(k) for k in range(3)]
    strain = [hat(9 + number) for number in range(6)]
    diagonal = strain[0] * strain[0] + strain[1] * strain[1] + strain[2] * strain[2]
    other = strain[3] * strain[3] + strain[4] * strain[4] + strain[5] * strain[5]
    size = 4.0 * jnp.sqrt((2.0 / 256.0) * diagonal + ((4.0 / 256.0) * other + EPSILON))
    cross = 0.0
    square = 0.0
    for number, (a, b) in enumerate(PAIRS):
        leonard = hat(3 + number) - (1.0 / 16.0) * velocity[a] * velocity[b]
        model = hat(15 + number) - size * strain[number]
        weighted = WEIGHTS[number] * model if WEIGHTS[number] != 1.0 else model
        cross = cross + leonard * weighted
        square = square + model * weighted
    return cross, square


def widen(k, source, near, far, count, even, wide):
    for i in range(count):
        one, two = near(i), far(i)
        wide[k, 3 - count + i] = jnp.where(even, two, one)
        wide[k, 3 + CX + i] = jnp.where(even, one, two)
    for x in range(CX):
        wide[k, 3 + x] = source(x).astype(F32)


def widen_scalars(t, rho, temp, near, far, even, wide):
    for k, source in ((3, rho), (4, temp)):
        number = (k - 3) * 4 + 2 * t
        widen(
            k,
            lambda x: source[t, x],
            lambda i: near[number + i].astype(F32),
            lambda i: far[number + i].astype(F32),
            2, even, wide,
        )


def inner_products(ops, t, flow, near, far, grad_yz, sums, high, wide, fields, hats):
    even = is_even()
    valid = (ops.lane >= 3) & (ops.lane < LANES - 3)
    band = band_of(jnp.maximum(ops.lane - 2, 0))
    for k in range(3):
        widen(
            k,
            lambda x: flow[t, k, x],
            lambda i: near[VELOCITY + t * 9 + k * 3 + i].astype(F32),
            lambda i: far[VELOCITY + t * 9 + k * 3 + i].astype(F32),
            3, even, wide,
        )
    for x in range(-1, CX + 1):
        grad = [[None] * 3 for _ in range(3)]
        for k in range(3):
            center = wide[k, x + 3]
            grad[0][k] = fourth(*(wide[k, x + 3 + step] for step in (1, -1, 2, -2)))
            if 0 <= x < CX:
                grad[1][k], grad[2][k] = grad_yz[k, 0, x], grad_yz[k, 1, x]
            else:
                grad[1][k] = 0.5 * (ops.y_up(center) - ops.y_down(center))
                grad[2][k] = fourth(*(turn(center, -step) for step in (1, -1, 2, -2)))
        strain = strain_of(grad)
        size = size_of(strain)
        velocity = [wide[k, x + 3] for k in range(3)]
        for number, values in enumerate(filter_fields(velocity, strain, size)):
            fields[number, x + 1] = values
    for x in range(CX):
        for number in range(21):
            along_x = fields[number, x] + fields[number, x + 2] + 2.0 * fields[number, x + 1]
            hats[number, x] = turn(along_x, 1) + turn(along_x, -1) + 2.0 * along_x
    for k in range(3):
        block = jnp.zeros((ROWS, LANES), F32)
        for q in range(CX + 6):
            block = jnp.where(band == q, turn(wide[k, q], BAND * q + 11), block)
        high[k] = block
    for x in range(CX):
        cross, square = products_of(lambda number: hats[number, x])
        sums[0, x] = jnp.where(valid, cross, 0.0)
        sums[1, x] = jnp.where(valid, square, 0.0)


def edge_products(ops, t, low, high, halo, sums, bands, spread):
    band = band_of(ops.lane)
    place = ops.lane - BAND * band
    from_low = place < 3
    from_high = (place == 11) | (place < 2)
    low_side = place < 7
    at_edge = ((place >= 3) & (place <= 5)) | ((place >= 8) & (place <= 10))
    for k in range(3):
        number = 3 * t + k
        far = halo[number // 2].astype(F32)
        shift = 6 * (number % 2)
        bands[0, k] = jnp.where(from_low, turn(far, -shift), low[number])
        bands[1, k] = jnp.where(from_high, turn(far, 8 - shift), high[k])
    for side in range(2):
        velocity = [bands[side, k] for k in range(3)]
        grad = [[None] * 3 for _ in range(3)]
        for k in range(3):
            center = velocity[k]
            grad[0][k] = fourth(*(turn(center, -BAND * step) for step in (1, -1, 2, -2)))
            grad[1][k] = 0.5 * (ops.y_up(center) - ops.y_down(center))
            grad[2][k] = fourth(*(turn(center, -step) for step in (1, -1, 2, -2)))
        strain = strain_of(grad)
        for number, values in enumerate(filter_fields(velocity, strain, size_of(strain))):
            if side == 0:
                spread[number] = values
            else:
                spread[number] = jnp.where(low_side, spread[number], values)
    for number in range(21):
        both = spread[number]
        spread[number] = turn(both, BAND) + turn(both, -BAND) + 2.0 * both
    for number in range(21):
        both = spread[number]
        spread[number] = turn(both, 1) + turn(both, -1) + 2.0 * both
    for part, values in enumerate(products_of(lambda number: spread[number])):
        values = jnp.where(at_edge, values, 0.0)
        for x in range(CX):
            sums[part, x] = sums[part, x] + jnp.where(band == x + 3, values, 0.0)


def add_columns(ops, total, first_lane, planes, scale=1.0):
    for x in range(CX):
        value = scale * jnp.sum(planes(x), axis=1, keepdims=True)
        total = jnp.where(ops.lane == first_lane + x, value, total)
    return total


def add_parts(ops, block, total):
    upper = total.astype(BF16).astype(F32)
    rest = total - upper
    middle = rest.astype(BF16).astype(F32)
    for number, part in enumerate((upper, middle, rest - middle)):
        block = jnp.where(ops.lane >> 5 == 1 + number, turn(part, 32 * (1 + number)), block)
    return block


def span_total(add_other, columns, other):
    total = columns[...]
    if add_other:
        parts = other.astype(F32)
        total = total + ((turn(parts, -32) + turn(parts, -64)) + turn(parts, -96))
    return total


def psi_terms(psi_wide, rate_yz, lap_yz, velocity, x):
    rates, laps = [], []
    for k in range(5):
        xs = [psi_wide[k, x + 3 + step] for step in (1, -1, 2, -2)]
        rates.append(rate_yz[k, x] + velocity * fourth(*xs))
        laps.append(lap_yz[k, x] + (xs[0] + xs[1]))
    return rates, laps


def inner_kernel(flow, near, far, grad_yz, sums, high, wide, fields, hats):
    inner_products(Ops(), 0, flow, near, far, grad_yz, sums, high, wide, fields, hats)


def first_kernel(
    rho, temp, psi, near, far, velocity, grad_yz, lap_yz, psi_rate, psi_lap,
    first, second, message, columns,
    wide, psi_wide, work,
):
    ops = Ops()
    even = is_even()
    for k in range(3):
        for i in range(1, CX + 5):
            wide[k, i] = velocity[k, i]
    widen_scalars(0, rho, temp, near, far, even, wide)
    for k in range(5):
        widen(
            k,
            lambda x: psi[k, x],
            lambda i: near[PSI + k * 2 + i].astype(F32),
            lambda i: far[PSI + k * 2 + i].astype(F32),
            2, even, psi_wide,
        )
    for x in range(CX):
        terms = state_terms(wide, grad_yz, lap_yz, x)
        rates, laps = psi_terms(psi_wide, psi_rate, psi_lap, terms[0][0], x)
        new, slope, sensitivity = affine_update(
            terms, [psi[k, x] for k in range(5)], rates, laps
        )
        for k in range(5):
            first[k, x] = new[k]
            second[k, x] = slope[k]
        work[x] = sensitivity
    columns[...] = add_columns(ops, jnp.zeros((ROWS, LANES), F32), 16, lambda x: work[x])
    items = [[part[k, x] for x in range(CX)] for part in (first, second) for k in range(5)]
    for number in range(2):
        message[number] = pack_strips(ops, items[8 * number : 8 * number + 8])


def edge_kernel(
    low, high, halo, inner, strips, sensitivity, message, columns, bands, spread, sums
):
    ops = Ops()
    for part in range(2):
        for x in range(CX):
            sums[part, x] = inner[part, x]
    edge_products(ops, 0, low, high, halo, sums, bands, spread)
    total = sensitivity[...]
    for part in range(2):
        total = add_columns(ops, total, 4 * part, lambda x: sums[part, x], 1.0 / 256.0)
    columns[...] = total
    message[0] = strips[0].astype(BF16)
    message[1] = add_parts(ops, strips[1], total).astype(BF16)


def later_kernel(
    flow, rho, temp, near, far, near_scalars, far_scalars,
    grad_yz, lap_yz, low, halo, first, second,
    wide, message, columns,
    high, fields, hats, work, bands, spread, sums,
):
    ops = Ops()
    inner_products(ops, 1, flow, near, far, grad_yz, sums, high, wide, fields, hats)
    widen_scalars(1, rho, temp, near_scalars, far_scalars, is_even(), wide)
    edge_products(ops, 1, low, high, halo, sums, bands, spread)
    for x in range(CX):
        _, _, lap, size, inv_rho = state_terms(wide, grad_yz, lap_yz, x)
        size_rho = size * inv_rho
        for part, source in enumerate((first, second)):
            total = lap[0] * source[0, x] + lap[1] * source[1, x] + lap[2] * source[2, x]
            work[part, x] = size_rho * (
                total + (1.0 / PRANDTL_TURB) * (lap[4] * source[4, x])
            )
    total = jnp.zeros((ROWS, LANES), F32)
    for part in range(2):
        total = add_columns(ops, total, 8 + 4 * part, lambda x: sums[part, x], 1.0 / 256.0)
        total = add_columns(ops, total, 20 + 4 * part, lambda x: work[part, x])
    columns[...] = total
    message[0] = add_parts(ops, jnp.zeros((ROWS, LANES), F32), total).astype(BF16)


def coefficients(ops, total):
    return total / (turn(total, -4) + EPSILON)


def middle_kernel(add_other, first, second, columns, other, psi, far, coef_first):
    ops = Ops()
    coef = coefficients(ops, span_total(add_other, columns, other[1]))
    for x in range(CX):
        coef_first[x] = jnp.broadcast_to(coef[:, x : x + 1], (ROWS, LANES))
    for x in range(CX):
        for k in range(5):
            psi[k, x] = first[k, x] + coef_first[x] * second[k, x]
    side = 1 - is_even().astype(jnp.int32)
    for k in range(5):
        for i in range(2):
            far[k, i] = psi[k, 2 * side + i].astype(BF16)


def base_kernel(
    add_other, span_cells,
    wide, grad_yz, lap_yz, psi, coef_first, columns, other, later, later_other,
    base, drift, spread, coef_grad, near,
    psi_halos, psi_wide, coef_planes, psi_rate, psi_lap,
):
    ops = Ops()
    side = is_even().astype(jnp.int32)
    for k in range(5):
        for i in range(2):
            near[k, i] = psi[k, 2 * side + i].astype(BF16)
    strips = [other[number].astype(F32) for number in range(2)]
    for k in range(5):
        for x in range(CX):
            psi_halos[k, x] = ops.strip(strips, k, x)
    total = span_total(add_other, columns, other[1]) + span_total(
        add_other, later, later_other[0]
    )
    coef = coefficients(ops, total)
    after = total + turn(coef, 20) * turn(total, -4)
    grads = jnp.where(ops.lane < 20, total, after) * (1.0 / span_cells)
    turned = jnp.concatenate([grads] * (LANES // ROWS), axis=0).T
    for t in range(2):
        coef_grad[t] = turned[16 + 4 * t : 20 + 4 * t, :ROWS]
    for x in range(CX):
        coef_planes[x] = jnp.broadcast_to(coef[:, 8 + x : 9 + x], (ROWS, LANES))
    for k in range(5):
        for x in range(CX):
            psi_halos[k, x] = psi_halos[k, x] + coef_first[x] * ops.strip(strips, 5 + k, x)
    zero = jnp.zeros((ROWS, LANES), F32)
    for k in range(5):
        for i in range(2):
            psi_wide[k, 1 + i] = zero
            psi_wide[k, 3 + CX + i] = zero
        for x in range(CX):
            psi_wide[k, 3 + x] = psi[k, x]
    for x in range(CX):
        for k in range(5):
            by_y, by_z, lap = across_terms(ops, psi[k, x], psi_halos[k, x])
            psi_rate[k, x] = wide[1, x + 3] * by_y + wide[2, x + 3] * by_z
            psi_lap[k, x] = lap
    for x in range(CX):
        terms = state_terms(wide, grad_yz, lap_yz, x)
        center = terms[0]
        rates, laps = psi_terms(psi_wide, psi_rate, psi_lap, center[0], x)
        new, slope, _ = affine_update(terms, [psi[k, x] for k in range(5)], rates, laps)
        for k in range(5):
            base[k, x] = new[k] + coef_planes[x] * slope[k]
        size, inv_rho = terms[3:]
        drift[x] = TIME_STEP * center[0]
        if x in (0, CX - 1):
            eddy = coef_planes[x] * size
            scaled = TIME_STEP * inv_rho
            spread[x // (CX - 1), 0] = scaled * (NU_MOL + eddy)
            spread[x // (CX - 1), 1] = scaled * (
                NU_MOL / PRANDTL + (1.0 / PRANDTL_TURB) * eddy
            )


def widen_kernel(far, out):
    for k in range(5):
        for i in range(2):
            out[k, i] = far[k, i].astype(F32)


def last_kernel(base, drift, spread, near_psi, far_psi, out):
    even = is_even()
    for k in range(5):
        ones = [near_psi[k, i].astype(F32) for i in range(2)]
        twos = [far_psi[k, i].astype(F32) for i in range(2)]
        far, near = (jnp.where(even, two, one) for one, two in zip(ones, twos))
        after, beyond = (jnp.where(even, one, two) for one, two in zip(ones, twos))
        low = drift[0] * ((1.0 / 12.0) * far - (2.0 / 3.0) * near)
        high = drift[CX - 1] * ((2.0 / 3.0) * after - (1.0 / 12.0) * beyond)
        if k != 3:
            kind = 1 if k == 4 else 0
            low = low + spread[0, kind] * near
            high = high + spread[1, kind] * after
        out[k, 0] = base[k, 0] + low
        out[k, 1] = base[k, 1] + drift[1] * ((1.0 / 12.0) * near)
        out[k, CX - 2] = base[k, CX - 2] - drift[CX - 2] * ((1.0 / 12.0) * after)
        out[k, CX - 1] = base[k, CX - 1] + high


def ring(axis):
    count = lax.axis_size(axis)
    forward = [(i, (i + 1) % count) for i in range(count)]
    return forward, [(target, source) for source, target in forward]


def pairs():
    count = lax.axis_size("gx")
    if count % 2:
        raise ValueError("odd gx")
    inside = [(i, i ^ 1) for i in range(count)]
    across = [(i, (i + 1 if i % 2 else i - 1) % count) for i in range(count)]
    return inside, across


def span_edges(message, strips):
    forward, backward = ring("gz")
    before = lax.ppermute(message, "gz", forward)
    if lax.axis_size("gz") == 2:
        return before
    after = lax.ppermute(message, "gz", backward)
    lane = lax.broadcasted_iota(jnp.int32, message.shape, 2)
    number = lax.broadcasted_iota(jnp.int32, message.shape, 0)
    low = jnp.where(number < strips, lane % STRIP < 2, lane % 6 < 3)
    return jnp.where(low, before, after)


def shape_of(dims, kind=F32):
    return jax.ShapeDtypeStruct(dims + (ROWS, LANES), kind)


def whole(count):
    return [pl.BlockSpec(memory_space=pltpu.VMEM)] * count


def scratch(*dims):
    return [pltpu.VMEM(d + (ROWS, LANES), F32) for d in dims]


def call(kernel, name, inputs, outputs, operations, buffers=(), in_specs=None):
    inputs = list(inputs)
    if in_specs:
        inputs[:4] = [
            pltpu.with_memory_space_constraint(a, pltpu.MemorySpace.HBM) for a in inputs[:4]
        ]
    size = sum(math.prod(a.shape) * a.dtype.itemsize for a in list(inputs) + list(outputs))
    return pl.pallas_call(
        kernel,
        in_specs=in_specs or whole(len(inputs)),
        out_specs=whole(len(outputs)),
        out_shape=list(outputs),
        scratch_shapes=list(buffers),
        compiler_params=pltpu.CompilerParams(vmem_limit_bytes=8 * 2**20),
        cost_estimate=pl.CostEstimate(
            flops=operations, bytes_accessed=size, transcendentals=0
        ),
        name=name,
    )(*inputs)


def span_sums(columns):
    if lax.axis_size("gz") == 2:
        return columns
    return lax.psum(columns, "gz")


def local(flow_far, rho_far, temp_far, psi_far):
    inside, across = pairs()
    add_other = lax.axis_size("gz") == 2
    field, planes, edges = shape_of((5, CX)), shape_of((5, CX + 6)), shape_of((5, 2), BF16)
    slopes = shape_of((5, 2, CX))
    inputs = (flow_far, rho_far, temp_far, psi_far)
    stay = [pl.BlockSpec(memory_space=pltpu.MemorySpace.HBM)] * 4
    far, ahead = call(
        message_kernel,
        "message",
        inputs,
        [shape_of((SCALARS,), BF16), shape_of(())],
        1_000_000,
        [pltpu.SemaphoreType.DMA(())],
        stay,
    )
    far = lax.ppermute(far, "gx", across)
    near, near_scalars, far_scalars, message, own_low, flow, rho, temp, psi = call(
        pack_kernel,
        "pack",
        inputs + (ahead,),
        [
            shape_of((SCALARS,), BF16),
            shape_of((SCALAR_PLANES,), BF16),
            shape_of((SCALAR_PLANES,), BF16),
            shape_of((STRIP_BLOCKS + BAND_BLOCKS,), BF16),
            shape_of((6,)),
            shape_of((2, 3, CX), BF16),
            shape_of((2, CX), BF16),
            shape_of((2, CX), BF16),
            field,
        ],
        2_000_000,
        [pltpu.SemaphoreType.DMA((4,))],
        stay + whole(1),
    )
    far_scalars = lax.ppermute(far_scalars, "gx", across)
    near = lax.ppermute(near, "gx", inside)
    near_scalars = lax.ppermute(near_scalars, "gx", inside)
    own_halo = span_edges(message, STRIP_BLOCKS)
    grad_0, grad_1, lap_0, lap_1, psi_rate, psi_lap = call(
        own_kernel,
        "own",
        (flow, rho, temp, psi, own_halo),
        [slopes, slopes, field, field, field, field],
        5_000_000,
        scratch((2, 5, CX), (5, CX)),
    )
    (token,) = call(token_kernel, "token", (far,), [shape_of(())], 100_000)
    message, low = call(
        bands_kernel,
        "bands",
        (own_low, near, far, token),
        [shape_of((BAND_BLOCKS,), BF16), shape_of((6,))],
        1_000_000,
    )
    halo = span_edges(message, 0)
    inner, high, velocity = call(
        inner_kernel,
        "inner",
        (flow, near, far, grad_0),
        [shape_of((2, CX)), shape_of((3,)), shape_of((3, CX + 6))],
        20_000_000,
        scratch((21, CX + 2), (21, CX)),
    )
    first, second, strips, sensitivity = call(
        first_kernel,
        "first",
        (rho, temp, psi, near_scalars, far_scalars, velocity, grad_0, lap_0, psi_rate, psi_lap),
        [field, field, shape_of((2,)), shape_of(())],
        10_000_000,
        scratch((5, CX + 6), (5, CX + 6), (CX,)),
    )
    message, columns = call(
        edge_kernel,
        "edge",
        (low, high, halo, inner, strips, sensitivity),
        [shape_of((2,), BF16), shape_of(())],
        20_000_000,
        scratch((2, 3), (21,), (2, CX)),
    )
    other = span_edges(message, 2)
    columns = span_sums(columns)
    wide, message, later = call(
        later_kernel,
        "later",
        (
            flow, rho, temp, near, far, near_scalars, far_scalars,
            grad_1, lap_1, low, halo, first, second,
        ),
        [planes, shape_of((1,), BF16), shape_of(())],
        20_000_000,
        scratch((3,), (21, CX + 2), (21, CX), (2, CX), (2, 3), (21,), (2, CX)),
    )
    later_other = span_edges(message, 1)
    later = span_sums(later)
    first, later = lax.optimization_barrier((first, later))
    psi, far, coef_first = call(
        functools.partial(middle_kernel, add_other),
        "middle",
        (first, second, columns, other),
        [field, edges, shape_of((CX,))],
        1_000_000,
    )
    far = lax.ppermute(far, "gx", across)
    base, drift, spread, coef_grad, near = call(
        functools.partial(base_kernel, add_other, LANES * lax.axis_size("gz")),
        "base",
        (wide, grad_1, lap_1, psi, coef_first, columns, other, later, later_other),
        [
            field, shape_of((CX,)), shape_of((2, 2)),
            jax.ShapeDtypeStruct((2, CX, ROWS), F32), edges,
        ],
        15_000_000,
        scratch((5, CX), (5, CX + 6), (CX,), (5, CX), (5, CX)),
    )
    near = lax.ppermute(near, "gx", inside)
    (far,) = call(widen_kernel, "widen", (far,), [shape_of((5, 2))], 100_000)
    (out,) = call(last_kernel, "last", (base, drift, spread, near, far), [field], 1_000_000)
    return out, coef_grad


def solution(mesh):
    return jax.shard_map(
        local,
        mesh=mesh,
        in_specs=(
            P(None, None, "gx", None, "gz"),
            P(None, "gx", None, "gz"),
            P(None, "gx", None, "gz"),
            P(None, "gx", None, "gz"),
        ),
        out_specs=(P(None, "gx", None, "gz"), P(None, "gx", None)),
        check_vma=False,
    )
```

```python
import functools
import math

import jax
import jax.numpy as jnp
from jax import lax
from jax.experimental import pallas as pl
from jax.experimental.pallas import tpu as pltpu
from jax.sharding import PartitionSpec as P

EPSILON = 1e-06
NU_MOL = 0.05
PRANDTL = 0.72
PRANDTL_TURB = 0.9
TIME_STEP = 0.04
PAIRS = ((0, 0), (1, 1), (2, 2), (0, 1), (0, 2), (1, 2))
WEIGHTS = (1.0, 1.0, 1.0, 2.0, 2.0, 2.0)

CX = 4
ROWS = 32
LANES = 128
STRIP = 4
F32 = jnp.float32
BF16 = jnp.bfloat16
SLOT_PSI = 4
BAND = 12
STRIP_BLOCKS = 2
BAND_BLOCKS = 3
VELOCITY = 0
SCALARS = 18
PSI = 8
SCALAR_PLANES = 18


def lane_ids():
    return lax.broadcasted_iota(jnp.int32, (ROWS, LANES), 1)


def row_ids():
    return lax.broadcasted_iota(jnp.int32, (ROWS, LANES), 0)


def turn(values, shift):
    shift = shift % LANES
    return values if shift == 0 else pltpu.roll(values, shift, 1)


class Ops:
    def __init__(self):
        self.lane = lane_ids()
        row = row_ids()
        self.top = row == ROWS - 1
        self.bottom = row == 0

    def z_at(self, values, halo, step):
        if step > 0:
            return turn(jnp.where(self.lane < step, halo, values), -step)
        return turn(jnp.where(self.lane >= LANES + step, halo, values), -step)

    def y_up(self, values):
        return jnp.where(self.top, 0.0, pltpu.roll(values, ROWS - 1, 0))

    def y_down(self, values):
        return jnp.where(self.bottom, 0.0, pltpu.roll(values, 1, 0))

    def strip(self, blocks, slot, x):
        return turn(blocks[slot // 8], -(STRIP * (4 * (slot % 8) + x) + 2))


def fourth(plus, minus, plus_2, minus_2):
    return (2.0 / 3.0) * (plus - minus) - (1.0 / 12.0) * (plus_2 - minus_2)


def strain_of(grad):
    return [
        grad[0][0],
        grad[1][1],
        grad[2][2],
        0.5 * (grad[0][1] + grad[1][0]),
        0.5 * (grad[0][2] + grad[2][0]),
        0.5 * (grad[1][2] + grad[2][1]),
    ]


def size_of(strain):
    diagonal = strain[0] * strain[0] + strain[1] * strain[1] + strain[2] * strain[2]
    other = strain[3] * strain[3] + strain[4] * strain[4] + strain[5] * strain[5]
    return jnp.sqrt(2.0 * diagonal + (4.0 * other + EPSILON))


def filter_fields(velocity, strain, size):
    products = [velocity[a] * velocity[b] for a, b in PAIRS]
    return list(velocity) + products + strain + [size * part for part in strain]


def pack_strips(ops, items):
    block = jnp.zeros((ROWS, LANES), F32)
    strip_id = ops.lane >> 2
    for slot, planes in enumerate(items):
        for x in range(CX):
            number = 4 * slot + x
            block = jnp.where(strip_id == number, turn(planes[x], STRIP * number + 2), block)
    return block


def place_halos(ops, t, own_halo, halos):
    strips = [own_halo[number].astype(F32) for number in range(STRIP_BLOCKS)]
    for k in range(3):
        number = 3 * t + k
        bands = own_halo[STRIP_BLOCKS + number // 2].astype(F32)
        for x in range(CX):
            halos[k, x] = turn(bands, -(BAND * (x + 3) + 3 + 6 * (number % 2)))
    for k in range(3, 5):
        for x in range(CX):
            halos[k, x] = ops.strip(strips, 2 * t + k - 3, x)


def y_terms(ops, values):
    up, down = ops.y_up(values), ops.y_down(values)
    return 0.5 * (up - down), (up + down) - 6.0 * values


def z_terms(ops, values, halo):
    zs = [ops.z_at(values, halo, step) for step in (1, -1, 2, -2)]
    return fourth(*zs), zs[0] + zs[1]


def state_terms(wide, grad_yz, lap_yz, x):
    grad = [[None] * 5 for _ in range(3)]
    lap = [None] * 5
    center = [wide[k, x + 3] for k in range(5)]
    for k in range(5):
        xs = [wide[k, x + 3 + step] for step in (1, -1, 2, -2)]
        grad[0][k] = fourth(*xs)
        grad[1][k], grad[2][k] = grad_yz[k, 0, x], grad_yz[k, 1, x]
        if k != 3:
            lap[k] = lap_yz[k, x] + (xs[0] + xs[1])
    size = size_of(strain_of(grad))
    return center, grad, lap, size, 1.0 / center[3]


def affine_update(terms, psi, rates, laps):
    center, grad, lap, size, inv_rho = terms
    work_mom = psi[0] * lap[0] + psi[1] * lap[1] + psi[2] * lap[2]
    work_heat = psi[4] * lap[4]
    turbulent = work_mom + work_heat * (1.0 / PRANDTL_TURB)
    inv_rho_2 = inv_rho * inv_rho
    size_rho = size * inv_rho
    first, second = [], []
    for k in range(5):
        rate = rates[k]
        if k == 3:
            rate = rate - (NU_MOL * work_mom + (NU_MOL / PRANDTL) * work_heat) * inv_rho_2
            eddy = -(size * turbulent) * inv_rho_2
        else:
            lap_psi = laps[k]
            if k < 3:
                for other in range(5):
                    rate = rate + psi[other] * grad[k][other]
                rate = rate + NU_MOL * (inv_rho * lap_psi)
                eddy = size_rho * lap_psi
            else:
                rate = rate + (NU_MOL / PRANDTL) * (inv_rho * lap_psi)
                eddy = (1.0 / PRANDTL_TURB) * (size_rho * lap_psi)
        first.append(psi[k] + TIME_STEP * rate)
        second.append(TIME_STEP * eddy)
    return first, second, size_rho * turbulent


def band_of(lane):
    return (lane * 43) >> 9


def is_even():
    return lax.rem(lax.axis_index("gx"), 2) == 0


def fill_scalars(out, side, rho, temp, psi):
    for t in range(2):
        for i in range(2):
            out[2 * t + i] = rho[t, 2 * side + i]
            out[4 + 2 * t + i] = temp[t, 2 * side + i]
    for k in range(5):
        for i in range(2):
            out[PSI + k * 2 + i] = psi[k, 2 * side + i].astype(BF16)


def merge_bands(ops, low, message, first):
    lower = ops.lane - BAND * band_of(ops.lane) < 6
    for number in range(BAND_BLOCKS):
        both = jnp.where(lower, low[2 * number], turn(low[2 * number + 1], 6))
        message[first + number] = both.astype(BF16)


def message_kernel(
    flow_far, rho_far, temp_far, psi_far, far, far_scalars, flow, rho, temp, psi, sems
):
    side = 1 - is_even().astype(jnp.int32)
    pieces = (
        (flow_far.at[:, :, pl.ds(side, 3)], far.reshape((2, 3, 3, ROWS, LANES))),
        (psi_far, psi),
        (rho_far, rho),
        (temp_far, temp),
        (flow_far, flow),
    )
    copies = [
        pltpu.make_async_copy(source, target, sems.at[number])
        for number, (source, target) in enumerate(pieces)
    ]
    for copy in copies:
        copy.start()
    for copy in copies[1:4]:
        copy.wait()
    fill_scalars(far_scalars, side, rho, temp, psi)
    copies[0].wait()
    copies[4].wait()


def pack_kernel(flow, rho, temp, psi, near, near_scalars, message, low):
    ops = Ops()
    side = is_even().astype(jnp.int32)
    for t in range(2):
        for k in range(3):
            for i in range(3):
                near[VELOCITY + t * 9 + k * 3 + i] = flow[t, k, side + i]
    fill_scalars(near_scalars, side, rho, temp, psi)
    items = []
    for t in range(2):
        for source in (rho, temp):
            items.append([source[t, x].astype(F32) for x in range(CX)])
    items += [[psi[k, x] for x in range(CX)] for k in range(5)]
    for number in range(STRIP_BLOCKS):
        message[number] = pack_strips(ops, items[8 * number : 8 * number + 8]).astype(BF16)
    band = band_of(ops.lane)
    for t in range(2):
        for k in range(3):
            block = jnp.zeros((ROWS, LANES), F32)
            for x in range(CX):
                moved = turn(flow[t, k, x].astype(F32), BAND * (x + 3) + 3)
                block = jnp.where(band == x + 3, moved, block)
            low[3 * t + k] = block
    merge_bands(ops, low, message, STRIP_BLOCKS)


def rows_kernel(flow, rho, temp, psi, grad_0, grad_1, lap_0, lap_1, psi_rate, psi_lap):
    ops = Ops()
    for t, grad_y, lap_y in ((0, grad_0, lap_0), (1, grad_1, lap_1)):
        for k in range(5):
            for x in range(CX):
                values = flow[t, k, x] if k < 3 else (rho if k == 3 else temp)[t, x]
                grad_y[k, x], lap_y[k, x] = y_terms(ops, values.astype(F32))
    for x in range(CX):
        along_y = flow[0, 1, x].astype(F32)
        for k in range(5):
            by_y, psi_lap[k, x] = y_terms(ops, psi[k, x])
            psi_rate[k, x] = along_y * by_y


def own_kernel(
    flow, rho, temp, psi, own_halo, grad_y_0, grad_y_1, lap_y_0, lap_y_1, rate_y, psi_lap_y,
    grad_0, grad_1, lap_0, lap_1, psi_rate, psi_lap,
    halos, psi_halos,
):
    ops = Ops()
    for t in range(2):
        place_halos(ops, t, own_halo, halos.at[t])
    strips = [own_halo[number].astype(F32) for number in range(STRIP_BLOCKS)]
    for k in range(5):
        for x in range(CX):
            psi_halos[k, x] = ops.strip(strips, SLOT_PSI + k, x)
    for t, grad_y, lap_y, grad_yz, lap_yz in (
        (0, grad_y_0, lap_y_0, grad_0, lap_0),
        (1, grad_y_1, lap_y_1, grad_1, lap_1),
    ):
        for k in range(5):
            for x in range(CX):
                values = flow[t, k, x] if k < 3 else (rho if k == 3 else temp)[t, x]
                by_z, both = z_terms(ops, values.astype(F32), halos[t, k, x])
                grad_yz[k, 0, x], grad_yz[k, 1, x] = grad_y[k, x], by_z
                lap_yz[k, x] = lap_y[k, x] + both
    for x in range(CX):
        along_z = flow[0, 2, x].astype(F32)
        for k in range(5):
            by_z, both = z_terms(ops, psi[k, x], psi_halos[k, x])
            psi_rate[k, x] = rate_y[k, x] + along_z * by_z
            psi_lap[k, x] = psi_lap_y[k, x] + both


def token_kernel(far, out):
    out[...] = far[0].astype(F32)


def bands_kernel(own_low, near, far, _, message, low):
    ops = Ops()
    even = is_even()
    band = band_of(ops.lane)
    for t in range(2):
        for k in range(3):
            block = own_low[3 * t + k]
            for i in range(3):
                number = VELOCITY + t * 9 + k * 3 + i
                one, two = near[number].astype(F32), far[number].astype(F32)
                moved = turn(jnp.where(even, two, one), BAND * i + 3)
                block = jnp.where(band == i, moved, block)
                moved = turn(jnp.where(even, one, two), BAND * (7 + i) + 3)
                block = jnp.where(band == 7 + i, moved, block)
            low[3 * t + k] = block
    merge_bands(ops, low, message, 0)


def products_of(hat):
    velocity = [hat(k) for k in range(3)]
    strain = [hat(9 + number) for number in range(6)]
    diagonal = strain[0] * strain[0] + strain[1] * strain[1] + strain[2] * strain[2]
    other = strain[3] * strain[3] + strain[4] * strain[4] + strain[5] * strain[5]
    size = 4.0 * jnp.sqrt((2.0 / 256.0) * diagonal + ((4.0 / 256.0) * other + EPSILON))
    cross = 0.0
    square = 0.0
    for number, (a, b) in enumerate(PAIRS):
        leonard = hat(3 + number) - (1.0 / 16.0) * velocity[a] * velocity[b]
        model = hat(15 + number) - size * strain[number]
        weighted = WEIGHTS[number] * model if WEIGHTS[number] != 1.0 else model
        cross = cross + leonard * weighted
        square = square + model * weighted
    return cross, square


def widen(k, source, near, far, count, even, wide):
    for i in range(count):
        one, two = near(i), far(i)
        wide[k, 3 - count + i] = jnp.where(even, two, one)
        wide[k, 3 + CX + i] = jnp.where(even, one, two)
    for x in range(CX):
        wide[k, 3 + x] = source(x).astype(F32)


def widen_scalars(t, rho, temp, near, far, even, wide):
    for k, source in ((3, rho), (4, temp)):
        number = (k - 3) * 4 + 2 * t
        widen(
            k,
            lambda x: source[t, x],
            lambda i: near[number + i].astype(F32),
            lambda i: far[number + i].astype(F32),
            2, even, wide,
        )


def inner_products(ops, t, flow, near, far, grad_yz, sums, high, wide, fields, hats):
    even = is_even()
    valid = (ops.lane >= 3) & (ops.lane < LANES - 3)
    band = band_of(jnp.maximum(ops.lane - 2, 0))
    for k in range(3):
        widen(
            k,
            lambda x: flow[t, k, x],
            lambda i: near[VELOCITY + t * 9 + k * 3 + i].astype(F32),
            lambda i: far[VELOCITY + t * 9 + k * 3 + i].astype(F32),
            3, even, wide,
        )
    for x in range(-1, CX + 1):
        grad = [[None] * 3 for _ in range(3)]
        for k in range(3):
            center = wide[k, x + 3]
            grad[0][k] = fourth(*(wide[k, x + 3 + step] for step in (1, -1, 2, -2)))
            if 0 <= x < CX:
                grad[1][k], grad[2][k] = grad_yz[k, 0, x], grad_yz[k, 1, x]
            else:
                grad[1][k] = 0.5 * (ops.y_up(center) - ops.y_down(center))
                grad[2][k] = fourth(*(turn(center, -step) for step in (1, -1, 2, -2)))
        strain = strain_of(grad)
        size = size_of(strain)
        velocity = [wide[k, x + 3] for k in range(3)]
        for number, values in enumerate(filter_fields(velocity, strain, size)):
            fields[number, x + 1] = values
    for x in range(CX):
        for number in range(21):
            along_x = fields[number, x] + fields[number, x + 2] + 2.0 * fields[number, x + 1]
            hats[number, x] = turn(along_x, 1) + turn(along_x, -1) + 2.0 * along_x
    for k in range(3):
        block = jnp.zeros((ROWS, LANES), F32)
        for q in range(CX + 6):
            block = jnp.where(band == q, turn(wide[k, q], BAND * q + 11), block)
        high[k] = block
    for x in range(CX):
        cross, square = products_of(lambda number: hats[number, x])
        sums[0, x] = jnp.where(valid, cross, 0.0)
        sums[1, x] = jnp.where(valid, square, 0.0)


def edge_products(ops, t, low, high, halo, sums, bands, spread):
    band = band_of(ops.lane)
    place = ops.lane - BAND * band
    from_low = place < 3
    from_high = (place == 11) | (place < 2)
    low_side = place < 7
    at_edge = ((place >= 3) & (place <= 5)) | ((place >= 8) & (place <= 10))
    for k in range(3):
        number = 3 * t + k
        far = halo[number // 2].astype(F32)
        shift = 6 * (number % 2)
        bands[0, k] = jnp.where(from_low, turn(far, -shift), low[number])
        bands[1, k] = jnp.where(from_high, turn(far, 8 - shift), high[k])
    for side in range(2):
        velocity = [bands[side, k] for k in range(3)]
        grad = [[None] * 3 for _ in range(3)]
        for k in range(3):
            center = velocity[k]
            grad[0][k] = fourth(*(turn(center, -BAND * step) for step in (1, -1, 2, -2)))
            grad[1][k] = 0.5 * (ops.y_up(center) - ops.y_down(center))
            grad[2][k] = fourth(*(turn(center, -step) for step in (1, -1, 2, -2)))
        strain = strain_of(grad)
        for number, values in enumerate(filter_fields(velocity, strain, size_of(strain))):
            if side == 0:
                spread[number] = values
            else:
                spread[number] = jnp.where(low_side, spread[number], values)
    for number in range(21):
        both = spread[number]
        spread[number] = turn(both, BAND) + turn(both, -BAND) + 2.0 * both
    for number in range(21):
        both = spread[number]
        spread[number] = turn(both, 1) + turn(both, -1) + 2.0 * both
    for part, values in enumerate(products_of(lambda number: spread[number])):
        values = jnp.where(at_edge, values, 0.0)
        for x in range(CX):
            sums[part, x] = sums[part, x] + jnp.where(band == x + 3, values, 0.0)


def add_columns(ops, total, first_lane, planes, scale=1.0):
    for x in range(CX):
        value = scale * jnp.sum(planes(x), axis=1, keepdims=True)
        total = jnp.where(ops.lane == first_lane + x, value, total)
    return total


def add_parts(ops, block, total):
    upper = total.astype(BF16).astype(F32)
    rest = total - upper
    middle = rest.astype(BF16).astype(F32)
    for number, part in enumerate((upper, middle, rest - middle)):
        block = jnp.where(ops.lane >> 5 == 1 + number, turn(part, 32 * (1 + number)), block)
    return block


def span_total(add_other, columns, other):
    total = columns[...]
    if add_other:
        parts = other.astype(F32)
        total = total + ((turn(parts, -32) + turn(parts, -64)) + turn(parts, -96))
    return total


def psi_terms(psi_wide, rate_yz, lap_yz, velocity, x):
    rates, laps = [], []
    for k in range(5):
        xs = [psi_wide[k, x + 3 + step] for step in (1, -1, 2, -2)]
        rates.append(rate_yz[k, x] + velocity * fourth(*xs))
        laps.append(lap_yz[k, x] + (xs[0] + xs[1]))
    return rates, laps


def inner_kernel(flow, near, far, grad_yz, sums, high, wide, fields, hats):
    inner_products(Ops(), 0, flow, near, far, grad_yz, sums, high, wide, fields, hats)


def first_kernel(
    rho, temp, psi, near, far, velocity, grad_yz, lap_yz, psi_rate, psi_lap,
    first, second, message, columns,
    wide, psi_wide, work,
):
    ops = Ops()
    even = is_even()
    for k in range(3):
        for i in range(1, CX + 5):
            wide[k, i] = velocity[k, i]
    widen_scalars(0, rho, temp, near, far, even, wide)
    for k in range(5):
        widen(
            k,
            lambda x: psi[k, x],
            lambda i: near[PSI + k * 2 + i].astype(F32),
            lambda i: far[PSI + k * 2 + i].astype(F32),
            2, even, psi_wide,
        )
    for x in range(CX):
        terms = state_terms(wide, grad_yz, lap_yz, x)
        rates, laps = psi_terms(psi_wide, psi_rate, psi_lap, terms[0][0], x)
        new, slope, sensitivity = affine_update(
            terms, [psi[k, x] for k in range(5)], rates, laps
        )
        for k in range(5):
            first[k, x] = new[k]
            second[k, x] = slope[k]
        work[x] = sensitivity
    columns[...] = add_columns(ops, jnp.zeros((ROWS, LANES), F32), 16, lambda x: work[x])
    items = [[part[k, x] for x in range(CX)] for part in (first, second) for k in range(5)]
    for number in range(2):
        message[number] = pack_strips(ops, items[8 * number : 8 * number + 8])


def edge_kernel(
    low, high, halo, inner, strips, sensitivity, message, columns, bands, spread, sums
):
    ops = Ops()
    for part in range(2):
        for x in range(CX):
            sums[part, x] = inner[part, x]
    edge_products(ops, 0, low, high, halo, sums, bands, spread)
    total = sensitivity[...]
    for part in range(2):
        total = add_columns(ops, total, 4 * part, lambda x: sums[part, x], 1.0 / 256.0)
    columns[...] = total
    message[0] = strips[0].astype(BF16)
    message[1] = add_parts(ops, strips[1], total).astype(BF16)


def later_kernel(
    flow, rho, temp, near, far, near_scalars, far_scalars,
    grad_yz, lap_yz, low, halo, first, second,
    wide, message, columns,
    high, fields, hats, work, bands, spread, sums,
):
    ops = Ops()
    inner_products(ops, 1, flow, near, far, grad_yz, sums, high, wide, fields, hats)
    widen_scalars(1, rho, temp, near_scalars, far_scalars, is_even(), wide)
    edge_products(ops, 1, low, high, halo, sums, bands, spread)
    for x in range(CX):
        _, _, lap, size, inv_rho = state_terms(wide, grad_yz, lap_yz, x)
        size_rho = size * inv_rho
        for part, source in enumerate((first, second)):
            total = lap[0] * source[0, x] + lap[1] * source[1, x] + lap[2] * source[2, x]
            work[part, x] = size_rho * (
                total + (1.0 / PRANDTL_TURB) * (lap[4] * source[4, x])
            )
    total = jnp.zeros((ROWS, LANES), F32)
    for part in range(2):
        total = add_columns(ops, total, 8 + 4 * part, lambda x: sums[part, x], 1.0 / 256.0)
        total = add_columns(ops, total, 20 + 4 * part, lambda x: work[part, x])
    columns[...] = total
    message[0] = add_parts(ops, jnp.zeros((ROWS, LANES), F32), total).astype(BF16)


def coefficients(ops, total):
    return total / (turn(total, -4) + EPSILON)


def middle_kernel(add_other, first, second, columns, other, psi, far, coef_first):
    ops = Ops()
    coef = coefficients(ops, span_total(add_other, columns, other[1]))
    for x in range(CX):
        coef_first[x] = jnp.broadcast_to(coef[:, x : x + 1], (ROWS, LANES))
    for x in range(CX):
        for k in range(5):
            psi[k, x] = first[k, x] + coef_first[x] * second[k, x]
    side = 1 - is_even().astype(jnp.int32)
    for k in range(5):
        for i in range(2):
            far[k, i] = psi[k, 2 * side + i].astype(BF16)


def base_kernel(
    add_other, span_cells,
    wide, grad_yz, lap_yz, psi, coef_first, columns, other, later, later_other,
    base, drift, spread, coef_grad, near,
    psi_halos, psi_wide, coef_planes, psi_rate, psi_lap,
):
    ops = Ops()
    side = is_even().astype(jnp.int32)
    for k in range(5):
        for i in range(2):
            near[k, i] = psi[k, 2 * side + i].astype(BF16)
    strips = [other[number].astype(F32) for number in range(2)]
    for k in range(5):
        for x in range(CX):
            psi_halos[k, x] = ops.strip(strips, k, x)
    total = span_total(add_other, columns, other[1]) + span_total(
        add_other, later, later_other[0]
    )
    coef = coefficients(ops, total)
    after = total + turn(coef, 20) * turn(total, -4)
    grads = jnp.where(ops.lane < 20, total, after) * (1.0 / span_cells)
    turned = jnp.concatenate([grads] * (LANES // ROWS), axis=0).T
    for t in range(2):
        coef_grad[t] = turned[16 + 4 * t : 20 + 4 * t, :ROWS]
    for x in range(CX):
        coef_planes[x] = jnp.broadcast_to(coef[:, 8 + x : 9 + x], (ROWS, LANES))
    for k in range(5):
        for x in range(CX):
            psi_halos[k, x] = psi_halos[k, x] + coef_first[x] * ops.strip(strips, 5 + k, x)
    zero = jnp.zeros((ROWS, LANES), F32)
    for k in range(5):
        for i in range(2):
            psi_wide[k, 1 + i] = zero
            psi_wide[k, 3 + CX + i] = zero
        for x in range(CX):
            psi_wide[k, 3 + x] = psi[k, x]
    for x in range(CX):
        for k in range(5):
            by_y, lap = y_terms(ops, psi[k, x])
            by_z, both = z_terms(ops, psi[k, x], psi_halos[k, x])
            psi_rate[k, x] = wide[1, x + 3] * by_y + wide[2, x + 3] * by_z
            psi_lap[k, x] = lap + both
    for x in range(CX):
        terms = state_terms(wide, grad_yz, lap_yz, x)
        center = terms[0]
        rates, laps = psi_terms(psi_wide, psi_rate, psi_lap, center[0], x)
        new, slope, _ = affine_update(terms, [psi[k, x] for k in range(5)], rates, laps)
        for k in range(5):
            base[k, x] = new[k] + coef_planes[x] * slope[k]
        size, inv_rho = terms[3:]
        drift[x] = TIME_STEP * center[0]
        if x in (0, CX - 1):
            eddy = coef_planes[x] * size
            scaled = TIME_STEP * inv_rho
            spread[x // (CX - 1), 0] = scaled * (NU_MOL + eddy)
            spread[x // (CX - 1), 1] = scaled * (
                NU_MOL / PRANDTL + (1.0 / PRANDTL_TURB) * eddy
            )


def widen_kernel(far, out):
    for k in range(5):
        for i in range(2):
            out[k, i] = far[k, i].astype(F32)


def last_kernel(base, drift, spread, near_psi, far_psi, out):
    even = is_even()
    for k in range(5):
        ones = [near_psi[k, i].astype(F32) for i in range(2)]
        twos = [far_psi[k, i].astype(F32) for i in range(2)]
        far, near = (jnp.where(even, two, one) for one, two in zip(ones, twos))
        after, beyond = (jnp.where(even, one, two) for one, two in zip(ones, twos))
        low = drift[0] * ((1.0 / 12.0) * far - (2.0 / 3.0) * near)
        high = drift[CX - 1] * ((2.0 / 3.0) * after - (1.0 / 12.0) * beyond)
        if k != 3:
            kind = 1 if k == 4 else 0
            low = low + spread[0, kind] * near
            high = high + spread[1, kind] * after
        out[k, 0] = base[k, 0] + low
        out[k, 1] = base[k, 1] + drift[1] * ((1.0 / 12.0) * near)
        out[k, CX - 2] = base[k, CX - 2] - drift[CX - 2] * ((1.0 / 12.0) * after)
        out[k, CX - 1] = base[k, CX - 1] + high


def ring(axis):
    count = lax.axis_size(axis)
    forward = [(i, (i + 1) % count) for i in range(count)]
    return forward, [(target, source) for source, target in forward]


def pairs():
    count = lax.axis_size("gx")
    if count % 2:
        raise ValueError("odd gx")
    inside = [(i, i ^ 1) for i in range(count)]
    across = [(i, (i + 1 if i % 2 else i - 1) % count) for i in range(count)]
    return inside, across


def span_edges(message, strips):
    forward, backward = ring("gz")
    before = lax.ppermute(message, "gz", forward)
    if lax.axis_size("gz") == 2:
        return before
    after = lax.ppermute(message, "gz", backward)
    lane = lax.broadcasted_iota(jnp.int32, message.shape, 2)
    number = lax.broadcasted_iota(jnp.int32, message.shape, 0)
    low = jnp.where(number < strips, lane % STRIP < 2, lane % 6 < 3)
    return jnp.where(low, before, after)


def shape_of(dims, kind=F32):
    return jax.ShapeDtypeStruct(dims + (ROWS, LANES), kind)


def whole(count):
    return [pl.BlockSpec(memory_space=pltpu.VMEM)] * count


def scratch(*dims):
    return [pltpu.VMEM(d + (ROWS, LANES), F32) for d in dims]


def call(kernel, name, inputs, outputs, operations, buffers=(), in_specs=None):
    inputs = list(inputs)
    if in_specs:
        inputs[:4] = [
            pltpu.with_memory_space_constraint(a, pltpu.MemorySpace.HBM) for a in inputs[:4]
        ]
    size = sum(math.prod(a.shape) * a.dtype.itemsize for a in list(inputs) + list(outputs))
    return pl.pallas_call(
        kernel,
        in_specs=in_specs or whole(len(inputs)),
        out_specs=whole(len(outputs)),
        out_shape=list(outputs),
        scratch_shapes=list(buffers),
        compiler_params=pltpu.CompilerParams(vmem_limit_bytes=8 * 2**20),
        cost_estimate=pl.CostEstimate(
            flops=operations, bytes_accessed=size, transcendentals=0
        ),
        name=name,
    )(*inputs)


def span_sums(columns):
    if lax.axis_size("gz") == 2:
        return columns
    return lax.psum(columns, "gz")


def local(flow_far, rho_far, temp_far, psi_far):
    inside, across = pairs()
    add_other = lax.axis_size("gz") == 2
    field, planes, edges = shape_of((5, CX)), shape_of((5, CX + 6)), shape_of((5, 2), BF16)
    slopes = shape_of((5, 2, CX))
    inputs = (flow_far, rho_far, temp_far, psi_far)
    stay = [pl.BlockSpec(memory_space=pltpu.MemorySpace.HBM)] * 4
    far, far_scalars, flow, rho, temp, psi = call(
        message_kernel,
        "message",
        inputs,
        [
            shape_of((SCALARS,), BF16),
            shape_of((SCALAR_PLANES,), BF16),
            shape_of((2, 3, CX), BF16),
            shape_of((2, CX), BF16),
            shape_of((2, CX), BF16),
            field,
        ],
        1_000_000,
        [pltpu.SemaphoreType.DMA((5,))],
        stay,
    )
    far = lax.ppermute(far, "gx", across)
    near, near_scalars, message, own_low = call(
        pack_kernel,
        "pack",
        (flow, rho, temp, psi),
        [
            shape_of((SCALARS,), BF16),
            shape_of((SCALAR_PLANES,), BF16),
            shape_of((STRIP_BLOCKS + BAND_BLOCKS,), BF16),
            shape_of((6,)),
        ],
        2_000_000,
    )
    far_scalars = lax.ppermute(far_scalars, "gx", across)
    near = lax.ppermute(near, "gx", inside)
    near_scalars = lax.ppermute(near_scalars, "gx", inside)
    own_halo = span_edges(message, STRIP_BLOCKS)
    rows = call(
        rows_kernel,
        "rows",
        (flow, rho, temp, psi),
        [field] * 6,
        3_000_000,
    )
    grad_0, grad_1, lap_0, lap_1, psi_rate, psi_lap = call(
        own_kernel,
        "own",
        (flow, rho, temp, psi, own_halo, *rows),
        [slopes, slopes, field, field, field, field],
        5_000_000,
        scratch((2, 5, CX), (5, CX)),
    )
    (token,) = call(token_kernel, "token", (far,), [shape_of(())], 100_000)
    message, low = call(
        bands_kernel,
        "bands",
        (own_low, near, far, token),
        [shape_of((BAND_BLOCKS,), BF16), shape_of((6,))],
        1_000_000,
    )
    halo = span_edges(message, 0)
    inner, high, velocity = call(
        inner_kernel,
        "inner",
        (flow, near, far, grad_0),
        [shape_of((2, CX)), shape_of((3,)), shape_of((3, CX + 6))],
        20_000_000,
        scratch((21, CX + 2), (21, CX)),
    )
    first, second, strips, sensitivity = call(
        first_kernel,
        "first",
        (rho, temp, psi, near_scalars, far_scalars, velocity, grad_0, lap_0, psi_rate, psi_lap),
        [field, field, shape_of((2,)), shape_of(())],
        10_000_000,
        scratch((5, CX + 6), (5, CX + 6), (CX,)),
    )
    message, columns = call(
        edge_kernel,
        "edge",
        (low, high, halo, inner, strips, sensitivity),
        [shape_of((2,), BF16), shape_of(())],
        20_000_000,
        scratch((2, 3), (21,), (2, CX)),
    )
    other = span_edges(message, 2)
    columns = span_sums(columns)
    wide, message, later = call(
        later_kernel,
        "later",
        (
            flow, rho, temp, near, far, near_scalars, far_scalars,
            grad_1, lap_1, low, halo, first, second,
        ),
        [planes, shape_of((1,), BF16), shape_of(())],
        20_000_000,
        scratch((3,), (21, CX + 2), (21, CX), (2, CX), (2, 3), (21,), (2, CX)),
    )
    later_other = span_edges(message, 1)
    later = span_sums(later)
    first, later = lax.optimization_barrier((first, later))
    psi, far, coef_first = call(
        functools.partial(middle_kernel, add_other),
        "middle",
        (first, second, columns, other),
        [field, edges, shape_of((CX,))],
        1_000_000,
    )
    far = lax.ppermute(far, "gx", across)
    base, drift, spread, coef_grad, near = call(
        functools.partial(base_kernel, add_other, LANES * lax.axis_size("gz")),
        "base",
        (wide, grad_1, lap_1, psi, coef_first, columns, other, later, later_other),
        [
            field, shape_of((CX,)), shape_of((2, 2)),
            jax.ShapeDtypeStruct((2, CX, ROWS), F32), edges,
        ],
        15_000_000,
        scratch((5, CX), (5, CX + 6), (CX,), (5, CX), (5, CX)),
    )
    near = lax.ppermute(near, "gx", inside)
    (far,) = call(widen_kernel, "widen", (far,), [shape_of((5, 2))], 100_000)
    (out,) = call(last_kernel, "last", (base, drift, spread, near, far), [field], 1_000_000)
    return out, coef_grad


def solution(mesh):
    return jax.shard_map(
        local,
        mesh=mesh,
        in_specs=(
            P(None, None, "gx", None, "gz"),
            P(None, "gx", None, "gz"),
            P(None, "gx", None, "gz"),
            P(None, "gx", None, "gz"),
        ),
        out_specs=(P(None, "gx", None, "gz"), P(None, "gx", None)),
        check_vma=False,
    )
```

```python
import functools
import math

import jax
import jax.numpy as jnp
from jax import lax
from jax.experimental import pallas as pl
from jax.experimental.pallas import tpu as pltpu
from jax.sharding import PartitionSpec as P

EPSILON = 1e-06
NU_MOL = 0.05
PRANDTL = 0.72
PRANDTL_TURB = 0.9
TIME_STEP = 0.04
PAIRS = ((0, 0), (1, 1), (2, 2), (0, 1), (0, 2), (1, 2))
WEIGHTS = (1.0, 1.0, 1.0, 2.0, 2.0, 2.0)

CX = 4
ROWS = 32
LANES = 128
STRIP = 4
F32 = jnp.float32
BF16 = jnp.bfloat16
SLOT_PSI = 4
BAND = 12
STRIP_BLOCKS = 2
BAND_BLOCKS = 3
VELOCITY = 0
SCALARS = 18
PSI = 8
SCALAR_PLANES = 18


def lane_ids():
    return lax.broadcasted_iota(jnp.int32, (ROWS, LANES), 1)


def row_ids():
    return lax.broadcasted_iota(jnp.int32, (ROWS, LANES), 0)


def turn(values, shift):
    shift = shift % LANES
    return values if shift == 0 else pltpu.roll(values, shift, 1)


class Ops:
    def __init__(self):
        self.lane = lane_ids()
        row = row_ids()
        self.top = row == ROWS - 1
        self.bottom = row == 0

    def z_at(self, values, halo, step):
        if step > 0:
            return turn(jnp.where(self.lane < step, halo, values), -step)
        return turn(jnp.where(self.lane >= LANES + step, halo, values), -step)

    def y_up(self, values):
        return jnp.where(self.top, 0.0, pltpu.roll(values, ROWS - 1, 0))

    def y_down(self, values):
        return jnp.where(self.bottom, 0.0, pltpu.roll(values, 1, 0))

    def strip(self, blocks, slot, x):
        return turn(blocks[slot // 8], -(STRIP * (4 * (slot % 8) + x) + 2))


def fourth(plus, minus, plus_2, minus_2):
    return (2.0 / 3.0) * (plus - minus) - (1.0 / 12.0) * (plus_2 - minus_2)


def strain_of(grad):
    return [
        grad[0][0],
        grad[1][1],
        grad[2][2],
        0.5 * (grad[0][1] + grad[1][0]),
        0.5 * (grad[0][2] + grad[2][0]),
        0.5 * (grad[1][2] + grad[2][1]),
    ]


def size_of(strain):
    diagonal = strain[0] * strain[0] + strain[1] * strain[1] + strain[2] * strain[2]
    other = strain[3] * strain[3] + strain[4] * strain[4] + strain[5] * strain[5]
    return jnp.sqrt(2.0 * diagonal + (4.0 * other + EPSILON))


def filter_fields(velocity, strain, size):
    products = [velocity[a] * velocity[b] for a, b in PAIRS]
    return list(velocity) + products + strain + [size * part for part in strain]


def pack_strips(ops, items):
    block = jnp.zeros((ROWS, LANES), F32)
    strip_id = ops.lane >> 2
    for slot, planes in enumerate(items):
        for x in range(CX):
            number = 4 * slot + x
            block = jnp.where(strip_id == number, turn(planes[x], STRIP * number + 2), block)
    return block


def place_halos(ops, t, own_halo, halos):
    strips = [own_halo[number].astype(F32) for number in range(STRIP_BLOCKS)]
    for k in range(3):
        number = 3 * t + k
        bands = own_halo[STRIP_BLOCKS + number // 2].astype(F32)
        for x in range(CX):
            halos[k, x] = turn(bands, -(BAND * (x + 3) + 3 + 6 * (number % 2)))
    for k in range(3, 5):
        for x in range(CX):
            halos[k, x] = ops.strip(strips, 2 * t + k - 3, x)


def y_terms(ops, values):
    up, down = ops.y_up(values), ops.y_down(values)
    return 0.5 * (up - down), (up + down) - 6.0 * values


def z_terms(ops, values, halo):
    zs = [ops.z_at(values, halo, step) for step in (1, -1, 2, -2)]
    return fourth(*zs), zs[0] + zs[1]


def state_terms(wide, grad_x, grad_yz, lap_velocity, lap_yz, sizes, x):
    grad = [[None] * 5 for _ in range(3)]
    lap = [None] * 5
    center = [wide[k, x + 3] for k in range(5)]
    for k in range(5):
        if k < 3:
            grad[0][k], lap[k] = grad_x[k, x], lap_velocity[k, x]
        else:
            xs = [wide[k, x + 3 + step] for step in (1, -1, 2, -2)]
            grad[0][k] = fourth(*xs)
            lap[k] = lap_yz[k, x] + (xs[0] + xs[1])
        grad[1][k], grad[2][k] = grad_yz[k, 0, x], grad_yz[k, 1, x]
    return center, grad, lap, sizes[x], 1.0 / center[3]


def affine_update(terms, psi, rates, laps):
    center, grad, lap, size, inv_rho = terms
    work_mom = psi[0] * lap[0] + psi[1] * lap[1] + psi[2] * lap[2]
    work_heat = psi[4] * lap[4]
    turbulent = work_mom + work_heat * (1.0 / PRANDTL_TURB)
    inv_rho_2 = inv_rho * inv_rho
    size_rho = size * inv_rho
    first, second = [], []
    for k in range(5):
        rate = rates[k]
        if k == 3:
            rate = rate - (NU_MOL * work_mom + (NU_MOL / PRANDTL) * work_heat) * inv_rho_2
            eddy = -(size * turbulent) * inv_rho_2
        else:
            lap_psi = laps[k]
            if k < 3:
                for other in range(5):
                    rate = rate + psi[other] * grad[k][other]
                rate = rate + NU_MOL * (inv_rho * lap_psi)
                eddy = size_rho * lap_psi
            else:
                rate = rate + (NU_MOL / PRANDTL) * (inv_rho * lap_psi)
                eddy = (1.0 / PRANDTL_TURB) * (size_rho * lap_psi)
        first.append(psi[k] + TIME_STEP * rate)
        second.append(TIME_STEP * eddy)
    return first, second, size_rho * turbulent


def band_of(lane):
    return (lane * 43) >> 9


def is_even():
    return lax.rem(lax.axis_index("gx"), 2) == 0


def fill_scalars(out, side, rho, temp, psi):
    for t in range(2):
        for i in range(2):
            out[2 * t + i] = rho[t, 2 * side + i]
            out[4 + 2 * t + i] = temp[t, 2 * side + i]
    for k in range(5):
        for i in range(2):
            out[PSI + k * 2 + i] = psi[k, 2 * side + i].astype(BF16)


def merge_bands(ops, low, message, first):
    lower = ops.lane - BAND * band_of(ops.lane) < 6
    for number in range(BAND_BLOCKS):
        both = jnp.where(lower, low[2 * number], turn(low[2 * number + 1], 6))
        message[first + number] = both.astype(BF16)


def message_kernel(
    flow_far, rho_far, temp_far, psi_far, far, far_scalars, flow, rho, temp, psi, sems
):
    side = 1 - is_even().astype(jnp.int32)
    pieces = (
        (flow_far.at[:, :, pl.ds(side, 3)], far.reshape((2, 3, 3, ROWS, LANES))),
        (psi_far, psi),
        (rho_far, rho),
        (temp_far, temp),
        (flow_far, flow),
    )
    copies = [
        pltpu.make_async_copy(source, target, sems.at[number])
        for number, (source, target) in enumerate(pieces)
    ]
    for copy in copies:
        copy.start()
    for copy in copies[1:4]:
        copy.wait()
    fill_scalars(far_scalars, side, rho, temp, psi)
    copies[0].wait()
    copies[4].wait()


def pack_kernel(flow, rho, temp, psi, near, near_scalars, message, low):
    ops = Ops()
    side = is_even().astype(jnp.int32)
    for t in range(2):
        for k in range(3):
            for i in range(3):
                near[VELOCITY + t * 9 + k * 3 + i] = flow[t, k, side + i]
    fill_scalars(near_scalars, side, rho, temp, psi)
    items = []
    for t in range(2):
        for source in (rho, temp):
            items.append([source[t, x].astype(F32) for x in range(CX)])
    items += [[psi[k, x] for x in range(CX)] for k in range(5)]
    for number in range(STRIP_BLOCKS):
        message[number] = pack_strips(ops, items[8 * number : 8 * number + 8]).astype(BF16)
    band = band_of(ops.lane)
    for t in range(2):
        for k in range(3):
            block = jnp.zeros((ROWS, LANES), F32)
            for x in range(CX):
                moved = turn(flow[t, k, x].astype(F32), BAND * (x + 3) + 3)
                block = jnp.where(band == x + 3, moved, block)
            low[3 * t + k] = block
    merge_bands(ops, low, message, STRIP_BLOCKS)


def rows_kernel(flow, rho, temp, psi, grad_0, grad_1, lap_0, lap_1, psi_rate, psi_lap):
    ops = Ops()
    for t, grad_y, lap_y in ((0, grad_0, lap_0), (1, grad_1, lap_1)):
        for k in range(5):
            for x in range(CX):
                values = flow[t, k, x] if k < 3 else (rho if k == 3 else temp)[t, x]
                grad_y[k, x], lap_y[k, x] = y_terms(ops, values.astype(F32))
    for x in range(CX):
        along_y = flow[0, 1, x].astype(F32)
        for k in range(5):
            by_y, psi_lap[k, x] = y_terms(ops, psi[k, x])
            psi_rate[k, x] = along_y * by_y


def own_kernel(
    flow, rho, temp, psi, own_halo, grad_y_0, grad_y_1, lap_y_0, lap_y_1, rate_y, psi_lap_y,
    grad_0, grad_1, lap_0, lap_1, psi_rate, psi_lap,
    halos, psi_halos,
):
    ops = Ops()
    for t in range(2):
        place_halos(ops, t, own_halo, halos.at[t])
    strips = [own_halo[number].astype(F32) for number in range(STRIP_BLOCKS)]
    for k in range(5):
        for x in range(CX):
            psi_halos[k, x] = ops.strip(strips, SLOT_PSI + k, x)
    for t, grad_y, lap_y, grad_yz, lap_yz in (
        (0, grad_y_0, lap_y_0, grad_0, lap_0),
        (1, grad_y_1, lap_y_1, grad_1, lap_1),
    ):
        for k in range(5):
            for x in range(CX):
                values = flow[t, k, x] if k < 3 else (rho if k == 3 else temp)[t, x]
                by_z, both = z_terms(ops, values.astype(F32), halos[t, k, x])
                grad_yz[k, 0, x], grad_yz[k, 1, x] = grad_y[k, x], by_z
                lap_yz[k, x] = lap_y[k, x] + both
    for x in range(CX):
        along_z = flow[0, 2, x].astype(F32)
        for k in range(5):
            by_z, both = z_terms(ops, psi[k, x], psi_halos[k, x])
            psi_rate[k, x] = rate_y[k, x] + along_z * by_z
            psi_lap[k, x] = psi_lap_y[k, x] + both


def token_kernel(far, out):
    out[...] = far[0].astype(F32)


def bands_kernel(own_low, near, far, _, message, low):
    ops = Ops()
    even = is_even()
    band = band_of(ops.lane)
    for t in range(2):
        for k in range(3):
            block = own_low[3 * t + k]
            for i in range(3):
                number = VELOCITY + t * 9 + k * 3 + i
                one, two = near[number].astype(F32), far[number].astype(F32)
                moved = turn(jnp.where(even, two, one), BAND * i + 3)
                block = jnp.where(band == i, moved, block)
                moved = turn(jnp.where(even, one, two), BAND * (7 + i) + 3)
                block = jnp.where(band == 7 + i, moved, block)
            low[3 * t + k] = block
    merge_bands(ops, low, message, 0)


def products_of(hat):
    velocity = [hat(k) for k in range(3)]
    strain = [hat(9 + number) for number in range(6)]
    diagonal = strain[0] * strain[0] + strain[1] * strain[1] + strain[2] * strain[2]
    other = strain[3] * strain[3] + strain[4] * strain[4] + strain[5] * strain[5]
    size = 4.0 * jnp.sqrt((2.0 / 256.0) * diagonal + ((4.0 / 256.0) * other + EPSILON))
    cross = 0.0
    square = 0.0
    for number, (a, b) in enumerate(PAIRS):
        leonard = hat(3 + number) - (1.0 / 16.0) * velocity[a] * velocity[b]
        model = hat(15 + number) - size * strain[number]
        weighted = WEIGHTS[number] * model if WEIGHTS[number] != 1.0 else model
        cross = cross + leonard * weighted
        square = square + model * weighted
    return cross, square


def widen(k, source, near, far, count, even, wide):
    for i in range(count):
        one, two = near(i), far(i)
        wide[k, 3 - count + i] = jnp.where(even, two, one)
        wide[k, 3 + CX + i] = jnp.where(even, one, two)
    for x in range(CX):
        wide[k, 3 + x] = source(x).astype(F32)


def widen_scalars(t, rho, temp, near, far, even, wide):
    for k, source in ((3, rho), (4, temp)):
        number = (k - 3) * 4 + 2 * t
        widen(
            k,
            lambda x: source[t, x],
            lambda i: near[number + i].astype(F32),
            lambda i: far[number + i].astype(F32),
            2, even, wide,
        )


def inner_products(
    ops, t, flow, near, far, grad_yz, lap_yz,
    sums, high, wide, grad_x, lap_velocity, sizes, fields, hats,
):
    even = is_even()
    valid = (ops.lane >= 3) & (ops.lane < LANES - 3)
    band = band_of(jnp.maximum(ops.lane - 2, 0))
    for k in range(3):
        widen(
            k,
            lambda x: flow[t, k, x],
            lambda i: near[VELOCITY + t * 9 + k * 3 + i].astype(F32),
            lambda i: far[VELOCITY + t * 9 + k * 3 + i].astype(F32),
            3, even, wide,
        )
    for x in range(-1, CX + 1):
        grad = [[None] * 3 for _ in range(3)]
        for k in range(3):
            center = wide[k, x + 3]
            xs = [wide[k, x + 3 + step] for step in (1, -1, 2, -2)]
            grad[0][k] = fourth(*xs)
            if 0 <= x < CX:
                grad_x[k, x] = grad[0][k]
                lap_velocity[k, x] = lap_yz[k, x] + (xs[0] + xs[1])
                grad[1][k], grad[2][k] = grad_yz[k, 0, x], grad_yz[k, 1, x]
            else:
                grad[1][k] = 0.5 * (ops.y_up(center) - ops.y_down(center))
                grad[2][k] = fourth(*(turn(center, -step) for step in (1, -1, 2, -2)))
        strain = strain_of(grad)
        size = size_of(strain)
        if 0 <= x < CX:
            sizes[x] = size
        velocity = [wide[k, x + 3] for k in range(3)]
        for number, values in enumerate(filter_fields(velocity, strain, size)):
            fields[number, x + 1] = values
    for x in range(CX):
        for number in range(21):
            along_x = fields[number, x] + fields[number, x + 2] + 2.0 * fields[number, x + 1]
            hats[number, x] = turn(along_x, 1) + turn(along_x, -1) + 2.0 * along_x
    for k in range(3):
        block = jnp.zeros((ROWS, LANES), F32)
        for q in range(CX + 6):
            block = jnp.where(band == q, turn(wide[k, q], BAND * q + 11), block)
        high[k] = block
    for x in range(CX):
        cross, square = products_of(lambda number: hats[number, x])
        sums[0, x] = jnp.where(valid, cross, 0.0)
        sums[1, x] = jnp.where(valid, square, 0.0)


def edge_products(ops, t, low, high, halo, sums, bands, spread):
    band = band_of(ops.lane)
    place = ops.lane - BAND * band
    from_low = place < 3
    from_high = (place == 11) | (place < 2)
    low_side = place < 7
    at_edge = ((place >= 3) & (place <= 5)) | ((place >= 8) & (place <= 10))
    for k in range(3):
        number = 3 * t + k
        far = halo[number // 2].astype(F32)
        shift = 6 * (number % 2)
        bands[0, k] = jnp.where(from_low, turn(far, -shift), low[number])
        bands[1, k] = jnp.where(from_high, turn(far, 8 - shift), high[k])
    for side in range(2):
        velocity = [bands[side, k] for k in range(3)]
        grad = [[None] * 3 for _ in range(3)]
        for k in range(3):
            center = velocity[k]
            grad[0][k] = fourth(*(turn(center, -BAND * step) for step in (1, -1, 2, -2)))
            grad[1][k] = 0.5 * (ops.y_up(center) - ops.y_down(center))
            grad[2][k] = fourth(*(turn(center, -step) for step in (1, -1, 2, -2)))
        strain = strain_of(grad)
        for number, values in enumerate(filter_fields(velocity, strain, size_of(strain))):
            if side == 0:
                spread[number] = values
            else:
                spread[number] = jnp.where(low_side, spread[number], values)
    for number in range(21):
        both = spread[number]
        spread[number] = turn(both, BAND) + turn(both, -BAND) + 2.0 * both
    for number in range(21):
        both = spread[number]
        spread[number] = turn(both, 1) + turn(both, -1) + 2.0 * both
    for part, values in enumerate(products_of(lambda number: spread[number])):
        values = jnp.where(at_edge, values, 0.0)
        for x in range(CX):
            sums[part, x] = sums[part, x] + jnp.where(band == x + 3, values, 0.0)


def add_columns(ops, total, first_lane, planes, scale=1.0):
    for x in range(CX):
        value = scale * jnp.sum(planes(x), axis=1, keepdims=True)
        total = jnp.where(ops.lane == first_lane + x, value, total)
    return total


def add_parts(ops, block, total):
    upper = total.astype(BF16).astype(F32)
    rest = total - upper
    middle = rest.astype(BF16).astype(F32)
    for number, part in enumerate((upper, middle, rest - middle)):
        block = jnp.where(ops.lane >> 5 == 1 + number, turn(part, 32 * (1 + number)), block)
    return block


def span_total(add_other, columns, other):
    total = columns[...]
    if add_other:
        parts = other.astype(F32)
        total = total + ((turn(parts, -32) + turn(parts, -64)) + turn(parts, -96))
    return total


def psi_terms(psi_wide, rate_yz, lap_yz, velocity, x):
    rates, laps = [], []
    for k in range(5):
        xs = [psi_wide[k, x + 3 + step] for step in (1, -1, 2, -2)]
        rates.append(rate_yz[k, x] + velocity * fourth(*xs))
        laps.append(lap_yz[k, x] + (xs[0] + xs[1]))
    return rates, laps


def inner_kernel(
    flow, near, far, grad_yz, lap_yz,
    sums, high, wide, grad_x, lap_velocity, sizes,
    fields, hats,
):
    inner_products(
        Ops(), 0, flow, near, far, grad_yz, lap_yz,
        sums, high, wide, grad_x, lap_velocity, sizes, fields, hats,
    )


def first_kernel(
    rho, temp, psi, near, far, velocity, grad_x, lap_velocity, sizes,
    grad_yz, lap_yz, psi_rate, psi_lap,
    first, second, message, columns,
    wide, psi_wide, work,
):
    ops = Ops()
    even = is_even()
    for k in range(3):
        for x in range(CX):
            wide[k, x + 3] = velocity[k, x + 3]
    widen_scalars(0, rho, temp, near, far, even, wide)
    for k in range(5):
        widen(
            k,
            lambda x: psi[k, x],
            lambda i: near[PSI + k * 2 + i].astype(F32),
            lambda i: far[PSI + k * 2 + i].astype(F32),
            2, even, psi_wide,
        )
    for x in range(CX):
        terms = state_terms(wide, grad_x, grad_yz, lap_velocity, lap_yz, sizes, x)
        rates, laps = psi_terms(psi_wide, psi_rate, psi_lap, terms[0][0], x)
        new, slope, sensitivity = affine_update(
            terms, [psi[k, x] for k in range(5)], rates, laps
        )
        for k in range(5):
            first[k, x] = new[k]
            second[k, x] = slope[k]
        work[x] = sensitivity
    columns[...] = add_columns(ops, jnp.zeros((ROWS, LANES), F32), 16, lambda x: work[x])
    items = [[part[k, x] for x in range(CX)] for part in (first, second) for k in range(5)]
    for number in range(2):
        message[number] = pack_strips(ops, items[8 * number : 8 * number + 8])


def edge_kernel(
    low, high, halo, inner, strips, sensitivity, message, columns, bands, spread, sums
):
    ops = Ops()
    for part in range(2):
        for x in range(CX):
            sums[part, x] = inner[part, x]
    edge_products(ops, 0, low, high, halo, sums, bands, spread)
    total = sensitivity[...]
    for part in range(2):
        total = add_columns(ops, total, 4 * part, lambda x: sums[part, x], 1.0 / 256.0)
    columns[...] = total
    message[0] = strips[0].astype(BF16)
    message[1] = add_parts(ops, strips[1], total).astype(BF16)


def later_kernel(
    flow, rho, temp, near, far, near_scalars, far_scalars,
    grad_yz, lap_yz, low, halo, first, second,
    wide, grad_x, lap_velocity, sizes, message, columns,
    high, fields, hats, work, bands, spread, sums,
):
    ops = Ops()
    inner_products(
        ops, 1, flow, near, far, grad_yz, lap_yz,
        sums, high, wide, grad_x, lap_velocity, sizes, fields, hats,
    )
    widen_scalars(1, rho, temp, near_scalars, far_scalars, is_even(), wide)
    edge_products(ops, 1, low, high, halo, sums, bands, spread)
    for x in range(CX):
        _, _, lap, size, inv_rho = state_terms(
            wide, grad_x, grad_yz, lap_velocity, lap_yz, sizes, x
        )
        size_rho = size * inv_rho
        for part, source in enumerate((first, second)):
            total = lap[0] * source[0, x] + lap[1] * source[1, x] + lap[2] * source[2, x]
            work[part, x] = size_rho * (
                total + (1.0 / PRANDTL_TURB) * (lap[4] * source[4, x])
            )
    total = jnp.zeros((ROWS, LANES), F32)
    for part in range(2):
        total = add_columns(ops, total, 8 + 4 * part, lambda x: sums[part, x], 1.0 / 256.0)
        total = add_columns(ops, total, 20 + 4 * part, lambda x: work[part, x])
    columns[...] = total
    message[0] = add_parts(ops, jnp.zeros((ROWS, LANES), F32), total).astype(BF16)


def coefficients(ops, total):
    return total / (turn(total, -4) + EPSILON)


def middle_kernel(add_other, first, second, columns, other, psi, far, coef_first):
    ops = Ops()
    coef = coefficients(ops, span_total(add_other, columns, other[1]))
    for x in range(CX):
        coef_first[x] = jnp.broadcast_to(coef[:, x : x + 1], (ROWS, LANES))
    for x in range(CX):
        for k in range(5):
            psi[k, x] = first[k, x] + coef_first[x] * second[k, x]
    side = 1 - is_even().astype(jnp.int32)
    for k in range(5):
        for i in range(2):
            far[k, i] = psi[k, 2 * side + i].astype(BF16)


def base_kernel(
    add_other, span_cells,
    wide, grad_x, lap_velocity, sizes, grad_yz, lap_yz, psi, coef_first,
    columns, other, later, later_other,
    base, drift, spread, coef_grad, near,
    psi_halos, psi_wide, coef_planes, psi_rate, psi_lap,
):
    ops = Ops()
    side = is_even().astype(jnp.int32)
    for k in range(5):
        for i in range(2):
            near[k, i] = psi[k, 2 * side + i].astype(BF16)
    strips = [other[number].astype(F32) for number in range(2)]
    for k in range(5):
        for x in range(CX):
            psi_halos[k, x] = ops.strip(strips, k, x)
    total = span_total(add_other, columns, other[1]) + span_total(
        add_other, later, later_other[0]
    )
    coef = coefficients(ops, total)
    after = total + turn(coef, 20) * turn(total, -4)
    grads = jnp.where(ops.lane < 20, total, after) * (1.0 / span_cells)
    turned = jnp.concatenate([grads] * (LANES // ROWS), axis=0).T
    for t in range(2):
        coef_grad[t] = turned[16 + 4 * t : 20 + 4 * t, :ROWS]
    for x in range(CX):
        coef_planes[x] = jnp.broadcast_to(coef[:, 8 + x : 9 + x], (ROWS, LANES))
    for k in range(5):
        for x in range(CX):
            psi_halos[k, x] = psi_halos[k, x] + coef_first[x] * ops.strip(strips, 5 + k, x)
    zero = jnp.zeros((ROWS, LANES), F32)
    for k in range(5):
        for i in range(2):
            psi_wide[k, 1 + i] = zero
            psi_wide[k, 3 + CX + i] = zero
        for x in range(CX):
            psi_wide[k, 3 + x] = psi[k, x]
    for x in range(CX):
        for k in range(5):
            by_y, lap = y_terms(ops, psi[k, x])
            by_z, both = z_terms(ops, psi[k, x], psi_halos[k, x])
            psi_rate[k, x] = wide[1, x + 3] * by_y + wide[2, x + 3] * by_z
            psi_lap[k, x] = lap + both
    for x in range(CX):
        terms = state_terms(wide, grad_x, grad_yz, lap_velocity, lap_yz, sizes, x)
        center = terms[0]
        rates, laps = psi_terms(psi_wide, psi_rate, psi_lap, center[0], x)
        new, slope, _ = affine_update(terms, [psi[k, x] for k in range(5)], rates, laps)
        for k in range(5):
            base[k, x] = new[k] + coef_planes[x] * slope[k]
        size, inv_rho = terms[3:]
        drift[x] = TIME_STEP * center[0]
        if x in (0, CX - 1):
            eddy = coef_planes[x] * size
            scaled = TIME_STEP * inv_rho
            spread[x // (CX - 1), 0] = scaled * (NU_MOL + eddy)
            spread[x // (CX - 1), 1] = scaled * (
                NU_MOL / PRANDTL + (1.0 / PRANDTL_TURB) * eddy
            )


def widen_kernel(far, out):
    for k in range(5):
        for i in range(2):
            out[k, i] = far[k, i].astype(F32)


def last_kernel(base, drift, spread, near_psi, far_psi, out):
    even = is_even()
    for k in range(5):
        ones = [near_psi[k, i].astype(F32) for i in range(2)]
        twos = [far_psi[k, i].astype(F32) for i in range(2)]
        far, near = (jnp.where(even, two, one) for one, two in zip(ones, twos))
        after, beyond = (jnp.where(even, one, two) for one, two in zip(ones, twos))
        low = drift[0] * ((1.0 / 12.0) * far - (2.0 / 3.0) * near)
        high = drift[CX - 1] * ((2.0 / 3.0) * after - (1.0 / 12.0) * beyond)
        if k != 3:
            kind = 1 if k == 4 else 0
            low = low + spread[0, kind] * near
            high = high + spread[1, kind] * after
        out[k, 0] = base[k, 0] + low
        out[k, 1] = base[k, 1] + drift[1] * ((1.0 / 12.0) * near)
        out[k, CX - 2] = base[k, CX - 2] - drift[CX - 2] * ((1.0 / 12.0) * after)
        out[k, CX - 1] = base[k, CX - 1] + high


def ring(axis):
    count = lax.axis_size(axis)
    forward = [(i, (i + 1) % count) for i in range(count)]
    return forward, [(target, source) for source, target in forward]


def pairs():
    count = lax.axis_size("gx")
    if count % 2:
        raise ValueError("odd gx")
    inside = [(i, i ^ 1) for i in range(count)]
    across = [(i, (i + 1 if i % 2 else i - 1) % count) for i in range(count)]
    return inside, across


def span_edges(message, strips):
    forward, backward = ring("gz")
    before = lax.ppermute(message, "gz", forward)
    if lax.axis_size("gz") == 2:
        return before
    after = lax.ppermute(message, "gz", backward)
    lane = lax.broadcasted_iota(jnp.int32, message.shape, 2)
    number = lax.broadcasted_iota(jnp.int32, message.shape, 0)
    low = jnp.where(number < strips, lane % STRIP < 2, lane % 6 < 3)
    return jnp.where(low, before, after)


def shape_of(dims, kind=F32):
    return jax.ShapeDtypeStruct(dims + (ROWS, LANES), kind)


def whole(count):
    return [pl.BlockSpec(memory_space=pltpu.VMEM)] * count


def scratch(*dims):
    return [pltpu.VMEM(d + (ROWS, LANES), F32) for d in dims]


def call(kernel, name, inputs, outputs, operations, buffers=(), in_specs=None):
    inputs = list(inputs)
    if in_specs:
        inputs[:4] = [
            pltpu.with_memory_space_constraint(a, pltpu.MemorySpace.HBM) for a in inputs[:4]
        ]
    size = sum(math.prod(a.shape) * a.dtype.itemsize for a in list(inputs) + list(outputs))
    return pl.pallas_call(
        kernel,
        in_specs=in_specs or whole(len(inputs)),
        out_specs=whole(len(outputs)),
        out_shape=list(outputs),
        scratch_shapes=list(buffers),
        compiler_params=pltpu.CompilerParams(vmem_limit_bytes=8 * 2**20),
        cost_estimate=pl.CostEstimate(
            flops=operations, bytes_accessed=size, transcendentals=0
        ),
        name=name,
    )(*inputs)


def span_sums(columns):
    if lax.axis_size("gz") == 2:
        return columns
    return lax.psum(columns, "gz")


def local(flow_far, rho_far, temp_far, psi_far):
    inside, across = pairs()
    add_other = lax.axis_size("gz") == 2
    field, planes, edges = shape_of((5, CX)), shape_of((5, CX + 6)), shape_of((5, 2), BF16)
    slopes = shape_of((5, 2, CX))
    inputs = (flow_far, rho_far, temp_far, psi_far)
    stay = [pl.BlockSpec(memory_space=pltpu.MemorySpace.HBM)] * 4
    far, far_scalars, flow, rho, temp, psi = call(
        message_kernel,
        "message",
        inputs,
        [
            shape_of((SCALARS,), BF16),
            shape_of((SCALAR_PLANES,), BF16),
            shape_of((2, 3, CX), BF16),
            shape_of((2, CX), BF16),
            shape_of((2, CX), BF16),
            field,
        ],
        1_000_000,
        [pltpu.SemaphoreType.DMA((5,))],
        stay,
    )
    far = lax.ppermute(far, "gx", across)
    near, near_scalars, message, own_low = call(
        pack_kernel,
        "pack",
        (flow, rho, temp, psi),
        [
            shape_of((SCALARS,), BF16),
            shape_of((SCALAR_PLANES,), BF16),
            shape_of((STRIP_BLOCKS + BAND_BLOCKS,), BF16),
            shape_of((6,)),
        ],
        2_000_000,
    )
    far_scalars = lax.ppermute(far_scalars, "gx", across)
    near = lax.ppermute(near, "gx", inside)
    near_scalars = lax.ppermute(near_scalars, "gx", inside)
    own_halo = span_edges(message, STRIP_BLOCKS)
    rows = call(
        rows_kernel,
        "rows",
        (flow, rho, temp, psi),
        [field] * 6,
        3_000_000,
    )
    grad_0, grad_1, lap_0, lap_1, psi_rate, psi_lap = call(
        own_kernel,
        "own",
        (flow, rho, temp, psi, own_halo, *rows),
        [slopes, slopes, field, field, field, field],
        5_000_000,
        scratch((2, 5, CX), (5, CX)),
    )
    (token,) = call(token_kernel, "token", (far,), [shape_of(())], 100_000)
    message, low = call(
        bands_kernel,
        "bands",
        (own_low, near, far, token),
        [shape_of((BAND_BLOCKS,), BF16), shape_of((6,))],
        1_000_000,
    )
    halo = span_edges(message, 0)
    inner, high, velocity, grad_x, lap_velocity, sizes = call(
        inner_kernel,
        "inner",
        (flow, near, far, grad_0, lap_0),
        [
            shape_of((2, CX)), shape_of((3,)), shape_of((3, CX + 6)),
            shape_of((3, CX)), shape_of((3, CX)), shape_of((CX,)),
        ],
        20_000_000,
        scratch((21, CX + 2), (21, CX)),
    )
    first, second, strips, sensitivity = call(
        first_kernel,
        "first",
        (
            rho, temp, psi, near_scalars, far_scalars, velocity, grad_x, lap_velocity, sizes,
            grad_0, lap_0, psi_rate, psi_lap,
        ),
        [field, field, shape_of((2,)), shape_of(())],
        10_000_000,
        scratch((5, CX + 6), (5, CX + 6), (CX,)),
    )
    message, columns = call(
        edge_kernel,
        "edge",
        (low, high, halo, inner, strips, sensitivity),
        [shape_of((2,), BF16), shape_of(())],
        20_000_000,
        scratch((2, 3), (21,), (2, CX)),
    )
    other = span_edges(message, 2)
    columns = span_sums(columns)
    wide, grad_x, lap_velocity, sizes, message, later = call(
        later_kernel,
        "later",
        (
            flow, rho, temp, near, far, near_scalars, far_scalars,
            grad_1, lap_1, low, halo, first, second,
        ),
        [
            planes, shape_of((3, CX)), shape_of((3, CX)), shape_of((CX,)),
            shape_of((1,), BF16), shape_of(()),
        ],
        20_000_000,
        scratch((3,), (21, CX + 2), (21, CX), (2, CX), (2, 3), (21,), (2, CX)),
    )
    later_other = span_edges(message, 1)
    later = span_sums(later)
    first, later = lax.optimization_barrier((first, later))
    psi, far, coef_first = call(
        functools.partial(middle_kernel, add_other),
        "middle",
        (first, second, columns, other),
        [field, edges, shape_of((CX,))],
        1_000_000,
    )
    far = lax.ppermute(far, "gx", across)
    base, drift, spread, coef_grad, near = call(
        functools.partial(base_kernel, add_other, LANES * lax.axis_size("gz")),
        "base",
        (
            wide, grad_x, lap_velocity, sizes, grad_1, lap_1, psi, coef_first,
            columns, other, later, later_other,
        ),
        [
            field, shape_of((CX,)), shape_of((2, 2)),
            jax.ShapeDtypeStruct((2, CX, ROWS), F32), edges,
        ],
        15_000_000,
        scratch((5, CX), (5, CX + 6), (CX,), (5, CX), (5, CX)),
    )
    near = lax.ppermute(near, "gx", inside)
    (far,) = call(widen_kernel, "widen", (far,), [shape_of((5, 2))], 100_000)
    (out,) = call(last_kernel, "last", (base, drift, spread, near, far), [field], 1_000_000)
    return out, coef_grad


def solution(mesh):
    return jax.shard_map(
        local,
        mesh=mesh,
        in_specs=(
            P(None, None, "gx", None, "gz"),
            P(None, "gx", None, "gz"),
            P(None, "gx", None, "gz"),
            P(None, "gx", None, "gz"),
        ),
        out_specs=(P(None, "gx", None, "gz"), P(None, "gx", None)),
        check_vma=False,
    )
```

```python
import functools
import math

import jax
import jax.numpy as jnp
from jax import lax
from jax.experimental import pallas as pl
from jax.experimental.pallas import tpu as pltpu
from jax.sharding import PartitionSpec as P

EPSILON = 1e-06
NU_MOL = 0.05
PRANDTL = 0.72
PRANDTL_TURB = 0.9
TIME_STEP = 0.04
PAIRS = ((0, 0), (1, 1), (2, 2), (0, 1), (0, 2), (1, 2))
WEIGHTS = (1.0, 1.0, 1.0, 2.0, 2.0, 2.0)

CX = 4
ROWS = 32
LANES = 128
STRIP = 4
F32 = jnp.float32
BF16 = jnp.bfloat16
SLOT_PSI = 4
BAND = 12
STRIP_BLOCKS = 2
BAND_BLOCKS = 3
VELOCITY = 0
SCALARS = 18
PSI = 8
SCALAR_PLANES = 18


def lane_ids():
    return lax.broadcasted_iota(jnp.int32, (ROWS, LANES), 1)


def row_ids():
    return lax.broadcasted_iota(jnp.int32, (ROWS, LANES), 0)


def turn(values, shift):
    shift = shift % LANES
    return values if shift == 0 else pltpu.roll(values, shift, 1)


class Ops:
    def __init__(self):
        self.lane = lane_ids()
        row = row_ids()
        self.top = row == ROWS - 1
        self.bottom = row == 0

    def z_at(self, values, halo, step):
        if step > 0:
            return turn(jnp.where(self.lane < step, halo, values), -step)
        return turn(jnp.where(self.lane >= LANES + step, halo, values), -step)

    def y_up(self, values):
        return jnp.where(self.top, 0.0, pltpu.roll(values, ROWS - 1, 0))

    def y_down(self, values):
        return jnp.where(self.bottom, 0.0, pltpu.roll(values, 1, 0))

    def strip(self, blocks, slot, x):
        return turn(blocks[slot // 8], -(STRIP * (4 * (slot % 8) + x) + 2))


def fourth(plus, minus, plus_2, minus_2):
    return (2.0 / 3.0) * (plus - minus) - (1.0 / 12.0) * (plus_2 - minus_2)


def strain_of(grad):
    return [
        grad[0][0],
        grad[1][1],
        grad[2][2],
        0.5 * (grad[0][1] + grad[1][0]),
        0.5 * (grad[0][2] + grad[2][0]),
        0.5 * (grad[1][2] + grad[2][1]),
    ]


def size_of(strain):
    diagonal = strain[0] * strain[0] + strain[1] * strain[1] + strain[2] * strain[2]
    other = strain[3] * strain[3] + strain[4] * strain[4] + strain[5] * strain[5]
    return jnp.sqrt(2.0 * diagonal + (4.0 * other + EPSILON))


def filter_fields(velocity, strain, size):
    products = [velocity[a] * velocity[b] for a, b in PAIRS]
    return list(velocity) + products + strain + [size * part for part in strain]


def pack_strips(ops, items):
    block = jnp.zeros((ROWS, LANES), F32)
    strip_id = ops.lane >> 2
    for slot, planes in enumerate(items):
        for x in range(CX):
            number = 4 * slot + x
            block = jnp.where(strip_id == number, turn(planes[x], STRIP * number + 2), block)
    return block


def place_halos(ops, t, own_halo, halos):
    strips = [own_halo[number].astype(F32) for number in range(STRIP_BLOCKS)]
    for k in range(3):
        number = 3 * t + k
        bands = own_halo[STRIP_BLOCKS + number // 2].astype(F32)
        for x in range(CX):
            halos[k, x] = turn(bands, -(BAND * (x + 3) + 3 + 6 * (number % 2)))
    for k in range(3, 5):
        for x in range(CX):
            halos[k, x] = ops.strip(strips, 2 * t + k - 3, x)


def y_terms(ops, values):
    up, down = ops.y_up(values), ops.y_down(values)
    return 0.5 * (up - down), (up + down) - 6.0 * values


def z_terms(ops, values, halo):
    zs = [ops.z_at(values, halo, step) for step in (1, -1, 2, -2)]
    return fourth(*zs), zs[0] + zs[1]


def state_terms(wide, grad_x, grad_yz, lap_velocity, lap_yz, sizes, x):
    grad = [[None] * 5 for _ in range(3)]
    lap = [None] * 5
    center = [wide[k, x + 3] for k in range(5)]
    for k in range(5):
        if k < 3:
            grad[0][k], lap[k] = grad_x[k, x], lap_velocity[k, x]
        else:
            xs = [wide[k, x + 3 + step] for step in (1, -1, 2, -2)]
            grad[0][k] = fourth(*xs)
            lap[k] = lap_yz[k, x] + (xs[0] + xs[1])
        grad[1][k], grad[2][k] = grad_yz[k, 0, x], grad_yz[k, 1, x]
    return center, grad, lap, sizes[x], 1.0 / center[3]


def affine_update(terms, psi, rates, laps):
    center, grad, lap, size, inv_rho = terms
    work_mom = psi[0] * lap[0] + psi[1] * lap[1] + psi[2] * lap[2]
    work_heat = psi[4] * lap[4]
    turbulent = work_mom + work_heat * (1.0 / PRANDTL_TURB)
    inv_rho_2 = inv_rho * inv_rho
    size_rho = size * inv_rho
    first, second = [], []
    for k in range(5):
        rate = rates[k]
        if k == 3:
            rate = rate - (NU_MOL * work_mom + (NU_MOL / PRANDTL) * work_heat) * inv_rho_2
            eddy = -(size * turbulent) * inv_rho_2
        else:
            lap_psi = laps[k]
            if k < 3:
                for other in range(5):
                    rate = rate + psi[other] * grad[k][other]
                rate = rate + NU_MOL * (inv_rho * lap_psi)
                eddy = size_rho * lap_psi
            else:
                rate = rate + (NU_MOL / PRANDTL) * (inv_rho * lap_psi)
                eddy = (1.0 / PRANDTL_TURB) * (size_rho * lap_psi)
        first.append(psi[k] + TIME_STEP * rate)
        second.append(TIME_STEP * eddy)
    return first, second, size_rho * turbulent


def band_of(lane):
    return (lane * 43) >> 9


def is_even():
    return lax.rem(lax.axis_index("gx"), 2) == 0


def fill_scalars(out, side, rho, temp, psi):
    for t in range(2):
        for i in range(2):
            out[2 * t + i] = rho[t, 2 * side + i]
            out[4 + 2 * t + i] = temp[t, 2 * side + i]
    for k in range(5):
        for i in range(2):
            out[PSI + k * 2 + i] = psi[k, 2 * side + i].astype(BF16)


def merge_bands(ops, low, message, first):
    lower = ops.lane - BAND * band_of(ops.lane) < 6
    for number in range(BAND_BLOCKS):
        both = jnp.where(lower, low[2 * number], turn(low[2 * number + 1], 6))
        message[first + number] = both.astype(BF16)


def message_kernel(
    flow_far, rho_far, temp_far, psi_far, far, far_scalars, flow, rho, temp, psi, sems
):
    side = 1 - is_even().astype(jnp.int32)
    pieces = (
        (flow_far.at[:, :, pl.ds(side, 3)], far.reshape((2, 3, 3, ROWS, LANES))),
        (psi_far, psi),
        (rho_far, rho),
        (temp_far, temp),
        (flow_far, flow),
    )
    copies = [
        pltpu.make_async_copy(source, target, sems.at[number])
        for number, (source, target) in enumerate(pieces)
    ]
    for copy in copies:
        copy.start()
    for copy in copies[1:4]:
        copy.wait()
    fill_scalars(far_scalars, side, rho, temp, psi)
    copies[0].wait()
    copies[4].wait()


def pack_kernel(flow, rho, temp, psi, near, near_scalars, message, low):
    ops = Ops()
    side = is_even().astype(jnp.int32)
    for t in range(2):
        for k in range(3):
            for i in range(3):
                near[VELOCITY + t * 9 + k * 3 + i] = flow[t, k, side + i]
    fill_scalars(near_scalars, side, rho, temp, psi)
    items = []
    for t in range(2):
        for source in (rho, temp):
            items.append([source[t, x].astype(F32) for x in range(CX)])
    items += [[psi[k, x] for x in range(CX)] for k in range(5)]
    for number in range(STRIP_BLOCKS):
        message[number] = pack_strips(ops, items[8 * number : 8 * number + 8]).astype(BF16)
    band = band_of(ops.lane)
    for t in range(2):
        for k in range(3):
            block = jnp.zeros((ROWS, LANES), F32)
            for x in range(CX):
                moved = turn(flow[t, k, x].astype(F32), BAND * (x + 3) + 3)
                block = jnp.where(band == x + 3, moved, block)
            low[3 * t + k] = block
    merge_bands(ops, low, message, STRIP_BLOCKS)


def rows_kernel(flow, rho, temp, psi, grad_0, grad_1, lap_0, lap_1, psi_rate, psi_lap):
    ops = Ops()
    for t, grad_y, lap_y in ((0, grad_0, lap_0), (1, grad_1, lap_1)):
        for k in range(5):
            for x in range(CX):
                values = flow[t, k, x] if k < 3 else (rho if k == 3 else temp)[t, x]
                grad_y[k, x], lap_y[k, x] = y_terms(ops, values.astype(F32))
    for x in range(CX):
        along_y = flow[0, 1, x].astype(F32)
        for k in range(5):
            by_y, psi_lap[k, x] = y_terms(ops, psi[k, x])
            psi_rate[k, x] = along_y * by_y


def own_kernel(
    flow, rho, temp, psi, own_halo, grad_y_0, grad_y_1, lap_y_0, lap_y_1, rate_y, psi_lap_y,
    grad_0, grad_1, lap_0, lap_1, psi_rate, psi_lap,
    halos, psi_halos,
):
    ops = Ops()
    for t in range(2):
        place_halos(ops, t, own_halo, halos.at[t])
    strips = [own_halo[number].astype(F32) for number in range(STRIP_BLOCKS)]
    for k in range(5):
        for x in range(CX):
            psi_halos[k, x] = ops.strip(strips, SLOT_PSI + k, x)
    for t, grad_y, lap_y, grad_yz, lap_yz in (
        (0, grad_y_0, lap_y_0, grad_0, lap_0),
        (1, grad_y_1, lap_y_1, grad_1, lap_1),
    ):
        for k in range(5):
            for x in range(CX):
                values = flow[t, k, x] if k < 3 else (rho if k == 3 else temp)[t, x]
                by_z, both = z_terms(ops, values.astype(F32), halos[t, k, x])
                grad_yz[k, 0, x], grad_yz[k, 1, x] = grad_y[k, x], by_z
                lap_yz[k, x] = lap_y[k, x] + both
    for x in range(CX):
        along_z = flow[0, 2, x].astype(F32)
        for k in range(5):
            by_z, both = z_terms(ops, psi[k, x], psi_halos[k, x])
            psi_rate[k, x] = rate_y[k, x] + along_z * by_z
            psi_lap[k, x] = psi_lap_y[k, x] + both


def token_kernel(far, _, out):
    out[...] = far[0].astype(F32)


def bands_kernel(own_low, near, far, _, message, low):
    ops = Ops()
    even = is_even()
    band = band_of(ops.lane)
    for t in range(2):
        for k in range(3):
            block = own_low[3 * t + k]
            for i in range(3):
                number = VELOCITY + t * 9 + k * 3 + i
                one, two = near[number].astype(F32), far[number].astype(F32)
                moved = turn(jnp.where(even, two, one), BAND * i + 3)
                block = jnp.where(band == i, moved, block)
                moved = turn(jnp.where(even, one, two), BAND * (7 + i) + 3)
                block = jnp.where(band == 7 + i, moved, block)
            low[3 * t + k] = block
    merge_bands(ops, low, message, 0)


def products_of(hat):
    velocity = [hat(k) for k in range(3)]
    strain = [hat(9 + number) for number in range(6)]
    diagonal = strain[0] * strain[0] + strain[1] * strain[1] + strain[2] * strain[2]
    other = strain[3] * strain[3] + strain[4] * strain[4] + strain[5] * strain[5]
    size = 4.0 * jnp.sqrt((2.0 / 256.0) * diagonal + ((4.0 / 256.0) * other + EPSILON))
    cross = 0.0
    square = 0.0
    for number, (a, b) in enumerate(PAIRS):
        leonard = hat(3 + number) - (1.0 / 16.0) * velocity[a] * velocity[b]
        model = hat(15 + number) - size * strain[number]
        weighted = WEIGHTS[number] * model if WEIGHTS[number] != 1.0 else model
        cross = cross + leonard * weighted
        square = square + model * weighted
    return cross, square


def widen(k, source, near, far, count, even, wide):
    for i in range(count):
        one, two = near(i), far(i)
        wide[k, 3 - count + i] = jnp.where(even, two, one)
        wide[k, 3 + CX + i] = jnp.where(even, one, two)
    for x in range(CX):
        wide[k, 3 + x] = source(x).astype(F32)


def widen_scalars(t, rho, temp, near, far, even, wide):
    for k, source in ((3, rho), (4, temp)):
        number = (k - 3) * 4 + 2 * t
        widen(
            k,
            lambda x: source[t, x],
            lambda i: near[number + i].astype(F32),
            lambda i: far[number + i].astype(F32),
            2, even, wide,
        )


def inner_products(
    ops, t, flow, near, far, grad_yz, lap_yz,
    sums, high, wide, grad_x, lap_velocity, sizes, fields, hats,
):
    even = is_even()
    valid = (ops.lane >= 3) & (ops.lane < LANES - 3)
    band = band_of(jnp.maximum(ops.lane - 2, 0))
    for k in range(3):
        widen(
            k,
            lambda x: flow[t, k, x],
            lambda i: near[VELOCITY + t * 9 + k * 3 + i].astype(F32),
            lambda i: far[VELOCITY + t * 9 + k * 3 + i].astype(F32),
            3, even, wide,
        )
    for x in range(-1, CX + 1):
        grad = [[None] * 3 for _ in range(3)]
        for k in range(3):
            center = wide[k, x + 3]
            xs = [wide[k, x + 3 + step] for step in (1, -1, 2, -2)]
            grad[0][k] = fourth(*xs)
            if 0 <= x < CX:
                grad_x[k, x] = grad[0][k]
                lap_velocity[k, x] = lap_yz[k, x] + (xs[0] + xs[1])
                grad[1][k], grad[2][k] = grad_yz[k, 0, x], grad_yz[k, 1, x]
            else:
                grad[1][k] = 0.5 * (ops.y_up(center) - ops.y_down(center))
                grad[2][k] = fourth(*(turn(center, -step) for step in (1, -1, 2, -2)))
        strain = strain_of(grad)
        size = size_of(strain)
        if 0 <= x < CX:
            sizes[x] = size
        velocity = [wide[k, x + 3] for k in range(3)]
        for number, values in enumerate(filter_fields(velocity, strain, size)):
            fields[number, x + 1] = values
    for x in range(CX):
        for number in range(21):
            along_x = fields[number, x] + fields[number, x + 2] + 2.0 * fields[number, x + 1]
            hats[number, x] = turn(along_x, 1) + turn(along_x, -1) + 2.0 * along_x
    for k in range(3):
        block = jnp.zeros((ROWS, LANES), F32)
        for q in range(CX + 6):
            block = jnp.where(band == q, turn(wide[k, q], BAND * q + 11), block)
        high[k] = block
    for x in range(CX):
        cross, square = products_of(lambda number: hats[number, x])
        sums[0, x] = jnp.where(valid, cross, 0.0)
        sums[1, x] = jnp.where(valid, square, 0.0)


def edge_products(ops, t, low, high, halo, sums, bands, spread):
    band = band_of(ops.lane)
    place = ops.lane - BAND * band
    from_low = place < 3
    from_high = (place == 11) | (place < 2)
    low_side = place < 7
    at_edge = ((place >= 3) & (place <= 5)) | ((place >= 8) & (place <= 10))
    for k in range(3):
        number = 3 * t + k
        far = halo[number // 2].astype(F32)
        shift = 6 * (number % 2)
        bands[0, k] = jnp.where(from_low, turn(far, -shift), low[number])
        bands[1, k] = jnp.where(from_high, turn(far, 8 - shift), high[k])
    for side in range(2):
        velocity = [bands[side, k] for k in range(3)]
        grad = [[None] * 3 for _ in range(3)]
        for k in range(3):
            center = velocity[k]
            grad[0][k] = fourth(*(turn(center, -BAND * step) for step in (1, -1, 2, -2)))
            grad[1][k] = 0.5 * (ops.y_up(center) - ops.y_down(center))
            grad[2][k] = fourth(*(turn(center, -step) for step in (1, -1, 2, -2)))
        strain = strain_of(grad)
        for number, values in enumerate(filter_fields(velocity, strain, size_of(strain))):
            if side == 0:
                spread[number] = values
            else:
                spread[number] = jnp.where(low_side, spread[number], values)
    for number in range(21):
        both = spread[number]
        spread[number] = turn(both, BAND) + turn(both, -BAND) + 2.0 * both
    for number in range(21):
        both = spread[number]
        spread[number] = turn(both, 1) + turn(both, -1) + 2.0 * both
    for part, values in enumerate(products_of(lambda number: spread[number])):
        values = jnp.where(at_edge, values, 0.0)
        for x in range(CX):
            sums[part, x] = sums[part, x] + jnp.where(band == x + 3, values, 0.0)


def add_columns(ops, total, first_lane, planes, scale=1.0):
    for x in range(CX):
        value = scale * jnp.sum(planes(x), axis=1, keepdims=True)
        total = jnp.where(ops.lane == first_lane + x, value, total)
    return total


def add_parts(ops, block, total):
    upper = total.astype(BF16).astype(F32)
    rest = total - upper
    middle = rest.astype(BF16).astype(F32)
    for number, part in enumerate((upper, middle, rest - middle)):
        block = jnp.where(ops.lane >> 5 == 1 + number, turn(part, 32 * (1 + number)), block)
    return block


def span_total(add_other, columns, other):
    total = columns[...]
    if add_other:
        parts = other.astype(F32)
        total = total + ((turn(parts, -32) + turn(parts, -64)) + turn(parts, -96))
    return total


def psi_terms(psi_wide, rate_yz, lap_yz, velocity, x):
    rates, laps = [], []
    for k in range(5):
        xs = [psi_wide[k, x + 3 + step] for step in (1, -1, 2, -2)]
        rates.append(rate_yz[k, x] + velocity * fourth(*xs))
        laps.append(lap_yz[k, x] + (xs[0] + xs[1]))
    return rates, laps


def inner_kernel(
    flow, near, far, grad_yz, lap_yz,
    sums, high, wide, grad_x, lap_velocity, sizes,
    fields, hats,
):
    inner_products(
        Ops(), 0, flow, near, far, grad_yz, lap_yz,
        sums, high, wide, grad_x, lap_velocity, sizes, fields, hats,
    )


def first_kernel(
    _, rho, temp, psi, near, far, velocity, grad_x, lap_velocity, sizes,
    grad_yz, lap_yz, psi_rate, psi_lap,
    first, second, message, columns,
    wide, psi_wide, work,
):
    ops = Ops()
    even = is_even()
    for k in range(3):
        for x in range(CX):
            wide[k, x + 3] = velocity[k, x + 3]
    widen_scalars(0, rho, temp, near, far, even, wide)
    for k in range(5):
        widen(
            k,
            lambda x: psi[k, x],
            lambda i: near[PSI + k * 2 + i].astype(F32),
            lambda i: far[PSI + k * 2 + i].astype(F32),
            2, even, psi_wide,
        )
    for x in range(CX):
        terms = state_terms(wide, grad_x, grad_yz, lap_velocity, lap_yz, sizes, x)
        rates, laps = psi_terms(psi_wide, psi_rate, psi_lap, terms[0][0], x)
        new, slope, sensitivity = affine_update(
            terms, [psi[k, x] for k in range(5)], rates, laps
        )
        for k in range(5):
            first[k, x] = new[k]
            second[k, x] = slope[k]
        work[x] = sensitivity
    columns[...] = add_columns(ops, jnp.zeros((ROWS, LANES), F32), 16, lambda x: work[x])
    items = [[part[k, x] for x in range(CX)] for part in (first, second) for k in range(5)]
    for number in range(2):
        message[number] = pack_strips(ops, items[8 * number : 8 * number + 8])


def edge_kernel(
    low, high, halo, inner, strips, sensitivity, message, columns, bands, spread, sums
):
    ops = Ops()
    for part in range(2):
        for x in range(CX):
            sums[part, x] = inner[part, x]
    edge_products(ops, 0, low, high, halo, sums, bands, spread)
    total = sensitivity[...]
    for part in range(2):
        total = add_columns(ops, total, 4 * part, lambda x: sums[part, x], 1.0 / 256.0)
    columns[...] = total
    message[0] = strips[0].astype(BF16)
    message[1] = add_parts(ops, strips[1], total).astype(BF16)


def later_kernel(
    flow, rho, temp, near, far, near_scalars, far_scalars,
    grad_yz, lap_yz, low, halo, first, second,
    wide, grad_x, lap_velocity, sizes, message, columns,
    high, fields, hats, work, bands, spread, sums,
):
    ops = Ops()
    inner_products(
        ops, 1, flow, near, far, grad_yz, lap_yz,
        sums, high, wide, grad_x, lap_velocity, sizes, fields, hats,
    )
    widen_scalars(1, rho, temp, near_scalars, far_scalars, is_even(), wide)
    edge_products(ops, 1, low, high, halo, sums, bands, spread)
    for x in range(CX):
        _, _, lap, size, inv_rho = state_terms(
            wide, grad_x, grad_yz, lap_velocity, lap_yz, sizes, x
        )
        size_rho = size * inv_rho
        for part, source in enumerate((first, second)):
            total = lap[0] * source[0, x] + lap[1] * source[1, x] + lap[2] * source[2, x]
            work[part, x] = size_rho * (
                total + (1.0 / PRANDTL_TURB) * (lap[4] * source[4, x])
            )
    total = jnp.zeros((ROWS, LANES), F32)
    for part in range(2):
        total = add_columns(ops, total, 8 + 4 * part, lambda x: sums[part, x], 1.0 / 256.0)
        total = add_columns(ops, total, 20 + 4 * part, lambda x: work[part, x])
    columns[...] = total
    message[0] = add_parts(ops, jnp.zeros((ROWS, LANES), F32), total).astype(BF16)


def coefficients(ops, total):
    return total / (turn(total, -4) + EPSILON)


def middle_kernel(add_other, first, second, columns, other, psi, far, coef_first):
    ops = Ops()
    coef = coefficients(ops, span_total(add_other, columns, other[1]))
    for x in range(CX):
        coef_first[x] = jnp.broadcast_to(coef[:, x : x + 1], (ROWS, LANES))
    for x in range(CX):
        for k in range(5):
            psi[k, x] = first[k, x] + coef_first[x] * second[k, x]
    side = 1 - is_even().astype(jnp.int32)
    for k in range(5):
        for i in range(2):
            far[k, i] = psi[k, 2 * side + i].astype(BF16)


def base_kernel(
    add_other, span_cells,
    wide, grad_x, lap_velocity, sizes, grad_yz, lap_yz, psi, coef_first,
    columns, other, later, later_other,
    base, drift, spread, coef_grad, near,
    psi_halos, psi_wide, coef_planes, psi_rate, psi_lap,
):
    ops = Ops()
    side = is_even().astype(jnp.int32)
    for k in range(5):
        for i in range(2):
            near[k, i] = psi[k, 2 * side + i].astype(BF16)
    strips = [other[number].astype(F32) for number in range(2)]
    for k in range(5):
        for x in range(CX):
            psi_halos[k, x] = ops.strip(strips, k, x)
    total = span_total(add_other, columns, other[1]) + span_total(
        add_other, later, later_other[0]
    )
    coef = coefficients(ops, total)
    after = total + turn(coef, 20) * turn(total, -4)
    grads = jnp.where(ops.lane < 20, total, after) * (1.0 / span_cells)
    turned = jnp.concatenate([grads] * (LANES // ROWS), axis=0).T
    for t in range(2):
        coef_grad[t] = turned[16 + 4 * t : 20 + 4 * t, :ROWS]
    for x in range(CX):
        coef_planes[x] = jnp.broadcast_to(coef[:, 8 + x : 9 + x], (ROWS, LANES))
    for k in range(5):
        for x in range(CX):
            psi_halos[k, x] = psi_halos[k, x] + coef_first[x] * ops.strip(strips, 5 + k, x)
    zero = jnp.zeros((ROWS, LANES), F32)
    for k in range(5):
        for i in range(2):
            psi_wide[k, 1 + i] = zero
            psi_wide[k, 3 + CX + i] = zero
        for x in range(CX):
            psi_wide[k, 3 + x] = psi[k, x]
    for x in range(CX):
        for k in range(5):
            by_y, lap = y_terms(ops, psi[k, x])
            by_z, both = z_terms(ops, psi[k, x], psi_halos[k, x])
            psi_rate[k, x] = wide[1, x + 3] * by_y + wide[2, x + 3] * by_z
            psi_lap[k, x] = lap + both
    for x in range(CX):
        terms = state_terms(wide, grad_x, grad_yz, lap_velocity, lap_yz, sizes, x)
        center = terms[0]
        rates, laps = psi_terms(psi_wide, psi_rate, psi_lap, center[0], x)
        new, slope, _ = affine_update(terms, [psi[k, x] for k in range(5)], rates, laps)
        for k in range(5):
            base[k, x] = new[k] + coef_planes[x] * slope[k]
        size, inv_rho = terms[3:]
        drift[x] = TIME_STEP * center[0]
        if x in (0, CX - 1):
            eddy = coef_planes[x] * size
            scaled = TIME_STEP * inv_rho
            spread[x // (CX - 1), 0] = scaled * (NU_MOL + eddy)
            spread[x // (CX - 1), 1] = scaled * (
                NU_MOL / PRANDTL + (1.0 / PRANDTL_TURB) * eddy
            )


def widen_kernel(far, out):
    for k in range(5):
        for i in range(2):
            out[k, i] = far[k, i].astype(F32)


def last_kernel(base, drift, spread, near_psi, far_psi, out):
    even = is_even()
    for k in range(5):
        ones = [near_psi[k, i].astype(F32) for i in range(2)]
        twos = [far_psi[k, i].astype(F32) for i in range(2)]
        far, near = (jnp.where(even, two, one) for one, two in zip(ones, twos))
        after, beyond = (jnp.where(even, one, two) for one, two in zip(ones, twos))
        low = drift[0] * ((1.0 / 12.0) * far - (2.0 / 3.0) * near)
        high = drift[CX - 1] * ((2.0 / 3.0) * after - (1.0 / 12.0) * beyond)
        if k != 3:
            kind = 1 if k == 4 else 0
            low = low + spread[0, kind] * near
            high = high + spread[1, kind] * after
        out[k, 0] = base[k, 0] + low
        out[k, 1] = base[k, 1] + drift[1] * ((1.0 / 12.0) * near)
        out[k, CX - 2] = base[k, CX - 2] - drift[CX - 2] * ((1.0 / 12.0) * after)
        out[k, CX - 1] = base[k, CX - 1] + high


def ring(axis):
    count = lax.axis_size(axis)
    forward = [(i, (i + 1) % count) for i in range(count)]
    return forward, [(target, source) for source, target in forward]


def pairs():
    count = lax.axis_size("gx")
    if count % 2:
        raise ValueError("odd gx")
    inside = [(i, i ^ 1) for i in range(count)]
    across = [(i, (i + 1 if i % 2 else i - 1) % count) for i in range(count)]
    return inside, across


def span_edges(message, strips):
    forward, backward = ring("gz")
    before = lax.ppermute(message, "gz", forward)
    if lax.axis_size("gz") == 2:
        return before
    after = lax.ppermute(message, "gz", backward)
    lane = lax.broadcasted_iota(jnp.int32, message.shape, 2)
    number = lax.broadcasted_iota(jnp.int32, message.shape, 0)
    low = jnp.where(number < strips, lane % STRIP < 2, lane % 6 < 3)
    return jnp.where(low, before, after)


def shape_of(dims, kind=F32):
    return jax.ShapeDtypeStruct(dims + (ROWS, LANES), kind)


def whole(count):
    return [pl.BlockSpec(memory_space=pltpu.VMEM)] * count


def scratch(*dims):
    return [pltpu.VMEM(d + (ROWS, LANES), F32) for d in dims]


def call(kernel, name, inputs, outputs, operations, buffers=(), in_specs=None):
    inputs = list(inputs)
    if in_specs:
        inputs[:4] = [
            pltpu.with_memory_space_constraint(a, pltpu.MemorySpace.HBM) for a in inputs[:4]
        ]
    size = sum(math.prod(a.shape) * a.dtype.itemsize for a in list(inputs) + list(outputs))
    return pl.pallas_call(
        kernel,
        in_specs=in_specs or whole(len(inputs)),
        out_specs=whole(len(outputs)),
        out_shape=list(outputs),
        scratch_shapes=list(buffers),
        compiler_params=pltpu.CompilerParams(vmem_limit_bytes=8 * 2**20),
        cost_estimate=pl.CostEstimate(
            flops=operations, bytes_accessed=size, transcendentals=0
        ),
        name=name,
    )(*inputs)


def span_sums(columns):
    if lax.axis_size("gz") == 2:
        return columns
    return lax.psum(columns, "gz")


def local(flow_far, rho_far, temp_far, psi_far):
    inside, across = pairs()
    add_other = lax.axis_size("gz") == 2
    field, planes, edges = shape_of((5, CX)), shape_of((5, CX + 6)), shape_of((5, 2), BF16)
    slopes = shape_of((5, 2, CX))
    inputs = (flow_far, rho_far, temp_far, psi_far)
    stay = [pl.BlockSpec(memory_space=pltpu.MemorySpace.HBM)] * 4
    far, far_scalars, flow, rho, temp, psi = call(
        message_kernel,
        "message",
        inputs,
        [
            shape_of((SCALARS,), BF16),
            shape_of((SCALAR_PLANES,), BF16),
            shape_of((2, 3, CX), BF16),
            shape_of((2, CX), BF16),
            shape_of((2, CX), BF16),
            field,
        ],
        1_000_000,
        [pltpu.SemaphoreType.DMA((5,))],
        stay,
    )
    far = lax.ppermute(far, "gx", across)
    near, near_scalars, message, own_low = call(
        pack_kernel,
        "pack",
        (flow, rho, temp, psi),
        [
            shape_of((SCALARS,), BF16),
            shape_of((SCALAR_PLANES,), BF16),
            shape_of((STRIP_BLOCKS + BAND_BLOCKS,), BF16),
            shape_of((6,)),
        ],
        2_000_000,
    )
    far_scalars = lax.ppermute(far_scalars, "gx", across)
    near = lax.ppermute(near, "gx", inside)
    near_scalars = lax.ppermute(near_scalars, "gx", inside)
    own_halo = span_edges(message, STRIP_BLOCKS)
    rows = call(
        rows_kernel,
        "rows",
        (flow, rho, temp, psi),
        [field] * 6,
        3_000_000,
    )
    grad_0, grad_1, lap_0, lap_1, psi_rate, psi_lap = call(
        own_kernel,
        "own",
        (flow, rho, temp, psi, own_halo, *rows),
        [slopes, slopes, field, field, field, field],
        5_000_000,
        scratch((2, 5, CX), (5, CX)),
    )
    (token,) = call(token_kernel, "token", (far, rows[5]), [shape_of(())], 100_000)
    message, low = call(
        bands_kernel,
        "bands",
        (own_low, near, far, token),
        [shape_of((BAND_BLOCKS,), BF16), shape_of((6,))],
        1_000_000,
    )
    halo = span_edges(message, 0)
    inner, high, velocity, grad_x, lap_velocity, sizes = call(
        inner_kernel,
        "inner",
        (flow, near, far, grad_0, lap_0),
        [
            shape_of((2, CX)), shape_of((3,)), shape_of((3, CX + 6)),
            shape_of((3, CX)), shape_of((3, CX)), shape_of((CX,)),
        ],
        20_000_000,
        scratch((21, CX + 2), (21, CX)),
    )
    (token,) = call(token_kernel, "later_token", (far_scalars, sizes), [shape_of(())], 100_000)
    first, second, strips, sensitivity = call(
        first_kernel,
        "first",
        (
            token, rho, temp, psi, near_scalars, far_scalars,
            velocity, grad_x, lap_velocity, sizes,
            grad_0, lap_0, psi_rate, psi_lap,
        ),
        [field, field, shape_of((2,)), shape_of(())],
        10_000_000,
        scratch((5, CX + 6), (5, CX + 6), (CX,)),
    )
    message, columns = call(
        edge_kernel,
        "edge",
        (low, high, halo, inner, strips, sensitivity),
        [shape_of((2,), BF16), shape_of(())],
        20_000_000,
        scratch((2, 3), (21,), (2, CX)),
    )
    other = span_edges(message, 2)
    columns = span_sums(columns)
    wide, grad_x, lap_velocity, sizes, message, later = call(
        later_kernel,
        "later",
        (
            flow, rho, temp, near, far, near_scalars, far_scalars,
            grad_1, lap_1, low, halo, first, second,
        ),
        [
            planes, shape_of((3, CX)), shape_of((3, CX)), shape_of((CX,)),
            shape_of((1,), BF16), shape_of(()),
        ],
        20_000_000,
        scratch((3,), (21, CX + 2), (21, CX), (2, CX), (2, 3), (21,), (2, CX)),
    )
    later_other = span_edges(message, 1)
    later = span_sums(later)
    first, later = lax.optimization_barrier((first, later))
    psi, far, coef_first = call(
        functools.partial(middle_kernel, add_other),
        "middle",
        (first, second, columns, other),
        [field, edges, shape_of((CX,))],
        1_000_000,
    )
    far = lax.ppermute(far, "gx", across)
    base, drift, spread, coef_grad, near = call(
        functools.partial(base_kernel, add_other, LANES * lax.axis_size("gz")),
        "base",
        (
            wide, grad_x, lap_velocity, sizes, grad_1, lap_1, psi, coef_first,
            columns, other, later, later_other,
        ),
        [
            field, shape_of((CX,)), shape_of((2, 2)),
            jax.ShapeDtypeStruct((2, CX, ROWS), F32), edges,
        ],
        15_000_000,
        scratch((5, CX), (5, CX + 6), (CX,), (5, CX), (5, CX)),
    )
    near = lax.ppermute(near, "gx", inside)
    (far,) = call(widen_kernel, "widen", (far,), [shape_of((5, 2))], 100_000)
    (out,) = call(last_kernel, "last", (base, drift, spread, near, far), [field], 1_000_000)
    return out, coef_grad


def solution(mesh):
    return jax.shard_map(
        local,
        mesh=mesh,
        in_specs=(
            P(None, None, "gx", None, "gz"),
            P(None, "gx", None, "gz"),
            P(None, "gx", None, "gz"),
            P(None, "gx", None, "gz"),
        ),
        out_specs=(P(None, "gx", None, "gz"), P(None, "gx", None)),
        check_vma=False,
    )
```

```python
import functools
import math

import jax
import jax.numpy as jnp
from jax import lax
from jax.experimental import pallas as pl
from jax.experimental.pallas import tpu as pltpu
from jax.sharding import PartitionSpec as P

EPSILON = 1e-06
NU_MOL = 0.05
PRANDTL = 0.72
PRANDTL_TURB = 0.9
TIME_STEP = 0.04
PAIRS = ((0, 0), (1, 1), (2, 2), (0, 1), (0, 2), (1, 2))
WEIGHTS = (1.0, 1.0, 1.0, 2.0, 2.0, 2.0)

CX = 4
ROWS = 32
LANES = 128
STRIP = 4
F32 = jnp.float32
BF16 = jnp.bfloat16
SLOT_PSI = 4
BAND = 12
STRIP_BLOCKS = 2
BAND_BLOCKS = 3
VELOCITY = 0
SCALARS = 18
MESSAGE = 22
PSI = 4
SCALAR_PLANES = 14


def lane_ids():
    return lax.broadcasted_iota(jnp.int32, (ROWS, LANES), 1)


def row_ids():
    return lax.broadcasted_iota(jnp.int32, (ROWS, LANES), 0)


def turn(values, shift):
    shift = shift % LANES
    return values if shift == 0 else pltpu.roll(values, shift, 1)


class Ops:
    def __init__(self):
        self.lane = lane_ids()
        row = row_ids()
        self.top = row == ROWS - 1
        self.bottom = row == 0

    def z_at(self, values, halo, step):
        if step > 0:
            return turn(jnp.where(self.lane < step, halo, values), -step)
        return turn(jnp.where(self.lane >= LANES + step, halo, values), -step)

    def y_up(self, values):
        return jnp.where(self.top, 0.0, pltpu.roll(values, ROWS - 1, 0))

    def y_down(self, values):
        return jnp.where(self.bottom, 0.0, pltpu.roll(values, 1, 0))

    def strip(self, blocks, slot, x):
        return turn(blocks[slot // 8], -(STRIP * (4 * (slot % 8) + x) + 2))


def fourth(plus, minus, plus_2, minus_2):
    return (2.0 / 3.0) * (plus - minus) - (1.0 / 12.0) * (plus_2 - minus_2)


def strain_of(grad):
    return [
        grad[0][0],
        grad[1][1],
        grad[2][2],
        0.5 * (grad[0][1] + grad[1][0]),
        0.5 * (grad[0][2] + grad[2][0]),
        0.5 * (grad[1][2] + grad[2][1]),
    ]


def size_of(strain):
    diagonal = strain[0] * strain[0] + strain[1] * strain[1] + strain[2] * strain[2]
    other = strain[3] * strain[3] + strain[4] * strain[4] + strain[5] * strain[5]
    return jnp.sqrt(2.0 * diagonal + (4.0 * other + EPSILON))


def filter_fields(velocity, strain, size):
    products = [velocity[a] * velocity[b] for a, b in PAIRS]
    return list(velocity) + products + strain + [size * part for part in strain]


def pack_strips(ops, items):
    block = jnp.zeros((ROWS, LANES), F32)
    strip_id = ops.lane >> 2
    for slot, planes in enumerate(items):
        for x in range(CX):
            number = 4 * slot + x
            block = jnp.where(strip_id == number, turn(planes[x], STRIP * number + 2), block)
    return block


def place_halos(ops, t, own_halo, halos):
    strips = [own_halo[number].astype(F32) for number in range(STRIP_BLOCKS)]
    for k in range(3):
        number = 3 * t + k
        bands = own_halo[STRIP_BLOCKS + number // 2].astype(F32)
        for x in range(CX):
            halos[k, x] = turn(bands, -(BAND * (x + 3) + 3 + 6 * (number % 2)))
    for k in range(3, 5):
        for x in range(CX):
            halos[k, x] = ops.strip(strips, 2 * t + k - 3, x)


def y_terms(ops, values):
    up, down = ops.y_up(values), ops.y_down(values)
    return 0.5 * (up - down), (up + down) - 6.0 * values


def z_terms(ops, values, halo):
    zs = [ops.z_at(values, halo, step) for step in (1, -1, 2, -2)]
    return fourth(*zs), zs[0] + zs[1]


def state_terms(wide, grad_x, grad_yz, lap_velocity, lap_yz, sizes, x):
    grad = [[None] * 5 for _ in range(3)]
    lap = [None] * 5
    center = [wide[k, x + 3] for k in range(5)]
    for k in range(5):
        if k < 3:
            grad[0][k], lap[k] = grad_x[k, x], lap_velocity[k, x]
        else:
            xs = [wide[k, x + 3 + step] for step in (1, -1, 2, -2)]
            grad[0][k] = fourth(*xs)
            lap[k] = lap_yz[k, x] + (xs[0] + xs[1])
        grad[1][k], grad[2][k] = grad_yz[k, 0, x], grad_yz[k, 1, x]
    return center, grad, lap, sizes[x], 1.0 / center[3]


def affine_update(terms, psi, rates, laps):
    center, grad, lap, size, inv_rho = terms
    work_mom = psi[0] * lap[0] + psi[1] * lap[1] + psi[2] * lap[2]
    work_heat = psi[4] * lap[4]
    turbulent = work_mom + work_heat * (1.0 / PRANDTL_TURB)
    inv_rho_2 = inv_rho * inv_rho
    size_rho = size * inv_rho
    first, second = [], []
    for k in range(5):
        rate = rates[k]
        if k == 3:
            rate = rate - (NU_MOL * work_mom + (NU_MOL / PRANDTL) * work_heat) * inv_rho_2
            eddy = -(size * turbulent) * inv_rho_2
        else:
            lap_psi = laps[k]
            if k < 3:
                for other in range(5):
                    rate = rate + psi[other] * grad[k][other]
                rate = rate + NU_MOL * (inv_rho * lap_psi)
                eddy = size_rho * lap_psi
            else:
                rate = rate + (NU_MOL / PRANDTL) * (inv_rho * lap_psi)
                eddy = (1.0 / PRANDTL_TURB) * (size_rho * lap_psi)
        first.append(psi[k] + TIME_STEP * rate)
        second.append(TIME_STEP * eddy)
    return first, second, size_rho * turbulent


def band_of(lane):
    return (lane * 43) >> 9


def is_even():
    return lax.rem(lax.axis_index("gx"), 2) == 0


def fill_scalars(out, side, rho, temp, psi):
    for i in range(2):
        out[i] = rho[0, 2 * side + i]
        out[2 + i] = temp[0, 2 * side + i]
    for k in range(5):
        for i in range(2):
            out[PSI + k * 2 + i] = psi[k, 2 * side + i].astype(BF16)


def merge_bands(ops, low, message, first):
    lower = ops.lane - BAND * band_of(ops.lane) < 6
    for number in range(BAND_BLOCKS):
        both = jnp.where(lower, low[2 * number], turn(low[2 * number + 1], 6))
        message[first + number] = both.astype(BF16)


def fill_later(out, side, rho, temp):
    for i in range(2):
        out[SCALARS + i] = rho[1, 2 * side + i]
        out[SCALARS + 2 + i] = temp[1, 2 * side + i]


def message_kernel(
    flow_far, rho_far, temp_far, psi_far, far, far_scalars, flow, rho, temp, psi, sems
):
    side = 1 - is_even().astype(jnp.int32)
    pieces = (
        (
            flow_far.at[:, :, pl.ds(side, 3)],
            far.at[pl.ds(VELOCITY, 18)].reshape((2, 3, 3, ROWS, LANES)),
        ),
        (psi_far, psi),
        (rho_far, rho),
        (temp_far, temp),
        (flow_far, flow),
    )
    copies = [
        pltpu.make_async_copy(source, target, sems.at[number])
        for number, (source, target) in enumerate(pieces)
    ]
    for copy in copies:
        copy.start()
    for copy in copies[1:4]:
        copy.wait()
    fill_scalars(far_scalars, side, rho, temp, psi)
    fill_later(far, side, rho, temp)
    copies[0].wait()
    copies[4].wait()


def pack_kernel(flow, rho, temp, psi, near, near_scalars, message, low):
    ops = Ops()
    side = is_even().astype(jnp.int32)
    for t in range(2):
        for k in range(3):
            for i in range(3):
                near[VELOCITY + t * 9 + k * 3 + i] = flow[t, k, side + i]
    fill_scalars(near_scalars, side, rho, temp, psi)
    fill_later(near, side, rho, temp)
    items = []
    for t in range(2):
        for source in (rho, temp):
            items.append([source[t, x].astype(F32) for x in range(CX)])
    items += [[psi[k, x] for x in range(CX)] for k in range(5)]
    for number in range(STRIP_BLOCKS):
        message[number] = pack_strips(ops, items[8 * number : 8 * number + 8]).astype(BF16)
    band = band_of(ops.lane)
    for t in range(2):
        for k in range(3):
            block = jnp.zeros((ROWS, LANES), F32)
            for x in range(CX):
                moved = turn(flow[t, k, x].astype(F32), BAND * (x + 3) + 3)
                block = jnp.where(band == x + 3, moved, block)
            low[3 * t + k] = block
    merge_bands(ops, low, message, STRIP_BLOCKS)


def rows_kernel(flow, rho, temp, psi, grad_0, grad_1, lap_0, lap_1, psi_rate, psi_lap):
    ops = Ops()
    for t, grad_y, lap_y in ((0, grad_0, lap_0), (1, grad_1, lap_1)):
        for k in range(5):
            for x in range(CX):
                values = flow[t, k, x] if k < 3 else (rho if k == 3 else temp)[t, x]
                grad_y[k, x], lap_y[k, x] = y_terms(ops, values.astype(F32))
    for x in range(CX):
        along_y = flow[0, 1, x].astype(F32)
        for k in range(5):
            by_y, psi_lap[k, x] = y_terms(ops, psi[k, x])
            psi_rate[k, x] = along_y * by_y


def own_kernel(
    flow, rho, temp, psi, own_halo, grad_y_0, grad_y_1, lap_y_0, lap_y_1, rate_y, psi_lap_y,
    grad_0, grad_1, lap_0, lap_1, psi_rate, psi_lap,
    halos, psi_halos,
):
    ops = Ops()
    for t in range(2):
        place_halos(ops, t, own_halo, halos.at[t])
    strips = [own_halo[number].astype(F32) for number in range(STRIP_BLOCKS)]
    for k in range(5):
        for x in range(CX):
            psi_halos[k, x] = ops.strip(strips, SLOT_PSI + k, x)
    for t, grad_y, lap_y, grad_yz, lap_yz in (
        (0, grad_y_0, lap_y_0, grad_0, lap_0),
        (1, grad_y_1, lap_y_1, grad_1, lap_1),
    ):
        for k in range(5):
            for x in range(CX):
                values = flow[t, k, x] if k < 3 else (rho if k == 3 else temp)[t, x]
                by_z, both = z_terms(ops, values.astype(F32), halos[t, k, x])
                grad_yz[k, 0, x], grad_yz[k, 1, x] = grad_y[k, x], by_z
                lap_yz[k, x] = lap_y[k, x] + both
    for x in range(CX):
        along_z = flow[0, 2, x].astype(F32)
        for k in range(5):
            by_z, both = z_terms(ops, psi[k, x], psi_halos[k, x])
            psi_rate[k, x] = rate_y[k, x] + along_z * by_z
            psi_lap[k, x] = psi_lap_y[k, x] + both


def token_kernel(far, _, out):
    out[...] = far[0].astype(F32)


def bands_kernel(own_low, near, far, _, message, low):
    ops = Ops()
    even = is_even()
    band = band_of(ops.lane)
    for t in range(2):
        for k in range(3):
            block = own_low[3 * t + k]
            for i in range(3):
                number = VELOCITY + t * 9 + k * 3 + i
                one, two = near[number].astype(F32), far[number].astype(F32)
                moved = turn(jnp.where(even, two, one), BAND * i + 3)
                block = jnp.where(band == i, moved, block)
                moved = turn(jnp.where(even, one, two), BAND * (7 + i) + 3)
                block = jnp.where(band == 7 + i, moved, block)
            low[3 * t + k] = block
    merge_bands(ops, low, message, 0)


def products_of(hat):
    velocity = [hat(k) for k in range(3)]
    strain = [hat(9 + number) for number in range(6)]
    diagonal = strain[0] * strain[0] + strain[1] * strain[1] + strain[2] * strain[2]
    other = strain[3] * strain[3] + strain[4] * strain[4] + strain[5] * strain[5]
    size = 4.0 * jnp.sqrt((2.0 / 256.0) * diagonal + ((4.0 / 256.0) * other + EPSILON))
    cross = 0.0
    square = 0.0
    for number, (a, b) in enumerate(PAIRS):
        leonard = hat(3 + number) - (1.0 / 16.0) * velocity[a] * velocity[b]
        model = hat(15 + number) - size * strain[number]
        weighted = WEIGHTS[number] * model if WEIGHTS[number] != 1.0 else model
        cross = cross + leonard * weighted
        square = square + model * weighted
    return cross, square


def widen(k, source, near, far, count, even, wide):
    for i in range(count):
        one, two = near(i), far(i)
        wide[k, 3 - count + i] = jnp.where(even, two, one)
        wide[k, 3 + CX + i] = jnp.where(even, one, two)
    for x in range(CX):
        wide[k, 3 + x] = source(x).astype(F32)


def widen_scalars(t, first, rho, temp, near, far, even, wide):
    for k, source in ((3, rho), (4, temp)):
        number = first + (k - 3) * 2
        widen(
            k,
            lambda x: source[t, x],
            lambda i: near[number + i].astype(F32),
            lambda i: far[number + i].astype(F32),
            2, even, wide,
        )


def inner_products(
    ops, t, flow, near, far, grad_yz, lap_yz,
    sums, high, wide, grad_x, lap_velocity, sizes, fields, hats,
):
    even = is_even()
    valid = (ops.lane >= 3) & (ops.lane < LANES - 3)
    band = band_of(jnp.maximum(ops.lane - 2, 0))
    for k in range(3):
        widen(
            k,
            lambda x: flow[t, k, x],
            lambda i: near[VELOCITY + t * 9 + k * 3 + i].astype(F32),
            lambda i: far[VELOCITY + t * 9 + k * 3 + i].astype(F32),
            3, even, wide,
        )
    for x in range(-1, CX + 1):
        grad = [[None] * 3 for _ in range(3)]
        for k in range(3):
            center = wide[k, x + 3]
            xs = [wide[k, x + 3 + step] for step in (1, -1, 2, -2)]
            grad[0][k] = fourth(*xs)
            if 0 <= x < CX:
                grad_x[k, x] = grad[0][k]
                lap_velocity[k, x] = lap_yz[k, x] + (xs[0] + xs[1])
                grad[1][k], grad[2][k] = grad_yz[k, 0, x], grad_yz[k, 1, x]
            else:
                grad[1][k] = 0.5 * (ops.y_up(center) - ops.y_down(center))
                grad[2][k] = fourth(*(turn(center, -step) for step in (1, -1, 2, -2)))
        strain = strain_of(grad)
        size = size_of(strain)
        if 0 <= x < CX:
            sizes[x] = size
        velocity = [wide[k, x + 3] for k in range(3)]
        for number, values in enumerate(filter_fields(velocity, strain, size)):
            fields[number, x + 1] = values
    for x in range(CX):
        for number in range(21):
            along_x = fields[number, x] + fields[number, x + 2] + 2.0 * fields[number, x + 1]
            hats[number, x] = turn(along_x, 1) + turn(along_x, -1) + 2.0 * along_x
    for k in range(3):
        block = jnp.zeros((ROWS, LANES), F32)
        for q in range(CX + 6):
            block = jnp.where(band == q, turn(wide[k, q], BAND * q + 11), block)
        high[k] = block
    for x in range(CX):
        cross, square = products_of(lambda number: hats[number, x])
        sums[0, x] = jnp.where(valid, cross, 0.0)
        sums[1, x] = jnp.where(valid, square, 0.0)


def edge_products(ops, t, low, high, halo, sums, bands, spread):
    band = band_of(ops.lane)
    place = ops.lane - BAND * band
    from_low = place < 3
    from_high = (place == 11) | (place < 2)
    low_side = place < 7
    at_edge = ((place >= 3) & (place <= 5)) | ((place >= 8) & (place <= 10))
    for k in range(3):
        number = 3 * t + k
        far = halo[number // 2].astype(F32)
        shift = 6 * (number % 2)
        bands[0, k] = jnp.where(from_low, turn(far, -shift), low[number])
        bands[1, k] = jnp.where(from_high, turn(far, 8 - shift), high[k])
    for side in range(2):
        velocity = [bands[side, k] for k in range(3)]
        grad = [[None] * 3 for _ in range(3)]
        for k in range(3):
            center = velocity[k]
            grad[0][k] = fourth(*(turn(center, -BAND * step) for step in (1, -1, 2, -2)))
            grad[1][k] = 0.5 * (ops.y_up(center) - ops.y_down(center))
            grad[2][k] = fourth(*(turn(center, -step) for step in (1, -1, 2, -2)))
        strain = strain_of(grad)
        for number, values in enumerate(filter_fields(velocity, strain, size_of(strain))):
            if side == 0:
                spread[number] = values
            else:
                spread[number] = jnp.where(low_side, spread[number], values)
    for number in range(21):
        both = spread[number]
        spread[number] = turn(both, BAND) + turn(both, -BAND) + 2.0 * both
    for number in range(21):
        both = spread[number]
        spread[number] = turn(both, 1) + turn(both, -1) + 2.0 * both
    for part, values in enumerate(products_of(lambda number: spread[number])):
        values = jnp.where(at_edge, values, 0.0)
        for x in range(CX):
            sums[part, x] = sums[part, x] + jnp.where(band == x + 3, values, 0.0)


def add_columns(ops, total, first_lane, planes, scale=1.0):
    for x in range(CX):
        value = scale * jnp.sum(planes(x), axis=1, keepdims=True)
        total = jnp.where(ops.lane == first_lane + x, value, total)
    return total


def add_parts(ops, block, total):
    upper = total.astype(BF16).astype(F32)
    rest = total - upper
    middle = rest.astype(BF16).astype(F32)
    for number, part in enumerate((upper, middle, rest - middle)):
        block = jnp.where(ops.lane >> 5 == 1 + number, turn(part, 32 * (1 + number)), block)
    return block


def span_total(add_other, columns, other):
    total = columns[...]
    if add_other:
        parts = other.astype(F32)
        total = total + ((turn(parts, -32) + turn(parts, -64)) + turn(parts, -96))
    return total


def psi_terms(psi_wide, rate_yz, lap_yz, velocity, x):
    rates, laps = [], []
    for k in range(5):
        xs = [psi_wide[k, x + 3 + step] for step in (1, -1, 2, -2)]
        rates.append(rate_yz[k, x] + velocity * fourth(*xs))
        laps.append(lap_yz[k, x] + (xs[0] + xs[1]))
    return rates, laps


def inner_kernel(
    flow, near, far, grad_yz, lap_yz,
    sums, high, wide, grad_x, lap_velocity, sizes,
    fields, hats,
):
    inner_products(
        Ops(), 0, flow, near, far, grad_yz, lap_yz,
        sums, high, wide, grad_x, lap_velocity, sizes, fields, hats,
    )


def first_kernel(
    _, rho, temp, psi, near, far, velocity, grad_x, lap_velocity, sizes,
    grad_yz, lap_yz, psi_rate, psi_lap,
    first, second, message, columns,
    wide, psi_wide, work,
):
    ops = Ops()
    even = is_even()
    for k in range(3):
        for x in range(CX):
            wide[k, x + 3] = velocity[k, x + 3]
    widen_scalars(0, 0, rho, temp, near, far, even, wide)
    for k in range(5):
        widen(
            k,
            lambda x: psi[k, x],
            lambda i: near[PSI + k * 2 + i].astype(F32),
            lambda i: far[PSI + k * 2 + i].astype(F32),
            2, even, psi_wide,
        )
    for x in range(CX):
        terms = state_terms(wide, grad_x, grad_yz, lap_velocity, lap_yz, sizes, x)
        rates, laps = psi_terms(psi_wide, psi_rate, psi_lap, terms[0][0], x)
        new, slope, sensitivity = affine_update(
            terms, [psi[k, x] for k in range(5)], rates, laps
        )
        for k in range(5):
            first[k, x] = new[k]
            second[k, x] = slope[k]
        work[x] = sensitivity
    columns[...] = add_columns(ops, jnp.zeros((ROWS, LANES), F32), 16, lambda x: work[x])
    items = [[part[k, x] for x in range(CX)] for part in (first, second) for k in range(5)]
    for number in range(2):
        message[number] = pack_strips(ops, items[8 * number : 8 * number + 8])


def edge_kernel(
    low, high, halo, inner, strips, sensitivity, message, columns, bands, spread, sums
):
    ops = Ops()
    for part in range(2):
        for x in range(CX):
            sums[part, x] = inner[part, x]
    edge_products(ops, 0, low, high, halo, sums, bands, spread)
    total = sensitivity[...]
    for part in range(2):
        total = add_columns(ops, total, 4 * part, lambda x: sums[part, x], 1.0 / 256.0)
    columns[...] = total
    message[0] = strips[0].astype(BF16)
    message[1] = add_parts(ops, strips[1], total).astype(BF16)


def later_kernel(
    flow, rho, temp, near, far, grad_yz, lap_yz, low, halo, first, second,
    wide, grad_x, lap_velocity, sizes, message, columns,
    high, fields, hats, work, bands, spread, sums,
):
    ops = Ops()
    inner_products(
        ops, 1, flow, near, far, grad_yz, lap_yz,
        sums, high, wide, grad_x, lap_velocity, sizes, fields, hats,
    )
    widen_scalars(1, SCALARS, rho, temp, near, far, is_even(), wide)
    edge_products(ops, 1, low, high, halo, sums, bands, spread)
    for x in range(CX):
        _, _, lap, size, inv_rho = state_terms(
            wide, grad_x, grad_yz, lap_velocity, lap_yz, sizes, x
        )
        size_rho = size * inv_rho
        for part, source in enumerate((first, second)):
            total = lap[0] * source[0, x] + lap[1] * source[1, x] + lap[2] * source[2, x]
            work[part, x] = size_rho * (
                total + (1.0 / PRANDTL_TURB) * (lap[4] * source[4, x])
            )
    total = jnp.zeros((ROWS, LANES), F32)
    for part in range(2):
        total = add_columns(ops, total, 8 + 4 * part, lambda x: sums[part, x], 1.0 / 256.0)
        total = add_columns(ops, total, 20 + 4 * part, lambda x: work[part, x])
    columns[...] = total
    message[0] = add_parts(ops, jnp.zeros((ROWS, LANES), F32), total).astype(BF16)


def coefficients(ops, total):
    return total / (turn(total, -4) + EPSILON)


def middle_kernel(add_other, first, second, columns, other, psi, far, coef_first):
    ops = Ops()
    coef = coefficients(ops, span_total(add_other, columns, other[1]))
    for x in range(CX):
        coef_first[x] = jnp.broadcast_to(coef[:, x : x + 1], (ROWS, LANES))
    for x in range(CX):
        for k in range(5):
            psi[k, x] = first[k, x] + coef_first[x] * second[k, x]
    side = 1 - is_even().astype(jnp.int32)
    for k in range(5):
        for i in range(2):
            far[k, i] = psi[k, 2 * side + i].astype(BF16)


def base_kernel(
    add_other, span_cells,
    wide, grad_x, lap_velocity, sizes, grad_yz, lap_yz, psi, coef_first,
    columns, other, later, later_other,
    base, drift, spread, coef_grad, near,
    psi_halos, psi_wide, coef_planes, psi_rate, psi_lap,
):
    ops = Ops()
    side = is_even().astype(jnp.int32)
    for k in range(5):
        for i in range(2):
            near[k, i] = psi[k, 2 * side + i].astype(BF16)
    strips = [other[number].astype(F32) for number in range(2)]
    for k in range(5):
        for x in range(CX):
            psi_halos[k, x] = ops.strip(strips, k, x)
    total = span_total(add_other, columns, other[1]) + span_total(
        add_other, later, later_other[0]
    )
    coef = coefficients(ops, total)
    after = total + turn(coef, 20) * turn(total, -4)
    grads = jnp.where(ops.lane < 20, total, after) * (1.0 / span_cells)
    turned = jnp.concatenate([grads] * (LANES // ROWS), axis=0).T
    for t in range(2):
        coef_grad[t] = turned[16 + 4 * t : 20 + 4 * t, :ROWS]
    for x in range(CX):
        coef_planes[x] = jnp.broadcast_to(coef[:, 8 + x : 9 + x], (ROWS, LANES))
    for k in range(5):
        for x in range(CX):
            psi_halos[k, x] = psi_halos[k, x] + coef_first[x] * ops.strip(strips, 5 + k, x)
    zero = jnp.zeros((ROWS, LANES), F32)
    for k in range(5):
        for i in range(2):
            psi_wide[k, 1 + i] = zero
            psi_wide[k, 3 + CX + i] = zero
        for x in range(CX):
            psi_wide[k, 3 + x] = psi[k, x]
    for x in range(CX):
        for k in range(5):
            by_y, lap = y_terms(ops, psi[k, x])
            by_z, both = z_terms(ops, psi[k, x], psi_halos[k, x])
            psi_rate[k, x] = wide[1, x + 3] * by_y + wide[2, x + 3] * by_z
            psi_lap[k, x] = lap + both
    for x in range(CX):
        terms = state_terms(wide, grad_x, grad_yz, lap_velocity, lap_yz, sizes, x)
        center = terms[0]
        rates, laps = psi_terms(psi_wide, psi_rate, psi_lap, center[0], x)
        new, slope, _ = affine_update(terms, [psi[k, x] for k in range(5)], rates, laps)
        for k in range(5):
            base[k, x] = new[k] + coef_planes[x] * slope[k]
        size, inv_rho = terms[3:]
        drift[x] = TIME_STEP * center[0]
        if x in (0, CX - 1):
            eddy = coef_planes[x] * size
            scaled = TIME_STEP * inv_rho
            spread[x // (CX - 1), 0] = scaled * (NU_MOL + eddy)
            spread[x // (CX - 1), 1] = scaled * (
                NU_MOL / PRANDTL + (1.0 / PRANDTL_TURB) * eddy
            )


def widen_kernel(far, out):
    for k in range(5):
        for i in range(2):
            out[k, i] = far[k, i].astype(F32)


def last_kernel(base, drift, spread, near_psi, far_psi, out_far, out, sems):
    even = is_even()
    copies = []
    for k in range(5):
        ones = [near_psi[k, i].astype(F32) for i in range(2)]
        twos = [far_psi[k, i].astype(F32) for i in range(2)]
        far, near = (jnp.where(even, two, one) for one, two in zip(ones, twos))
        after, beyond = (jnp.where(even, one, two) for one, two in zip(ones, twos))
        low = drift[0] * ((1.0 / 12.0) * far - (2.0 / 3.0) * near)
        high = drift[CX - 1] * ((2.0 / 3.0) * after - (1.0 / 12.0) * beyond)
        if k != 3:
            kind = 1 if k == 4 else 0
            low = low + spread[0, kind] * near
            high = high + spread[1, kind] * after
        out[k, 0] = base[k, 0] + low
        out[k, 1] = base[k, 1] + drift[1] * ((1.0 / 12.0) * near)
        out[k, CX - 2] = base[k, CX - 2] - drift[CX - 2] * ((1.0 / 12.0) * after)
        out[k, CX - 1] = base[k, CX - 1] + high
        copies.append(pltpu.make_async_copy(out.at[k], out_far.at[k], sems.at[k]))
        copies[k].start()
    for copy in copies:
        copy.wait()


def ring(axis):
    count = lax.axis_size(axis)
    forward = [(i, (i + 1) % count) for i in range(count)]
    return forward, [(target, source) for source, target in forward]


def pairs():
    count = lax.axis_size("gx")
    if count % 2:
        raise ValueError("odd gx")
    inside = [(i, i ^ 1) for i in range(count)]
    across = [(i, (i + 1 if i % 2 else i - 1) % count) for i in range(count)]
    return inside, across


def span_edges(message, strips):
    forward, backward = ring("gz")
    before = lax.ppermute(message, "gz", forward)
    if lax.axis_size("gz") == 2:
        return before
    after = lax.ppermute(message, "gz", backward)
    lane = lax.broadcasted_iota(jnp.int32, message.shape, 2)
    number = lax.broadcasted_iota(jnp.int32, message.shape, 0)
    low = jnp.where(number < strips, lane % STRIP < 2, lane % 6 < 3)
    return jnp.where(low, before, after)


def shape_of(dims, kind=F32):
    return jax.ShapeDtypeStruct(dims + (ROWS, LANES), kind)


def whole(count):
    return [pl.BlockSpec(memory_space=pltpu.VMEM)] * count


def scratch(*dims):
    return [pltpu.VMEM(d + (ROWS, LANES), F32) for d in dims]


def call(kernel, name, inputs, outputs, operations, buffers=(), in_specs=None, out_specs=None):
    inputs = list(inputs)
    if in_specs:
        inputs[:4] = [
            pltpu.with_memory_space_constraint(a, pltpu.MemorySpace.HBM) for a in inputs[:4]
        ]
    size = sum(math.prod(a.shape) * a.dtype.itemsize for a in list(inputs) + list(outputs))
    return pl.pallas_call(
        kernel,
        in_specs=in_specs or whole(len(inputs)),
        out_specs=out_specs or whole(len(outputs)),
        out_shape=list(outputs),
        scratch_shapes=list(buffers),
        compiler_params=pltpu.CompilerParams(vmem_limit_bytes=8 * 2**20),
        cost_estimate=pl.CostEstimate(
            flops=operations, bytes_accessed=size, transcendentals=0
        ),
        name=name,
    )(*inputs)


def span_sums(columns):
    if lax.axis_size("gz") == 2:
        return columns
    return lax.psum(columns, "gz")


def local(flow_far, rho_far, temp_far, psi_far):
    inside, across = pairs()
    add_other = lax.axis_size("gz") == 2
    field, planes, edges = shape_of((5, CX)), shape_of((5, CX + 6)), shape_of((5, 2), BF16)
    slopes = shape_of((5, 2, CX))
    inputs = (flow_far, rho_far, temp_far, psi_far)
    stay = [pl.BlockSpec(memory_space=pltpu.MemorySpace.HBM)] * 4
    far, far_scalars, flow, rho, temp, psi = call(
        message_kernel,
        "message",
        inputs,
        [
            shape_of((MESSAGE,), BF16),
            shape_of((SCALAR_PLANES,), BF16),
            shape_of((2, 3, CX), BF16),
            shape_of((2, CX), BF16),
            shape_of((2, CX), BF16),
            field,
        ],
        1_000_000,
        [pltpu.SemaphoreType.DMA((5,))],
        stay,
    )
    far = lax.ppermute(far, "gx", across)
    near, near_scalars, message, own_low = call(
        pack_kernel,
        "pack",
        (flow, rho, temp, psi),
        [
            shape_of((MESSAGE,), BF16),
            shape_of((SCALAR_PLANES,), BF16),
            shape_of((STRIP_BLOCKS + BAND_BLOCKS,), BF16),
            shape_of((6,)),
        ],
        2_000_000,
    )
    far_scalars = lax.ppermute(far_scalars, "gx", across)
    near = lax.ppermute(near, "gx", inside)
    near_scalars = lax.ppermute(near_scalars, "gx", inside)
    own_halo = span_edges(message, STRIP_BLOCKS)
    rows = call(
        rows_kernel,
        "rows",
        (flow, rho, temp, psi),
        [field] * 6,
        3_000_000,
    )
    grad_0, grad_1, lap_0, lap_1, psi_rate, psi_lap = call(
        own_kernel,
        "own",
        (flow, rho, temp, psi, own_halo, *rows),
        [slopes, slopes, field, field, field, field],
        5_000_000,
        scratch((2, 5, CX), (5, CX)),
    )
    (token,) = call(token_kernel, "token", (far, rows[5]), [shape_of(())], 100_000)
    message, low = call(
        bands_kernel,
        "bands",
        (own_low, near, far, token),
        [shape_of((BAND_BLOCKS,), BF16), shape_of((6,))],
        1_000_000,
    )
    halo = span_edges(message, 0)
    inner, high, velocity, grad_x, lap_velocity, sizes = call(
        inner_kernel,
        "inner",
        (flow, near, far, grad_0, lap_0),
        [
            shape_of((2, CX)), shape_of((3,)), shape_of((3, CX + 6)),
            shape_of((3, CX)), shape_of((3, CX)), shape_of((CX,)),
        ],
        20_000_000,
        scratch((21, CX + 2), (21, CX)),
    )
    (token,) = call(token_kernel, "later_token", (far_scalars, sizes), [shape_of(())], 100_000)
    first, second, strips, sensitivity = call(
        first_kernel,
        "first",
        (
            token, rho, temp, psi, near_scalars, far_scalars,
            velocity, grad_x, lap_velocity, sizes,
            grad_0, lap_0, psi_rate, psi_lap,
        ),
        [field, field, shape_of((2,)), shape_of(())],
        10_000_000,
        scratch((5, CX + 6), (5, CX + 6), (CX,)),
    )
    message, columns = call(
        edge_kernel,
        "edge",
        (low, high, halo, inner, strips, sensitivity),
        [shape_of((2,), BF16), shape_of(())],
        20_000_000,
        scratch((2, 3), (21,), (2, CX)),
    )
    other = span_edges(message, 2)
    columns = span_sums(columns)
    wide, grad_x, lap_velocity, sizes, message, later = call(
        later_kernel,
        "later",
        (
            flow, rho, temp, near, far, grad_1, lap_1, low, halo, first, second,
        ),
        [
            planes, shape_of((3, CX)), shape_of((3, CX)), shape_of((CX,)),
            shape_of((1,), BF16), shape_of(()),
        ],
        20_000_000,
        scratch((3,), (21, CX + 2), (21, CX), (2, CX), (2, 3), (21,), (2, CX)),
    )
    later_other = span_edges(message, 1)
    later = span_sums(later)
    first, later = lax.optimization_barrier((first, later))
    psi, far, coef_first = call(
        functools.partial(middle_kernel, add_other),
        "middle",
        (first, second, columns, other),
        [field, edges, shape_of((CX,))],
        1_000_000,
    )
    far = lax.ppermute(far, "gx", across)
    base, drift, spread, coef_grad, near = call(
        functools.partial(base_kernel, add_other, LANES * lax.axis_size("gz")),
        "base",
        (
            wide, grad_x, lap_velocity, sizes, grad_1, lap_1, psi, coef_first,
            columns, other, later, later_other,
        ),
        [
            field, shape_of((CX,)), shape_of((2, 2)),
            jax.ShapeDtypeStruct((2, CX, ROWS), F32), edges,
        ],
        15_000_000,
        scratch((5, CX), (5, CX + 6), (CX,), (5, CX), (5, CX)),
    )
    near = lax.ppermute(near, "gx", inside)
    (far,) = call(widen_kernel, "widen", (far,), [shape_of((5, 2))], 100_000)
    (out,) = call(
        last_kernel,
        "last",
        (base, drift, spread, near, far),
        [field],
        1_000_000,
        scratch((5, CX)) + [pltpu.SemaphoreType.DMA((5,))],
        out_specs=stay[:1],
    )
    return out, coef_grad


def solution(mesh):
    return jax.shard_map(
        local,
        mesh=mesh,
        in_specs=(
            P(None, None, "gx", None, "gz"),
            P(None, "gx", None, "gz"),
            P(None, "gx", None, "gz"),
            P(None, "gx", None, "gz"),
        ),
        out_specs=(P(None, "gx", None, "gz"), P(None, "gx", None)),
        check_vma=False,
    )
```

```python
import functools
import math

import jax
import jax.numpy as jnp
from jax import lax
from jax.experimental import pallas as pl
from jax.experimental.pallas import tpu as pltpu
from jax.sharding import PartitionSpec as P

EPSILON = 1e-06
NU_MOL = 0.05
PRANDTL = 0.72
PRANDTL_TURB = 0.9
TIME_STEP = 0.04
PAIRS = ((0, 0), (1, 1), (2, 2), (0, 1), (0, 2), (1, 2))
WEIGHTS = (1.0, 1.0, 1.0, 2.0, 2.0, 2.0)

CX = 4
ROWS = 32
LANES = 128
STRIP = 4
F32 = jnp.float32
BF16 = jnp.bfloat16
SLOT_PSI = 4
BAND = 12
STRIP_BLOCKS = 2
BAND_BLOCKS = 3
VELOCITY = 0
SCALARS = 18
MESSAGE = 22
PSI = 4
SCALAR_PLANES = 14


def lane_ids():
    return lax.broadcasted_iota(jnp.int32, (ROWS, LANES), 1)


def row_ids():
    return lax.broadcasted_iota(jnp.int32, (ROWS, LANES), 0)


def turn(values, shift):
    shift = shift % LANES
    return values if shift == 0 else pltpu.roll(values, shift, 1)


class Ops:
    def __init__(self):
        self.lane = lane_ids()
        row = row_ids()
        self.top = row == ROWS - 1
        self.bottom = row == 0

    def z_at(self, values, halo, step):
        if step > 0:
            return turn(jnp.where(self.lane < step, halo, values), -step)
        return turn(jnp.where(self.lane >= LANES + step, halo, values), -step)

    def y_up(self, values):
        return jnp.where(self.top, 0.0, pltpu.roll(values, ROWS - 1, 0))

    def y_down(self, values):
        return jnp.where(self.bottom, 0.0, pltpu.roll(values, 1, 0))

    def strip(self, blocks, slot, x):
        return turn(blocks[slot // 8], -(STRIP * (4 * (slot % 8) + x) + 2))


def fourth(plus, minus, plus_2, minus_2):
    return (2.0 / 3.0) * (plus - minus) - (1.0 / 12.0) * (plus_2 - minus_2)


def strain_of(grad):
    return [
        grad[0][0],
        grad[1][1],
        grad[2][2],
        0.5 * (grad[0][1] + grad[1][0]),
        0.5 * (grad[0][2] + grad[2][0]),
        0.5 * (grad[1][2] + grad[2][1]),
    ]


def size_of(strain):
    diagonal = strain[0] * strain[0] + strain[1] * strain[1] + strain[2] * strain[2]
    other = strain[3] * strain[3] + strain[4] * strain[4] + strain[5] * strain[5]
    return jnp.sqrt(2.0 * diagonal + (4.0 * other + EPSILON))


def filter_fields(velocity, strain, size):
    products = [velocity[a] * velocity[b] for a, b in PAIRS]
    return list(velocity) + products + strain + [size * part for part in strain]


def pack_strips(ops, items):
    block = jnp.zeros((ROWS, LANES), F32)
    strip_id = ops.lane >> 2
    for slot, planes in enumerate(items):
        for x in range(CX):
            number = 4 * slot + x
            block = jnp.where(strip_id == number, turn(planes[x], STRIP * number + 2), block)
    return block


def place_halos(ops, t, own_halo, halos):
    strips = [own_halo[number].astype(F32) for number in range(STRIP_BLOCKS)]
    for k in range(3):
        number = 3 * t + k
        bands = own_halo[STRIP_BLOCKS + number // 2].astype(F32)
        for x in range(CX):
            halos[k, x] = turn(bands, -(BAND * (x + 3) + 3 + 6 * (number % 2)))
    for k in range(3, 5):
        for x in range(CX):
            halos[k, x] = ops.strip(strips, 2 * t + k - 3, x)


def y_terms(ops, values):
    up, down = ops.y_up(values), ops.y_down(values)
    return 0.5 * (up - down), (up + down) - 6.0 * values


def z_terms(ops, values, halo):
    zs = [ops.z_at(values, halo, step) for step in (1, -1, 2, -2)]
    return fourth(*zs), zs[0] + zs[1]


def state_terms(wide, grad_x, grad_yz, lap_velocity, lap_yz, sizes, x):
    grad = [[None] * 5 for _ in range(3)]
    lap = [None] * 5
    center = [wide[k, x + 3] for k in range(5)]
    for k in range(5):
        if k < 3:
            grad[0][k], lap[k] = grad_x[k, x], lap_velocity[k, x]
        else:
            xs = [wide[k, x + 3 + step] for step in (1, -1, 2, -2)]
            grad[0][k] = fourth(*xs)
            lap[k] = lap_yz[k, x] + (xs[0] + xs[1])
        grad[1][k], grad[2][k] = grad_yz[k, 0, x], grad_yz[k, 1, x]
    return center, grad, lap, sizes[x], 1.0 / center[3]


def affine_update(terms, psi, rates, laps):
    center, grad, lap, size, inv_rho = terms
    work_mom = psi[0] * lap[0] + psi[1] * lap[1] + psi[2] * lap[2]
    work_heat = psi[4] * lap[4]
    turbulent = work_mom + work_heat * (1.0 / PRANDTL_TURB)
    inv_rho_2 = inv_rho * inv_rho
    size_rho = size * inv_rho
    first, second = [], []
    for k in range(5):
        rate = rates[k]
        if k == 3:
            rate = rate - (NU_MOL * work_mom + (NU_MOL / PRANDTL) * work_heat) * inv_rho_2
            eddy = -(size * turbulent) * inv_rho_2
        else:
            lap_psi = laps[k]
            if k < 3:
                for other in range(5):
                    rate = rate + psi[other] * grad[k][other]
                rate = rate + NU_MOL * (inv_rho * lap_psi)
                eddy = size_rho * lap_psi
            else:
                rate = rate + (NU_MOL / PRANDTL) * (inv_rho * lap_psi)
                eddy = (1.0 / PRANDTL_TURB) * (size_rho * lap_psi)
        first.append(psi[k] + TIME_STEP * rate)
        second.append(TIME_STEP * eddy)
    return first, second, size_rho * turbulent


def band_of(lane):
    return (lane * 43) >> 9


def is_even():
    return lax.rem(lax.axis_index("gx"), 2) == 0


def fill_scalars(out, side, rho, temp, psi):
    for i in range(2):
        out[i] = rho[0, 2 * side + i]
        out[2 + i] = temp[0, 2 * side + i]
    for k in range(5):
        for i in range(2):
            out[PSI + k * 2 + i] = psi[k, 2 * side + i].astype(BF16)


def merge_bands(ops, low, message, first):
    lower = ops.lane - BAND * band_of(ops.lane) < 6
    for number in range(BAND_BLOCKS):
        both = jnp.where(lower, low[2 * number], turn(low[2 * number + 1], 6))
        message[first + number] = both.astype(BF16)


def fill_later(out, side, rho, temp):
    for i in range(2):
        out[SCALARS + i] = rho[1, 2 * side + i]
        out[SCALARS + 2 + i] = temp[1, 2 * side + i]


def message_kernel(
    flow_far, rho_far, temp_far, psi_far, far, far_scalars, flow, rho, temp, psi, sems
):
    side = 1 - is_even().astype(jnp.int32)
    pieces = (
        (
            flow_far.at[:, :, pl.ds(side, 3)],
            far.at[pl.ds(VELOCITY, 18)].reshape((2, 3, 3, ROWS, LANES)),
        ),
        (psi_far, psi),
        (rho_far, rho),
        (temp_far, temp),
        (flow_far, flow),
    )
    copies = [
        pltpu.make_async_copy(source, target, sems.at[number])
        for number, (source, target) in enumerate(pieces)
    ]
    for copy in copies:
        copy.start()
    for copy in copies[1:4]:
        copy.wait()
    fill_scalars(far_scalars, side, rho, temp, psi)
    fill_later(far, side, rho, temp)
    copies[0].wait()
    copies[4].wait()


def pack_kernel(flow, rho, temp, psi, near, near_scalars, message, low):
    ops = Ops()
    side = is_even().astype(jnp.int32)
    for t in range(2):
        for k in range(3):
            for i in range(3):
                near[VELOCITY + t * 9 + k * 3 + i] = flow[t, k, side + i]
    fill_scalars(near_scalars, side, rho, temp, psi)
    fill_later(near, side, rho, temp)
    items = []
    for t in range(2):
        for source in (rho, temp):
            items.append([source[t, x].astype(F32) for x in range(CX)])
    items += [[psi[k, x] for x in range(CX)] for k in range(5)]
    for number in range(STRIP_BLOCKS):
        message[number] = pack_strips(ops, items[8 * number : 8 * number + 8]).astype(BF16)
    band = band_of(ops.lane)
    for t in range(2):
        for k in range(3):
            block = jnp.zeros((ROWS, LANES), F32)
            for x in range(CX):
                moved = turn(flow[t, k, x].astype(F32), BAND * (x + 3) + 3)
                block = jnp.where(band == x + 3, moved, block)
            low[3 * t + k] = block
    merge_bands(ops, low, message, STRIP_BLOCKS)


def rows_kernel(flow, rho, temp, psi, grad_0, grad_1, lap_0, lap_1, psi_rate, psi_lap):
    ops = Ops()
    for t, grad_y, lap_y in ((0, grad_0, lap_0), (1, grad_1, lap_1)):
        for k in range(5):
            for x in range(CX):
                values = flow[t, k, x] if k < 3 else (rho if k == 3 else temp)[t, x]
                grad_y[k, x], lap_y[k, x] = y_terms(ops, values.astype(F32))
    for x in range(CX):
        along_y = flow[0, 1, x].astype(F32)
        for k in range(5):
            by_y, psi_lap[k, x] = y_terms(ops, psi[k, x])
            psi_rate[k, x] = along_y * by_y


def own_kernel(
    flow, rho, temp, psi, own_halo, grad_y_0, grad_y_1, lap_y_0, lap_y_1, rate_y, psi_lap_y,
    grad_0, grad_1, lap_0, lap_1, psi_rate, psi_lap,
    halos, psi_halos,
):
    ops = Ops()
    for t in range(2):
        place_halos(ops, t, own_halo, halos.at[t])
    strips = [own_halo[number].astype(F32) for number in range(STRIP_BLOCKS)]
    for k in range(5):
        for x in range(CX):
            psi_halos[k, x] = ops.strip(strips, SLOT_PSI + k, x)
    for t, grad_y, lap_y, grad_yz, lap_yz in (
        (0, grad_y_0, lap_y_0, grad_0, lap_0),
        (1, grad_y_1, lap_y_1, grad_1, lap_1),
    ):
        for k in range(5):
            for x in range(CX):
                values = flow[t, k, x] if k < 3 else (rho if k == 3 else temp)[t, x]
                by_z, both = z_terms(ops, values.astype(F32), halos[t, k, x])
                grad_yz[k, 0, x], grad_yz[k, 1, x] = grad_y[k, x], by_z
                lap_yz[k, x] = lap_y[k, x] + both
    for x in range(CX):
        along_z = flow[0, 2, x].astype(F32)
        for k in range(5):
            by_z, both = z_terms(ops, psi[k, x], psi_halos[k, x])
            psi_rate[k, x] = rate_y[k, x] + along_z * by_z
            psi_lap[k, x] = psi_lap_y[k, x] + both


def token_kernel(far, _, out):
    out[...] = far[0].astype(F32)


def bands_kernel(own_low, near, far, _, message, low):
    ops = Ops()
    even = is_even()
    band = band_of(ops.lane)
    for t in range(2):
        for k in range(3):
            block = own_low[3 * t + k]
            for i in range(3):
                number = VELOCITY + t * 9 + k * 3 + i
                one, two = near[number].astype(F32), far[number].astype(F32)
                moved = turn(jnp.where(even, two, one), BAND * i + 3)
                block = jnp.where(band == i, moved, block)
                moved = turn(jnp.where(even, one, two), BAND * (7 + i) + 3)
                block = jnp.where(band == 7 + i, moved, block)
            low[3 * t + k] = block
    merge_bands(ops, low, message, 0)


def products_of(hat):
    velocity = [hat(k) for k in range(3)]
    strain = [hat(9 + number) for number in range(6)]
    diagonal = strain[0] * strain[0] + strain[1] * strain[1] + strain[2] * strain[2]
    other = strain[3] * strain[3] + strain[4] * strain[4] + strain[5] * strain[5]
    size = 4.0 * jnp.sqrt((2.0 / 256.0) * diagonal + ((4.0 / 256.0) * other + EPSILON))
    cross = 0.0
    square = 0.0
    for number, (a, b) in enumerate(PAIRS):
        leonard = hat(3 + number) - (1.0 / 16.0) * velocity[a] * velocity[b]
        model = hat(15 + number) - size * strain[number]
        weighted = WEIGHTS[number] * model if WEIGHTS[number] != 1.0 else model
        cross = cross + leonard * weighted
        square = square + model * weighted
    return cross, square


def widen(k, source, near, far, count, even, wide):
    for i in range(count):
        one, two = near(i), far(i)
        wide[k, 3 - count + i] = jnp.where(even, two, one)
        wide[k, 3 + CX + i] = jnp.where(even, one, two)
    for x in range(CX):
        wide[k, 3 + x] = source(x).astype(F32)


def widen_scalars(t, first, rho, temp, near, far, even, wide):
    for k, source in ((3, rho), (4, temp)):
        number = first + (k - 3) * 2
        widen(
            k,
            lambda x: source[t, x],
            lambda i: near[number + i].astype(F32),
            lambda i: far[number + i].astype(F32),
            2, even, wide,
        )


def inner_products(
    ops, t, flow, near, far, grad_yz, lap_yz,
    sums, high, wide, grad_x, lap_velocity, sizes, fields, hats,
):
    even = is_even()
    valid = (ops.lane >= 3) & (ops.lane < LANES - 3)
    band = band_of(jnp.maximum(ops.lane - 2, 0))
    for k in range(3):
        widen(
            k,
            lambda x: flow[t, k, x],
            lambda i: near[VELOCITY + t * 9 + k * 3 + i].astype(F32),
            lambda i: far[VELOCITY + t * 9 + k * 3 + i].astype(F32),
            3, even, wide,
        )
    for x in range(-1, CX + 1):
        grad = [[None] * 3 for _ in range(3)]
        for k in range(3):
            center = wide[k, x + 3]
            xs = [wide[k, x + 3 + step] for step in (1, -1, 2, -2)]
            grad[0][k] = fourth(*xs)
            if 0 <= x < CX:
                grad_x[k, x] = grad[0][k]
                lap_velocity[k, x] = lap_yz[k, x] + (xs[0] + xs[1])
                grad[1][k], grad[2][k] = grad_yz[k, 0, x], grad_yz[k, 1, x]
            else:
                grad[1][k] = 0.5 * (ops.y_up(center) - ops.y_down(center))
                grad[2][k] = fourth(*(turn(center, -step) for step in (1, -1, 2, -2)))
        strain = strain_of(grad)
        size = size_of(strain)
        if 0 <= x < CX:
            sizes[x] = size
        velocity = [wide[k, x + 3] for k in range(3)]
        for number, values in enumerate(filter_fields(velocity, strain, size)):
            fields[number, x + 1] = values
    for x in range(CX):
        for number in range(21):
            along_x = fields[number, x] + fields[number, x + 2] + 2.0 * fields[number, x + 1]
            hats[number, x] = turn(along_x, 1) + turn(along_x, -1) + 2.0 * along_x
    for k in range(3):
        block = jnp.zeros((ROWS, LANES), F32)
        for q in range(CX + 6):
            block = jnp.where(band == q, turn(wide[k, q], BAND * q + 11), block)
        high[k] = block
    for x in range(CX):
        cross, square = products_of(lambda number: hats[number, x])
        sums[0, x] = jnp.where(valid, cross, 0.0)
        sums[1, x] = jnp.where(valid, square, 0.0)


def edge_products(ops, t, low, high, halo, sums, bands, spread):
    band = band_of(ops.lane)
    place = ops.lane - BAND * band
    from_low = place < 3
    from_high = (place == 11) | (place < 2)
    low_side = place < 7
    at_edge = ((place >= 3) & (place <= 5)) | ((place >= 8) & (place <= 10))
    for k in range(3):
        number = 3 * t + k
        far = halo[number // 2].astype(F32)
        shift = 6 * (number % 2)
        bands[0, k] = jnp.where(from_low, turn(far, -shift), low[number])
        bands[1, k] = jnp.where(from_high, turn(far, 8 - shift), high[k])
    for side in range(2):
        velocity = [bands[side, k] for k in range(3)]
        grad = [[None] * 3 for _ in range(3)]
        for k in range(3):
            center = velocity[k]
            grad[0][k] = fourth(*(turn(center, -BAND * step) for step in (1, -1, 2, -2)))
            grad[1][k] = 0.5 * (ops.y_up(center) - ops.y_down(center))
            grad[2][k] = fourth(*(turn(center, -step) for step in (1, -1, 2, -2)))
        strain = strain_of(grad)
        for number, values in enumerate(filter_fields(velocity, strain, size_of(strain))):
            if side == 0:
                spread[number] = values
            else:
                spread[number] = jnp.where(low_side, spread[number], values)
    for number in range(21):
        both = spread[number]
        spread[number] = turn(both, BAND) + turn(both, -BAND) + 2.0 * both
    for number in range(21):
        both = spread[number]
        spread[number] = turn(both, 1) + turn(both, -1) + 2.0 * both
    for part, values in enumerate(products_of(lambda number: spread[number])):
        values = jnp.where(at_edge, values, 0.0)
        for x in range(CX):
            sums[part, x] = sums[part, x] + jnp.where(band == x + 3, values, 0.0)


def add_columns(ops, total, first_lane, planes, scale=1.0):
    for x in range(CX):
        value = scale * jnp.sum(planes(x), axis=1, keepdims=True)
        total = jnp.where(ops.lane == first_lane + x, value, total)
    return total


def add_parts(ops, block, total):
    upper = total.astype(BF16).astype(F32)
    rest = total - upper
    middle = rest.astype(BF16).astype(F32)
    for number, part in enumerate((upper, middle, rest - middle)):
        block = jnp.where(ops.lane >> 5 == 1 + number, turn(part, 32 * (1 + number)), block)
    return block


def span_total(add_other, columns, other):
    total = columns[...]
    if add_other:
        parts = other.astype(F32)
        total = total + ((turn(parts, -32) + turn(parts, -64)) + turn(parts, -96))
    return total


def psi_terms(psi_wide, rate_yz, lap_yz, velocity, x):
    rates, laps = [], []
    for k in range(5):
        xs = [psi_wide[k, x + 3 + step] for step in (1, -1, 2, -2)]
        rates.append(rate_yz[k, x] + velocity * fourth(*xs))
        laps.append(lap_yz[k, x] + (xs[0] + xs[1]))
    return rates, laps


def inner_kernel(
    flow, near, far, grad_yz, lap_yz,
    sums, high, wide, grad_x, lap_velocity, sizes,
    fields, hats,
):
    inner_products(
        Ops(), 0, flow, near, far, grad_yz, lap_yz,
        sums, high, wide, grad_x, lap_velocity, sizes, fields, hats,
    )


def first_kernel(
    _, products, rho, temp, psi, near, far, velocity, grad_x, lap_velocity, sizes,
    grad_yz, lap_yz, psi_rate, psi_lap,
    first, second, message, columns,
    wide, psi_wide, work,
):
    ops = Ops()
    even = is_even()
    for k in range(3):
        for x in range(CX):
            wide[k, x + 3] = velocity[k, x + 3]
    widen_scalars(0, 0, rho, temp, near, far, even, wide)
    for k in range(5):
        widen(
            k,
            lambda x: psi[k, x],
            lambda i: near[PSI + k * 2 + i].astype(F32),
            lambda i: far[PSI + k * 2 + i].astype(F32),
            2, even, psi_wide,
        )
    for x in range(CX):
        terms = state_terms(wide, grad_x, grad_yz, lap_velocity, lap_yz, sizes, x)
        rates, laps = psi_terms(psi_wide, psi_rate, psi_lap, terms[0][0], x)
        new, slope, sensitivity = affine_update(
            terms, [psi[k, x] for k in range(5)], rates, laps
        )
        for k in range(5):
            first[k, x] = new[k]
            second[k, x] = slope[k]
        work[x] = sensitivity
    total = add_columns(ops, products[...], 16, lambda x: work[x])
    columns[...] = total
    items = [[part[k, x] for x in range(CX)] for part in (first, second) for k in range(5)]
    message[0] = pack_strips(ops, items[:8]).astype(BF16)
    message[1] = add_parts(ops, pack_strips(ops, items[8:]), total).astype(BF16)


def edge_kernel(low, high, halo, inner, columns, bands, spread, sums):
    ops = Ops()
    for part in range(2):
        for x in range(CX):
            sums[part, x] = inner[part, x]
    edge_products(ops, 0, low, high, halo, sums, bands, spread)
    total = jnp.zeros((ROWS, LANES), F32)
    for part in range(2):
        total = add_columns(ops, total, 4 * part, lambda x: sums[part, x], 1.0 / 256.0)
    columns[...] = total


def later_kernel(
    flow, rho, temp, near, far, grad_yz, lap_yz, low, halo, first, second,
    wide, grad_x, lap_velocity, sizes, message, columns,
    high, fields, hats, work, bands, spread, sums,
):
    ops = Ops()
    inner_products(
        ops, 1, flow, near, far, grad_yz, lap_yz,
        sums, high, wide, grad_x, lap_velocity, sizes, fields, hats,
    )
    widen_scalars(1, SCALARS, rho, temp, near, far, is_even(), wide)
    edge_products(ops, 1, low, high, halo, sums, bands, spread)
    for x in range(CX):
        _, _, lap, size, inv_rho = state_terms(
            wide, grad_x, grad_yz, lap_velocity, lap_yz, sizes, x
        )
        size_rho = size * inv_rho
        for part, source in enumerate((first, second)):
            total = lap[0] * source[0, x] + lap[1] * source[1, x] + lap[2] * source[2, x]
            work[part, x] = size_rho * (
                total + (1.0 / PRANDTL_TURB) * (lap[4] * source[4, x])
            )
    total = jnp.zeros((ROWS, LANES), F32)
    for part in range(2):
        total = add_columns(ops, total, 8 + 4 * part, lambda x: sums[part, x], 1.0 / 256.0)
        total = add_columns(ops, total, 20 + 4 * part, lambda x: work[part, x])
    columns[...] = total
    message[0] = add_parts(ops, jnp.zeros((ROWS, LANES), F32), total).astype(BF16)


def coefficients(ops, total):
    return total / (turn(total, -4) + EPSILON)


def middle_kernel(add_other, first, second, columns, other, psi, far, coef_first):
    ops = Ops()
    coef = coefficients(ops, span_total(add_other, columns, other[1]))
    for x in range(CX):
        coef_first[x] = jnp.broadcast_to(coef[:, x : x + 1], (ROWS, LANES))
    for x in range(CX):
        for k in range(5):
            psi[k, x] = first[k, x] + coef_first[x] * second[k, x]
    side = 1 - is_even().astype(jnp.int32)
    for k in range(5):
        for i in range(2):
            far[k, i] = psi[k, 2 * side + i].astype(BF16)


def base_kernel(
    add_other, span_cells,
    wide, grad_x, lap_velocity, sizes, grad_yz, lap_yz, psi, coef_first,
    columns, other, later, later_other,
    base, drift, spread, coef_grad, near,
    psi_halos, psi_wide, coef_planes, psi_rate, psi_lap,
):
    ops = Ops()
    side = is_even().astype(jnp.int32)
    for k in range(5):
        for i in range(2):
            near[k, i] = psi[k, 2 * side + i].astype(BF16)
    strips = [other[number].astype(F32) for number in range(2)]
    for k in range(5):
        for x in range(CX):
            psi_halos[k, x] = ops.strip(strips, k, x)
    total = span_total(add_other, columns, other[1]) + span_total(
        add_other, later, later_other[0]
    )
    coef = coefficients(ops, total)
    after = total + turn(coef, 20) * turn(total, -4)
    grads = jnp.where(ops.lane < 20, total, after) * (1.0 / span_cells)
    turned = jnp.concatenate([grads] * (LANES // ROWS), axis=0).T
    for t in range(2):
        coef_grad[t] = turned[16 + 4 * t : 20 + 4 * t, :ROWS]
    for x in range(CX):
        coef_planes[x] = jnp.broadcast_to(coef[:, 8 + x : 9 + x], (ROWS, LANES))
    for k in range(5):
        for x in range(CX):
            psi_halos[k, x] = psi_halos[k, x] + coef_first[x] * ops.strip(strips, 5 + k, x)
    zero = jnp.zeros((ROWS, LANES), F32)
    for k in range(5):
        for i in range(2):
            psi_wide[k, 1 + i] = zero
            psi_wide[k, 3 + CX + i] = zero
        for x in range(CX):
            psi_wide[k, 3 + x] = psi[k, x]
    for x in range(CX):
        for k in range(5):
            by_y, lap = y_terms(ops, psi[k, x])
            by_z, both = z_terms(ops, psi[k, x], psi_halos[k, x])
            psi_rate[k, x] = wide[1, x + 3] * by_y + wide[2, x + 3] * by_z
            psi_lap[k, x] = lap + both
    for x in range(CX):
        terms = state_terms(wide, grad_x, grad_yz, lap_velocity, lap_yz, sizes, x)
        center = terms[0]
        rates, laps = psi_terms(psi_wide, psi_rate, psi_lap, center[0], x)
        new, slope, _ = affine_update(terms, [psi[k, x] for k in range(5)], rates, laps)
        for k in range(5):
            base[k, x] = new[k] + coef_planes[x] * slope[k]
        size, inv_rho = terms[3:]
        drift[x] = TIME_STEP * center[0]
        if x in (0, CX - 1):
            eddy = coef_planes[x] * size
            scaled = TIME_STEP * inv_rho
            spread[x // (CX - 1), 0] = scaled * (NU_MOL + eddy)
            spread[x // (CX - 1), 1] = scaled * (
                NU_MOL / PRANDTL + (1.0 / PRANDTL_TURB) * eddy
            )


def widen_kernel(far, out):
    for k in range(5):
        for i in range(2):
            out[k, i] = far[k, i].astype(F32)


def last_kernel(base, drift, spread, near_psi, far_psi, out_far, out, sems):
    even = is_even()
    copies = []
    for k in range(5):
        ones = [near_psi[k, i].astype(F32) for i in range(2)]
        twos = [far_psi[k, i].astype(F32) for i in range(2)]
        far, near = (jnp.where(even, two, one) for one, two in zip(ones, twos))
        after, beyond = (jnp.where(even, one, two) for one, two in zip(ones, twos))
        low = drift[0] * ((1.0 / 12.0) * far - (2.0 / 3.0) * near)
        high = drift[CX - 1] * ((2.0 / 3.0) * after - (1.0 / 12.0) * beyond)
        if k != 3:
            kind = 1 if k == 4 else 0
            low = low + spread[0, kind] * near
            high = high + spread[1, kind] * after
        out[k, 0] = base[k, 0] + low
        out[k, 1] = base[k, 1] + drift[1] * ((1.0 / 12.0) * near)
        out[k, CX - 2] = base[k, CX - 2] - drift[CX - 2] * ((1.0 / 12.0) * after)
        out[k, CX - 1] = base[k, CX - 1] + high
        copies.append(pltpu.make_async_copy(out.at[k], out_far.at[k], sems.at[k]))
        copies[k].start()
    for copy in copies:
        copy.wait()


def ring(axis):
    count = lax.axis_size(axis)
    forward = [(i, (i + 1) % count) for i in range(count)]
    return forward, [(target, source) for source, target in forward]


def pairs():
    count = lax.axis_size("gx")
    if count % 2:
        raise ValueError("odd gx")
    inside = [(i, i ^ 1) for i in range(count)]
    across = [(i, (i + 1 if i % 2 else i - 1) % count) for i in range(count)]
    return inside, across


def span_edges(message, strips):
    forward, backward = ring("gz")
    before = lax.ppermute(message, "gz", forward)
    if lax.axis_size("gz") == 2:
        return before
    after = lax.ppermute(message, "gz", backward)
    lane = lax.broadcasted_iota(jnp.int32, message.shape, 2)
    number = lax.broadcasted_iota(jnp.int32, message.shape, 0)
    low = jnp.where(number < strips, lane % STRIP < 2, lane % 6 < 3)
    return jnp.where(low, before, after)


def shape_of(dims, kind=F32):
    return jax.ShapeDtypeStruct(dims + (ROWS, LANES), kind)


def whole(count):
    return [pl.BlockSpec(memory_space=pltpu.VMEM)] * count


def scratch(*dims):
    return [pltpu.VMEM(d + (ROWS, LANES), F32) for d in dims]


def call(kernel, name, inputs, outputs, operations, buffers=(), in_specs=None, out_specs=None):
    inputs = list(inputs)
    if in_specs:
        inputs[:4] = [
            pltpu.with_memory_space_constraint(a, pltpu.MemorySpace.HBM) for a in inputs[:4]
        ]
    size = sum(math.prod(a.shape) * a.dtype.itemsize for a in list(inputs) + list(outputs))
    return pl.pallas_call(
        kernel,
        in_specs=in_specs or whole(len(inputs)),
        out_specs=out_specs or whole(len(outputs)),
        out_shape=list(outputs),
        scratch_shapes=list(buffers),
        compiler_params=pltpu.CompilerParams(vmem_limit_bytes=8 * 2**20),
        cost_estimate=pl.CostEstimate(
            flops=operations, bytes_accessed=size, transcendentals=0
        ),
        name=name,
    )(*inputs)


def span_sums(columns):
    if lax.axis_size("gz") == 2:
        return columns
    return lax.psum(columns, "gz")


def local(flow_far, rho_far, temp_far, psi_far):
    inside, across = pairs()
    add_other = lax.axis_size("gz") == 2
    field, planes, edges = shape_of((5, CX)), shape_of((5, CX + 6)), shape_of((5, 2), BF16)
    slopes = shape_of((5, 2, CX))
    inputs = (flow_far, rho_far, temp_far, psi_far)
    stay = [pl.BlockSpec(memory_space=pltpu.MemorySpace.HBM)] * 4
    far, far_scalars, flow, rho, temp, psi = call(
        message_kernel,
        "message",
        inputs,
        [
            shape_of((MESSAGE,), BF16),
            shape_of((SCALAR_PLANES,), BF16),
            shape_of((2, 3, CX), BF16),
            shape_of((2, CX), BF16),
            shape_of((2, CX), BF16),
            field,
        ],
        1_000_000,
        [pltpu.SemaphoreType.DMA((5,))],
        stay,
    )
    far = lax.ppermute(far, "gx", across)
    near, near_scalars, message, own_low = call(
        pack_kernel,
        "pack",
        (flow, rho, temp, psi),
        [
            shape_of((MESSAGE,), BF16),
            shape_of((SCALAR_PLANES,), BF16),
            shape_of((STRIP_BLOCKS + BAND_BLOCKS,), BF16),
            shape_of((6,)),
        ],
        2_000_000,
    )
    far_scalars = lax.ppermute(far_scalars, "gx", across)
    near = lax.ppermute(near, "gx", inside)
    near_scalars = lax.ppermute(near_scalars, "gx", inside)
    own_halo = span_edges(message, STRIP_BLOCKS)
    rows = call(
        rows_kernel,
        "rows",
        (flow, rho, temp, psi),
        [field] * 6,
        3_000_000,
    )
    grad_0, grad_1, lap_0, lap_1, psi_rate, psi_lap = call(
        own_kernel,
        "own",
        (flow, rho, temp, psi, own_halo, *rows),
        [slopes, slopes, field, field, field, field],
        5_000_000,
        scratch((2, 5, CX), (5, CX)),
    )
    (token,) = call(token_kernel, "token", (far, rows[5]), [shape_of(())], 100_000)
    message, low = call(
        bands_kernel,
        "bands",
        (own_low, near, far, token),
        [shape_of((BAND_BLOCKS,), BF16), shape_of((6,))],
        1_000_000,
    )
    halo = span_edges(message, 0)
    inner, high, velocity, grad_x, lap_velocity, sizes = call(
        inner_kernel,
        "inner",
        (flow, near, far, grad_0, lap_0),
        [
            shape_of((2, CX)), shape_of((3,)), shape_of((3, CX + 6)),
            shape_of((3, CX)), shape_of((3, CX)), shape_of((CX,)),
        ],
        20_000_000,
        scratch((21, CX + 2), (21, CX)),
    )
    (products,) = call(
        edge_kernel,
        "edge",
        (low, high, halo, inner),
        [shape_of(())],
        20_000_000,
        scratch((2, 3), (21,), (2, CX)),
    )
    (token,) = call(token_kernel, "later_token", (far_scalars, products), [shape_of(())], 100_000)
    first, second, message, columns = call(
        first_kernel,
        "first",
        (
            token, products, rho, temp, psi, near_scalars, far_scalars,
            velocity, grad_x, lap_velocity, sizes, grad_0, lap_0, psi_rate, psi_lap,
        ),
        [field, field, shape_of((2,), BF16), shape_of(())],
        10_000_000,
        scratch((5, CX + 6), (5, CX + 6), (CX,)),
    )
    other = span_edges(message, 2)
    columns = span_sums(columns)
    wide, grad_x, lap_velocity, sizes, message, later = call(
        later_kernel,
        "later",
        (
            flow, rho, temp, near, far, grad_1, lap_1, low, halo, first, second,
        ),
        [
            planes, shape_of((3, CX)), shape_of((3, CX)), shape_of((CX,)),
            shape_of((1,), BF16), shape_of(()),
        ],
        20_000_000,
        scratch((3,), (21, CX + 2), (21, CX), (2, CX), (2, 3), (21,), (2, CX)),
    )
    later_other = span_edges(message, 1)
    later = span_sums(later)
    first, later = lax.optimization_barrier((first, later))
    psi, far, coef_first = call(
        functools.partial(middle_kernel, add_other),
        "middle",
        (first, second, columns, other),
        [field, edges, shape_of((CX,))],
        1_000_000,
    )
    far = lax.ppermute(far, "gx", across)
    base, drift, spread, coef_grad, near = call(
        functools.partial(base_kernel, add_other, LANES * lax.axis_size("gz")),
        "base",
        (
            wide, grad_x, lap_velocity, sizes, grad_1, lap_1, psi, coef_first,
            columns, other, later, later_other,
        ),
        [
            field, shape_of((CX,)), shape_of((2, 2)),
            jax.ShapeDtypeStruct((2, CX, ROWS), F32), edges,
        ],
        15_000_000,
        scratch((5, CX), (5, CX + 6), (CX,), (5, CX), (5, CX)),
    )
    near = lax.ppermute(near, "gx", inside)
    (far,) = call(widen_kernel, "widen", (far,), [shape_of((5, 2))], 100_000)
    (out,) = call(
        last_kernel,
        "last",
        (base, drift, spread, near, far),
        [field],
        1_000_000,
        scratch((5, CX)) + [pltpu.SemaphoreType.DMA((5,))],
        out_specs=stay[:1],
    )
    return out, coef_grad


def solution(mesh):
    return jax.shard_map(
        local,
        mesh=mesh,
        in_specs=(
            P(None, None, "gx", None, "gz"),
            P(None, "gx", None, "gz"),
            P(None, "gx", None, "gz"),
            P(None, "gx", None, "gz"),
        ),
        out_specs=(P(None, "gx", None, "gz"), P(None, "gx", None)),
        check_vma=False,
    )
```

```python
import functools
import math

import jax
import jax.numpy as jnp
from jax import lax
from jax.experimental import pallas as pl
from jax.experimental.pallas import tpu as pltpu
from jax.sharding import PartitionSpec as P

EPSILON = 1e-06
NU_MOL = 0.05
PRANDTL = 0.72
PRANDTL_TURB = 0.9
TIME_STEP = 0.04
PAIRS = ((0, 0), (1, 1), (2, 2), (0, 1), (0, 2), (1, 2))
WEIGHTS = (1.0, 1.0, 1.0, 2.0, 2.0, 2.0)

CX = 4
ROWS = 32
LANES = 128
STRIP = 4
F32 = jnp.float32
BF16 = jnp.bfloat16
SLOT_PSI = 4
BAND = 12
STRIP_BLOCKS = 2
BAND_BLOCKS = 3
VELOCITY = 0
SCALARS = 18
PSI = 8
SCALAR_PLANES = 18


def lane_ids():
    return lax.broadcasted_iota(jnp.int32, (ROWS, LANES), 1)


def row_ids():
    return lax.broadcasted_iota(jnp.int32, (ROWS, LANES), 0)


def turn(values, shift):
    shift = shift % LANES
    return values if shift == 0 else pltpu.roll(values, shift, 1)


class Ops:
    def __init__(self):
        self.lane = lane_ids()
        row = row_ids()
        self.top = row == ROWS - 1
        self.bottom = row == 0

    def z_at(self, values, halo, step):
        if step > 0:
            return turn(jnp.where(self.lane < step, halo, values), -step)
        return turn(jnp.where(self.lane >= LANES + step, halo, values), -step)

    def y_up(self, values):
        return jnp.where(self.top, 0.0, pltpu.roll(values, ROWS - 1, 0))

    def y_down(self, values):
        return jnp.where(self.bottom, 0.0, pltpu.roll(values, 1, 0))

    def strip(self, blocks, slot, x):
        return turn(blocks[slot // 8], -(STRIP * (4 * (slot % 8) + x) + 2))


def fourth(plus, minus, plus_2, minus_2):
    return (2.0 / 3.0) * (plus - minus) - (1.0 / 12.0) * (plus_2 - minus_2)


def strain_of(grad):
    return [
        grad[0][0],
        grad[1][1],
        grad[2][2],
        0.5 * (grad[0][1] + grad[1][0]),
        0.5 * (grad[0][2] + grad[2][0]),
        0.5 * (grad[1][2] + grad[2][1]),
    ]


def size_of(strain):
    diagonal = strain[0] * strain[0] + strain[1] * strain[1] + strain[2] * strain[2]
    other = strain[3] * strain[3] + strain[4] * strain[4] + strain[5] * strain[5]
    return jnp.sqrt(2.0 * diagonal + (4.0 * other + EPSILON))


def filter_fields(velocity, strain, size):
    products = [velocity[a] * velocity[b] for a, b in PAIRS]
    return list(velocity) + products + strain + [size * part for part in strain]


def pack_strips(ops, items):
    block = jnp.zeros((ROWS, LANES), F32)
    strip_id = ops.lane >> 2
    for slot, planes in enumerate(items):
        for x in range(CX):
            number = 4 * slot + x
            block = jnp.where(strip_id == number, turn(planes[x], STRIP * number + 2), block)
    return block


def place_halos(ops, t, own_halo, halos):
    strips = [own_halo[number].astype(F32) for number in range(STRIP_BLOCKS)]
    for k in range(3):
        number = 3 * t + k
        bands = own_halo[STRIP_BLOCKS + number // 2].astype(F32)
        for x in range(CX):
            halos[k, x] = turn(bands, -(BAND * (x + 3) + 3 + 6 * (number % 2)))
    for k in range(3, 5):
        for x in range(CX):
            halos[k, x] = ops.strip(strips, 2 * t + k - 3, x)


def y_terms(ops, values):
    up, down = ops.y_up(values), ops.y_down(values)
    return 0.5 * (up - down), (up + down) - 6.0 * values


def z_terms(ops, values, halo):
    zs = [ops.z_at(values, halo, step) for step in (1, -1, 2, -2)]
    return fourth(*zs), zs[0] + zs[1]


def state_terms(wide, grad_x, grad_yz, lap_velocity, lap_yz, sizes, x):
    grad = [[None] * 5 for _ in range(3)]
    lap = [None] * 5
    center = [wide[k, x + 3] for k in range(5)]
    for k in range(5):
        if k < 3:
            grad[0][k], lap[k] = grad_x[k, x], lap_velocity[k, x]
        else:
            xs = [wide[k, x + 3 + step] for step in (1, -1, 2, -2)]
            grad[0][k] = fourth(*xs)
            lap[k] = lap_yz[k, x] + (xs[0] + xs[1])
        grad[1][k], grad[2][k] = grad_yz[k, 0, x], grad_yz[k, 1, x]
    return center, grad, lap, sizes[x], 1.0 / center[3]


def affine_update(terms, psi, rates, laps):
    center, grad, lap, size, inv_rho = terms
    work_mom = psi[0] * lap[0] + psi[1] * lap[1] + psi[2] * lap[2]
    work_heat = psi[4] * lap[4]
    turbulent = work_mom + work_heat * (1.0 / PRANDTL_TURB)
    inv_rho_2 = inv_rho * inv_rho
    size_rho = size * inv_rho
    first, second = [], []
    for k in range(5):
        rate = rates[k]
        if k == 3:
            rate = rate - (NU_MOL * work_mom + (NU_MOL / PRANDTL) * work_heat) * inv_rho_2
            eddy = -(size * turbulent) * inv_rho_2
        else:
            lap_psi = laps[k]
            if k < 3:
                for other in range(5):
                    rate = rate + psi[other] * grad[k][other]
                rate = rate + NU_MOL * (inv_rho * lap_psi)
                eddy = size_rho * lap_psi
            else:
                rate = rate + (NU_MOL / PRANDTL) * (inv_rho * lap_psi)
                eddy = (1.0 / PRANDTL_TURB) * (size_rho * lap_psi)
        first.append(psi[k] + TIME_STEP * rate)
        second.append(TIME_STEP * eddy)
    return first, second, size_rho * turbulent


def band_of(lane):
    return (lane * 43) >> 9


def is_even():
    return lax.rem(lax.axis_index("gx"), 2) == 0


def fill_scalars(out, side, rho, temp, psi):
    for t in range(2):
        for i in range(2):
            out[2 * t + i] = rho[t, 2 * side + i]
            out[4 + 2 * t + i] = temp[t, 2 * side + i]
    for k in range(5):
        for i in range(2):
            out[PSI + k * 2 + i] = psi[k, 2 * side + i].astype(BF16)


def merge_bands(ops, low, message, first):
    lower = ops.lane - BAND * band_of(ops.lane) < 6
    for number in range(BAND_BLOCKS):
        both = jnp.where(lower, low[2 * number], turn(low[2 * number + 1], 6))
        message[first + number] = both.astype(BF16)


def message_kernel(
    flow_far, rho_far, temp_far, psi_far, far, far_scalars, flow, rho, temp, psi, sems
):
    side = 1 - is_even().astype(jnp.int32)
    pieces = (
        (flow_far.at[:, :, pl.ds(side, 3)], far.reshape((2, 3, 3, ROWS, LANES))),
        (psi_far, psi),
        (rho_far, rho),
        (temp_far, temp),
        (flow_far, flow),
    )
    copies = [
        pltpu.make_async_copy(source, target, sems.at[number])
        for number, (source, target) in enumerate(pieces)
    ]
    for copy in copies:
        copy.start()
    for copy in copies[1:4]:
        copy.wait()
    fill_scalars(far_scalars, side, rho, temp, psi)
    copies[0].wait()
    copies[4].wait()


def pack_kernel(flow, rho, temp, psi, near, near_scalars, message, low):
    ops = Ops()
    side = is_even().astype(jnp.int32)
    for t in range(2):
        for k in range(3):
            for i in range(3):
                near[VELOCITY + t * 9 + k * 3 + i] = flow[t, k, side + i]
    fill_scalars(near_scalars, side, rho, temp, psi)
    items = []
    for t in range(2):
        for source in (rho, temp):
            items.append([source[t, x].astype(F32) for x in range(CX)])
    items += [[psi[k, x] for x in range(CX)] for k in range(5)]
    for number in range(STRIP_BLOCKS):
        message[number] = pack_strips(ops, items[8 * number : 8 * number + 8]).astype(BF16)
    band = band_of(ops.lane)
    for t in range(2):
        for k in range(3):
            block = jnp.zeros((ROWS, LANES), F32)
            for x in range(CX):
                moved = turn(flow[t, k, x].astype(F32), BAND * (x + 3) + 3)
                block = jnp.where(band == x + 3, moved, block)
            low[3 * t + k] = block
    merge_bands(ops, low, message, STRIP_BLOCKS)


def rows_kernel(flow, rho, temp, psi, grad_0, grad_1, lap_0, lap_1, psi_rate, psi_lap):
    ops = Ops()
    for t, grad_y, lap_y in ((0, grad_0, lap_0), (1, grad_1, lap_1)):
        for k in range(5):
            for x in range(CX):
                values = flow[t, k, x] if k < 3 else (rho if k == 3 else temp)[t, x]
                grad_y[k, x], lap_y[k, x] = y_terms(ops, values.astype(F32))
    for x in range(CX):
        along_y = flow[0, 1, x].astype(F32)
        for k in range(5):
            by_y, psi_lap[k, x] = y_terms(ops, psi[k, x])
            psi_rate[k, x] = along_y * by_y


def own_kernel(
    flow, rho, temp, psi, own_halo, grad_y_0, grad_y_1, lap_y_0, lap_y_1, rate_y, psi_lap_y,
    grad_0, grad_1, lap_0, lap_1, psi_rate, psi_lap,
    halos, psi_halos,
):
    ops = Ops()
    for t in range(2):
        place_halos(ops, t, own_halo, halos.at[t])
    strips = [own_halo[number].astype(F32) for number in range(STRIP_BLOCKS)]
    for k in range(5):
        for x in range(CX):
            psi_halos[k, x] = ops.strip(strips, SLOT_PSI + k, x)
    for t, grad_y, lap_y, grad_yz, lap_yz in (
        (0, grad_y_0, lap_y_0, grad_0, lap_0),
        (1, grad_y_1, lap_y_1, grad_1, lap_1),
    ):
        for k in range(5):
            for x in range(CX):
                values = flow[t, k, x] if k < 3 else (rho if k == 3 else temp)[t, x]
                by_z, both = z_terms(ops, values.astype(F32), halos[t, k, x])
                grad_yz[k, 0, x], grad_yz[k, 1, x] = grad_y[k, x], by_z
                lap_yz[k, x] = lap_y[k, x] + both
    for x in range(CX):
        along_z = flow[0, 2, x].astype(F32)
        for k in range(5):
            by_z, both = z_terms(ops, psi[k, x], psi_halos[k, x])
            psi_rate[k, x] = rate_y[k, x] + along_z * by_z
            psi_lap[k, x] = psi_lap_y[k, x] + both


def token_kernel(far, _, out):
    out[...] = far[0].astype(F32)


def bands_kernel(own_low, near, far, _, message, low):
    ops = Ops()
    even = is_even()
    band = band_of(ops.lane)
    for t in range(2):
        for k in range(3):
            block = own_low[3 * t + k]
            for i in range(3):
                number = VELOCITY + t * 9 + k * 3 + i
                one, two = near[number].astype(F32), far[number].astype(F32)
                moved = turn(jnp.where(even, two, one), BAND * i + 3)
                block = jnp.where(band == i, moved, block)
                moved = turn(jnp.where(even, one, two), BAND * (7 + i) + 3)
                block = jnp.where(band == 7 + i, moved, block)
            low[3 * t + k] = block
    merge_bands(ops, low, message, 0)


def products_of(hat):
    velocity = [hat(k) for k in range(3)]
    strain = [hat(9 + number) for number in range(6)]
    diagonal = strain[0] * strain[0] + strain[1] * strain[1] + strain[2] * strain[2]
    other = strain[3] * strain[3] + strain[4] * strain[4] + strain[5] * strain[5]
    size = 4.0 * jnp.sqrt((2.0 / 256.0) * diagonal + ((4.0 / 256.0) * other + EPSILON))
    cross = 0.0
    square = 0.0
    for number, (a, b) in enumerate(PAIRS):
        leonard = hat(3 + number) - (1.0 / 16.0) * velocity[a] * velocity[b]
        model = hat(15 + number) - size * strain[number]
        weighted = WEIGHTS[number] * model if WEIGHTS[number] != 1.0 else model
        cross = cross + leonard * weighted
        square = square + model * weighted
    return cross, square


def widen(k, source, near, far, count, even, wide):
    for i in range(count):
        one, two = near(i), far(i)
        wide[k, 3 - count + i] = jnp.where(even, two, one)
        wide[k, 3 + CX + i] = jnp.where(even, one, two)
    for x in range(CX):
        wide[k, 3 + x] = source(x).astype(F32)


def widen_scalars(t, rho, temp, near, far, even, wide):
    for k, source in ((3, rho), (4, temp)):
        number = (k - 3) * 4 + 2 * t
        widen(
            k,
            lambda x: source[t, x],
            lambda i: near[number + i].astype(F32),
            lambda i: far[number + i].astype(F32),
            2, even, wide,
        )


def inner_products(
    ops, t, flow, near, far, grad_yz, lap_yz,
    sums, high, wide, grad_x, lap_velocity, sizes, fields, hats,
):
    even = is_even()
    valid = (ops.lane >= 3) & (ops.lane < LANES - 3)
    band = band_of(jnp.maximum(ops.lane - 2, 0))
    for k in range(3):
        widen(
            k,
            lambda x: flow[t, k, x],
            lambda i: near[VELOCITY + t * 9 + k * 3 + i].astype(F32),
            lambda i: far[VELOCITY + t * 9 + k * 3 + i].astype(F32),
            3, even, wide,
        )
    for x in range(-1, CX + 1):
        grad = [[None] * 3 for _ in range(3)]
        for k in range(3):
            center = wide[k, x + 3]
            xs = [wide[k, x + 3 + step] for step in (1, -1, 2, -2)]
            grad[0][k] = fourth(*xs)
            if 0 <= x < CX:
                grad_x[k, x] = grad[0][k]
                lap_velocity[k, x] = lap_yz[k, x] + (xs[0] + xs[1])
                grad[1][k], grad[2][k] = grad_yz[k, 0, x], grad_yz[k, 1, x]
            else:
                grad[1][k] = 0.5 * (ops.y_up(center) - ops.y_down(center))
                grad[2][k] = fourth(*(turn(center, -step) for step in (1, -1, 2, -2)))
        strain = strain_of(grad)
        size = size_of(strain)
        if 0 <= x < CX:
            sizes[x] = size
        velocity = [wide[k, x + 3] for k in range(3)]
        for number, values in enumerate(filter_fields(velocity, strain, size)):
            fields[number, x + 1] = values
    for x in range(CX):
        for number in range(21):
            along_x = fields[number, x] + fields[number, x + 2] + 2.0 * fields[number, x + 1]
            hats[number, x] = turn(along_x, 1) + turn(along_x, -1) + 2.0 * along_x
    for k in range(3):
        block = jnp.zeros((ROWS, LANES), F32)
        for q in range(CX + 6):
            block = jnp.where(band == q, turn(wide[k, q], BAND * q + 11), block)
        high[k] = block
    for x in range(CX):
        cross, square = products_of(lambda number: hats[number, x])
        sums[0, x] = jnp.where(valid, cross, 0.0)
        sums[1, x] = jnp.where(valid, square, 0.0)


def edge_products(ops, t, low, high, halo, sums, bands, spread):
    band = band_of(ops.lane)
    place = ops.lane - BAND * band
    from_low = place < 3
    from_high = (place == 11) | (place < 2)
    low_side = place < 7
    at_edge = ((place >= 3) & (place <= 5)) | ((place >= 8) & (place <= 10))
    for k in range(3):
        number = 3 * t + k
        far = halo[number // 2].astype(F32)
        shift = 6 * (number % 2)
        bands[0, k] = jnp.where(from_low, turn(far, -shift), low[number])
        bands[1, k] = jnp.where(from_high, turn(far, 8 - shift), high[k])
    for side in range(2):
        velocity = [bands[side, k] for k in range(3)]
        grad = [[None] * 3 for _ in range(3)]
        for k in range(3):
            center = velocity[k]
            grad[0][k] = fourth(*(turn(center, -BAND * step) for step in (1, -1, 2, -2)))
            grad[1][k] = 0.5 * (ops.y_up(center) - ops.y_down(center))
            grad[2][k] = fourth(*(turn(center, -step) for step in (1, -1, 2, -2)))
        strain = strain_of(grad)
        for number, values in enumerate(filter_fields(velocity, strain, size_of(strain))):
            if side == 0:
                spread[number] = values
            else:
                spread[number] = jnp.where(low_side, spread[number], values)
    for number in range(21):
        both = spread[number]
        spread[number] = turn(both, BAND) + turn(both, -BAND) + 2.0 * both
    for number in range(21):
        both = spread[number]
        spread[number] = turn(both, 1) + turn(both, -1) + 2.0 * both
    for part, values in enumerate(products_of(lambda number: spread[number])):
        values = jnp.where(at_edge, values, 0.0)
        for x in range(CX):
            sums[part, x] = sums[part, x] + jnp.where(band == x + 3, values, 0.0)


def add_columns(ops, total, first_lane, planes, scale=1.0):
    for x in range(CX):
        value = scale * jnp.sum(planes(x), axis=1, keepdims=True)
        total = jnp.where(ops.lane == first_lane + x, value, total)
    return total


def add_parts(ops, block, total):
    upper = total.astype(BF16).astype(F32)
    rest = total - upper
    middle = rest.astype(BF16).astype(F32)
    for number, part in enumerate((upper, middle, rest - middle)):
        block = jnp.where(ops.lane >> 5 == 1 + number, turn(part, 32 * (1 + number)), block)
    return block


def span_total(add_other, columns, other):
    total = columns[...]
    if add_other:
        parts = other.astype(F32)
        total = total + ((turn(parts, -32) + turn(parts, -64)) + turn(parts, -96))
    return total


def psi_terms(psi_wide, rate_yz, lap_yz, velocity, x):
    rates, laps = [], []
    for k in range(5):
        xs = [psi_wide[k, x + 3 + step] for step in (1, -1, 2, -2)]
        rates.append(rate_yz[k, x] + velocity * fourth(*xs))
        laps.append(lap_yz[k, x] + (xs[0] + xs[1]))
    return rates, laps


def inner_kernel(
    flow, near, far, grad_yz, lap_yz,
    sums, high, wide, grad_x, lap_velocity, sizes,
    fields, hats,
):
    inner_products(
        Ops(), 0, flow, near, far, grad_yz, lap_yz,
        sums, high, wide, grad_x, lap_velocity, sizes, fields, hats,
    )


def first_kernel(
    _, products, rho, temp, psi, near, far, velocity, grad_x, lap_velocity, sizes,
    grad_yz, lap_yz, psi_rate, psi_lap,
    first, second, message, columns,
    wide, psi_wide, work,
):
    ops = Ops()
    even = is_even()
    for k in range(3):
        for x in range(CX):
            wide[k, x + 3] = velocity[k, x + 3]
    widen_scalars(0, rho, temp, near, far, even, wide)
    for k in range(5):
        widen(
            k,
            lambda x: psi[k, x],
            lambda i: near[PSI + k * 2 + i].astype(F32),
            lambda i: far[PSI + k * 2 + i].astype(F32),
            2, even, psi_wide,
        )
    for x in range(CX):
        terms = state_terms(wide, grad_x, grad_yz, lap_velocity, lap_yz, sizes, x)
        rates, laps = psi_terms(psi_wide, psi_rate, psi_lap, terms[0][0], x)
        new, slope, sensitivity = affine_update(
            terms, [psi[k, x] for k in range(5)], rates, laps
        )
        for k in range(5):
            first[k, x] = new[k]
            second[k, x] = slope[k]
        work[x] = sensitivity
    total = add_columns(ops, products[...], 16, lambda x: work[x])
    columns[...] = total
    items = [[part[k, x] for x in range(CX)] for part in (first, second) for k in range(5)]
    message[0] = pack_strips(ops, items[:8]).astype(BF16)
    message[1] = add_parts(ops, pack_strips(ops, items[8:]), total).astype(BF16)


def edge_kernel(low, high, halo, inner, columns, bands, spread, sums):
    ops = Ops()
    for part in range(2):
        for x in range(CX):
            sums[part, x] = inner[part, x]
    edge_products(ops, 0, low, high, halo, sums, bands, spread)
    total = jnp.zeros((ROWS, LANES), F32)
    for part in range(2):
        total = add_columns(ops, total, 4 * part, lambda x: sums[part, x], 1.0 / 256.0)
    columns[...] = total


def later_kernel(
    flow, rho, temp, near, far, near_scalars, far_scalars,
    grad_yz, lap_yz, low, halo, first, second,
    wide, grad_x, lap_velocity, sizes, message, columns,
    high, fields, hats, work, bands, spread, sums,
):
    ops = Ops()
    inner_products(
        ops, 1, flow, near, far, grad_yz, lap_yz,
        sums, high, wide, grad_x, lap_velocity, sizes, fields, hats,
    )
    widen_scalars(1, rho, temp, near_scalars, far_scalars, is_even(), wide)
    edge_products(ops, 1, low, high, halo, sums, bands, spread)
    for x in range(CX):
        _, _, lap, size, inv_rho = state_terms(
            wide, grad_x, grad_yz, lap_velocity, lap_yz, sizes, x
        )
        size_rho = size * inv_rho
        for part, source in enumerate((first, second)):
            total = lap[0] * source[0, x] + lap[1] * source[1, x] + lap[2] * source[2, x]
            work[part, x] = size_rho * (
                total + (1.0 / PRANDTL_TURB) * (lap[4] * source[4, x])
            )
    total = jnp.zeros((ROWS, LANES), F32)
    for part in range(2):
        total = add_columns(ops, total, 8 + 4 * part, lambda x: sums[part, x], 1.0 / 256.0)
        total = add_columns(ops, total, 20 + 4 * part, lambda x: work[part, x])
    columns[...] = total
    message[0] = add_parts(ops, jnp.zeros((ROWS, LANES), F32), total).astype(BF16)


def coefficients(ops, total):
    return total / (turn(total, -4) + EPSILON)


def middle_kernel(add_other, first, second, columns, other, psi, far, coef_first):
    ops = Ops()
    coef = coefficients(ops, span_total(add_other, columns, other[1]))
    for x in range(CX):
        coef_first[x] = jnp.broadcast_to(coef[:, x : x + 1], (ROWS, LANES))
    for x in range(CX):
        for k in range(5):
            psi[k, x] = first[k, x] + coef_first[x] * second[k, x]
    side = 1 - is_even().astype(jnp.int32)
    for k in range(5):
        for i in range(2):
            far[k, i] = psi[k, 2 * side + i].astype(BF16)


def base_kernel(
    add_other, span_cells,
    wide, grad_x, lap_velocity, sizes, grad_yz, lap_yz, psi, coef_first,
    columns, other, later, later_other,
    base, drift, spread, coef_grad, near,
    psi_halos, psi_wide, coef_planes, psi_rate, psi_lap,
):
    ops = Ops()
    side = is_even().astype(jnp.int32)
    for k in range(5):
        for i in range(2):
            near[k, i] = psi[k, 2 * side + i].astype(BF16)
    strips = [other[number].astype(F32) for number in range(2)]
    for k in range(5):
        for x in range(CX):
            psi_halos[k, x] = ops.strip(strips, k, x)
    total = span_total(add_other, columns, other[1]) + span_total(
        add_other, later, later_other[0]
    )
    coef = coefficients(ops, total)
    after = total + turn(coef, 20) * turn(total, -4)
    grads = jnp.where(ops.lane < 20, total, after) * (1.0 / span_cells)
    turned = jnp.concatenate([grads] * (LANES // ROWS), axis=0).T
    for t in range(2):
        coef_grad[t] = turned[16 + 4 * t : 20 + 4 * t, :ROWS]
    for x in range(CX):
        coef_planes[x] = jnp.broadcast_to(coef[:, 8 + x : 9 + x], (ROWS, LANES))
    for k in range(5):
        for x in range(CX):
            psi_halos[k, x] = psi_halos[k, x] + coef_first[x] * ops.strip(strips, 5 + k, x)
    zero = jnp.zeros((ROWS, LANES), F32)
    for k in range(5):
        for i in range(2):
            psi_wide[k, 1 + i] = zero
            psi_wide[k, 3 + CX + i] = zero
        for x in range(CX):
            psi_wide[k, 3 + x] = psi[k, x]
    for x in range(CX):
        for k in range(5):
            by_y, lap = y_terms(ops, psi[k, x])
            by_z, both = z_terms(ops, psi[k, x], psi_halos[k, x])
            psi_rate[k, x] = wide[1, x + 3] * by_y + wide[2, x + 3] * by_z
            psi_lap[k, x] = lap + both
    for x in range(CX):
        terms = state_terms(wide, grad_x, grad_yz, lap_velocity, lap_yz, sizes, x)
        center = terms[0]
        rates, laps = psi_terms(psi_wide, psi_rate, psi_lap, center[0], x)
        new, slope, _ = affine_update(terms, [psi[k, x] for k in range(5)], rates, laps)
        for k in range(5):
            base[k, x] = new[k] + coef_planes[x] * slope[k]
        size, inv_rho = terms[3:]
        drift[x] = TIME_STEP * center[0]
        if x in (0, CX - 1):
            eddy = coef_planes[x] * size
            scaled = TIME_STEP * inv_rho
            spread[x // (CX - 1), 0] = scaled * (NU_MOL + eddy)
            spread[x // (CX - 1), 1] = scaled * (
                NU_MOL / PRANDTL + (1.0 / PRANDTL_TURB) * eddy
            )


def widen_kernel(far, out):
    for k in range(5):
        for i in range(2):
            out[k, i] = far[k, i].astype(F32)


def last_kernel(base, drift, spread, near_psi, far_psi, out_far, out, sems):
    even = is_even()
    copies = []
    for k in range(5):
        ones = [near_psi[k, i].astype(F32) for i in range(2)]
        twos = [far_psi[k, i].astype(F32) for i in range(2)]
        far, near = (jnp.where(even, two, one) for one, two in zip(ones, twos))
        after, beyond = (jnp.where(even, one, two) for one, two in zip(ones, twos))
        low = drift[0] * ((1.0 / 12.0) * far - (2.0 / 3.0) * near)
        high = drift[CX - 1] * ((2.0 / 3.0) * after - (1.0 / 12.0) * beyond)
        if k != 3:
            kind = 1 if k == 4 else 0
            low = low + spread[0, kind] * near
            high = high + spread[1, kind] * after
        out[k, 0] = base[k, 0] + low
        out[k, 1] = base[k, 1] + drift[1] * ((1.0 / 12.0) * near)
        out[k, CX - 2] = base[k, CX - 2] - drift[CX - 2] * ((1.0 / 12.0) * after)
        out[k, CX - 1] = base[k, CX - 1] + high
        copies.append(pltpu.make_async_copy(out.at[k], out_far.at[k], sems.at[k]))
        copies[k].start()
    for copy in copies:
        copy.wait()


def ring(axis):
    count = lax.axis_size(axis)
    forward = [(i, (i + 1) % count) for i in range(count)]
    return forward, [(target, source) for source, target in forward]


def pairs():
    count = lax.axis_size("gx")
    if count % 2:
        raise ValueError("odd gx")
    inside = [(i, i ^ 1) for i in range(count)]
    across = [(i, (i + 1 if i % 2 else i - 1) % count) for i in range(count)]
    return inside, across


def span_edges(message, strips):
    forward, backward = ring("gz")
    before = lax.ppermute(message, "gz", forward)
    if lax.axis_size("gz") == 2:
        return before
    after = lax.ppermute(message, "gz", backward)
    lane = lax.broadcasted_iota(jnp.int32, message.shape, 2)
    number = lax.broadcasted_iota(jnp.int32, message.shape, 0)
    low = jnp.where(number < strips, lane % STRIP < 2, lane % 6 < 3)
    return jnp.where(low, before, after)


def shape_of(dims, kind=F32):
    return jax.ShapeDtypeStruct(dims + (ROWS, LANES), kind)


def whole(count):
    return [pl.BlockSpec(memory_space=pltpu.VMEM)] * count


def scratch(*dims):
    return [pltpu.VMEM(d + (ROWS, LANES), F32) for d in dims]


def call(kernel, name, inputs, outputs, operations, buffers=(), in_specs=None, out_specs=None):
    inputs = list(inputs)
    if in_specs:
        inputs[:4] = [
            pltpu.with_memory_space_constraint(a, pltpu.MemorySpace.HBM) for a in inputs[:4]
        ]
    size = sum(math.prod(a.shape) * a.dtype.itemsize for a in list(inputs) + list(outputs))
    return pl.pallas_call(
        kernel,
        in_specs=in_specs or whole(len(inputs)),
        out_specs=out_specs or whole(len(outputs)),
        out_shape=list(outputs),
        scratch_shapes=list(buffers),
        compiler_params=pltpu.CompilerParams(vmem_limit_bytes=8 * 2**20),
        cost_estimate=pl.CostEstimate(
            flops=operations, bytes_accessed=size, transcendentals=0
        ),
        name=name,
    )(*inputs)


def span_sums(columns):
    if lax.axis_size("gz") == 2:
        return columns
    return lax.psum(columns, "gz")


def local(flow_far, rho_far, temp_far, psi_far):
    inside, across = pairs()
    add_other = lax.axis_size("gz") == 2
    field, planes, edges = shape_of((5, CX)), shape_of((5, CX + 6)), shape_of((5, 2), BF16)
    slopes = shape_of((5, 2, CX))
    inputs = (flow_far, rho_far, temp_far, psi_far)
    stay = [pl.BlockSpec(memory_space=pltpu.MemorySpace.HBM)] * 4
    far, far_scalars, flow, rho, temp, psi = call(
        message_kernel,
        "message",
        inputs,
        [
            shape_of((SCALARS,), BF16),
            shape_of((SCALAR_PLANES,), BF16),
            shape_of((2, 3, CX), BF16),
            shape_of((2, CX), BF16),
            shape_of((2, CX), BF16),
            field,
        ],
        1_000_000,
        [pltpu.SemaphoreType.DMA((5,))],
        stay,
    )
    far = lax.ppermute(far, "gx", across)
    near, near_scalars, message, own_low = call(
        pack_kernel,
        "pack",
        (flow, rho, temp, psi),
        [
            shape_of((SCALARS,), BF16),
            shape_of((SCALAR_PLANES,), BF16),
            shape_of((STRIP_BLOCKS + BAND_BLOCKS,), BF16),
            shape_of((6,)),
        ],
        2_000_000,
    )
    far_scalars = lax.ppermute(far_scalars, "gx", across)
    near = lax.ppermute(near, "gx", inside)
    near_scalars = lax.ppermute(near_scalars, "gx", inside)
    own_halo = span_edges(message, STRIP_BLOCKS)
    rows = call(
        rows_kernel,
        "rows",
        (flow, rho, temp, psi),
        [field] * 6,
        3_000_000,
    )
    grad_0, grad_1, lap_0, lap_1, psi_rate, psi_lap = call(
        own_kernel,
        "own",
        (flow, rho, temp, psi, own_halo, *rows),
        [slopes, slopes, field, field, field, field],
        5_000_000,
        scratch((2, 5, CX), (5, CX)),
    )
    (token,) = call(token_kernel, "token", (far, rows[5]), [shape_of(())], 100_000)
    message, low = call(
        bands_kernel,
        "bands",
        (own_low, near, far, token),
        [shape_of((BAND_BLOCKS,), BF16), shape_of((6,))],
        1_000_000,
    )
    halo = span_edges(message, 0)
    inner, high, velocity, grad_x, lap_velocity, sizes = call(
        inner_kernel,
        "inner",
        (flow, near, far, grad_0, lap_0),
        [
            shape_of((2, CX)), shape_of((3,)), shape_of((3, CX + 6)),
            shape_of((3, CX)), shape_of((3, CX)), shape_of((CX,)),
        ],
        20_000_000,
        scratch((21, CX + 2), (21, CX)),
    )
    (products,) = call(
        edge_kernel,
        "edge",
        (low, high, halo, inner),
        [shape_of(())],
        20_000_000,
        scratch((2, 3), (21,), (2, CX)),
    )
    (token,) = call(token_kernel, "later_token", (far_scalars, products), [shape_of(())], 100_000)
    first, second, message, columns = call(
        first_kernel,
        "first",
        (
            token, products, rho, temp, psi, near_scalars, far_scalars,
            velocity, grad_x, lap_velocity, sizes, grad_0, lap_0, psi_rate, psi_lap,
        ),
        [field, field, shape_of((2,), BF16), shape_of(())],
        10_000_000,
        scratch((5, CX + 6), (5, CX + 6), (CX,)),
    )
    other = span_edges(message, 2)
    columns = span_sums(columns)
    wide, grad_x, lap_velocity, sizes, message, later = call(
        later_kernel,
        "later",
        (
            flow, rho, temp, near, far, near_scalars, far_scalars,
            grad_1, lap_1, low, halo, first, second,
        ),
        [
            planes, shape_of((3, CX)), shape_of((3, CX)), shape_of((CX,)),
            shape_of((1,), BF16), shape_of(()),
        ],
        20_000_000,
        scratch((3,), (21, CX + 2), (21, CX), (2, CX), (2, 3), (21,), (2, CX)),
    )
    later_other = span_edges(message, 1)
    later = span_sums(later)
    first, later = lax.optimization_barrier((first, later))
    psi, far, coef_first = call(
        functools.partial(middle_kernel, add_other),
        "middle",
        (first, second, columns, other),
        [field, edges, shape_of((CX,))],
        1_000_000,
    )
    far = lax.ppermute(far, "gx", across)
    base, drift, spread, coef_grad, near = call(
        functools.partial(base_kernel, add_other, LANES * lax.axis_size("gz")),
        "base",
        (
            wide, grad_x, lap_velocity, sizes, grad_1, lap_1, psi, coef_first,
            columns, other, later, later_other,
        ),
        [
            field, shape_of((CX,)), shape_of((2, 2)),
            jax.ShapeDtypeStruct((2, CX, ROWS), F32), edges,
        ],
        15_000_000,
        scratch((5, CX), (5, CX + 6), (CX,), (5, CX), (5, CX)),
    )
    near = lax.ppermute(near, "gx", inside)
    (far,) = call(widen_kernel, "widen", (far,), [shape_of((5, 2))], 100_000)
    (out,) = call(
        last_kernel,
        "last",
        (base, drift, spread, near, far),
        [field],
        1_000_000,
        scratch((5, CX)) + [pltpu.SemaphoreType.DMA((5,))],
        out_specs=stay[:1],
    )
    return out, coef_grad


def solution(mesh):
    return jax.shard_map(
        local,
        mesh=mesh,
        in_specs=(
            P(None, None, "gx", None, "gz"),
            P(None, "gx", None, "gz"),
            P(None, "gx", None, "gz"),
            P(None, "gx", None, "gz"),
        ),
        out_specs=(P(None, "gx", None, "gz"), P(None, "gx", None)),
        check_vma=False,
    )
```

```python
import functools
import math

import jax
import jax.numpy as jnp
from jax import lax
from jax.experimental import pallas as pl
from jax.experimental.pallas import tpu as pltpu
from jax.sharding import PartitionSpec as P

EPSILON = 1e-06
NU_MOL = 0.05
PRANDTL = 0.72
PRANDTL_TURB = 0.9
TIME_STEP = 0.04
PAIRS = ((0, 0), (1, 1), (2, 2), (0, 1), (0, 2), (1, 2))
WEIGHTS = (1.0, 1.0, 1.0, 2.0, 2.0, 2.0)

CX = 4
ROWS = 32
LANES = 128
STRIP = 4
F32 = jnp.float32
BF16 = jnp.bfloat16
SLOT_PSI = 4
BAND = 12
STRIP_BLOCKS = 2
BAND_BLOCKS = 3
VELOCITY = 0
SCALARS = 18
PSI = 8
SCALAR_PLANES = 18


def lane_ids():
    return lax.broadcasted_iota(jnp.int32, (ROWS, LANES), 1)


def row_ids():
    return lax.broadcasted_iota(jnp.int32, (ROWS, LANES), 0)


def turn(values, shift):
    shift = shift % LANES
    return values if shift == 0 else pltpu.roll(values, shift, 1)


class Ops:
    def __init__(self):
        self.lane = lane_ids()
        row = row_ids()
        self.top = row == ROWS - 1
        self.bottom = row == 0

    def z_at(self, values, halo, step):
        if step > 0:
            return turn(jnp.where(self.lane < step, halo, values), -step)
        return turn(jnp.where(self.lane >= LANES + step, halo, values), -step)

    def y_up(self, values):
        return jnp.where(self.top, 0.0, pltpu.roll(values, ROWS - 1, 0))

    def y_down(self, values):
        return jnp.where(self.bottom, 0.0, pltpu.roll(values, 1, 0))

    def strip(self, blocks, slot, x):
        return turn(blocks[slot // 8], -(STRIP * (4 * (slot % 8) + x) + 2))


def fourth(plus, minus, plus_2, minus_2):
    return (2.0 / 3.0) * (plus - minus) - (1.0 / 12.0) * (plus_2 - minus_2)


def strain_of(grad):
    return [
        grad[0][0],
        grad[1][1],
        grad[2][2],
        0.5 * (grad[0][1] + grad[1][0]),
        0.5 * (grad[0][2] + grad[2][0]),
        0.5 * (grad[1][2] + grad[2][1]),
    ]


def size_of(strain):
    diagonal = strain[0] * strain[0] + strain[1] * strain[1] + strain[2] * strain[2]
    other = strain[3] * strain[3] + strain[4] * strain[4] + strain[5] * strain[5]
    return jnp.sqrt(2.0 * diagonal + (4.0 * other + EPSILON))


def filter_fields(velocity, strain, size):
    products = [velocity[a] * velocity[b] for a, b in PAIRS]
    return list(velocity) + products + strain + [size * part for part in strain]


def pack_strips(ops, items):
    block = jnp.zeros((ROWS, LANES), F32)
    strip_id = ops.lane >> 2
    for slot, planes in enumerate(items):
        for x in range(CX):
            number = 4 * slot + x
            block = jnp.where(strip_id == number, turn(planes[x], STRIP * number + 2), block)
    return block


def place_halos(ops, t, own_halo, halos):
    strips = [own_halo[number].astype(F32) for number in range(STRIP_BLOCKS)]
    for k in range(3):
        number = 3 * t + k
        bands = own_halo[STRIP_BLOCKS + number // 2].astype(F32)
        for x in range(CX):
            halos[k, x] = turn(bands, -(BAND * (x + 3) + 3 + 6 * (number % 2)))
    for k in range(3, 5):
        for x in range(CX):
            halos[k, x] = ops.strip(strips, 2 * t + k - 3, x)


def y_terms(ops, values):
    up, down = ops.y_up(values), ops.y_down(values)
    return 0.5 * (up - down), (up + down) - 6.0 * values


def z_terms(ops, values, halo):
    zs = [ops.z_at(values, halo, step) for step in (1, -1, 2, -2)]
    return fourth(*zs), zs[0] + zs[1]


def state_terms(wide, grad_x, grad_yz, lap_velocity, lap_yz, sizes, x):
    grad = [[None] * 5 for _ in range(3)]
    lap = [None] * 5
    center = [wide[k, x + 3] for k in range(5)]
    for k in range(5):
        if k < 3:
            grad[0][k], lap[k] = grad_x[k, x], lap_velocity[k, x]
        else:
            xs = [wide[k, x + 3 + step] for step in (1, -1, 2, -2)]
            grad[0][k] = fourth(*xs)
            lap[k] = lap_yz[k, x] + (xs[0] + xs[1])
        grad[1][k], grad[2][k] = grad_yz[k, 0, x], grad_yz[k, 1, x]
    return center, grad, lap, sizes[x], 1.0 / center[3]


def affine_update(terms, psi, rates, laps):
    center, grad, lap, size, inv_rho = terms
    work_mom = psi[0] * lap[0] + psi[1] * lap[1] + psi[2] * lap[2]
    work_heat = psi[4] * lap[4]
    turbulent = work_mom + work_heat * (1.0 / PRANDTL_TURB)
    inv_rho_2 = inv_rho * inv_rho
    size_rho = size * inv_rho
    first, second = [], []
    for k in range(5):
        rate = rates[k]
        if k == 3:
            rate = rate - (NU_MOL * work_mom + (NU_MOL / PRANDTL) * work_heat) * inv_rho_2
            eddy = -(size * turbulent) * inv_rho_2
        else:
            lap_psi = laps[k]
            if k < 3:
                for other in range(5 if k == 0 else 0):
                    rate = rate + psi[other] * grad[k][other]
                rate = rate + NU_MOL * (inv_rho * lap_psi)
                eddy = size_rho * lap_psi
            else:
                rate = rate + (NU_MOL / PRANDTL) * (inv_rho * lap_psi)
                eddy = (1.0 / PRANDTL_TURB) * (size_rho * lap_psi)
        first.append(psi[k] + TIME_STEP * rate)
        second.append(TIME_STEP * eddy)
    return first, second, size_rho * turbulent


def band_of(lane):
    return (lane * 43) >> 9


def is_even():
    return lax.rem(lax.axis_index("gx"), 2) == 0


def fill_scalars(out, side, rho, temp, psi):
    for t in range(2):
        for i in range(2):
            out[2 * t + i] = rho[t, 2 * side + i]
            out[4 + 2 * t + i] = temp[t, 2 * side + i]
    for k in range(5):
        for i in range(2):
            out[PSI + k * 2 + i] = psi[k, 2 * side + i].astype(BF16)


def merge_bands(ops, low, message, first):
    lower = ops.lane - BAND * band_of(ops.lane) < 6
    for number in range(BAND_BLOCKS):
        both = jnp.where(lower, low[2 * number], turn(low[2 * number + 1], 6))
        message[first + number] = both.astype(BF16)


def message_kernel(
    flow_far, rho_far, temp_far, psi_far, far, far_scalars, flow, rho, temp, psi, sems
):
    side = 1 - is_even().astype(jnp.int32)
    pieces = (
        (flow_far.at[:, :, pl.ds(side, 3)], far.reshape((2, 3, 3, ROWS, LANES))),
        (psi_far, psi),
        (rho_far, rho),
        (temp_far, temp),
        (flow_far, flow),
    )
    copies = [
        pltpu.make_async_copy(source, target, sems.at[number])
        for number, (source, target) in enumerate(pieces)
    ]
    for copy in copies:
        copy.start()
    for copy in copies[1:4]:
        copy.wait()
    fill_scalars(far_scalars, side, rho, temp, psi)
    copies[0].wait()
    copies[4].wait()


def pack_kernel(flow, rho, temp, psi, near, near_scalars, message, low):
    ops = Ops()
    side = is_even().astype(jnp.int32)
    for t in range(2):
        for k in range(3):
            for i in range(3):
                near[VELOCITY + t * 9 + k * 3 + i] = flow[t, k, side + i]
    fill_scalars(near_scalars, side, rho, temp, psi)
    items = []
    for t in range(2):
        for source in (rho, temp):
            items.append([source[t, x].astype(F32) for x in range(CX)])
    items += [[psi[k, x] for x in range(CX)] for k in range(5)]
    for number in range(STRIP_BLOCKS):
        message[number] = pack_strips(ops, items[8 * number : 8 * number + 8]).astype(BF16)
    band = band_of(ops.lane)
    for t in range(2):
        for k in range(3):
            block = jnp.zeros((ROWS, LANES), F32)
            for x in range(CX):
                moved = turn(flow[t, k, x].astype(F32), BAND * (x + 3) + 3)
                block = jnp.where(band == x + 3, moved, block)
            low[3 * t + k] = block
    merge_bands(ops, low, message, STRIP_BLOCKS)


def rows_kernel(flow, rho, temp, psi, grad_0, grad_1, lap_0, lap_1, psi_rate, psi_lap):
    ops = Ops()
    for t, grad_y, lap_y in ((0, grad_0, lap_0), (1, grad_1, lap_1)):
        for k in range(5):
            for x in range(CX):
                values = flow[t, k, x] if k < 3 else (rho if k == 3 else temp)[t, x]
                grad_y[k, x], lap_y[k, x] = y_terms(ops, values.astype(F32))
    for x in range(CX):
        along_y = flow[0, 1, x].astype(F32)
        for k in range(5):
            by_y, psi_lap[k, x] = y_terms(ops, psi[k, x])
            psi_rate[k, x] = along_y * by_y


def own_kernel(
    flow, rho, temp, psi, own_halo, grad_y_0, grad_y_1, lap_y_0, lap_y_1, rate_y, psi_lap_y,
    grad_0, grad_1, lap_0, lap_1, psi_rate, psi_lap,
    halos, psi_halos,
):
    ops = Ops()
    for t in range(2):
        place_halos(ops, t, own_halo, halos.at[t])
    strips = [own_halo[number].astype(F32) for number in range(STRIP_BLOCKS)]
    for k in range(5):
        for x in range(CX):
            psi_halos[k, x] = ops.strip(strips, SLOT_PSI + k, x)
    for t, grad_y, lap_y, grad_yz, lap_yz in (
        (0, grad_y_0, lap_y_0, grad_0, lap_0),
        (1, grad_y_1, lap_y_1, grad_1, lap_1),
    ):
        for k in range(5):
            for x in range(CX):
                values = flow[t, k, x] if k < 3 else (rho if k == 3 else temp)[t, x]
                by_z, both = z_terms(ops, values.astype(F32), halos[t, k, x])
                grad_yz[k, 0, x], grad_yz[k, 1, x] = grad_y[k, x], by_z
                lap_yz[k, x] = lap_y[k, x] + both
    for x in range(CX):
        along_z = flow[0, 2, x].astype(F32)
        for k in range(5):
            by_z, both = z_terms(ops, psi[k, x], psi_halos[k, x])
            rate = rate_y[k, x] + along_z * by_z
            for other in range(5 if k in (1, 2) else 0):
                rate = rate + psi[other, x] * grad_0[other, k - 1, x]
            psi_rate[k, x] = rate
            psi_lap[k, x] = psi_lap_y[k, x] + both


def token_kernel(far, _, out):
    out[...] = far[0].astype(F32)


def bands_kernel(own_low, near, far, _, message, low):
    ops = Ops()
    even = is_even()
    band = band_of(ops.lane)
    for t in range(2):
        for k in range(3):
            block = own_low[3 * t + k]
            for i in range(3):
                number = VELOCITY + t * 9 + k * 3 + i
                one, two = near[number].astype(F32), far[number].astype(F32)
                moved = turn(jnp.where(even, two, one), BAND * i + 3)
                block = jnp.where(band == i, moved, block)
                moved = turn(jnp.where(even, one, two), BAND * (7 + i) + 3)
                block = jnp.where(band == 7 + i, moved, block)
            low[3 * t + k] = block
    merge_bands(ops, low, message, 0)


def products_of(hat):
    velocity = [hat(k) for k in range(3)]
    strain = [hat(9 + number) for number in range(6)]
    diagonal = strain[0] * strain[0] + strain[1] * strain[1] + strain[2] * strain[2]
    other = strain[3] * strain[3] + strain[4] * strain[4] + strain[5] * strain[5]
    size = 4.0 * jnp.sqrt((2.0 / 256.0) * diagonal + ((4.0 / 256.0) * other + EPSILON))
    cross = 0.0
    square = 0.0
    for number, (a, b) in enumerate(PAIRS):
        leonard = hat(3 + number) - (1.0 / 16.0) * velocity[a] * velocity[b]
        model = hat(15 + number) - size * strain[number]
        weighted = WEIGHTS[number] * model if WEIGHTS[number] != 1.0 else model
        cross = cross + leonard * weighted
        square = square + model * weighted
    return cross, square


def widen(k, source, near, far, count, even, wide):
    for i in range(count):
        one, two = near(i), far(i)
        wide[k, 3 - count + i] = jnp.where(even, two, one)
        wide[k, 3 + CX + i] = jnp.where(even, one, two)
    for x in range(CX):
        wide[k, 3 + x] = source(x).astype(F32)


def widen_scalars(t, rho, temp, near, far, even, wide):
    for k, source in ((3, rho), (4, temp)):
        number = (k - 3) * 4 + 2 * t
        widen(
            k,
            lambda x: source[t, x],
            lambda i: near[number + i].astype(F32),
            lambda i: far[number + i].astype(F32),
            2, even, wide,
        )


def inner_products(
    ops, t, flow, near, far, grad_yz, lap_yz,
    sums, high, wide, grad_x, lap_velocity, sizes, fields, hats,
):
    even = is_even()
    valid = (ops.lane >= 3) & (ops.lane < LANES - 3)
    band = band_of(jnp.maximum(ops.lane - 2, 0))
    for k in range(3):
        widen(
            k,
            lambda x: flow[t, k, x],
            lambda i: near[VELOCITY + t * 9 + k * 3 + i].astype(F32),
            lambda i: far[VELOCITY + t * 9 + k * 3 + i].astype(F32),
            3, even, wide,
        )
    for x in range(-1, CX + 1):
        grad = [[None] * 3 for _ in range(3)]
        for k in range(3):
            center = wide[k, x + 3]
            xs = [wide[k, x + 3 + step] for step in (1, -1, 2, -2)]
            grad[0][k] = fourth(*xs)
            if 0 <= x < CX:
                grad_x[k, x] = grad[0][k]
                lap_velocity[k, x] = lap_yz[k, x] + (xs[0] + xs[1])
                grad[1][k], grad[2][k] = grad_yz[k, 0, x], grad_yz[k, 1, x]
            else:
                grad[1][k] = 0.5 * (ops.y_up(center) - ops.y_down(center))
                grad[2][k] = fourth(*(turn(center, -step) for step in (1, -1, 2, -2)))
        strain = strain_of(grad)
        size = size_of(strain)
        if 0 <= x < CX:
            sizes[x] = size
        velocity = [wide[k, x + 3] for k in range(3)]
        for number, values in enumerate(filter_fields(velocity, strain, size)):
            fields[number, x + 1] = values
    for x in range(CX):
        for number in range(21):
            along_x = fields[number, x] + fields[number, x + 2] + 2.0 * fields[number, x + 1]
            hats[number, x] = turn(along_x, 1) + turn(along_x, -1) + 2.0 * along_x
    for k in range(3):
        block = jnp.zeros((ROWS, LANES), F32)
        for q in range(CX + 6):
            block = jnp.where(band == q, turn(wide[k, q], BAND * q + 11), block)
        high[k] = block
    for x in range(CX):
        cross, square = products_of(lambda number: hats[number, x])
        sums[0, x] = jnp.where(valid, cross, 0.0)
        sums[1, x] = jnp.where(valid, square, 0.0)


def edge_products(ops, t, low, high, halo, sums, bands, spread):
    band = band_of(ops.lane)
    place = ops.lane - BAND * band
    from_low = place < 3
    from_high = (place == 11) | (place < 2)
    low_side = place < 7
    at_edge = ((place >= 3) & (place <= 5)) | ((place >= 8) & (place <= 10))
    for k in range(3):
        number = 3 * t + k
        far = halo[number // 2].astype(F32)
        shift = 6 * (number % 2)
        bands[0, k] = jnp.where(from_low, turn(far, -shift), low[number])
        bands[1, k] = jnp.where(from_high, turn(far, 8 - shift), high[k])
    for side in range(2):
        velocity = [bands[side, k] for k in range(3)]
        grad = [[None] * 3 for _ in range(3)]
        for k in range(3):
            center = velocity[k]
            grad[0][k] = fourth(*(turn(center, -BAND * step) for step in (1, -1, 2, -2)))
            grad[1][k] = 0.5 * (ops.y_up(center) - ops.y_down(center))
            grad[2][k] = fourth(*(turn(center, -step) for step in (1, -1, 2, -2)))
        strain = strain_of(grad)
        for number, values in enumerate(filter_fields(velocity, strain, size_of(strain))):
            if side == 0:
                spread[number] = values
            else:
                spread[number] = jnp.where(low_side, spread[number], values)
    for number in range(21):
        both = spread[number]
        spread[number] = turn(both, BAND) + turn(both, -BAND) + 2.0 * both
    for number in range(21):
        both = spread[number]
        spread[number] = turn(both, 1) + turn(both, -1) + 2.0 * both
    for part, values in enumerate(products_of(lambda number: spread[number])):
        values = jnp.where(at_edge, values, 0.0)
        for x in range(CX):
            sums[part, x] = sums[part, x] + jnp.where(band == x + 3, values, 0.0)


def add_columns(ops, total, first_lane, planes, scale=1.0):
    for x in range(CX):
        value = scale * jnp.sum(planes(x), axis=1, keepdims=True)
        total = jnp.where(ops.lane == first_lane + x, value, total)
    return total


def add_parts(ops, block, total):
    upper = total.astype(BF16).astype(F32)
    rest = total - upper
    middle = rest.astype(BF16).astype(F32)
    for number, part in enumerate((upper, middle, rest - middle)):
        block = jnp.where(ops.lane >> 5 == 1 + number, turn(part, 32 * (1 + number)), block)
    return block


def span_total(add_other, columns, other):
    total = columns[...]
    if add_other:
        parts = other.astype(F32)
        total = total + ((turn(parts, -32) + turn(parts, -64)) + turn(parts, -96))
    return total


def psi_terms(psi_wide, rate_yz, lap_yz, velocity, x):
    rates, laps = [], []
    for k in range(5):
        xs = [psi_wide[k, x + 3 + step] for step in (1, -1, 2, -2)]
        rates.append(rate_yz[k, x] + velocity * fourth(*xs))
        laps.append(lap_yz[k, x] + (xs[0] + xs[1]))
    return rates, laps


def inner_kernel(
    flow, near, far, grad_yz, lap_yz,
    sums, high, wide, grad_x, lap_velocity, sizes,
    fields, hats,
):
    inner_products(
        Ops(), 0, flow, near, far, grad_yz, lap_yz,
        sums, high, wide, grad_x, lap_velocity, sizes, fields, hats,
    )


def first_kernel(
    _, products, rho, temp, psi, near, far, velocity, grad_x, lap_velocity, sizes,
    grad_yz, lap_yz, psi_rate, psi_lap,
    first, second, message, columns,
    wide, psi_wide, work,
):
    ops = Ops()
    even = is_even()
    for k in range(3):
        for x in range(CX):
            wide[k, x + 3] = velocity[k, x + 3]
    widen_scalars(0, rho, temp, near, far, even, wide)
    for k in range(5):
        widen(
            k,
            lambda x: psi[k, x],
            lambda i: near[PSI + k * 2 + i].astype(F32),
            lambda i: far[PSI + k * 2 + i].astype(F32),
            2, even, psi_wide,
        )
    for x in range(CX):
        terms = state_terms(wide, grad_x, grad_yz, lap_velocity, lap_yz, sizes, x)
        rates, laps = psi_terms(psi_wide, psi_rate, psi_lap, terms[0][0], x)
        new, slope, sensitivity = affine_update(
            terms, [psi[k, x] for k in range(5)], rates, laps
        )
        for k in range(5):
            first[k, x] = new[k]
            second[k, x] = slope[k]
        work[x] = sensitivity
    total = add_columns(ops, products[...], 16, lambda x: work[x])
    columns[...] = total
    items = [[part[k, x] for x in range(CX)] for part in (first, second) for k in range(5)]
    message[0] = pack_strips(ops, items[:8]).astype(BF16)
    message[1] = add_parts(ops, pack_strips(ops, items[8:]), total).astype(BF16)


def edge_kernel(low, high, halo, inner, columns, bands, spread, sums):
    ops = Ops()
    for part in range(2):
        for x in range(CX):
            sums[part, x] = inner[part, x]
    edge_products(ops, 0, low, high, halo, sums, bands, spread)
    total = jnp.zeros((ROWS, LANES), F32)
    for part in range(2):
        total = add_columns(ops, total, 4 * part, lambda x: sums[part, x], 1.0 / 256.0)
    columns[...] = total


def later_kernel(
    flow, rho, temp, near, far, near_scalars, far_scalars,
    grad_yz, lap_yz, low, halo, first, second,
    wide, grad_x, lap_velocity, sizes, message, columns,
    high, fields, hats, work, bands, spread, sums,
):
    ops = Ops()
    inner_products(
        ops, 1, flow, near, far, grad_yz, lap_yz,
        sums, high, wide, grad_x, lap_velocity, sizes, fields, hats,
    )
    widen_scalars(1, rho, temp, near_scalars, far_scalars, is_even(), wide)
    edge_products(ops, 1, low, high, halo, sums, bands, spread)
    for x in range(CX):
        _, _, lap, size, inv_rho = state_terms(
            wide, grad_x, grad_yz, lap_velocity, lap_yz, sizes, x
        )
        size_rho = size * inv_rho
        for part, source in enumerate((first, second)):
            total = lap[0] * source[0, x] + lap[1] * source[1, x] + lap[2] * source[2, x]
            work[part, x] = size_rho * (
                total + (1.0 / PRANDTL_TURB) * (lap[4] * source[4, x])
            )
    total = jnp.zeros((ROWS, LANES), F32)
    for part in range(2):
        total = add_columns(ops, total, 8 + 4 * part, lambda x: sums[part, x], 1.0 / 256.0)
        total = add_columns(ops, total, 20 + 4 * part, lambda x: work[part, x])
    columns[...] = total
    message[0] = add_parts(ops, jnp.zeros((ROWS, LANES), F32), total).astype(BF16)


def coefficients(ops, total):
    return total / (turn(total, -4) + EPSILON)


def middle_kernel(add_other, first, second, columns, other, psi, far, coef_first):
    ops = Ops()
    coef = coefficients(ops, span_total(add_other, columns, other[1]))
    for x in range(CX):
        coef_first[x] = jnp.broadcast_to(coef[:, x : x + 1], (ROWS, LANES))
    for x in range(CX):
        for k in range(5):
            psi[k, x] = first[k, x] + coef_first[x] * second[k, x]
    side = 1 - is_even().astype(jnp.int32)
    for k in range(5):
        for i in range(2):
            far[k, i] = psi[k, 2 * side + i].astype(BF16)


def base_kernel(
    add_other, span_cells,
    wide, grad_x, lap_velocity, sizes, grad_yz, lap_yz, psi, coef_first,
    columns, other, later, later_other,
    base, drift, spread, coef_grad, near,
    psi_halos, psi_wide, coef_planes, psi_rate, psi_lap,
):
    ops = Ops()
    side = is_even().astype(jnp.int32)
    for k in range(5):
        for i in range(2):
            near[k, i] = psi[k, 2 * side + i].astype(BF16)
    strips = [other[number].astype(F32) for number in range(2)]
    for k in range(5):
        for x in range(CX):
            psi_halos[k, x] = ops.strip(strips, k, x)
    total = span_total(add_other, columns, other[1]) + span_total(
        add_other, later, later_other[0]
    )
    coef = coefficients(ops, total)
    after = total + turn(coef, 20) * turn(total, -4)
    grads = jnp.where(ops.lane < 20, total, after) * (1.0 / span_cells)
    turned = jnp.concatenate([grads] * (LANES // ROWS), axis=0).T
    for t in range(2):
        coef_grad[t] = turned[16 + 4 * t : 20 + 4 * t, :ROWS]
    for x in range(CX):
        coef_planes[x] = jnp.broadcast_to(coef[:, 8 + x : 9 + x], (ROWS, LANES))
    for k in range(5):
        for x in range(CX):
            psi_halos[k, x] = psi_halos[k, x] + coef_first[x] * ops.strip(strips, 5 + k, x)
    zero = jnp.zeros((ROWS, LANES), F32)
    for k in range(5):
        for i in range(2):
            psi_wide[k, 1 + i] = zero
            psi_wide[k, 3 + CX + i] = zero
        for x in range(CX):
            psi_wide[k, 3 + x] = psi[k, x]
    for x in range(CX):
        for k in range(5):
            by_y, lap = y_terms(ops, psi[k, x])
            by_z, both = z_terms(ops, psi[k, x], psi_halos[k, x])
            rate = wide[1, x + 3] * by_y + wide[2, x + 3] * by_z
            for other in range(5 if k in (1, 2) else 0):
                rate = rate + psi[other, x] * grad_yz[other, k - 1, x]
            psi_rate[k, x] = rate
            psi_lap[k, x] = lap + both
    for x in range(CX):
        terms = state_terms(wide, grad_x, grad_yz, lap_velocity, lap_yz, sizes, x)
        center = terms[0]
        rates, laps = psi_terms(psi_wide, psi_rate, psi_lap, center[0], x)
        new, slope, _ = affine_update(terms, [psi[k, x] for k in range(5)], rates, laps)
        for k in range(5):
            base[k, x] = new[k] + coef_planes[x] * slope[k]
        size, inv_rho = terms[3:]
        drift[x] = TIME_STEP * center[0]
        if x in (0, CX - 1):
            eddy = coef_planes[x] * size
            scaled = TIME_STEP * inv_rho
            spread[x // (CX - 1), 0] = scaled * (NU_MOL + eddy)
            spread[x // (CX - 1), 1] = scaled * (
                NU_MOL / PRANDTL + (1.0 / PRANDTL_TURB) * eddy
            )


def widen_kernel(far, out):
    for k in range(5):
        for i in range(2):
            out[k, i] = far[k, i].astype(F32)


def last_kernel(base, drift, spread, near_psi, far_psi, out_far, out, sems):
    even = is_even()
    copies = []
    for k in range(5):
        ones = [near_psi[k, i].astype(F32) for i in range(2)]
        twos = [far_psi[k, i].astype(F32) for i in range(2)]
        far, near = (jnp.where(even, two, one) for one, two in zip(ones, twos))
        after, beyond = (jnp.where(even, one, two) for one, two in zip(ones, twos))
        low = drift[0] * ((1.0 / 12.0) * far - (2.0 / 3.0) * near)
        high = drift[CX - 1] * ((2.0 / 3.0) * after - (1.0 / 12.0) * beyond)
        if k != 3:
            kind = 1 if k == 4 else 0
            low = low + spread[0, kind] * near
            high = high + spread[1, kind] * after
        out[k, 0] = base[k, 0] + low
        out[k, 1] = base[k, 1] + drift[1] * ((1.0 / 12.0) * near)
        out[k, CX - 2] = base[k, CX - 2] - drift[CX - 2] * ((1.0 / 12.0) * after)
        out[k, CX - 1] = base[k, CX - 1] + high
        copies.append(pltpu.make_async_copy(out.at[k], out_far.at[k], sems.at[k]))
        copies[k].start()
    for copy in copies:
        copy.wait()


def ring(axis):
    count = lax.axis_size(axis)
    forward = [(i, (i + 1) % count) for i in range(count)]
    return forward, [(target, source) for source, target in forward]


def pairs():
    count = lax.axis_size("gx")
    if count % 2:
        raise ValueError("odd gx")
    inside = [(i, i ^ 1) for i in range(count)]
    across = [(i, (i + 1 if i % 2 else i - 1) % count) for i in range(count)]
    return inside, across


def span_edges(message, strips):
    forward, backward = ring("gz")
    before = lax.ppermute(message, "gz", forward)
    if lax.axis_size("gz") == 2:
        return before
    after = lax.ppermute(message, "gz", backward)
    lane = lax.broadcasted_iota(jnp.int32, message.shape, 2)
    number = lax.broadcasted_iota(jnp.int32, message.shape, 0)
    low = jnp.where(number < strips, lane % STRIP < 2, lane % 6 < 3)
    return jnp.where(low, before, after)


def shape_of(dims, kind=F32):
    return jax.ShapeDtypeStruct(dims + (ROWS, LANES), kind)


def whole(count):
    return [pl.BlockSpec(memory_space=pltpu.VMEM)] * count


def scratch(*dims):
    return [pltpu.VMEM(d + (ROWS, LANES), F32) for d in dims]


def call(kernel, name, inputs, outputs, operations, buffers=(), in_specs=None, out_specs=None):
    inputs = list(inputs)
    if in_specs:
        inputs[:4] = [
            pltpu.with_memory_space_constraint(a, pltpu.MemorySpace.HBM) for a in inputs[:4]
        ]
    size = sum(math.prod(a.shape) * a.dtype.itemsize for a in list(inputs) + list(outputs))
    return pl.pallas_call(
        kernel,
        in_specs=in_specs or whole(len(inputs)),
        out_specs=out_specs or whole(len(outputs)),
        out_shape=list(outputs),
        scratch_shapes=list(buffers),
        compiler_params=pltpu.CompilerParams(vmem_limit_bytes=8 * 2**20),
        cost_estimate=pl.CostEstimate(
            flops=operations, bytes_accessed=size, transcendentals=0
        ),
        name=name,
    )(*inputs)


def span_sums(columns):
    if lax.axis_size("gz") == 2:
        return columns
    return lax.psum(columns, "gz")


def local(flow_far, rho_far, temp_far, psi_far):
    inside, across = pairs()
    add_other = lax.axis_size("gz") == 2
    field, planes, edges = shape_of((5, CX)), shape_of((5, CX + 6)), shape_of((5, 2), BF16)
    slopes = shape_of((5, 2, CX))
    inputs = (flow_far, rho_far, temp_far, psi_far)
    stay = [pl.BlockSpec(memory_space=pltpu.MemorySpace.HBM)] * 4
    far, far_scalars, flow, rho, temp, psi = call(
        message_kernel,
        "message",
        inputs,
        [
            shape_of((SCALARS,), BF16),
            shape_of((SCALAR_PLANES,), BF16),
            shape_of((2, 3, CX), BF16),
            shape_of((2, CX), BF16),
            shape_of((2, CX), BF16),
            field,
        ],
        1_000_000,
        [pltpu.SemaphoreType.DMA((5,))],
        stay,
    )
    far = lax.ppermute(far, "gx", across)
    near, near_scalars, message, own_low = call(
        pack_kernel,
        "pack",
        (flow, rho, temp, psi),
        [
            shape_of((SCALARS,), BF16),
            shape_of((SCALAR_PLANES,), BF16),
            shape_of((STRIP_BLOCKS + BAND_BLOCKS,), BF16),
            shape_of((6,)),
        ],
        2_000_000,
    )
    far_scalars = lax.ppermute(far_scalars, "gx", across)
    near = lax.ppermute(near, "gx", inside)
    near_scalars = lax.ppermute(near_scalars, "gx", inside)
    own_halo = span_edges(message, STRIP_BLOCKS)
    rows = call(
        rows_kernel,
        "rows",
        (flow, rho, temp, psi),
        [field] * 6,
        3_000_000,
    )
    grad_0, grad_1, lap_0, lap_1, psi_rate, psi_lap = call(
        own_kernel,
        "own",
        (flow, rho, temp, psi, own_halo, *rows),
        [slopes, slopes, field, field, field, field],
        5_000_000,
        scratch((2, 5, CX), (5, CX)),
    )
    (token,) = call(token_kernel, "token", (far, rows[5]), [shape_of(())], 100_000)
    message, low = call(
        bands_kernel,
        "bands",
        (own_low, near, far, token),
        [shape_of((BAND_BLOCKS,), BF16), shape_of((6,))],
        1_000_000,
    )
    halo = span_edges(message, 0)
    inner, high, velocity, grad_x, lap_velocity, sizes = call(
        inner_kernel,
        "inner",
        (flow, near, far, grad_0, lap_0),
        [
            shape_of((2, CX)), shape_of((3,)), shape_of((3, CX + 6)),
            shape_of((3, CX)), shape_of((3, CX)), shape_of((CX,)),
        ],
        20_000_000,
        scratch((21, CX + 2), (21, CX)),
    )
    (products,) = call(
        edge_kernel,
        "edge",
        (low, high, halo, inner),
        [shape_of(())],
        20_000_000,
        scratch((2, 3), (21,), (2, CX)),
    )
    (token,) = call(token_kernel, "later_token", (far_scalars, products), [shape_of(())], 100_000)
    first, second, message, columns = call(
        first_kernel,
        "first",
        (
            token, products, rho, temp, psi, near_scalars, far_scalars,
            velocity, grad_x, lap_velocity, sizes, grad_0, lap_0, psi_rate, psi_lap,
        ),
        [field, field, shape_of((2,), BF16), shape_of(())],
        10_000_000,
        scratch((5, CX + 6), (5, CX + 6), (CX,)),
    )
    other = span_edges(message, 2)
    columns = span_sums(columns)
    wide, grad_x, lap_velocity, sizes, message, later = call(
        later_kernel,
        "later",
        (
            flow, rho, temp, near, far, near_scalars, far_scalars,
            grad_1, lap_1, low, halo, first, second,
        ),
        [
            planes, shape_of((3, CX)), shape_of((3, CX)), shape_of((CX,)),
            shape_of((1,), BF16), shape_of(()),
        ],
        20_000_000,
        scratch((3,), (21, CX + 2), (21, CX), (2, CX), (2, 3), (21,), (2, CX)),
    )
    later_other = span_edges(message, 1)
    later = span_sums(later)
    first, later = lax.optimization_barrier((first, later))
    psi, far, coef_first = call(
        functools.partial(middle_kernel, add_other),
        "middle",
        (first, second, columns, other),
        [field, edges, shape_of((CX,))],
        1_000_000,
    )
    far = lax.ppermute(far, "gx", across)
    base, drift, spread, coef_grad, near = call(
        functools.partial(base_kernel, add_other, LANES * lax.axis_size("gz")),
        "base",
        (
            wide, grad_x, lap_velocity, sizes, grad_1, lap_1, psi, coef_first,
            columns, other, later, later_other,
        ),
        [
            field, shape_of((CX,)), shape_of((2, 2)),
            jax.ShapeDtypeStruct((2, CX, ROWS), F32), edges,
        ],
        15_000_000,
        scratch((5, CX), (5, CX + 6), (CX,), (5, CX), (5, CX)),
    )
    near = lax.ppermute(near, "gx", inside)
    (far,) = call(widen_kernel, "widen", (far,), [shape_of((5, 2))], 100_000)
    (out,) = call(
        last_kernel,
        "last",
        (base, drift, spread, near, far),
        [field],
        1_000_000,
        scratch((5, CX)) + [pltpu.SemaphoreType.DMA((5,))],
        out_specs=stay[:1],
    )
    return out, coef_grad


def solution(mesh):
    return jax.shard_map(
        local,
        mesh=mesh,
        in_specs=(
            P(None, None, "gx", None, "gz"),
            P(None, "gx", None, "gz"),
            P(None, "gx", None, "gz"),
            P(None, "gx", None, "gz"),
        ),
        out_specs=(P(None, "gx", None, "gz"), P(None, "gx", None)),
        check_vma=False,
    )
```

```python
import functools
import math

import jax
import jax.numpy as jnp
from jax import lax
from jax.experimental import pallas as pl
from jax.experimental.pallas import tpu as pltpu
from jax.sharding import PartitionSpec as P

EPSILON = 1e-06
NU_MOL = 0.05
PRANDTL = 0.72
PRANDTL_TURB = 0.9
TIME_STEP = 0.04
PAIRS = ((0, 0), (1, 1), (2, 2), (0, 1), (0, 2), (1, 2))
WEIGHTS = (1.0, 1.0, 1.0, 2.0, 2.0, 2.0)

CX = 4
ROWS = 32
LANES = 128
STRIP = 4
F32 = jnp.float32
BF16 = jnp.bfloat16
SLOT_PSI = 4
BAND = 12
STRIP_BLOCKS = 2
BAND_BLOCKS = 3
VELOCITY = 0
SCALARS = 18
PSI = 8
SCALAR_PLANES = 18


def lane_ids():
    return lax.broadcasted_iota(jnp.int32, (ROWS, LANES), 1)


def row_ids():
    return lax.broadcasted_iota(jnp.int32, (ROWS, LANES), 0)


def turn(values, shift):
    shift = shift % LANES
    return values if shift == 0 else pltpu.roll(values, shift, 1)


class Ops:
    def __init__(self):
        self.lane = lane_ids()
        row = row_ids()
        self.top = row == ROWS - 1
        self.bottom = row == 0

    def z_at(self, values, halo, step):
        if step > 0:
            return turn(jnp.where(self.lane < step, halo, values), -step)
        return turn(jnp.where(self.lane >= LANES + step, halo, values), -step)

    def y_up(self, values):
        return jnp.where(self.top, 0.0, pltpu.roll(values, ROWS - 1, 0))

    def y_down(self, values):
        return jnp.where(self.bottom, 0.0, pltpu.roll(values, 1, 0))

    def strip(self, blocks, slot, x):
        return turn(blocks[slot // 8], -(STRIP * (4 * (slot % 8) + x) + 2))


def fourth(plus, minus, plus_2, minus_2):
    return (2.0 / 3.0) * (plus - minus) - (1.0 / 12.0) * (plus_2 - minus_2)


def strain_of(grad):
    return [
        grad[0][0],
        grad[1][1],
        grad[2][2],
        0.5 * (grad[0][1] + grad[1][0]),
        0.5 * (grad[0][2] + grad[2][0]),
        0.5 * (grad[1][2] + grad[2][1]),
    ]


def size_of(strain):
    diagonal = strain[0] * strain[0] + strain[1] * strain[1] + strain[2] * strain[2]
    other = strain[3] * strain[3] + strain[4] * strain[4] + strain[5] * strain[5]
    return jnp.sqrt(2.0 * diagonal + (4.0 * other + EPSILON))


def filter_fields(velocity, strain, size):
    products = [velocity[a] * velocity[b] for a, b in PAIRS]
    return list(velocity) + products + strain + [size * part for part in strain]


def pack_strips(ops, items):
    block = jnp.zeros((ROWS, LANES), F32)
    strip_id = ops.lane >> 2
    for slot, planes in enumerate(items):
        for x in range(CX):
            number = 4 * slot + x
            block = jnp.where(strip_id == number, turn(planes[x], STRIP * number + 2), block)
    return block


def place_halos(ops, t, own_halo, halos):
    strips = [own_halo[number].astype(F32) for number in range(STRIP_BLOCKS)]
    for k in range(3):
        number = 3 * t + k
        bands = own_halo[STRIP_BLOCKS + number // 2].astype(F32)
        for x in range(CX):
            halos[k, x] = turn(bands, -(BAND * (x + 3) + 3 + 6 * (number % 2)))
    for k in range(3, 5):
        for x in range(CX):
            halos[k, x] = ops.strip(strips, 2 * t + k - 3, x)


def y_terms(ops, values):
    up, down = ops.y_up(values), ops.y_down(values)
    return 0.5 * (up - down), (up + down) - 6.0 * values


def z_terms(ops, values, halo):
    zs = [ops.z_at(values, halo, step) for step in (1, -1, 2, -2)]
    return fourth(*zs), zs[0] + zs[1]


def state_terms(wide, grad_x, grad_yz, lap_velocity, lap_yz, sizes, x):
    grad = [[None] * 5 for _ in range(3)]
    lap = [None] * 5
    center = [wide[k, x + 3] for k in range(5)]
    for k in range(5):
        if k < 3:
            grad[0][k], lap[k] = grad_x[k, x], lap_velocity[k, x]
        else:
            xs = [wide[k, x + 3 + step] for step in (1, -1, 2, -2)]
            grad[0][k] = fourth(*xs)
            if k != 3:
                lap[k] = lap_yz[k, x] + (xs[0] + xs[1])
        grad[1][k], grad[2][k] = grad_yz[k, 0, x], grad_yz[k, 1, x]
    return center, grad, lap, sizes[x], 1.0 / center[3]


def affine_update(terms, psi, rates, laps):
    center, grad, lap, size, inv_rho = terms
    work_mom = psi[0] * lap[0] + psi[1] * lap[1] + psi[2] * lap[2]
    work_heat = psi[4] * lap[4]
    turbulent = work_mom + work_heat * (1.0 / PRANDTL_TURB)
    inv_rho_2 = inv_rho * inv_rho
    size_rho = size * inv_rho
    first, second = [], []
    for k in range(5):
        rate = rates[k]
        if k == 3:
            rate = rate - (NU_MOL * work_mom + (NU_MOL / PRANDTL) * work_heat) * inv_rho_2
            eddy = -(size * turbulent) * inv_rho_2
        else:
            lap_psi = laps[k]
            if k < 3:
                for other in range(5):
                    rate = rate + psi[other] * grad[k][other]
                rate = rate + NU_MOL * (inv_rho * lap_psi)
                eddy = size_rho * lap_psi
            else:
                rate = rate + (NU_MOL / PRANDTL) * (inv_rho * lap_psi)
                eddy = (1.0 / PRANDTL_TURB) * (size_rho * lap_psi)
        first.append(psi[k] + TIME_STEP * rate)
        second.append(TIME_STEP * eddy)
    return first, second, size_rho * turbulent


def band_of(lane):
    return (lane * 43) >> 9


def is_even():
    return lax.rem(lax.axis_index("gx"), 2) == 0


def fill_scalars(out, side, rho, temp, psi):
    for t in range(2):
        for i in range(2):
            out[2 * t + i] = rho[t, 2 * side + i]
            out[4 + 2 * t + i] = temp[t, 2 * side + i]
    for k in range(5):
        for i in range(2):
            out[PSI + k * 2 + i] = psi[k, 2 * side + i].astype(BF16)


def merge_bands(ops, low, message, first):
    lower = ops.lane - BAND * band_of(ops.lane) < 6
    for number in range(BAND_BLOCKS):
        both = jnp.where(lower, low[2 * number], turn(low[2 * number + 1], 6))
        message[first + number] = both.astype(BF16)


def message_kernel(
    flow_far, rho_far, temp_far, psi_far, far, far_scalars, flow, rho, temp, psi, sems
):
    side = 1 - is_even().astype(jnp.int32)
    pieces = (
        (flow_far.at[:, :, pl.ds(side, 3)], far.reshape((2, 3, 3, ROWS, LANES))),
        (psi_far, psi),
        (rho_far, rho),
        (temp_far, temp),
        (flow_far, flow),
    )
    copies = [
        pltpu.make_async_copy(source, target, sems.at[number])
        for number, (source, target) in enumerate(pieces)
    ]
    for copy in copies:
        copy.start()
    for copy in copies[1:4]:
        copy.wait()
    fill_scalars(far_scalars, side, rho, temp, psi)
    copies[0].wait()
    copies[4].wait()


def pack_kernel(flow, rho, temp, psi, near, near_scalars, message, low):
    ops = Ops()
    side = is_even().astype(jnp.int32)
    for t in range(2):
        for k in range(3):
            for i in range(3):
                near[VELOCITY + t * 9 + k * 3 + i] = flow[t, k, side + i]
    fill_scalars(near_scalars, side, rho, temp, psi)
    items = []
    for t in range(2):
        for source in (rho, temp):
            items.append([source[t, x].astype(F32) for x in range(CX)])
    items += [[psi[k, x] for x in range(CX)] for k in range(5)]
    for number in range(STRIP_BLOCKS):
        message[number] = pack_strips(ops, items[8 * number : 8 * number + 8]).astype(BF16)
    band = band_of(ops.lane)
    for t in range(2):
        for k in range(3):
            block = jnp.zeros((ROWS, LANES), F32)
            for x in range(CX):
                moved = turn(flow[t, k, x].astype(F32), BAND * (x + 3) + 3)
                block = jnp.where(band == x + 3, moved, block)
            low[3 * t + k] = block
    merge_bands(ops, low, message, STRIP_BLOCKS)


def rows_kernel(flow, rho, temp, psi, grad_0, grad_1, lap_0, lap_1, psi_rate, psi_lap):
    ops = Ops()
    for t, grad_y, lap_y in ((0, grad_0, lap_0), (1, grad_1, lap_1)):
        for k in range(5):
            for x in range(CX):
                values = flow[t, k, x] if k < 3 else (rho if k == 3 else temp)[t, x]
                grad_y[k, x], lap = y_terms(ops, values.astype(F32))
                if k != 3:
                    lap_y[k, x] = lap
    for x in range(CX):
        along_y = flow[0, 1, x].astype(F32)
        for k in range(5):
            by_y, psi_lap[k, x] = y_terms(ops, psi[k, x])
            psi_rate[k, x] = along_y * by_y


def own_kernel(
    flow, rho, temp, psi, own_halo, grad_y_0, grad_y_1, lap_y_0, lap_y_1, rate_y, psi_lap_y,
    grad_0, grad_1, lap_0, lap_1, psi_rate, psi_lap,
    halos, psi_halos,
):
    ops = Ops()
    for t in range(2):
        place_halos(ops, t, own_halo, halos.at[t])
    strips = [own_halo[number].astype(F32) for number in range(STRIP_BLOCKS)]
    for k in range(5):
        for x in range(CX):
            psi_halos[k, x] = ops.strip(strips, SLOT_PSI + k, x)
    for t, grad_y, lap_y, grad_yz, lap_yz in (
        (0, grad_y_0, lap_y_0, grad_0, lap_0),
        (1, grad_y_1, lap_y_1, grad_1, lap_1),
    ):
        for k in range(5):
            for x in range(CX):
                values = flow[t, k, x] if k < 3 else (rho if k == 3 else temp)[t, x]
                by_z, both = z_terms(ops, values.astype(F32), halos[t, k, x])
                grad_yz[k, 0, x], grad_yz[k, 1, x] = grad_y[k, x], by_z
                if k != 3:
                    lap_yz[k, x] = lap_y[k, x] + both
    for x in range(CX):
        along_z = flow[0, 2, x].astype(F32)
        for k in range(5):
            by_z, both = z_terms(ops, psi[k, x], psi_halos[k, x])
            psi_rate[k, x] = rate_y[k, x] + along_z * by_z
            psi_lap[k, x] = psi_lap_y[k, x] + both


def token_kernel(far, _, out):
    out[...] = far[0].astype(F32)


def bands_kernel(own_low, near, far, _, message, low):
    ops = Ops()
    even = is_even()
    band = band_of(ops.lane)
    for t in range(2):
        for k in range(3):
            block = own_low[3 * t + k]
            for i in range(3):
                number = VELOCITY + t * 9 + k * 3 + i
                one, two = near[number].astype(F32), far[number].astype(F32)
                moved = turn(jnp.where(even, two, one), BAND * i + 3)
                block = jnp.where(band == i, moved, block)
                moved = turn(jnp.where(even, one, two), BAND * (7 + i) + 3)
                block = jnp.where(band == 7 + i, moved, block)
            low[3 * t + k] = block
    merge_bands(ops, low, message, 0)


def products_of(hat):
    velocity = [hat(k) for k in range(3)]
    strain = [hat(9 + number) for number in range(6)]
    diagonal = strain[0] * strain[0] + strain[1] * strain[1] + strain[2] * strain[2]
    other = strain[3] * strain[3] + strain[4] * strain[4] + strain[5] * strain[5]
    size = 4.0 * jnp.sqrt((2.0 / 256.0) * diagonal + ((4.0 / 256.0) * other + EPSILON))
    cross = 0.0
    square = 0.0
    for number, (a, b) in enumerate(PAIRS):
        leonard = hat(3 + number) - (1.0 / 16.0) * velocity[a] * velocity[b]
        model = hat(15 + number) - size * strain[number]
        weighted = WEIGHTS[number] * model if WEIGHTS[number] != 1.0 else model
        cross = cross + leonard * weighted
        square = square + model * weighted
    return cross, square


def widen(k, source, near, far, count, even, wide):
    for i in range(count):
        one, two = near(i), far(i)
        wide[k, 3 - count + i] = jnp.where(even, two, one)
        wide[k, 3 + CX + i] = jnp.where(even, one, two)
    for x in range(CX):
        wide[k, 3 + x] = source(x).astype(F32)


def widen_scalars(t, rho, temp, near, far, even, wide):
    for k, source in ((3, rho), (4, temp)):
        number = (k - 3) * 4 + 2 * t
        widen(
            k,
            lambda x: source[t, x],
            lambda i: near[number + i].astype(F32),
            lambda i: far[number + i].astype(F32),
            2, even, wide,
        )


def inner_products(
    ops, t, flow, near, far, grad_yz, lap_yz,
    sums, high, wide, grad_x, lap_velocity, sizes, fields, hats,
):
    even = is_even()
    valid = (ops.lane >= 3) & (ops.lane < LANES - 3)
    band = band_of(jnp.maximum(ops.lane - 2, 0))
    for k in range(3):
        widen(
            k,
            lambda x: flow[t, k, x],
            lambda i: near[VELOCITY + t * 9 + k * 3 + i].astype(F32),
            lambda i: far[VELOCITY + t * 9 + k * 3 + i].astype(F32),
            3, even, wide,
        )
    for x in range(-1, CX + 1):
        grad = [[None] * 3 for _ in range(3)]
        for k in range(3):
            center = wide[k, x + 3]
            xs = [wide[k, x + 3 + step] for step in (1, -1, 2, -2)]
            grad[0][k] = fourth(*xs)
            if 0 <= x < CX:
                grad_x[k, x] = grad[0][k]
                lap_velocity[k, x] = lap_yz[k, x] + (xs[0] + xs[1])
                grad[1][k], grad[2][k] = grad_yz[k, 0, x], grad_yz[k, 1, x]
            else:
                grad[1][k] = 0.5 * (ops.y_up(center) - ops.y_down(center))
                grad[2][k] = fourth(*(turn(center, -step) for step in (1, -1, 2, -2)))
        strain = strain_of(grad)
        size = size_of(strain)
        if 0 <= x < CX:
            sizes[x] = size
        velocity = [wide[k, x + 3] for k in range(3)]
        for number, values in enumerate(filter_fields(velocity, strain, size)):
            fields[number, x + 1] = values
    for x in range(CX):
        for number in range(21):
            along_x = fields[number, x] + fields[number, x + 2] + 2.0 * fields[number, x + 1]
            hats[number, x] = turn(along_x, 1) + turn(along_x, -1) + 2.0 * along_x
    for k in range(3):
        block = jnp.zeros((ROWS, LANES), F32)
        for q in range(CX + 6):
            block = jnp.where(band == q, turn(wide[k, q], BAND * q + 11), block)
        high[k] = block
    for x in range(CX):
        cross, square = products_of(lambda number: hats[number, x])
        sums[0, x] = jnp.where(valid, cross, 0.0)
        sums[1, x] = jnp.where(valid, square, 0.0)


def edge_products(ops, t, low, high, halo, sums, bands, spread):
    band = band_of(ops.lane)
    place = ops.lane - BAND * band
    from_low = place < 3
    from_high = (place == 11) | (place < 2)
    low_side = place < 7
    at_edge = ((place >= 3) & (place <= 5)) | ((place >= 8) & (place <= 10))
    for k in range(3):
        number = 3 * t + k
        far = halo[number // 2].astype(F32)
        shift = 6 * (number % 2)
        bands[0, k] = jnp.where(from_low, turn(far, -shift), low[number])
        bands[1, k] = jnp.where(from_high, turn(far, 8 - shift), high[k])
    for side in range(2):
        velocity = [bands[side, k] for k in range(3)]
        grad = [[None] * 3 for _ in range(3)]
        for k in range(3):
            center = velocity[k]
            grad[0][k] = fourth(*(turn(center, -BAND * step) for step in (1, -1, 2, -2)))
            grad[1][k] = 0.5 * (ops.y_up(center) - ops.y_down(center))
            grad[2][k] = fourth(*(turn(center, -step) for step in (1, -1, 2, -2)))
        strain = strain_of(grad)
        for number, values in enumerate(filter_fields(velocity, strain, size_of(strain))):
            if side == 0:
                spread[number] = values
            else:
                spread[number] = jnp.where(low_side, spread[number], values)
    for number in range(21):
        both = spread[number]
        spread[number] = turn(both, BAND) + turn(both, -BAND) + 2.0 * both
    for number in range(21):
        both = spread[number]
        spread[number] = turn(both, 1) + turn(both, -1) + 2.0 * both
    for part, values in enumerate(products_of(lambda number: spread[number])):
        values = jnp.where(at_edge, values, 0.0)
        for x in range(CX):
            sums[part, x] = sums[part, x] + jnp.where(band == x + 3, values, 0.0)


def add_columns(ops, total, first_lane, planes, scale=1.0):
    for x in range(CX):
        value = scale * jnp.sum(planes(x), axis=1, keepdims=True)
        total = jnp.where(ops.lane == first_lane + x, value, total)
    return total


def add_parts(ops, block, total):
    upper = total.astype(BF16).astype(F32)
    rest = total - upper
    middle = rest.astype(BF16).astype(F32)
    for number, part in enumerate((upper, middle, rest - middle)):
        block = jnp.where(ops.lane >> 5 == 1 + number, turn(part, 32 * (1 + number)), block)
    return block


def span_total(add_other, columns, other):
    total = columns[...]
    if add_other:
        parts = other.astype(F32)
        total = total + ((turn(parts, -32) + turn(parts, -64)) + turn(parts, -96))
    return total


def psi_terms(psi_wide, rate_yz, lap_yz, velocity, x):
    rates, laps = [], []
    for k in range(5):
        xs = [psi_wide[k, x + 3 + step] for step in (1, -1, 2, -2)]
        rates.append(rate_yz[k, x] + velocity * fourth(*xs))
        laps.append(lap_yz[k, x] + (xs[0] + xs[1]))
    return rates, laps


def inner_kernel(
    flow, near, far, grad_yz, lap_yz,
    sums, high, wide, grad_x, lap_velocity, sizes,
    fields, hats,
):
    inner_products(
        Ops(), 0, flow, near, far, grad_yz, lap_yz,
        sums, high, wide, grad_x, lap_velocity, sizes, fields, hats,
    )


def first_kernel(
    _, products, rho, temp, psi, near, far, velocity, grad_x, lap_velocity, sizes,
    grad_yz, lap_yz, psi_rate, psi_lap,
    first, second, message, columns,
    wide, psi_wide, work,
):
    ops = Ops()
    even = is_even()
    for k in range(3):
        for x in range(CX):
            wide[k, x + 3] = velocity[k, x + 3]
    widen_scalars(0, rho, temp, near, far, even, wide)
    for k in range(5):
        widen(
            k,
            lambda x: psi[k, x],
            lambda i: near[PSI + k * 2 + i].astype(F32),
            lambda i: far[PSI + k * 2 + i].astype(F32),
            2, even, psi_wide,
        )
    for x in range(CX):
        terms = state_terms(wide, grad_x, grad_yz, lap_velocity, lap_yz, sizes, x)
        rates, laps = psi_terms(psi_wide, psi_rate, psi_lap, terms[0][0], x)
        new, slope, sensitivity = affine_update(
            terms, [psi[k, x] for k in range(5)], rates, laps
        )
        for k in range(5):
            first[k, x] = new[k]
            second[k, x] = slope[k]
        work[x] = sensitivity
    total = add_columns(ops, products[...], 16, lambda x: work[x])
    columns[...] = total
    items = [[part[k, x] for x in range(CX)] for part in (first, second) for k in range(5)]
    message[0] = pack_strips(ops, items[:8]).astype(BF16)
    message[1] = add_parts(ops, pack_strips(ops, items[8:]), total).astype(BF16)


def edge_kernel(low, high, halo, inner, columns, bands, spread, sums):
    ops = Ops()
    for part in range(2):
        for x in range(CX):
            sums[part, x] = inner[part, x]
    edge_products(ops, 0, low, high, halo, sums, bands, spread)
    total = jnp.zeros((ROWS, LANES), F32)
    for part in range(2):
        total = add_columns(ops, total, 4 * part, lambda x: sums[part, x], 1.0 / 256.0)
    columns[...] = total


def later_kernel(
    flow, rho, temp, near, far, near_scalars, far_scalars,
    grad_yz, lap_yz, low, halo, first, second,
    wide, grad_x, lap_velocity, sizes, message, columns,
    high, fields, hats, work, bands, spread, sums,
):
    ops = Ops()
    inner_products(
        ops, 1, flow, near, far, grad_yz, lap_yz,
        sums, high, wide, grad_x, lap_velocity, sizes, fields, hats,
    )
    widen_scalars(1, rho, temp, near_scalars, far_scalars, is_even(), wide)
    edge_products(ops, 1, low, high, halo, sums, bands, spread)
    for x in range(CX):
        _, _, lap, size, inv_rho = state_terms(
            wide, grad_x, grad_yz, lap_velocity, lap_yz, sizes, x
        )
        size_rho = size * inv_rho
        for part, source in enumerate((first, second)):
            total = lap[0] * source[0, x] + lap[1] * source[1, x] + lap[2] * source[2, x]
            work[part, x] = size_rho * (
                total + (1.0 / PRANDTL_TURB) * (lap[4] * source[4, x])
            )
    total = jnp.zeros((ROWS, LANES), F32)
    for part in range(2):
        total = add_columns(ops, total, 8 + 4 * part, lambda x: sums[part, x], 1.0 / 256.0)
        total = add_columns(ops, total, 20 + 4 * part, lambda x: work[part, x])
    columns[...] = total
    message[0] = add_parts(ops, jnp.zeros((ROWS, LANES), F32), total).astype(BF16)


def coefficients(ops, total):
    return total / (turn(total, -4) + EPSILON)


def middle_kernel(add_other, first, second, columns, other, psi, far, coef_first):
    ops = Ops()
    coef = coefficients(ops, span_total(add_other, columns, other[1]))
    for x in range(CX):
        coef_first[x] = jnp.broadcast_to(coef[:, x : x + 1], (ROWS, LANES))
    for x in range(CX):
        for k in range(5):
            psi[k, x] = first[k, x] + coef_first[x] * second[k, x]
    side = 1 - is_even().astype(jnp.int32)
    for k in range(5):
        for i in range(2):
            far[k, i] = psi[k, 2 * side + i].astype(BF16)


def base_kernel(
    add_other, span_cells,
    wide, grad_x, lap_velocity, sizes, grad_yz, lap_yz, psi, coef_first,
    columns, other, later, later_other,
    base, drift, spread, coef_grad, near,
    psi_halos, psi_wide, coef_planes, psi_rate, psi_lap,
):
    ops = Ops()
    side = is_even().astype(jnp.int32)
    for k in range(5):
        for i in range(2):
            near[k, i] = psi[k, 2 * side + i].astype(BF16)
    strips = [other[number].astype(F32) for number in range(2)]
    for k in range(5):
        for x in range(CX):
            psi_halos[k, x] = ops.strip(strips, k, x)
    total = span_total(add_other, columns, other[1]) + span_total(
        add_other, later, later_other[0]
    )
    coef = coefficients(ops, total)
    after = total + turn(coef, 20) * turn(total, -4)
    grads = jnp.where(ops.lane < 20, total, after) * (1.0 / span_cells)
    turned = jnp.concatenate([grads] * (LANES // ROWS), axis=0).T
    for t in range(2):
        coef_grad[t] = turned[16 + 4 * t : 20 + 4 * t, :ROWS]
    for x in range(CX):
        coef_planes[x] = jnp.broadcast_to(coef[:, 8 + x : 9 + x], (ROWS, LANES))
    for k in range(5):
        for x in range(CX):
            psi_halos[k, x] = psi_halos[k, x] + coef_first[x] * ops.strip(strips, 5 + k, x)
    zero = jnp.zeros((ROWS, LANES), F32)
    for k in range(5):
        for i in range(2):
            psi_wide[k, 1 + i] = zero
            psi_wide[k, 3 + CX + i] = zero
        for x in range(CX):
            psi_wide[k, 3 + x] = psi[k, x]
    for x in range(CX):
        for k in range(5):
            by_y, lap = y_terms(ops, psi[k, x])
            by_z, both = z_terms(ops, psi[k, x], psi_halos[k, x])
            psi_rate[k, x] = wide[1, x + 3] * by_y + wide[2, x + 3] * by_z
            psi_lap[k, x] = lap + both
    for x in range(CX):
        terms = state_terms(wide, grad_x, grad_yz, lap_velocity, lap_yz, sizes, x)
        center = terms[0]
        rates, laps = psi_terms(psi_wide, psi_rate, psi_lap, center[0], x)
        new, slope, _ = affine_update(terms, [psi[k, x] for k in range(5)], rates, laps)
        for k in range(5):
            base[k, x] = new[k] + coef_planes[x] * slope[k]
        size, inv_rho = terms[3:]
        drift[x] = TIME_STEP * center[0]
        if x in (0, CX - 1):
            eddy = coef_planes[x] * size
            scaled = TIME_STEP * inv_rho
            spread[x // (CX - 1), 0] = scaled * (NU_MOL + eddy)
            spread[x // (CX - 1), 1] = scaled * (
                NU_MOL / PRANDTL + (1.0 / PRANDTL_TURB) * eddy
            )


def widen_kernel(far, out):
    for k in range(5):
        for i in range(2):
            out[k, i] = far[k, i].astype(F32)


def last_kernel(base, drift, spread, near_psi, far_psi, out_far, out, sems):
    even = is_even()
    copies = []
    for k in range(5):
        ones = [near_psi[k, i].astype(F32) for i in range(2)]
        twos = [far_psi[k, i].astype(F32) for i in range(2)]
        far, near = (jnp.where(even, two, one) for one, two in zip(ones, twos))
        after, beyond = (jnp.where(even, one, two) for one, two in zip(ones, twos))
        low = drift[0] * ((1.0 / 12.0) * far - (2.0 / 3.0) * near)
        high = drift[CX - 1] * ((2.0 / 3.0) * after - (1.0 / 12.0) * beyond)
        if k != 3:
            kind = 1 if k == 4 else 0
            low = low + spread[0, kind] * near
            high = high + spread[1, kind] * after
        out[k, 0] = base[k, 0] + low
        out[k, 1] = base[k, 1] + drift[1] * ((1.0 / 12.0) * near)
        out[k, CX - 2] = base[k, CX - 2] - drift[CX - 2] * ((1.0 / 12.0) * after)
        out[k, CX - 1] = base[k, CX - 1] + high
        copies.append(pltpu.make_async_copy(out.at[k], out_far.at[k], sems.at[k]))
        copies[k].start()
    for copy in copies:
        copy.wait()


def ring(axis):
    count = lax.axis_size(axis)
    forward = [(i, (i + 1) % count) for i in range(count)]
    return forward, [(target, source) for source, target in forward]


def pairs():
    count = lax.axis_size("gx")
    if count % 2:
        raise ValueError("odd gx")
    inside = [(i, i ^ 1) for i in range(count)]
    across = [(i, (i + 1 if i % 2 else i - 1) % count) for i in range(count)]
    return inside, across


def span_edges(message, strips):
    forward, backward = ring("gz")
    before = lax.ppermute(message, "gz", forward)
    if lax.axis_size("gz") == 2:
        return before
    after = lax.ppermute(message, "gz", backward)
    lane = lax.broadcasted_iota(jnp.int32, message.shape, 2)
    number = lax.broadcasted_iota(jnp.int32, message.shape, 0)
    low = jnp.where(number < strips, lane % STRIP < 2, lane % 6 < 3)
    return jnp.where(low, before, after)


def shape_of(dims, kind=F32):
    return jax.ShapeDtypeStruct(dims + (ROWS, LANES), kind)


def whole(count):
    return [pl.BlockSpec(memory_space=pltpu.VMEM)] * count


def scratch(*dims):
    return [pltpu.VMEM(d + (ROWS, LANES), F32) for d in dims]


def call(kernel, name, inputs, outputs, operations, buffers=(), in_specs=None, out_specs=None):
    inputs = list(inputs)
    if in_specs:
        inputs[:4] = [
            pltpu.with_memory_space_constraint(a, pltpu.MemorySpace.HBM) for a in inputs[:4]
        ]
    size = sum(math.prod(a.shape) * a.dtype.itemsize for a in list(inputs) + list(outputs))
    return pl.pallas_call(
        kernel,
        in_specs=in_specs or whole(len(inputs)),
        out_specs=out_specs or whole(len(outputs)),
        out_shape=list(outputs),
        scratch_shapes=list(buffers),
        compiler_params=pltpu.CompilerParams(vmem_limit_bytes=8 * 2**20),
        cost_estimate=pl.CostEstimate(
            flops=operations, bytes_accessed=size, transcendentals=0
        ),
        name=name,
    )(*inputs)


def span_sums(columns):
    if lax.axis_size("gz") == 2:
        return columns
    return lax.psum(columns, "gz")


def local(flow_far, rho_far, temp_far, psi_far):
    inside, across = pairs()
    add_other = lax.axis_size("gz") == 2
    field, planes, edges = shape_of((5, CX)), shape_of((5, CX + 6)), shape_of((5, 2), BF16)
    slopes = shape_of((5, 2, CX))
    inputs = (flow_far, rho_far, temp_far, psi_far)
    stay = [pl.BlockSpec(memory_space=pltpu.MemorySpace.HBM)] * 4
    far, far_scalars, flow, rho, temp, psi = call(
        message_kernel,
        "message",
        inputs,
        [
            shape_of((SCALARS,), BF16),
            shape_of((SCALAR_PLANES,), BF16),
            shape_of((2, 3, CX), BF16),
            shape_of((2, CX), BF16),
            shape_of((2, CX), BF16),
            field,
        ],
        1_000_000,
        [pltpu.SemaphoreType.DMA((5,))],
        stay,
    )
    far = lax.ppermute(far, "gx", across)
    near, near_scalars, message, own_low = call(
        pack_kernel,
        "pack",
        (flow, rho, temp, psi),
        [
            shape_of((SCALARS,), BF16),
            shape_of((SCALAR_PLANES,), BF16),
            shape_of((STRIP_BLOCKS + BAND_BLOCKS,), BF16),
            shape_of((6,)),
        ],
        2_000_000,
    )
    far_scalars = lax.ppermute(far_scalars, "gx", across)
    near = lax.ppermute(near, "gx", inside)
    near_scalars = lax.ppermute(near_scalars, "gx", inside)
    own_halo = span_edges(message, STRIP_BLOCKS)
    rows = call(
        rows_kernel,
        "rows",
        (flow, rho, temp, psi),
        [field] * 6,
        3_000_000,
    )
    grad_0, grad_1, lap_0, lap_1, psi_rate, psi_lap = call(
        own_kernel,
        "own",
        (flow, rho, temp, psi, own_halo, *rows),
        [slopes, slopes, field, field, field, field],
        5_000_000,
        scratch((2, 5, CX), (5, CX)),
    )
    (token,) = call(token_kernel, "token", (far, rows[5]), [shape_of(())], 100_000)
    message, low = call(
        bands_kernel,
        "bands",
        (own_low, near, far, token),
        [shape_of((BAND_BLOCKS,), BF16), shape_of((6,))],
        1_000_000,
    )
    halo = span_edges(message, 0)
    inner, high, velocity, grad_x, lap_velocity, sizes = call(
        inner_kernel,
        "inner",
        (flow, near, far, grad_0, lap_0),
        [
            shape_of((2, CX)), shape_of((3,)), shape_of((3, CX + 6)),
            shape_of((3, CX)), shape_of((3, CX)), shape_of((CX,)),
        ],
        20_000_000,
        scratch((21, CX + 2), (21, CX)),
    )
    (products,) = call(
        edge_kernel,
        "edge",
        (low, high, halo, inner),
        [shape_of(())],
        20_000_000,
        scratch((2, 3), (21,), (2, CX)),
    )
    (token,) = call(token_kernel, "later_token", (far_scalars, products), [shape_of(())], 100_000)
    first, second, message, columns = call(
        first_kernel,
        "first",
        (
            token, products, rho, temp, psi, near_scalars, far_scalars,
            velocity, grad_x, lap_velocity, sizes, grad_0, lap_0, psi_rate, psi_lap,
        ),
        [field, field, shape_of((2,), BF16), shape_of(())],
        10_000_000,
        scratch((5, CX + 6), (5, CX + 6), (CX,)),
    )
    other = span_edges(message, 2)
    columns = span_sums(columns)
    wide, grad_x, lap_velocity, sizes, message, later = call(
        later_kernel,
        "later",
        (
            flow, rho, temp, near, far, near_scalars, far_scalars,
            grad_1, lap_1, low, halo, first, second,
        ),
        [
            planes, shape_of((3, CX)), shape_of((3, CX)), shape_of((CX,)),
            shape_of((1,), BF16), shape_of(()),
        ],
        20_000_000,
        scratch((3,), (21, CX + 2), (21, CX), (2, CX), (2, 3), (21,), (2, CX)),
    )
    later_other = span_edges(message, 1)
    later = span_sums(later)
    first, later = lax.optimization_barrier((first, later))
    psi, far, coef_first = call(
        functools.partial(middle_kernel, add_other),
        "middle",
        (first, second, columns, other),
        [field, edges, shape_of((CX,))],
        1_000_000,
    )
    far = lax.ppermute(far, "gx", across)
    base, drift, spread, coef_grad, near = call(
        functools.partial(base_kernel, add_other, LANES * lax.axis_size("gz")),
        "base",
        (
            wide, grad_x, lap_velocity, sizes, grad_1, lap_1, psi, coef_first,
            columns, other, later, later_other,
        ),
        [
            field, shape_of((CX,)), shape_of((2, 2)),
            jax.ShapeDtypeStruct((2, CX, ROWS), F32), edges,
        ],
        15_000_000,
        scratch((5, CX), (5, CX + 6), (CX,), (5, CX), (5, CX)),
    )
    near = lax.ppermute(near, "gx", inside)
    (far,) = call(widen_kernel, "widen", (far,), [shape_of((5, 2))], 100_000)
    (out,) = call(
        last_kernel,
        "last",
        (base, drift, spread, near, far),
        [field],
        1_000_000,
        scratch((5, CX)) + [pltpu.SemaphoreType.DMA((5,))],
        out_specs=stay[:1],
    )
    return out, coef_grad


def solution(mesh):
    return jax.shard_map(
        local,
        mesh=mesh,
        in_specs=(
            P(None, None, "gx", None, "gz"),
            P(None, "gx", None, "gz"),
            P(None, "gx", None, "gz"),
            P(None, "gx", None, "gz"),
        ),
        out_specs=(P(None, "gx", None, "gz"), P(None, "gx", None)),
        check_vma=False,
    )
```
